32 devices in a mesh: row: 4 (over y, x), col: 8 (over z, core).
Axes of the slice: x: 2, y: 2, z: 4, core: 2. Of those that a mesh axis runs over, the one named last changes fastest.
Arguments:
- tokens: bfloat16 [8192, 2048], P('row', 'col'), may hold values from -6 to 6
- gain_attn: float32 [2048], P('col'), may hold values from 0.5 to 1.5
- gain_ffn: float32 [2048], P('col'), may hold values from 0.5 to 1.5
- gain_query: float32 [128], replicated, may hold values from 0.5 to 1.5
- gain_key: float32 [128], replicated, may hold values from 0.5 to 1.5
- w_query: bfloat16 [2048, 1024], P('col', 'row'), may hold values from -0.125 to 0.125
- w_key: bfloat16 [2048, 1024], P('col', 'row'), may hold values from -0.125 to 0.125
- w_value: bfloat16 [2048, 1024], P('col', 'row'), may hold values from -0.125 to 0.125
- w_out: bfloat16 [1024, 2048], P('col', 'row'), may hold values from -3 to 3
- w_router: bfloat16 [2048, 32], P('col', 'row'), may hold values from -0.0625 to 0.0625
- w_gate: bfloat16 [32, 2048, 1024], P('col', 'row'), may hold values from -0.125 to 0.125
- w_up: bfloat16 [32, 2048, 1024], P('col', 'row'), may hold values from -0.125 to 0.125
- w_down: bfloat16 [32, 1024, 2048], P('col', None, 'row'), may hold values from -0.75 to 0.75
- routes: int32 [8192, 8], P('row'), may hold values from 0 to 31, all different within a row; in each aligned block of 1024 rows (0 to 1023, 1024 to 2047, ...) at most 512 rows name the same one
- lengths: int32 [8, 4], P('row'), may hold values from 1 to 512, 1024 in all within a row
- cotangent: bfloat16 [8192, 2048], P('row', 'col'), may hold values from -6 to 6
Outputs:
- mixed: bfloat16 [8192, 2048], P('row', 'col')
- input_grad: float32 [8192, 2048], P('row', 'col')
- grad_gain_attn: float32 [2048], P('col')
- grad_gain_ffn: float32 [2048], P('col')
- grad_gain_query: float32 [128], replicated
- grad_gain_key: float32 [128], replicated
- grad_query: float32 [2048, 1024], P('col', 'row')
- grad_key: float32 [2048, 1024], P('col', 'row')
- grad_value: float32 [2048, 1024], P('col', 'row')
- grad_out: float32 [1024, 2048], P('col', 'row')
- grad_router: float32 [2048, 32], P('col', 'row')
- grad_gate: float32 [32, 2048, 1024], P('col', 'row')
- grad_up: float32 [32, 2048, 1024], P('col', 'row')
- grad_down: float32 [32, 1024, 2048], P('col', None, 'row')
The draws below stay inside these ranges and needn't reach their ends.
Inputs may be any that keep to these rules, and one draw needn't show every extreme that they name: `routes`: in each aligned block of 1024 rows (one group), each row names 8 different experts and no expert is named more than 512 times; in every draw some expert is named exactly 512 times in a block. `lengths`: each row sums to 1024; the last entry counts padded rows; the largest entry of each row is exactly 512.
All inputs are finite; a program needn't handle non-finite values.
Results may differ from the reference program's by a relative error of at most 0.02.
Values may be sent and summed in bfloat16 or wider, within the bound.
A program may use at most 384 MiB of HBM per device.

```python
import math
import jax
import jax.numpy as jnp
import numpy as np
from jax import lax

D = 2048
HEAD = 128
HEADS = 8
HD = 1024
FF = 1024
EXPERTS = 32
TOPK = 8
GROUP_TOK = 1024
GROUPS = 8
TOKENS = 8192
CAP = 512


def level_of(own_key, shape, cuts, smallest, high):
    factor_of, own = 1.0, jax.random.fold_in(own_key, 6)
    for axis_at, parts in cuts:
        steps = jnp.exp(jax.random.uniform(jax.random.fold_in(own, axis_at), (parts,), jnp.float32, smallest / len(cuts), high / len(cuts)))
        factor_of = factor_of * jnp.repeat(steps, shape[axis_at] // parts).reshape([-1 if axis == axis_at else 1 for axis in range(len(shape))])
    return factor_of


def split_up(amount, total, most, slope):
    portions = [(1 << 20) // math.isqrt(standing ** slope) + 1 for standing in range(2, amount + 1)]
    surplus, given = total - most - (amount - 1), [1] * (amount - 1)
    while surplus > 0:
        free = [i for i in range(amount - 1) if given[i] < most]
        pool, left = sum([portions[i] for i in free]), surplus
        for i in free:
            extra = min(most - given[i], max(1, left * portions[i] // pool), surplus)
            given[i] = given[i] + extra
            surplus = surplus - extra
    return np.array([most] + given)


def ragged_sizes(key, amount, total, bound, slope):
    if amount == 2:
        one = jax.random.randint(key, (), max(1, total - bound), min(bound, total - 1) + 1)
        return jnp.stack([one, total - one])
    sizes = jnp.asarray(split_up(amount, total, bound, slope), jnp.int32)
    couples = (amount - 1) // 2
    giver, taker = sizes[1:1 + 2 * couples:2], sizes[2:2 + 2 * couples:2]
    slack = jnp.minimum(giver - 1, bound - taker)
    passed = jax.random.randint(jax.random.fold_in(key, 1), (couples,), 0, 1 << 20) % (slack + 1)
    sizes = sizes.at[1:1 + 2 * couples:2].set(giver - passed).at[2:2 + 2 * couples:2].set(taker + passed)
    return sizes[jax.random.permutation(jax.random.fold_in(key, 2), amount)]


def deal_out(own_key, own, number, rows, amount, top, reach, skew):
    sequence = jax.random.permutation(own_key, amount)
    crowded, common = shares(amount, rows * top, reach, skew, True), shares(amount, rows * top, reach, skew, False)
    places = jnp.arange(amount)

    def named(tallies, turn):
        used = int((tallies > 0).sum())
        fixed = max(1, used // 4)
        shifted = fixed + (places - fixed + turn * (used - fixed)) % max(1, amount - fixed)
        return jnp.zeros((amount,), jnp.int32).at[sequence[jnp.where(places < fixed, places, shifted)]].set(jnp.asarray(tallies, jnp.int32))

    tallies = jnp.where(number % 4 == 0, named(crowded, number // 4), named(common, number - number // 4 - 1))
    mixed = jax.random.permutation(jax.random.fold_in(own, 3), amount)
    giver, taker = mixed[0:amount // 2 * 2:2], mixed[1:amount // 2 * 2:2]
    slack = jnp.minimum(tallies[giver] - 1, reach - tallies[taker]) // 2
    slack = jnp.where((giver == sequence[0]) | (taker == sequence[0]) | (tallies[taker] == 0), 0, jnp.maximum(slack, 0))
    shifted = jax.random.randint(jax.random.fold_in(own, 4), (amount // 2,), 0, 1 << 20) % (slack + 1)
    tallies = tallies.at[giver].add(-shifted).at[taker].add(shifted)
    members = jnp.searchsorted(jnp.cumsum(tallies), jnp.arange(rows * top), side="right").astype(jnp.int32)
    listing = members.reshape(top, rows).T
    listing = listing[jax.random.permutation(jax.random.fold_in(own, 1), rows)]
    turn = jax.random.randint(jax.random.fold_in(own, 2), (rows, 1), 0, top)
    return jnp.take_along_axis(listing, (jnp.arange(top)[None, :] + turn) % top, axis=1)


def shares(amount, total, bound, slope, full):
    loads = [(1 << 20) // math.isqrt(rank ** slope) + 1 for rank in range(1, amount + 1)]
    largest = bound if full else min(bound, max(-(-total // amount), total * loads[0] // sum(loads)))
    least = 1 if total - largest >= amount - 1 else 0
    counts, spare = [largest] + [least] * (amount - 1), total - largest - least * (amount - 1)
    while spare > 0:
        candidates = [i for i in range(1, amount) if counts[i] < largest] or [i for i in range(1, amount) if counts[i] < bound]
        mass, budget = sum([loads[i] for i in candidates]), spare
        for i in candidates:
            addition = min(bound - counts[i], max(1, budget * loads[i] // mass), spare)
            counts[i] = counts[i] + addition
            spare = spare - addition
    return np.array(counts)


def centred(key, dims, deviation, limit, split=(), kind=jnp.bfloat16):
    entries = deviation * jax.random.normal(key, dims, jnp.float32)
    if split:
        entries = entries * level_of(key, dims, split, -0.22, 0.18)
    return jnp.clip(entries, -limit, limit).astype(kind)


def setup_inputs(seed: int = 0) -> dict:
    seeds = jax.random.split(jax.random.key(seed), 17)
    tokens = centred(seeds[0], (TOKENS, D), 1.0, 6.0, ((0, 4), (1, 8)))
    gain_attn = jnp.clip(1.0 + 0.1 * jax.random.normal(seeds[1], (D,), jnp.float32), 0.5, 1.5)
    gain_ffn = jnp.clip(1.0 + 0.1 * jax.random.normal(seeds[2], (D,), jnp.float32), 0.5, 1.5)
    gain_query = jnp.clip(1.0 + 0.1 * jax.random.normal(seeds[3], (HEAD,), jnp.float32), 0.5, 1.5)
    gain_key = jnp.clip(1.0 + 0.1 * jax.random.normal(seeds[4], (HEAD,), jnp.float32), 0.5, 1.5)
    w_query = centred(seeds[5], (D, HD), D ** -0.5, 0.125, ((0, 8), (1, 4)))
    w_key = centred(seeds[6], (D, HD), D ** -0.5, 0.125, ((0, 8), (1, 4)))
    w_value = centred(seeds[7], (D, HD), D ** -0.5, 0.125, ((0, 8), (1, 4)))
    w_out = centred(seeds[8], (HD, D), (4 * HD // GROUP_TOK) ** -0.5, 3.0, ((0, 8), (1, 4)))
    w_router = centred(seeds[9], (D, EXPERTS), (4 * D) ** -0.5, 0.0625, ((0, 8), (1, 4)))
    w_gate = centred(seeds[10], (EXPERTS, D, FF), D ** -0.5, 0.125, ((0, 8), (1, 4)))
    w_up = centred(seeds[11], (EXPERTS, D, FF), D ** -0.5, 0.125, ((0, 8), (1, 4)))
    w_down = centred(seeds[12], (EXPERTS, FF, D), (FF // 16) ** -0.5, 0.75, ((0, 8), (2, 4)))
    routes_keys = jax.random.split(jax.random.fold_in(seeds[13], 1), TOKENS // GROUP_TOK)
    routes_turns = jax.random.permutation(jax.random.fold_in(seeds[13], 3), TOKENS // GROUP_TOK)
    routes = jax.vmap(lambda own, number: deal_out(jax.random.fold_in(seeds[13], 2), own, number, GROUP_TOK, EXPERTS, TOPK, CAP, 1))(routes_keys, routes_turns).reshape((TOKENS, TOPK))
    lengths = jax.vmap(lambda own: ragged_sizes(own, 4, GROUP_TOK, GROUP_TOK // 2, 1))(jax.random.split(seeds[14], GROUPS)).reshape((GROUPS, 4)).astype(jnp.int32)
    cotangent = centred(seeds[15], (TOKENS, D), 1.0, 6.0, ((0, 4), (1, 8)))
    return {"tokens": tokens, "gain_attn": gain_attn, "gain_ffn": gain_ffn, "gain_query": gain_query, "gain_key": gain_key, "w_query": w_query, "w_key": w_key, "w_value": w_value, "w_out": w_out, "w_router": w_router, "w_gate": w_gate, "w_up": w_up, "w_down": w_down, "routes": routes, "lengths": lengths, "cotangent": cotangent}


EPSILON = 1e-06
ROPE_BASE = 10000.0
MASKED = -1e+30

@jax.custom_vjp
def low(v):
    return lax.optimization_barrier(v.astype(jnp.bfloat16)).astype(jnp.float32)

@jax.custom_vjp
def low_back(v):
    return v

def low_keep(v):
    return (low(v), None)

def low_pass(kept, grad):
    return (grad,)

def back_keep(v):
    return (v, None)

def back_low(kept, grad):
    return (low(grad),)
low.defvjp(low_keep, low_pass)
low_back.defvjp(back_keep, back_low)

def inverse_rms(values):
    return lax.rsqrt(lax.optimization_barrier(jnp.mean(values * values, -1, keepdims=True)) + EPSILON)

def rotary(values, position):
    half = values.shape[-1] // 2
    inverse = jnp.exp(-math.log(ROPE_BASE) * 2.0 / values.shape[-1] * jnp.arange(half, dtype=jnp.float32))
    angles = position[:, None] * inverse[None, :]
    cosine = jnp.cos(angles)[:, None, :]
    sine = jnp.sin(angles)[:, None, :]
    first = values[..., :half]
    second = values[..., half:]
    return jnp.concatenate([first * cosine - second * sine, second * cosine + first * sine], -1)

def layout(lengths_row, group):
    ends = jnp.cumsum(lengths_row).astype(jnp.int32)
    starts = (ends - lengths_row).astype(jnp.int32)
    row_index = jnp.arange(group, dtype=jnp.int32)
    segment = lax.optimization_barrier(jnp.sum((row_index[:, None] >= ends[None, :]).astype(jnp.int32), 1))
    member = segment[:, None] == jnp.arange(lengths_row.shape[0], dtype=jnp.int32)[None, :]
    position = (row_index - lax.optimization_barrier(jnp.sum(jnp.where(member, starts[None, :], 0), 1))).astype(jnp.float32)
    live = (segment < lengths_row.shape[0] - 1).astype(jnp.float32)
    return (segment, position, live)

def slot_table(route_rows, experts, capacity):
    flat_experts = route_rows.reshape(-1).astype(jnp.int32)
    hits = (flat_experts[:, None] == jnp.arange(experts, dtype=jnp.int32)[None, :]).astype(jnp.int32)
    before = jnp.cumsum(hits, 0) - hits
    place = lax.optimization_barrier(jnp.sum(before * hits, 1))
    flat = (flat_experts * capacity + place).astype(jnp.int32)
    pairs = flat_experts.shape[0]
    slot_token = jnp.zeros((experts * capacity,), jnp.int32).at[flat].set(jnp.arange(pairs, dtype=jnp.int32) // route_rows.shape[1])
    slot_live = jnp.zeros((experts * capacity,), jnp.float32).at[flat].set(1.0)
    return (flat, slot_token, slot_live)

def forward(inputs, params, segment, position, route_rows, flat, slot_token, slot_live):
    highest = lax.Precision.HIGHEST
    gain_attn, gain_ffn, gain_query, gain_key, w_query, w_key, w_value, w_out, w_router, w_gate, w_up, w_down = params
    normed = low(inputs * inverse_rms(inputs) * gain_attn)
    query_pre = low_back(jnp.dot(normed, w_query, precision=highest)).reshape(GROUP_TOK, HEADS, HEAD)
    key_pre = low_back(jnp.dot(normed, w_key, precision=highest)).reshape(GROUP_TOK, HEADS, HEAD)
    value_pre = low_back(jnp.dot(normed, w_value, precision=highest)).reshape(GROUP_TOK, HEADS, HEAD)
    queries = low(rotary(query_pre * inverse_rms(query_pre) * gain_query, position))
    keys_rot = low(rotary(key_pre * inverse_rms(key_pre) * gain_key, position))
    values_low = low(value_pre)
    raw = jnp.einsum('qhd,khd->hqk', queries, keys_rot, precision=highest) * HEAD ** (-0.5)
    same = (segment[:, None] == segment[None, :])[None]
    scores = jnp.where(same, low_back(raw), MASKED)
    probs = low(jax.nn.softmax(scores, -1))
    attended = low_back(low(jnp.einsum('hqk,khd->qhd', probs, values_low, precision=highest))).reshape(GROUP_TOK, HEADS * HEAD)
    branch = low_back(jnp.dot(attended, w_out, precision=highest))
    hidden = inputs + branch
    normed_ffn = low(hidden * inverse_rms(hidden) * gain_ffn)
    logits = low_back(jnp.dot(normed_ffn, w_router, precision=highest))
    gates = jax.nn.softmax(jnp.take_along_axis(logits, route_rows, 1), -1)
    expert_in = low_back(normed_ffn[slot_token] * slot_live[:, None]).reshape(EXPERTS, CAP, D)
    gate_pre = low_back(jnp.einsum('ecd,edf->ecf', expert_in, w_gate, precision=highest))
    up_pre = low_back(jnp.einsum('ecd,edf->ecf', expert_in, w_up, precision=highest))
    inner = low(jax.nn.silu(gate_pre) * up_pre)
    expert_out = low(low_back(jnp.einsum('ecf,efd->ecd', inner, w_down, precision=highest))).reshape(EXPERTS * CAP, D)
    picked = expert_out[flat].reshape(GROUP_TOK, TOPK, D)
    return hidden + lax.optimization_barrier(jnp.sum(gates[:, :, None] * picked, 1))

def reference(tokens, gain_attn, gain_ffn, gain_query, gain_key, w_query, w_key, w_value, w_out, w_router, w_gate, w_up, w_down, routes, lengths, cotangent):
    params = tuple((item.astype(jnp.float32) for item in (gain_attn, gain_ffn, gain_query, gain_key, w_query, w_key, w_value, w_out, w_router, w_gate, w_up, w_down)))
    inputs_all = tokens.astype(jnp.float32).reshape(GROUPS, GROUP_TOK, D)
    grads_all = cotangent.astype(jnp.float32).reshape(GROUPS, GROUP_TOK, D)
    routes_all = routes.reshape(GROUPS, GROUP_TOK, TOPK)

    def step(totals, item):
        inputs, upstream, route_rows, lengths_row = item
        segment, position, live = layout(lengths_row, GROUP_TOK)
        flat, slot_token, slot_live = slot_table(route_rows, EXPERTS, CAP)

        def apply(values, weights):
            return forward(values, weights, segment, position, route_rows, flat, slot_token, slot_live)
        result, pull = jax.vjp(apply, inputs, params)
        input_grad, param_grads = pull(upstream * live[:, None])
        totals = jax.tree.map(jnp.add, totals, param_grads)
        return (totals, (result.astype(jnp.bfloat16), input_grad))
    zeros = jax.tree.map(jnp.zeros_like, params)
    totals, (mixed, input_grad) = lax.scan(step, zeros, (inputs_all, grads_all, routes_all, lengths))
    return (mixed.reshape(TOKENS, D), input_grad.reshape(TOKENS, D), totals[0], totals[1], totals[2], totals[3], totals[4], totals[5], totals[6], totals[7], totals[8], totals[9], totals[10], totals[11])
```

```python
import functools
import math

import jax
import jax.numpy as jnp
from jax import lax
from jax.experimental import pallas as pl
from jax.experimental.pallas import tpu as pltpu
from jax.sharding import PartitionSpec as P

EPSILON = 1e-06
ROPE_BASE = 10000.0
MASKED = -1e30
F32 = jnp.float32
BF16 = jnp.bfloat16
VMEM_LIMIT = 60 * 1024 * 1024


def inverse_rms(values):
    return lax.rsqrt(jnp.mean(values * values, -1, keepdims=True) + EPSILON)


def rope_tables(position, head):
    half = head // 2
    inverse = jnp.exp(-math.log(ROPE_BASE) * 2.0 / head * jnp.arange(half, dtype=F32))
    angles = position[:, None] * inverse[None, :]
    return jnp.cos(angles)[:, None, :], jnp.sin(angles)[:, None, :]


def rotary(values, cosine, sine):
    half = values.shape[-1] // 2
    first = values[..., :half]
    second = values[..., half:]
    return jnp.concatenate([first * cosine - second * sine, second * cosine + first * sine], -1)


def layout(lengths_row, group):
    ends = jnp.cumsum(lengths_row)
    starts = ends - lengths_row
    row_index = jnp.arange(group, dtype=jnp.int32)
    segment = jnp.sum((row_index[:, None] >= ends[None, :]).astype(jnp.int32), 1)
    member = segment[:, None] == jnp.arange(lengths_row.shape[0], dtype=jnp.int32)[None, :]
    position = (row_index - jnp.sum(jnp.where(member, starts[None, :], 0), 1)).astype(F32)
    live = (segment < lengths_row.shape[0] - 1).astype(F32)
    return (segment, position, live)


def nn(a, b):
    return lax.dot_general(a, b, (((1,), (0,)), ((), ())), preferred_element_type=F32)


def nt(a, b):
    return lax.dot_general(a, b, (((1,), (1,)), ((), ())), preferred_element_type=F32)


def tn(a, b):
    return lax.dot_general(a, b, (((0,), (0,)), ((), ())), preferred_element_type=F32)


def expert_body(
    counts, place, gate, hn, dy, wg, wu, wd, xe_o, dyr_o, hg_o, dgp_o, dup_o, ye_o, dxe_o, tok_o
):
    e, g, i = pl.program_id(0), pl.program_id(1), pl.program_id(2)
    rows = xe_o.shape[2]
    base = i * rows

    @pl.when(i == 0)
    def _():
        tok_o[...] = jnp.zeros_like(tok_o)

    @pl.when(counts[e, g] <= base)
    def _():
        for ref in (xe_o, dyr_o, hg_o, dgp_o, dup_o, ye_o, dxe_o):
            ref[...] = jnp.zeros_like(ref)

    @pl.when(counts[e, g] > base)
    def _():
        slot = lax.broadcasted_iota(jnp.int32, (rows, place.shape[3]), 0) + base
        hit = slot == place[0, 0]
        pick = jnp.where(hit, 1.0, 0.0).astype(BF16)
        weight = jnp.sum(jnp.where(hit, gate[0, 0], 0.0), 1, keepdims=True)
        xe = nn(pick, hn[0]).astype(BF16)
        xe_o[0, 0] = xe
        gp = nn(xe, wg[0])
        up = nn(xe, wu[0])
        sig = jax.nn.sigmoid(gp)
        silu = gp * sig
        hid = silu * up
        hg = (hid * weight).astype(BF16)
        hg_o[0, 0] = hg
        ye_o[0, 0] = nn(hg, wd[0]).astype(BF16)
        dyr = nn(pick, dy[0]).astype(BF16)
        dyr_o[0, 0] = dyr
        back = nt(dyr, wd[0])
        dgate = jnp.sum(back * hid, 1, keepdims=True)
        dhid = back * weight
        dgp = (dhid * up * sig * (1.0 + gp * (1.0 - sig))).astype(BF16)
        dup = (dhid * silu).astype(BF16)
        dgp_o[0, 0] = dgp
        dup_o[0, 0] = dup
        dots = jnp.sum(dgp.astype(F32) * gp + dup.astype(F32) * up, 1, keepdims=True)
        dxe_o[0, 0] = (nt(dgp, wg[0]) + nt(dup, wu[0])).astype(BF16)
        tok_o[0, 0, 0:1, :] += jnp.sum(jnp.where(hit, dgate, 0.0), 0, keepdims=True)
        tok_o[0, 0, 1:2, :] += jnp.sum(jnp.where(hit, dots, 0.0), 0, keepdims=True)


def expert_pass(counts, place, gate, hn, dy, wg, wu, wd, capacity):
    experts, width, ff = wg.shape
    micro, group, _ = hn.shape
    rows = min(256, capacity)
    blocks = capacity // rows
    tall = lambda e, g, i, c: (e, g, i, 0)
    line = lambda e, g, i, c: (e, g, 0, 0)
    whole = lambda e, g, i, c: (g, 0, 0)
    matrix = lambda e, g, i, c: (e, 0, 0)
    slots = lambda n: jax.ShapeDtypeStruct((experts, micro, capacity, n), BF16)
    sizes = (width, width, ff, ff, ff, width, width)
    flops = 2 * experts * micro * capacity * width * (6 * ff + 2 * group)
    return pl.pallas_call(
        expert_body,
        grid_spec=pltpu.PrefetchScalarGridSpec(
            num_scalar_prefetch=1,
            grid=(experts, micro, blocks),
            in_specs=[
                pl.BlockSpec((1, 1, 1, group), line),
                pl.BlockSpec((1, 1, 1, group), line),
                pl.BlockSpec((1, group, width), whole, pipeline_mode=pl.Buffered(1)),
                pl.BlockSpec((1, group, width), whole, pipeline_mode=pl.Buffered(1)),
                pl.BlockSpec((1, width, ff), matrix),
                pl.BlockSpec((1, width, ff), matrix),
                pl.BlockSpec((1, ff, width), matrix),
            ],
            out_specs=[pl.BlockSpec((1, 1, rows, n), tall) for n in sizes]
            + [pl.BlockSpec((1, 1, 2, group), line)],
        ),
        out_shape=[slots(n) for n in sizes]
        + [jax.ShapeDtypeStruct((experts, micro, 2, group), F32)],
        compiler_params=pltpu.CompilerParams(vmem_limit_bytes=VMEM_LIMIT),
        cost_estimate=pl.CostEstimate(
            flops=flops, bytes_accessed=100 << 20, transcendentals=experts * micro * capacity * ff
        ),
        name="expert_pass",
    )(counts, place, gate, hn, dy, wg, wu, wd)


def grads_body(xe, dgp, dup, hg, dyr, gg_o, gu_o, gd_o):
    part = xe[0]
    gg_o[0] = tn(part, dgp[0]).astype(BF16)
    gu_o[0] = tn(part, dup[0]).astype(BF16)
    gd_o[0] = tn(hg[0], dyr[0]).astype(BF16)


def expert_grads(xe, dgp, dup, hg, dyr):
    experts, micro, capacity, width = xe.shape
    ff = dgp.shape[3]
    rows = micro * capacity
    xe, dyr = (a.reshape(experts, rows, width) for a in (xe, dyr))
    dgp, dup, hg = (a.reshape(experts, rows, ff) for a in (dgp, dup, hg))
    part = min(512, width)
    return pl.pallas_call(
        grads_body,
        grid=(experts, width // part),
        in_specs=[
            pl.BlockSpec((1, rows, part), lambda e, r: (e, 0, r)),
            pl.BlockSpec((1, rows, ff), lambda e, r: (e, 0, 0)),
            pl.BlockSpec((1, rows, ff), lambda e, r: (e, 0, 0)),
            pl.BlockSpec((1, rows, ff), lambda e, r: (e, 0, 0)),
            pl.BlockSpec((1, rows, part), lambda e, r: (e, 0, r)),
        ],
        out_specs=[
            pl.BlockSpec((1, part, ff), lambda e, r: (e, r, 0)),
            pl.BlockSpec((1, part, ff), lambda e, r: (e, r, 0)),
            pl.BlockSpec((1, ff, part), lambda e, r: (e, 0, r)),
        ],
        out_shape=[
            jax.ShapeDtypeStruct((experts, width, ff), BF16),
            jax.ShapeDtypeStruct((experts, width, ff), BF16),
            jax.ShapeDtypeStruct((experts, ff, width), BF16),
        ],
        compiler_params=pltpu.CompilerParams(vmem_limit_bytes=VMEM_LIMIT),
        cost_estimate=pl.CostEstimate(
            flops=6 * experts * rows * width * ff, bytes_accessed=experts * 26 << 20, transcendentals=0
        ),
        name="expert_grads",
    )(xe, dgp, dup, hg, dyr)


def combine_body(place, *refs):
    out = refs[-1]
    slots = refs[:-1]
    total = jnp.zeros((out.shape[1], out.shape[2]), F32)
    at = 0
    for ref in slots:
        capacity = ref.shape[2]
        for e in range(ref.shape[0]):
            slot = lax.broadcasted_iota(jnp.int32, (out.shape[1], capacity), 1)
            pick = jnp.where(slot == place[0, :, at : at + 1], 1.0, 0.0).astype(BF16)
            total = total + nn(pick, ref[e, 0])
            at += 1
    out[0] = total.astype(BF16)


def combine(place, slots):
    micro, group, local = place.shape
    capacity, width = slots[0].shape[2:]
    tile = min(256, group)
    return pl.pallas_call(
        combine_body,
        grid=(micro, group // tile),
        in_specs=[pl.BlockSpec((1, tile, local), lambda g, i: (g, i, 0))]
        + [
            pl.BlockSpec((s.shape[0], 1, capacity, width), lambda g, i: (0, g, 0, 0))
            for s in slots
        ],
        out_specs=pl.BlockSpec((1, tile, width), lambda g, i: (g, i, 0)),
        out_shape=jax.ShapeDtypeStruct((micro, group, width), BF16),
        compiler_params=pltpu.CompilerParams(vmem_limit_bytes=VMEM_LIMIT),
        cost_estimate=pl.CostEstimate(
            flops=2 * micro * group * local * capacity * width,
            bytes_accessed=micro * (local * capacity + group) * width * 2,
            transcendentals=0,
        ),
        name="combine",
    )(place, *slots).reshape(micro * group, width)


def shards(
    tokens,
    gain_attn,
    gain_ffn,
    gain_query,
    gain_key,
    w_query,
    w_key,
    w_value,
    w_out,
    w_router,
    w_gate,
    w_up,
    w_down,
    routes,
    lengths,
    cotangent,
):
    n_col = lax.axis_size("col")
    n_row = lax.axis_size("row")
    col = lax.axis_index("col")
    micro, spans = lengths.shape
    rows, part = tokens.shape
    group = rows // micro
    width = part * n_col
    head = gain_query.shape[0]
    local_exp = w_gate.shape[0]
    experts = local_exp * n_col
    topk = routes.shape[1]
    capacity = 2 * group * topk // experts
    local_heads = w_out.shape[0] // head
    hd = w_out.shape[0] * n_col
    scale = head ** (-0.5)

    def gather(value, axis_name, axis):
        return lax.all_gather(value, axis_name, axis=axis, tiled=True)

    def mine(value, axis):
        size = value.shape[axis] // n_col
        return lax.dynamic_slice_in_dim(value, col * size, size, axis)

    step = max(1, local_exp // 2)
    chunks = [slice(at, at + step) for at in range(0, local_exp, step)]
    big = [
        (
            gather(w_gate[c], "row", 1),
            gather(w_up[c], "row", 1),
            gather(w_down[c], "row", 2),
        )
        for c in chunks
    ]

    inputs_low = gather(tokens, "col", 1)
    packed = jnp.concatenate([w_query, w_key, w_value], 0)
    packed = gather(packed, "row", 1).reshape(3, part, n_col, local_heads * head)
    w_heads = lax.all_to_all(
        packed.transpose(2, 0, 1, 3), "col", split_axis=0, concat_axis=0, tiled=True
    )
    w_heads = w_heads.transpose(1, 0, 2, 3).reshape(3, width, local_heads * head)
    full_o = gather(gather(w_out, "row", 1), "col", 0)
    full_r = gather(gather(w_router, "row", 1), "col", 0)
    gains = gather(jnp.stack([gain_attn, gain_ffn]), "col", 1)
    upstream_low = gather(cotangent, "col", 1)

    segment, position, live = jax.vmap(lambda l: layout(l, group))(lengths)
    position = position.reshape(rows)
    live = live.reshape(rows)
    member = jnp.any(
        routes[:, None, :] == jnp.arange(experts, dtype=jnp.int32)[None, :, None], -1
    )
    member_f = member.astype(F32)
    member_loc = mine(member_f, 1).reshape(micro, group, local_exp)
    lower = (
        jnp.arange(group, dtype=jnp.int32)[:, None] > jnp.arange(group, dtype=jnp.int32)[None, :]
    ).astype(BF16)
    before = jnp.einsum("st,gte->gse", lower, member_loc.astype(BF16), preferred_element_type=F32)
    place = jnp.where(member_loc > 0, before, -1.0).astype(jnp.int32)
    counts = jnp.sum(member_loc, 1).astype(jnp.int32).T
    place_t = place.transpose(2, 0, 1)[:, :, None, :]

    inputs = inputs_low.astype(F32)
    scale_one = inverse_rms(inputs)
    normed = (inputs * scale_one * gains[0]).astype(BF16)
    query_pre, key_pre, value_pre = (nn(normed, w_heads[j]) for j in range(3))
    shape = (rows, local_heads, head)
    cosine, sine = rope_tables(position, head)

    def head_norm(values, gain):
        return rotary(values * inverse_rms(values) * gain, cosine, sine)

    query_rot, query_pull = jax.vjp(head_norm, query_pre.reshape(shape), gain_query)
    key_rot, key_pull = jax.vjp(head_norm, key_pre.reshape(shape), gain_key)
    batch = (micro, group, local_heads, head)
    queries = query_rot.astype(BF16).reshape(batch)
    keys_low = key_rot.astype(BF16).reshape(batch)
    values_low = value_pre.astype(BF16).reshape(batch)
    same = (segment[:, :, None] == segment[:, None, :])[:, None]

    def scores_of():
        raw = jnp.einsum("gqhd,gkhd->ghqk", queries, keys_low, preferred_element_type=F32) * scale
        return jnp.where(same, raw, MASKED)

    scores = scores_of()
    highest = jnp.max(scores, -1, keepdims=True)
    log_total = highest + jnp.log(jnp.sum(jnp.exp(scores - highest), -1, keepdims=True))
    probs_low = jnp.exp(scores - log_total).astype(BF16)
    attended = jnp.einsum(
        "ghqk,gkhd->gqhd", probs_low, values_low, preferred_element_type=F32
    ).astype(BF16)
    attended_full = gather(attended.reshape(rows, local_heads * head), "col", 1)

    hidden = inputs + nn(attended_full, full_o)
    scale_two = inverse_rms(hidden)
    normed_ffn = (hidden * scale_two * gains[1]).astype(BF16)
    logits = nn(normed_ffn, full_r)
    peak = jnp.max(jnp.where(member, logits, -jnp.inf), -1, keepdims=True)
    raised = jnp.where(member, jnp.exp(jnp.where(member, logits - peak, 0.0)), 0.0)
    gates = raised / jnp.sum(raised, -1, keepdims=True)
    gate_t = mine(gates, 1).reshape(micro, group, local_exp).transpose(2, 0, 1)[:, :, None, :]
    upstream_full = (upstream_low * live[:, None].astype(BF16)).reshape(micro, group, width)
    hn = normed_ffn.reshape(micro, group, width)

    outs, weight_grads = [], []
    for c, (wg, wu, wd) in zip(chunks, big):
        xe, dyr, hg, dgp, dup, ye, dxe, tok = expert_pass(
            counts[c], place_t[c], gate_t[c], hn, upstream_full, wg, wu, wd, capacity
        )
        outs.append((ye, dxe, tok))
        gg, gu, gd = expert_grads(xe, dgp, dup, hg, dyr)
        weight_grads.append(
            (
                lax.psum_scatter(gg, "row", scatter_dimension=1, tiled=True),
                lax.psum_scatter(gu, "row", scatter_dimension=1, tiled=True),
                lax.psum_scatter(gd, "row", scatter_dimension=2, tiled=True),
            )
        )
    grad_gate, grad_up, grad_down = (
        jnp.concatenate([w[j] for w in weight_grads], 0).astype(F32) for j in range(3)
    )
    back_sum = lax.psum_scatter(
        combine(place, [o[1] for o in outs]), "col", scatter_dimension=1, tiled=True
    )
    mixed_sum = lax.psum_scatter(
        combine(place, [o[0] for o in outs]), "col", scatter_dimension=1, tiled=True
    )
    tok = jnp.concatenate([o[2] for o in outs], 0)
    tok = gather(tok, "col", 0)
    gate_dots = tok[:, :, 0].reshape(experts, rows).T
    hidden_part = mine(hidden, 1)
    mixed = (hidden_part + mixed_sum.astype(F32)).astype(BF16)

    selected = gates * (gate_dots - jnp.sum(gates * gate_dots, -1, keepdims=True))
    logit_grad = selected.astype(BF16)
    router_part = mine(full_r, 0)
    normed_grad = back_sum.astype(F32) + nt(logit_grad, router_part)
    grad_router = tn(mine(normed_ffn, 1), logit_grad)
    scaled_two = hidden_part * scale_two
    grad_gain_ffn = jnp.sum(normed_grad * scaled_two, 0)
    dot_two = jnp.sum(tok[:, :, 1].reshape(experts, rows), 0) + jnp.sum(
        logit_grad.astype(F32) * logits, 1
    )
    upstream_part = cotangent.astype(F32) * live[:, None]
    hidden_grad = (
        upstream_part
        + scale_two * (normed_grad * gain_ffn)
        - hidden_part * scale_two**2 * dot_two[:, None] / width
    )

    branch_grad = hidden_grad.astype(BF16)
    attended_grad = lax.psum_scatter(
        nt(branch_grad, mine(full_o, 1)).astype(BF16), "col", scatter_dimension=1, tiled=True
    ).reshape(batch)
    grad_out = tn(attended_full, branch_grad)
    scores_again = scores_of()
    probs = jnp.exp(scores_again - log_total)
    probs_again = probs.astype(BF16)
    probs_grad = jnp.einsum(
        "gqhd,gkhd->ghqk", attended_grad, values_low, preferred_element_type=F32
    )
    values_grad = jnp.einsum(
        "ghqk,gqhd->gkhd", probs_again, attended_grad, preferred_element_type=F32
    )
    score_grad = (probs * (probs_grad - jnp.sum(probs_grad * probs, -1, keepdims=True))).astype(
        BF16
    )
    query_grad_rot = (
        jnp.einsum("ghqk,gkhd->gqhd", score_grad, keys_low, preferred_element_type=F32) * scale
    )
    key_grad_rot = (
        jnp.einsum("ghqk,gqhd->gkhd", score_grad, queries, preferred_element_type=F32) * scale
    )
    query_grad, gain_query_part = query_pull(query_grad_rot.reshape(shape))
    key_grad, gain_key_part = key_pull(key_grad_rot.reshape(shape))
    flat = (rows, local_heads * head)
    heads_grad = [
        v.reshape(flat).astype(BF16) for v in (query_grad, key_grad, values_grad)
    ]
    back_heads = sum(nt(g, w_heads[j]) for j, g in enumerate(heads_grad))
    normed_back = lax.psum_scatter(
        back_heads.astype(BF16), "col", scatter_dimension=1, tiled=True
    ).astype(F32)
    pre = (query_pre, key_pre, value_pre)
    dot_part = sum(jnp.sum(g.astype(F32) * p, -1) for g, p in zip(heads_grad, pre))
    dot_one, gain_query_sum, gain_key_sum = lax.psum(
        (dot_part, gain_query_part, gain_key_part), "col"
    )
    scale_one_part = scale_one
    inputs_part = tokens.astype(F32)
    grad_gain_attn = jnp.sum(normed_back * inputs_part * scale_one_part, 0)
    input_grad = (
        hidden_grad
        + scale_one_part * (normed_back * gain_attn)
        - inputs_part * scale_one_part**2 * dot_one[:, None] / width
    )

    heads_weights = jnp.stack([tn(normed, g) for g in heads_grad]).astype(BF16)
    heads_weights = heads_weights.reshape(3, n_col, part, local_heads * head).transpose(1, 0, 2, 3)
    heads_weights = lax.all_to_all(heads_weights, "col", split_axis=0, concat_axis=0, tiled=True)
    heads_weights = heads_weights.transpose(1, 2, 0, 3).reshape(3 * part, hd)
    heads_weights = lax.psum_scatter(heads_weights, "row", scatter_dimension=1, tiled=True)
    grad_query, grad_key, grad_value = (
        heads_weights[j * part : (j + 1) * part].astype(F32) for j in range(3)
    )
    out_weights = lax.all_to_all(
        grad_out.astype(BF16).reshape(n_col, local_heads * head, part),
        "col",
        split_axis=0,
        concat_axis=0,
        tiled=True,
    )
    out_weights = out_weights.transpose(1, 0, 2).reshape(local_heads * head, width)
    grad_out = lax.psum_scatter(out_weights, "row", scatter_dimension=1, tiled=True).astype(F32)
    grad_router = lax.psum_scatter(
        grad_router.astype(BF16), "row", scatter_dimension=1, tiled=True
    ).astype(F32)
    grad_gain_attn, grad_gain_ffn, grad_gain_query, grad_gain_key = lax.psum(
        (grad_gain_attn, grad_gain_ffn, gain_query_sum, gain_key_sum), "row"
    )
    return (
        mixed,
        input_grad,
        grad_gain_attn,
        grad_gain_ffn,
        grad_gain_query,
        grad_gain_key,
        grad_query,
        grad_key,
        grad_value,
        grad_out,
        grad_router,
        grad_gate,
        grad_up,
        grad_down,
    )


def solution(mesh):
    placed = (
        P("row", "col"),
        P("col"),
        P("col"),
        P(),
        P(),
        P("col", "row"),
        P("col", "row"),
        P("col", "row"),
        P("col", "row"),
        P("col", "row"),
        P("col", "row", None),
        P("col", "row", None),
        P("col", None, "row"),
        P("row", None),
        P("row", None),
        P("row", "col"),
    )
    return jax.shard_map(
        shards,
        mesh=mesh,
        in_specs=placed,
        out_specs=(
            P("row", "col"),
            P("row", "col"),
            P("col"),
            P("col"),
            P(),
            P(),
            P("col", "row"),
            P("col", "row"),
            P("col", "row"),
            P("col", "row"),
            P("col", "row"),
            P("col", "row", None),
            P("col", "row", None),
            P("col", None, "row"),
        ),
        check_vma=False,
    )
```

```python
import functools
import math

import jax
import jax.numpy as jnp
from jax import lax
from jax.experimental import pallas as pl
from jax.experimental.pallas import tpu as pltpu
from jax.sharding import PartitionSpec as P

EPSILON = 1e-06
ROPE_BASE = 10000.0
MASKED = -1e30
F32 = jnp.float32
BF16 = jnp.bfloat16
VMEM_LIMIT = 60 * 1024 * 1024
MESH = pl.DeviceIdType.MESH


def inverse_rms(values):
    return lax.rsqrt(jnp.mean(values * values, -1, keepdims=True) + EPSILON)


def rope_tables(position, head):
    half = head // 2
    inverse = jnp.exp(-math.log(ROPE_BASE) * 2.0 / head * jnp.arange(half, dtype=F32))
    angles = position[:, None] * inverse[None, :]
    return jnp.cos(angles)[:, None, :], jnp.sin(angles)[:, None, :]


def rotary(values, cosine, sine):
    half = values.shape[-1] // 2
    first = values[..., :half]
    second = values[..., half:]
    return jnp.concatenate([first * cosine - second * sine, second * cosine + first * sine], -1)


def layout(lengths_row, group):
    ends = jnp.cumsum(lengths_row)
    starts = ends - lengths_row
    row_index = jnp.arange(group, dtype=jnp.int32)
    segment = jnp.sum((row_index[:, None] >= ends[None, :]).astype(jnp.int32), 1)
    member = segment[:, None] == jnp.arange(lengths_row.shape[0], dtype=jnp.int32)[None, :]
    position = (row_index - jnp.sum(jnp.where(member, starts[None, :], 0), 1)).astype(F32)
    live = (segment < lengths_row.shape[0] - 1).astype(F32)
    return (segment, position, live)


def nn(a, b):
    return lax.dot_general(a, b, (((1,), (0,)), ((), ())), preferred_element_type=F32)


def nt(a, b):
    return lax.dot_general(a, b, (((1,), (1,)), ((), ())), preferred_element_type=F32)


def tn(a, b):
    return lax.dot_general(a, b, (((0,), (0,)), ((), ())), preferred_element_type=F32)


def expert_body(
    counts, place, gate, hn, dy, wg, wu, wd, xe_o, dyr_o, hg_o, dgp_o, dup_o, ye_o, dxe_o, tok_o
):
    e, g, i = pl.program_id(0), pl.program_id(1), pl.program_id(2)
    rows = xe_o.shape[2]
    base = i * rows

    @pl.when(i == 0)
    def _():
        tok_o[...] = jnp.zeros_like(tok_o)

    @pl.when(counts[e, g] <= base)
    def _():
        for ref in (xe_o, dyr_o, hg_o, dgp_o, dup_o, ye_o, dxe_o):
            ref[...] = jnp.zeros_like(ref)

    @pl.when(counts[e, g] > base)
    def _():
        slot = lax.broadcasted_iota(jnp.int32, (rows, place.shape[3]), 0) + base
        hit = slot == place[0, 0]
        pick = jnp.where(hit, 1.0, 0.0).astype(BF16)
        weight = jnp.sum(jnp.where(hit, gate[0, 0], 0.0), 1, keepdims=True)
        xe = nn(pick, hn[0]).astype(BF16)
        xe_o[0, 0] = xe
        gp = nn(xe, wg[0])
        up = nn(xe, wu[0])
        sig = jax.nn.sigmoid(gp)
        silu = gp * sig
        hid = silu * up
        hg = (hid * weight).astype(BF16)
        hg_o[0, 0] = hg
        ye_o[0, 0] = nn(hg, wd[0]).astype(BF16)
        dyr = nn(pick, dy[0]).astype(BF16)
        dyr_o[0, 0] = dyr
        back = nt(dyr, wd[0])
        dgate = jnp.sum(back * hid, 1, keepdims=True)
        dhid = back * weight
        dgp = (dhid * up * sig * (1.0 + gp * (1.0 - sig))).astype(BF16)
        dup = (dhid * silu).astype(BF16)
        dgp_o[0, 0] = dgp
        dup_o[0, 0] = dup
        dots = jnp.sum(dgp.astype(F32) * gp + dup.astype(F32) * up, 1, keepdims=True)
        dxe_o[0, 0] = (nt(dgp, wg[0]) + nt(dup, wu[0])).astype(BF16)
        tok_o[0, 0, 0:1, :] += jnp.sum(jnp.where(hit, dgate, 0.0), 0, keepdims=True)
        tok_o[0, 0, 1:2, :] += jnp.sum(jnp.where(hit, dots, 0.0), 0, keepdims=True)


def expert_pass(counts, place, gate, hn, dy, wg, wu, wd, capacity):
    experts, width, ff = wg.shape
    micro, group, _ = hn.shape
    rows = min(256, capacity)
    blocks = capacity // rows
    tall = lambda e, g, i, c: (e, g, i, 0)
    line = lambda e, g, i, c: (e, g, 0, 0)
    whole = lambda e, g, i, c: (g, 0, 0)
    matrix = lambda e, g, i, c: (e, 0, 0)
    slots = lambda n: jax.ShapeDtypeStruct((experts, micro, capacity, n), BF16)
    sizes = (width, width, ff, ff, ff, width, width)
    flops = 2 * experts * micro * capacity * width * (6 * ff + 2 * group)
    return pl.pallas_call(
        expert_body,
        grid_spec=pltpu.PrefetchScalarGridSpec(
            num_scalar_prefetch=1,
            grid=(experts, micro, blocks),
            in_specs=[
                pl.BlockSpec((1, 1, 1, group), line),
                pl.BlockSpec((1, 1, 1, group), line),
                pl.BlockSpec((1, group, width), whole, pipeline_mode=pl.Buffered(1)),
                pl.BlockSpec((1, group, width), whole, pipeline_mode=pl.Buffered(1)),
                pl.BlockSpec((1, width, ff), matrix),
                pl.BlockSpec((1, width, ff), matrix),
                pl.BlockSpec((1, ff, width), matrix),
            ],
            out_specs=[pl.BlockSpec((1, 1, rows, n), tall) for n in sizes]
            + [pl.BlockSpec((1, 1, 2, group), line)],
        ),
        out_shape=[slots(n) for n in sizes]
        + [jax.ShapeDtypeStruct((experts, micro, 2, group), F32)],
        compiler_params=pltpu.CompilerParams(vmem_limit_bytes=VMEM_LIMIT),
        cost_estimate=pl.CostEstimate(
            flops=flops, bytes_accessed=100 << 20, transcendentals=experts * micro * capacity * ff
        ),
        name="expert_pass",
    )(counts, place, gate, hn, dy, wg, wu, wd)


def grads_body(xe, dgp, dup, hg, dyr, gg_o, gu_o, gd_o):
    part = xe[0]
    gg_o[0] = tn(part, dgp[0]).astype(BF16)
    gu_o[0] = tn(part, dup[0]).astype(BF16)
    gd_o[0] = tn(hg[0], dyr[0]).astype(BF16)


def expert_grads(xe, dgp, dup, hg, dyr):
    experts, micro, capacity, width = xe.shape
    ff = dgp.shape[3]
    rows = micro * capacity
    xe, dyr = (a.reshape(experts, rows, width) for a in (xe, dyr))
    dgp, dup, hg = (a.reshape(experts, rows, ff) for a in (dgp, dup, hg))
    part = min(512, width)
    return pl.pallas_call(
        grads_body,
        grid=(experts, width // part),
        in_specs=[
            pl.BlockSpec((1, rows, part), lambda e, r: (e, 0, r)),
            pl.BlockSpec((1, rows, ff), lambda e, r: (e, 0, 0)),
            pl.BlockSpec((1, rows, ff), lambda e, r: (e, 0, 0)),
            pl.BlockSpec((1, rows, ff), lambda e, r: (e, 0, 0)),
            pl.BlockSpec((1, rows, part), lambda e, r: (e, 0, r)),
        ],
        out_specs=[
            pl.BlockSpec((1, part, ff), lambda e, r: (e, r, 0)),
            pl.BlockSpec((1, part, ff), lambda e, r: (e, r, 0)),
            pl.BlockSpec((1, ff, part), lambda e, r: (e, 0, r)),
        ],
        out_shape=[
            jax.ShapeDtypeStruct((experts, width, ff), BF16),
            jax.ShapeDtypeStruct((experts, width, ff), BF16),
            jax.ShapeDtypeStruct((experts, ff, width), BF16),
        ],
        compiler_params=pltpu.CompilerParams(vmem_limit_bytes=VMEM_LIMIT),
        cost_estimate=pl.CostEstimate(
            flops=6 * experts * rows * width * ff, bytes_accessed=experts * 26 << 20, transcendentals=0
        ),
        name="expert_grads",
    )(xe, dgp, dup, hg, dyr)


def combine_body(place, *refs):
    out = refs[-1]
    slots = refs[:-1]
    total = jnp.zeros((out.shape[1], out.shape[2]), F32)
    at = 0
    for ref in slots:
        capacity = ref.shape[2]
        for e in range(ref.shape[0]):
            slot = lax.broadcasted_iota(jnp.int32, (out.shape[1], capacity), 1)
            pick = jnp.where(slot == place[0, :, at : at + 1], 1.0, 0.0).astype(BF16)
            total = total + nn(pick, ref[e, 0])
            at += 1
    out[0] = total.astype(BF16)


def combine(place, slots):
    micro, group, local = place.shape
    capacity, width = slots[0].shape[2:]
    tile = min(256, group)
    return pl.pallas_call(
        combine_body,
        grid=(micro, group // tile),
        in_specs=[pl.BlockSpec((1, tile, local), lambda g, i: (g, i, 0))]
        + [
            pl.BlockSpec((s.shape[0], 1, capacity, width), lambda g, i: (0, g, 0, 0))
            for s in slots
        ],
        out_specs=pl.BlockSpec((1, tile, width), lambda g, i: (g, i, 0)),
        out_shape=jax.ShapeDtypeStruct((micro, group, width), BF16),
        compiler_params=pltpu.CompilerParams(vmem_limit_bytes=VMEM_LIMIT),
        cost_estimate=pl.CostEstimate(
            flops=2 * micro * group * local * capacity * width,
            bytes_accessed=micro * (local * capacity + group) * width * 2,
            transcendentals=0,
        ),
        name="combine",
    )(place, *slots).reshape(micro * group, width)


def places():
    col = lax.axis_index("col")
    row = lax.axis_index("row")
    n_col = lax.axis_size("col")
    pair, core = col // 2, col % 2

    def at(pair_index, core_index):
        return (row, pair_index * 2 + core_index)

    return col, n_col // 2, pair, core, at


def greet(pairs, pair, core, at):
    barrier = pltpu.get_barrier_semaphore()
    pl.semaphore_signal(barrier, inc=1, device_id=at(pair, 1 - core), device_id_type=MESH)

    @pl.when(pair > 0)
    def _():
        pl.semaphore_signal(barrier, inc=1, device_id=at(pair - 1, core), device_id_type=MESH)

    @pl.when(pair < pairs - 1)
    def _():
        pl.semaphore_signal(barrier, inc=1, device_id=at(pair + 1, core), device_id_type=MESH)

    peers = 1 + jnp.where(pair > 0, 1, 0) + jnp.where(pair < pairs - 1, 1, 0)
    pl.semaphore_wait(barrier, peers)


def gather_body(axes, *refs):
    n = len(axes)
    ins, outs = refs[:n], refs[n : 2 * n]
    own_sem, right_s, right_r, left_s, left_r, side_s, side_r = refs[2 * n :]
    col, pairs, pair, core, at = places()

    def block(j, source):
        ref = outs[j]
        size = ins[j].shape[axes[j]]
        start = pl.multiple_of(source * size, size)
        if axes[j] == 0:
            return ref.at[pl.ds(start, size)]
        return ref.at[:, pl.ds(start, size)]

    def send(j, src, source, sems, recvs, slot, where):
        return pltpu.make_async_remote_copy(
            src_ref=src,
            dst_ref=block(j, source),
            send_sem=sems.at[j, slot],
            recv_sem=recvs.at[j, slot],
            device_id=where,
            device_id_type=MESH,
        )

    greet(pairs, pair, core, at)

    def right(j, s):
        source = (pair - s) * 2 + core
        src = ins[j] if s == 0 else block(j, source)
        return send(j, src, source, right_s, right_r, s, at(pair + 1, core))

    def left(j, s):
        source = (pair + s) * 2 + core
        src = ins[j] if s == 0 else block(j, source)
        return send(j, src, source, left_s, left_r, s, at(pair - 1, core))

    def side(j, source_pair, first=False):
        source = source_pair * 2 + core
        src = ins[j] if first else block(j, source)
        return pltpu.make_async_remote_copy(
            src_ref=src,
            dst_ref=block(j, source),
            send_sem=side_s.at[j, source_pair],
            recv_sem=side_r.at[j, source_pair],
            device_id=at(pair, 1 - core),
            device_id_type=MESH,
        )

    def arrived(j, recvs, slot, source):
        pltpu.make_async_remote_copy(
            src_ref=ins[j],
            dst_ref=block(j, source),
            send_sem=recvs.at[j, slot],
            recv_sem=recvs.at[j, slot],
            device_id=at(pair, 1 - core),
            device_id_type=MESH,
        ).wait_recv()

    for j in range(n):

        @pl.when(pair < pairs - 1)
        def _():
            right(j, 0).start()

        @pl.when(pair > 0)
        def _():
            left(j, 0).start()

    for j in range(n):
        side(j, pair, True).start()
        pltpu.make_async_copy(ins[j], block(j, col), own_sem.at[j]).start()
    for s in range(1, pairs):
        for j in range(n):

            @pl.when(pair >= s)
            def _():
                arrived(j, right_r, s - 1, (pair - s) * 2 + core)

                @pl.when(pair < pairs - 1)
                def _():
                    right(j, s).start()

                side(j, pair - s).start()

            @pl.when(pair + s < pairs)
            def _():
                arrived(j, left_r, s - 1, (pair + s) * 2 + core)

                @pl.when(pair > 0)
                def _():
                    left(j, s).start()

                side(j, pair + s).start()

    for j in range(n):
        pltpu.make_async_copy(ins[j], block(j, col), own_sem.at[j]).wait()
        for p in range(pairs):
            side(j, p).wait_send()
            arrived(j, side_r, p, p * 2 + 1 - core)
        for s in range(pairs):

            @pl.when((pair >= s) & (pair < pairs - 1))
            def _():
                right(j, s).wait_send()

            @pl.when((pair + s < pairs) & (pair > 0))
            def _():
                left(j, s).wait_send()


def gather_col(arrays, axes, ident):
    n_col = lax.axis_size("col")
    pairs, n = n_col // 2, len(arrays)
    shapes = [
        tuple(d * n_col if at == axis else d for at, d in enumerate(a.shape))
        for a, axis in zip(arrays, axes)
    ]
    dma = pltpu.SemaphoreType.DMA
    return pl.pallas_call(
        functools.partial(gather_body, axes),
        in_specs=[pl.BlockSpec(memory_space=pl.ANY)] * n,
        out_specs=[pl.BlockSpec(memory_space=pl.ANY)] * n,
        out_shape=[jax.ShapeDtypeStruct(s, a.dtype) for s, a in zip(shapes, arrays)],
        scratch_shapes=[dma((n,))] + [dma((n, pairs))] * 6,
        compiler_params=pltpu.CompilerParams(collective_id=ident, has_side_effects=True),
        cost_estimate=pl.CostEstimate(
            flops=0,
            bytes_accessed=sum(math.prod(s) for s in shapes) * 16,
            transcendentals=0,
        ),
        name="gather_col",
    )(*arrays)


def scatter_body(
    part, x, out, acc, side, from_left, from_right, load, side_s, side_r, right_s, right_r, left_s, left_r
):
    col, pairs, pair, core, at = places()
    rows = out.shape[0]
    tile = min(256, rows)

    def block(owner):
        return x.at[:, pl.ds(pl.multiple_of(owner * part, part), part)]

    def fetch(d):
        return pltpu.make_async_copy(block(d * 2 + core), acc.at[d], load.at[d])

    def across(d):
        return pltpu.make_async_remote_copy(
            src_ref=block(d * 2 + 1 - core),
            dst_ref=side.at[d],
            send_sem=side_s.at[d],
            recv_sem=side_r.at[d],
            device_id=at(pair, 1 - core),
            device_id_type=MESH,
        )

    def right(d):
        return pltpu.make_async_remote_copy(
            src_ref=acc.at[d],
            dst_ref=from_left.at[d],
            send_sem=right_s.at[d],
            recv_sem=right_r.at[d],
            device_id=at(pair + 1, core),
            device_id_type=MESH,
        )

    def left(d):
        return pltpu.make_async_remote_copy(
            src_ref=acc.at[d],
            dst_ref=from_right.at[d],
            send_sem=left_s.at[d],
            recv_sem=left_r.at[d],
            device_id=at(pair - 1, core),
            device_id_type=MESH,
        )

    greet(pairs, pair, core, at)
    order = []
    for t in range(pairs):
        for d in (pairs - 1 - t, t):
            if d not in order:
                order.append(d)
    for d in order:
        across(d).start()
        fetch(d).start()

    def add(into, *refs):
        def step(i, _):
            at_rows = pl.ds(pl.multiple_of(i * tile, tile), tile)
            total = refs[0][at_rows, :].astype(F32)
            for ref in refs[1:]:
                total = total + ref[at_rows, :].astype(F32)
            into[at_rows, :] = total.astype(into.dtype)
            return 0

        lax.fori_loop(0, rows // tile, step, 0)

    def ready(d):
        fetch(d).wait()
        across(d).wait_recv()

    def go_right(d):
        ready(d)

        @pl.when(pair > 0)
        def _():
            right(d).wait_recv()
            add(acc.at[d], acc.at[d], side.at[d], from_left.at[d])

        @pl.when(pair == 0)
        def _():
            add(acc.at[d], acc.at[d], side.at[d])

        right(d).start()

    def go_left(d):
        ready(d)

        @pl.when(pair < pairs - 1)
        def _():
            left(d).wait_recv()
            add(acc.at[d], acc.at[d], side.at[d], from_right.at[d])

        @pl.when(pair == pairs - 1)
        def _():
            add(acc.at[d], acc.at[d], side.at[d])

        left(d).start()

    for t in range(pairs - 1):
        far, near = pairs - 1 - t, t

        @pl.when(far > pair)
        def _():
            go_right(far)

        @pl.when(near < pair)
        def _():
            go_left(near)

    ready(pair)

    @pl.when(pair == 0)
    def _():
        left(pair).wait_recv()
        add(out, acc.at[pair], side.at[pair], from_right.at[pair])

    @pl.when(pair == pairs - 1)
    def _():
        right(pair).wait_recv()
        add(out, acc.at[pair], side.at[pair], from_left.at[pair])

    @pl.when((pair > 0) & (pair < pairs - 1))
    def _():
        left(pair).wait_recv()
        right(pair).wait_recv()
        add(out, acc.at[pair], side.at[pair], from_left.at[pair], from_right.at[pair])

    for d in range(pairs):
        across(d).wait_send()

        @pl.when(pair < d)
        def _():
            right(d).wait_send()

        @pl.when(pair > d)
        def _():
            left(d).wait_send()


def scatter_col(x, ident):
    n_col = lax.axis_size("col")
    pairs = n_col // 2
    rows, part = x.shape[0], x.shape[1] // n_col
    dma = pltpu.SemaphoreType.DMA
    buffer = pltpu.VMEM((pairs, rows, part), BF16)
    return pl.pallas_call(
        functools.partial(scatter_body, part),
        in_specs=[pl.BlockSpec(memory_space=pl.ANY)],
        out_specs=pl.BlockSpec(memory_space=pltpu.VMEM),
        out_shape=jax.ShapeDtypeStruct((rows, part), F32),
        scratch_shapes=[buffer] * 4 + [dma((pairs,))] * 7,
        compiler_params=pltpu.CompilerParams(
            vmem_limit_bytes=VMEM_LIMIT, collective_id=ident, has_side_effects=True
        ),
        cost_estimate=pl.CostEstimate(
            flops=0, bytes_accessed=rows * part * n_col * 24, transcendentals=0
        ),
        name="scatter_col",
    )(x)


def shards(
    tokens,
    gain_attn,
    gain_ffn,
    gain_query,
    gain_key,
    w_query,
    w_key,
    w_value,
    w_out,
    w_router,
    w_gate,
    w_up,
    w_down,
    routes,
    lengths,
    cotangent,
):
    n_col = lax.axis_size("col")
    n_row = lax.axis_size("row")
    col = lax.axis_index("col")
    micro, spans = lengths.shape
    rows, part = tokens.shape
    group = rows // micro
    width = part * n_col
    head = gain_query.shape[0]
    local_exp = w_gate.shape[0]
    experts = local_exp * n_col
    topk = routes.shape[1]
    capacity = 2 * group * topk // experts
    local_heads = w_out.shape[0] // head
    hd = w_out.shape[0] * n_col
    scale = head ** (-0.5)

    def gather(value, axis_name, axis):
        return lax.all_gather(value, axis_name, axis=axis, tiled=True)

    def mine(value, axis):
        size = value.shape[axis] // n_col
        return lax.dynamic_slice_in_dim(value, col * size, size, axis)

    step = max(1, local_exp // 2)
    chunks = [slice(at, at + step) for at in range(0, local_exp, step)]
    big = [
        (
            gather(w_gate[c], "row", 1),
            gather(w_up[c], "row", 1),
            gather(w_down[c], "row", 2),
        )
        for c in chunks
    ]

    packed = jnp.concatenate([w_query, w_key, w_value], 0)
    packed = gather(packed, "row", 1).reshape(3, part, n_col, local_heads * head)
    w_heads = lax.all_to_all(
        packed.transpose(2, 0, 1, 3), "col", split_axis=0, concat_axis=0, tiled=True
    )
    w_heads = w_heads.transpose(1, 0, 2, 3).reshape(3, width, local_heads * head)
    router_t = gather(w_router, "row", 1).T
    inputs_low, gains, full_rt = gather_col(
        [tokens, jnp.stack([gain_attn, gain_ffn]), router_t], (1, 1, 1), 0
    )
    full_r = full_rt.T
    upstream_low, full_o = gather_col([cotangent, gather(w_out, "row", 1)], (1, 0), 1)

    segment, position, live = jax.vmap(lambda l: layout(l, group))(lengths)
    position = position.reshape(rows)
    live = live.reshape(rows)
    member = jnp.any(
        routes[:, None, :] == jnp.arange(experts, dtype=jnp.int32)[None, :, None], -1
    )
    member_f = member.astype(F32)
    member_loc = mine(member_f, 1).reshape(micro, group, local_exp)
    lower = (
        jnp.arange(group, dtype=jnp.int32)[:, None] > jnp.arange(group, dtype=jnp.int32)[None, :]
    ).astype(BF16)
    before = jnp.einsum("st,gte->gse", lower, member_loc.astype(BF16), preferred_element_type=F32)
    place = jnp.where(member_loc > 0, before, -1.0).astype(jnp.int32)
    counts = jnp.sum(member_loc, 1).astype(jnp.int32).T
    place_t = place.transpose(2, 0, 1)[:, :, None, :]

    inputs = inputs_low.astype(F32)
    scale_one = inverse_rms(inputs)
    normed = (inputs * scale_one * gains[0]).astype(BF16)
    query_pre, key_pre, value_pre = (nn(normed, w_heads[j]) for j in range(3))
    shape = (rows, local_heads, head)
    cosine, sine = rope_tables(position, head)

    def head_norm(values, gain):
        return rotary(values * inverse_rms(values) * gain, cosine, sine)

    query_rot, query_pull = jax.vjp(head_norm, query_pre.reshape(shape), gain_query)
    key_rot, key_pull = jax.vjp(head_norm, key_pre.reshape(shape), gain_key)
    batch = (micro, group, local_heads, head)
    queries = query_rot.astype(BF16).reshape(batch)
    keys_low = key_rot.astype(BF16).reshape(batch)
    values_low = value_pre.astype(BF16).reshape(batch)
    same = (segment[:, :, None] == segment[:, None, :])[:, None]

    def scores_of():
        raw = jnp.einsum("gqhd,gkhd->ghqk", queries, keys_low, preferred_element_type=F32) * scale
        return jnp.where(same, raw, MASKED)

    scores = scores_of()
    highest = jnp.max(scores, -1, keepdims=True)
    log_total = highest + jnp.log(jnp.sum(jnp.exp(scores - highest), -1, keepdims=True))
    probs_low = jnp.exp(scores - log_total).astype(BF16)
    attended = jnp.einsum(
        "ghqk,gkhd->gqhd", probs_low, values_low, preferred_element_type=F32
    ).astype(BF16)
    (attended_full,) = gather_col([attended.reshape(rows, local_heads * head)], (1,), 2)

    hidden = inputs + nn(attended_full, full_o)
    scale_two = inverse_rms(hidden)
    normed_ffn = (hidden * scale_two * gains[1]).astype(BF16)
    logits = nn(normed_ffn, full_r)
    peak = jnp.max(jnp.where(member, logits, -jnp.inf), -1, keepdims=True)
    raised = jnp.where(member, jnp.exp(jnp.where(member, logits - peak, 0.0)), 0.0)
    gates = raised / jnp.sum(raised, -1, keepdims=True)
    gate_t = mine(gates, 1).reshape(micro, group, local_exp).transpose(2, 0, 1)[:, :, None, :]
    upstream_full = (upstream_low * live[:, None].astype(BF16)).reshape(micro, group, width)
    hn = normed_ffn.reshape(micro, group, width)

    outs, weight_grads = [], []
    for c, (wg, wu, wd) in zip(chunks, big):
        xe, dyr, hg, dgp, dup, ye, dxe, tok = expert_pass(
            counts[c], place_t[c], gate_t[c], hn, upstream_full, wg, wu, wd, capacity
        )
        gg, gu, gd = expert_grads(xe, dgp, dup, hg, dyr)
        hn, upstream_full, ye, dxe, tok, gg, gu, gd = lax.optimization_barrier(
            (hn, upstream_full, ye, dxe, tok, gg, gu, gd)
        )
        outs.append((ye, dxe, tok))
        weight_grads.append(
            [
                lax.psum_scatter(gg, "row", scatter_dimension=1, tiled=True),
                lax.psum_scatter(gu, "row", scatter_dimension=1, tiled=True),
                lax.psum_scatter(gd, "row", scatter_dimension=2, tiled=True),
            ]
        )
    def tie(value, c, j):
        value, done = lax.optimization_barrier((value, weight_grads[c][j]))
        weight_grads[c][j] = done
        return value

    back_sum = scatter_col(combine(place, [tie(o[1], 0, 2) for o in outs]), 3)
    mixed_sum = scatter_col(combine(place, [o[0] for o in outs]), 4)
    tok = jnp.concatenate([o[2] for o in outs], 0)
    tok = gather(tok, "col", 0)
    gate_dots = tok[:, :, 0].reshape(experts, rows).T
    hidden_part = mine(hidden, 1)
    mixed = (hidden_part + mixed_sum).astype(BF16)

    selected = gates * (gate_dots - jnp.sum(gates * gate_dots, -1, keepdims=True))
    logit_grad = selected.astype(BF16)
    router_part = mine(full_r, 0)
    normed_grad = back_sum + nt(logit_grad, router_part)
    grad_router = tn(mine(normed_ffn, 1), logit_grad)
    scaled_two = hidden_part * scale_two
    grad_gain_ffn = jnp.sum(normed_grad * scaled_two, 0)
    dot_two = jnp.sum(tok[:, :, 1].reshape(experts, rows), 0) + jnp.sum(
        logit_grad.astype(F32) * logits, 1
    )
    upstream_part = cotangent.astype(F32) * live[:, None]
    hidden_grad = (
        upstream_part
        + scale_two * (normed_grad * gain_ffn)
        - hidden_part * scale_two**2 * dot_two[:, None] / width
    )

    branch_grad = tie(hidden_grad.astype(BF16), 0, 0)
    attended_grad = scatter_col(nt(branch_grad, mine(full_o, 1)).astype(BF16), 5)
    attended_grad = tie(attended_grad.astype(BF16).reshape(batch), 0, 1)
    grad_out = tn(attended_full, branch_grad)
    scores_again = scores_of()
    probs = jnp.exp(scores_again - log_total)
    probs_again = probs.astype(BF16)
    probs_grad = jnp.einsum(
        "gqhd,gkhd->ghqk", attended_grad, values_low, preferred_element_type=F32
    )
    values_grad = jnp.einsum(
        "ghqk,gqhd->gkhd", probs_again, attended_grad, preferred_element_type=F32
    )
    score_grad = (probs * (probs_grad - jnp.sum(probs_grad * probs, -1, keepdims=True))).astype(
        BF16
    )
    query_grad_rot = (
        jnp.einsum("ghqk,gkhd->gqhd", score_grad, keys_low, preferred_element_type=F32) * scale
    )
    key_grad_rot = (
        jnp.einsum("ghqk,gqhd->gkhd", score_grad, queries, preferred_element_type=F32) * scale
    )
    query_grad, gain_query_part = query_pull(query_grad_rot.reshape(shape))
    key_grad, gain_key_part = key_pull(key_grad_rot.reshape(shape))
    flat = (rows, local_heads * head)
    heads_grad = [
        v.reshape(flat).astype(BF16) for v in (query_grad, key_grad, values_grad)
    ]
    back_heads = sum(nt(g, w_heads[j]) for j, g in enumerate(heads_grad))
    normed_back = scatter_col(tie(back_heads.astype(BF16), -1, 2), 6)
    pre = (query_pre, key_pre, value_pre)
    dot_part = sum(jnp.sum(g.astype(F32) * p, -1) for g, p in zip(heads_grad, pre))
    dot_one, gain_query_sum, gain_key_sum = lax.psum(
        (dot_part, gain_query_part, gain_key_part), "col"
    )
    scale_one_part = scale_one
    inputs_part = tokens.astype(F32)
    grad_gain_attn = jnp.sum(normed_back * inputs_part * scale_one_part, 0)
    input_grad = (
        hidden_grad
        + scale_one_part * (normed_back * gain_attn)
        - inputs_part * scale_one_part**2 * dot_one[:, None] / width
    )

    grad_gate, grad_up, grad_down = (
        jnp.concatenate([w[j] for w in weight_grads], 0).astype(F32) for j in range(3)
    )

    heads_weights = jnp.stack([tn(normed, g) for g in heads_grad]).astype(BF16)
    heads_weights = heads_weights.reshape(3, n_col, part, local_heads * head).transpose(1, 0, 2, 3)
    heads_weights = lax.all_to_all(heads_weights, "col", split_axis=0, concat_axis=0, tiled=True)
    heads_weights = heads_weights.transpose(1, 2, 0, 3).reshape(3 * part, hd)
    heads_weights = lax.psum_scatter(heads_weights, "row", scatter_dimension=1, tiled=True)
    grad_query, grad_key, grad_value = (
        heads_weights[j * part : (j + 1) * part].astype(F32) for j in range(3)
    )
    out_weights = lax.all_to_all(
        grad_out.astype(BF16).reshape(n_col, local_heads * head, part),
        "col",
        split_axis=0,
        concat_axis=0,
        tiled=True,
    )
    out_weights = out_weights.transpose(1, 0, 2).reshape(local_heads * head, width)
    grad_out = lax.psum_scatter(out_weights, "row", scatter_dimension=1, tiled=True).astype(F32)
    grad_router = lax.psum_scatter(
        grad_router.astype(BF16), "row", scatter_dimension=1, tiled=True
    ).astype(F32)
    grad_gain_attn, grad_gain_ffn, grad_gain_query, grad_gain_key = lax.psum(
        (grad_gain_attn, grad_gain_ffn, gain_query_sum, gain_key_sum), "row"
    )
    return (
        mixed,
        input_grad,
        grad_gain_attn,
        grad_gain_ffn,
        grad_gain_query,
        grad_gain_key,
        grad_query,
        grad_key,
        grad_value,
        grad_out,
        grad_router,
        grad_gate,
        grad_up,
        grad_down,
    )


def solution(mesh):
    placed = (
        P("row", "col"),
        P("col"),
        P("col"),
        P(),
        P(),
        P("col", "row"),
        P("col", "row"),
        P("col", "row"),
        P("col", "row"),
        P("col", "row"),
        P("col", "row", None),
        P("col", "row", None),
        P("col", None, "row"),
        P("row", None),
        P("row", None),
        P("row", "col"),
    )
    return jax.shard_map(
        shards,
        mesh=mesh,
        in_specs=placed,
        out_specs=(
            P("row", "col"),
            P("row", "col"),
            P("col"),
            P("col"),
            P(),
            P(),
            P("col", "row"),
            P("col", "row"),
            P("col", "row"),
            P("col", "row"),
            P("col", "row"),
            P("col", "row", None),
            P("col", "row", None),
            P("col", None, "row"),
        ),
        check_vma=False,
    )
```

```python
import functools
import math

import jax
import jax.numpy as jnp
from jax import lax
from jax.experimental import pallas as pl
from jax.experimental.pallas import tpu as pltpu
from jax.sharding import PartitionSpec as P

EPSILON = 1e-06
ROPE_BASE = 10000.0
MASKED = -1e30
F32 = jnp.float32
BF16 = jnp.bfloat16
VMEM_LIMIT = 60 * 1024 * 1024
MESH = pl.DeviceIdType.MESH


def inverse_rms(values):
    return lax.rsqrt(jnp.mean(values * values, -1, keepdims=True) + EPSILON)


def rope_tables(position, head):
    half = head // 2
    inverse = jnp.exp(-math.log(ROPE_BASE) * 2.0 / head * jnp.arange(half, dtype=F32))
    angles = position[:, None] * inverse[None, :]
    return jnp.cos(angles)[:, None, :], jnp.sin(angles)[:, None, :]


def rotary(values, cosine, sine):
    half = values.shape[-1] // 2
    first = values[..., :half]
    second = values[..., half:]
    return jnp.concatenate([first * cosine - second * sine, second * cosine + first * sine], -1)


def layout(lengths_row, group):
    ends = jnp.cumsum(lengths_row)
    starts = ends - lengths_row
    row_index = jnp.arange(group, dtype=jnp.int32)
    segment = jnp.sum((row_index[:, None] >= ends[None, :]).astype(jnp.int32), 1)
    member = segment[:, None] == jnp.arange(lengths_row.shape[0], dtype=jnp.int32)[None, :]
    position = (row_index - jnp.sum(jnp.where(member, starts[None, :], 0), 1)).astype(F32)
    live = (segment < lengths_row.shape[0] - 1).astype(F32)
    return (segment, position, live)


def nn(a, b):
    return lax.dot_general(a, b, (((1,), (0,)), ((), ())), preferred_element_type=F32)


def nt(a, b):
    return lax.dot_general(a, b, (((1,), (1,)), ((), ())), preferred_element_type=F32)


def tn(a, b):
    return lax.dot_general(a, b, (((0,), (0,)), ((), ())), preferred_element_type=F32)


def expert_body(
    counts, place, gate, hn, dy, wg, wu, wd, xe_o, dyr_o, hg_o, dgp_o, dup_o, ye_o, dxe_o, tok_o
):
    e, g, i = pl.program_id(0), pl.program_id(1), pl.program_id(2)
    rows = xe_o.shape[2]
    base = i * rows

    @pl.when(i == 0)
    def _():
        tok_o[...] = jnp.zeros_like(tok_o)

    @pl.when(counts[e, g] <= base)
    def _():
        for ref in (xe_o, dyr_o, hg_o, dgp_o, dup_o, ye_o, dxe_o):
            ref[...] = jnp.zeros_like(ref)

    @pl.when(counts[e, g] > base)
    def _():
        slot = lax.broadcasted_iota(jnp.int32, (rows, place.shape[3]), 0) + base
        hit = slot == place[0, 0]
        pick = jnp.where(hit, 1.0, 0.0).astype(BF16)
        weight = jnp.sum(jnp.where(hit, gate[0, 0], 0.0), 1, keepdims=True)
        xe = nn(pick, hn[0]).astype(BF16)
        xe_o[0, 0] = xe
        gp = nn(xe, wg[0])
        up = nn(xe, wu[0])
        sig = jax.nn.sigmoid(gp)
        silu = gp * sig
        hid = silu * up
        hg = (hid * weight).astype(BF16)
        hg_o[0, 0] = hg
        ye_o[0, 0] = nn(hg, wd[0]).astype(BF16)
        dyr = nn(pick, dy[0]).astype(BF16)
        dyr_o[0, 0] = dyr
        back = nt(dyr, wd[0])
        dgate = jnp.sum(back * hid, 1, keepdims=True)
        dhid = back * weight
        dgp = (dhid * up * sig * (1.0 + gp * (1.0 - sig))).astype(BF16)
        dup = (dhid * silu).astype(BF16)
        dgp_o[0, 0] = dgp
        dup_o[0, 0] = dup
        dots = jnp.sum(dgp.astype(F32) * gp + dup.astype(F32) * up, 1, keepdims=True)
        dxe_o[0, 0] = (nt(dgp, wg[0]) + nt(dup, wu[0])).astype(BF16)
        tok_o[0, 0, 0:1, :] += jnp.sum(jnp.where(hit, dgate, 0.0), 0, keepdims=True)
        tok_o[0, 0, 1:2, :] += jnp.sum(jnp.where(hit, dots, 0.0), 0, keepdims=True)


def expert_pass(counts, place, gate, hn, dy, wg, wu, wd, capacity, first):
    experts = counts.shape[0]
    _, width, ff = wg.shape
    micro, group, _ = hn.shape
    rows = min(256, capacity)
    blocks = capacity // rows
    tall = lambda e, g, i, c: (e, g, i, 0)
    line = lambda e, g, i, c: (e, g, 0, 0)
    whole = lambda e, g, i, c: (g, 0, 0)
    matrix = lambda e, g, i, c: (e + first, 0, 0)
    slots = lambda n: jax.ShapeDtypeStruct((experts, micro, capacity, n), BF16)
    sizes = (width, width, ff, ff, ff, width, width)
    flops = 2 * experts * micro * capacity * width * (6 * ff + 2 * group)
    return pl.pallas_call(
        expert_body,
        grid_spec=pltpu.PrefetchScalarGridSpec(
            num_scalar_prefetch=1,
            grid=(experts, micro, blocks),
            in_specs=[
                pl.BlockSpec((1, 1, 1, group), line),
                pl.BlockSpec((1, 1, 1, group), line),
                pl.BlockSpec((1, group, width), whole, pipeline_mode=pl.Buffered(1)),
                pl.BlockSpec((1, group, width), whole, pipeline_mode=pl.Buffered(1)),
                pl.BlockSpec((1, width, ff), matrix),
                pl.BlockSpec((1, width, ff), matrix),
                pl.BlockSpec((1, ff, width), matrix),
            ],
            out_specs=[pl.BlockSpec((1, 1, rows, n), tall) for n in sizes]
            + [pl.BlockSpec((1, 1, 2, group), line)],
        ),
        out_shape=[slots(n) for n in sizes]
        + [jax.ShapeDtypeStruct((experts, micro, 2, group), F32)],
        compiler_params=pltpu.CompilerParams(vmem_limit_bytes=VMEM_LIMIT),
        cost_estimate=pl.CostEstimate(
            flops=flops, bytes_accessed=100 << 20, transcendentals=experts * micro * capacity * ff
        ),
        name="expert_pass",
    )(counts, place, gate, hn, dy, wg, wu, wd)


def grads_body(xe, dgp, dup, hg, dyr, gg_o, gu_o, gd_o):
    part = xe[0]
    gg_o[0] = tn(part, dgp[0]).astype(BF16)
    gu_o[0] = tn(part, dup[0]).astype(BF16)
    gd_o[0] = tn(hg[0], dyr[0]).astype(BF16)


def expert_grads(xe, dgp, dup, hg, dyr):
    experts, micro, capacity, width = xe.shape
    ff = dgp.shape[3]
    rows = micro * capacity
    xe, dyr = (a.reshape(experts, rows, width) for a in (xe, dyr))
    dgp, dup, hg = (a.reshape(experts, rows, ff) for a in (dgp, dup, hg))
    part = min(512, width)
    return pl.pallas_call(
        grads_body,
        grid=(experts, width // part),
        in_specs=[
            pl.BlockSpec((1, rows, part), lambda e, r: (e, 0, r)),
            pl.BlockSpec((1, rows, ff), lambda e, r: (e, 0, 0)),
            pl.BlockSpec((1, rows, ff), lambda e, r: (e, 0, 0)),
            pl.BlockSpec((1, rows, ff), lambda e, r: (e, 0, 0)),
            pl.BlockSpec((1, rows, part), lambda e, r: (e, 0, r)),
        ],
        out_specs=[
            pl.BlockSpec((1, part, ff), lambda e, r: (e, r, 0)),
            pl.BlockSpec((1, part, ff), lambda e, r: (e, r, 0)),
            pl.BlockSpec((1, ff, part), lambda e, r: (e, 0, r)),
        ],
        out_shape=[
            jax.ShapeDtypeStruct((experts, width, ff), BF16),
            jax.ShapeDtypeStruct((experts, width, ff), BF16),
            jax.ShapeDtypeStruct((experts, ff, width), BF16),
        ],
        compiler_params=pltpu.CompilerParams(vmem_limit_bytes=VMEM_LIMIT),
        cost_estimate=pl.CostEstimate(
            flops=6 * experts * rows * width * ff, bytes_accessed=experts * 26 << 20, transcendentals=0
        ),
        name="expert_grads",
    )(xe, dgp, dup, hg, dyr)


def combine_body(place, *refs):
    out = refs[-1]
    slots = refs[:-1]
    total = jnp.zeros((out.shape[1], out.shape[2]), F32)
    at = 0
    for ref in slots:
        capacity = ref.shape[2]
        for e in range(ref.shape[0]):
            slot = lax.broadcasted_iota(jnp.int32, (out.shape[1], capacity), 1)
            pick = jnp.where(slot == place[0, :, at : at + 1], 1.0, 0.0).astype(BF16)
            total = total + nn(pick, ref[e, 0])
            at += 1
    out[0] = total.astype(BF16)


def combine(place, slots):
    micro, group, local = place.shape
    capacity, width = slots[0].shape[2:]
    tile = min(256, group)
    return pl.pallas_call(
        combine_body,
        grid=(micro, group // tile),
        in_specs=[pl.BlockSpec((1, tile, local), lambda g, i: (g, i, 0))]
        + [
            pl.BlockSpec((s.shape[0], 1, capacity, width), lambda g, i: (0, g, 0, 0))
            for s in slots
        ],
        out_specs=pl.BlockSpec((1, tile, width), lambda g, i: (g, i, 0)),
        out_shape=jax.ShapeDtypeStruct((micro, group, width), BF16),
        compiler_params=pltpu.CompilerParams(vmem_limit_bytes=VMEM_LIMIT),
        cost_estimate=pl.CostEstimate(
            flops=2 * micro * group * local * capacity * width,
            bytes_accessed=micro * (local * capacity + group) * width * 2,
            transcendentals=0,
        ),
        name="combine",
    )(place, *slots).reshape(micro * group, width)


def places():
    row, col = lax.axis_index("row"), lax.axis_index("col")
    n_row, n_col = lax.axis_size("row"), lax.axis_size("col")
    return row, col, n_row, n_col


def remote(src, dst, send_sem, recv_sem, where):
    return pltpu.make_async_remote_copy(
        src_ref=src,
        dst_ref=dst,
        send_sem=send_sem,
        recv_sem=recv_sem,
        device_id=where,
        device_id_type=MESH,
    )


def shake(sources, targets):
    barrier = pltpu.get_barrier_semaphore()
    for ok, where in sources:
        if ok is True:
            pl.semaphore_signal(barrier, inc=1, device_id=where, device_id_type=MESH)
        else:

            @pl.when(ok)
            def _():
                pl.semaphore_signal(barrier, inc=1, device_id=where, device_id_type=MESH)

    count = 0
    for ok in targets:
        count = count + (1 if ok is True else jnp.where(ok, 1, 0))
    pl.semaphore_wait(barrier, count)


def line_peers():
    row, col, n_row, n_col = places()
    pair, core = col // 2, col % 2
    return [
        (True, (row, pair * 2 + 1 - core)),
        (pair > 0, (row, (pair - 1) * 2 + core)),
        (pair < n_col // 2 - 1, (row, (pair + 1) * 2 + core)),
    ]


def row_peers():
    row, col, n_row, n_col = places()
    return [(True, ((row + k) % n_row, col)) for k in range(1, n_row)]


def col_slice(ref, index, size):
    return ref.at[..., pl.ds(pl.multiple_of(index * size, size), size)]


def line_gather(axes, ins, outs, sems):
    own_sem, right_s, right_r, left_s, left_r, side_s, side_r = sems
    n = len(ins)
    row, col, n_row, n_col = places()
    pairs, pair, core = n_col // 2, col // 2, col % 2

    def at(pair_index, core_index):
        return (row, pair_index * 2 + core_index)

    def block(j, source):
        size = ins[j].shape[axes[j]]
        if axes[j] == 0:
            return outs[j].at[pl.ds(pl.multiple_of(source * size, size), size)]
        return col_slice(outs[j], source, size)

    def right(j, s):
        source = (pair - s) * 2 + core
        src = ins[j] if s == 0 else block(j, source)
        return remote(src, block(j, source), right_s.at[j, s], right_r.at[j, s], at(pair + 1, core))

    def left(j, s):
        source = (pair + s) * 2 + core
        src = ins[j] if s == 0 else block(j, source)
        return remote(src, block(j, source), left_s.at[j, s], left_r.at[j, s], at(pair - 1, core))

    def side(j, source_pair, first=False):
        source = source_pair * 2 + core
        src = ins[j] if first else block(j, source)
        return remote(
            src,
            block(j, source),
            side_s.at[j, source_pair],
            side_r.at[j, source_pair],
            at(pair, 1 - core),
        )

    def arrived(j, recvs, slot, source):
        remote(
            ins[j], block(j, source), recvs.at[j, slot], recvs.at[j, slot], at(pair, 1 - core)
        ).wait_recv()

    def own(j):
        return pltpu.make_async_copy(ins[j], block(j, col), own_sem.at[j])

    def begin():
        for j in range(n):

            @pl.when(pair < pairs - 1)
            def _():
                right(j, 0).start()

            @pl.when(pair > 0)
            def _():
                left(j, 0).start()

        for j in range(n):
            side(j, pair, True).start()
            own(j).start()

    def middle():
        for s in range(1, pairs):
            for j in range(n):

                @pl.when(pair >= s)
                def _():
                    arrived(j, right_r, s - 1, (pair - s) * 2 + core)

                    @pl.when(pair < pairs - 1)
                    def _():
                        right(j, s).start()

                    side(j, pair - s).start()

                @pl.when(pair + s < pairs)
                def _():
                    arrived(j, left_r, s - 1, (pair + s) * 2 + core)

                    @pl.when(pair > 0)
                    def _():
                        left(j, s).start()

                    side(j, pair + s).start()

    def end():
        for j in range(n):
            own(j).wait()
            for p in range(pairs):
                side(j, p).wait_send()
                arrived(j, side_r, p, p * 2 + 1 - core)
            for s in range(pairs):

                @pl.when((pair >= s) & (pair < pairs - 1))
                def _():
                    right(j, s).wait_send()

                @pl.when((pair + s < pairs) & (pair > 0))
                def _():
                    left(j, s).wait_send()

    return begin, middle, end


def line_sems(n, pairs):
    dma = pltpu.SemaphoreType.DMA
    return [dma((n,))] + [dma((n, pairs))] * 6


def front_body(
    tokens, gains, cot, wq, wk, wv, wo, wr, wd, x_o, gains_o, dy_o, wh_o, wo_o, wr_o, wd_o, *sems
):
    line, (heads_s, heads_r, row_s, row_r, own_s, down_s, down_r) = sems[:7], sems[7:]
    row, col, n_row, n_col = places()
    head = wh_o.shape[2]
    part = wq.shape[0]
    per = wq.shape[1] // head
    shared = wd.shape[2]
    small = [(wo, wo_o), (wr, wr_o)]
    begin, middle, end = line_gather(
        (1, 1, 1), [tokens, gains, cot], [x_o, gains_o, dy_o], line
    )

    def heads_dst(m, source):
        return wh_o.at[m, pl.ds(pl.multiple_of(source * part, part), part), :]

    def heads(m, r, j):
        src = (wq, wk, wv)[m].at[:, pl.ds(j * head, head)]
        return remote(
            src,
            heads_dst(m, col),
            heads_s.at[m, r * per + j],
            heads_r.at[m, col],
            (r, row * per + j),
        )

    def heads_own(m, j):
        src = (wq, wk, wv)[m].at[:, pl.ds(j * head, head)]
        return pltpu.make_async_copy(src, heads_dst(m, col), own_s.at[m])

    def to_self(r, j):
        return (row == r) & (col == row * per + j)

    def heads_come(m, c):
        return remote(
            heads_dst(m, c), heads_dst(m, c), heads_r.at[m, c], heads_r.at[m, c], (row, col)
        )

    def from_self(c):
        return (row == col // per) & (col == c)

    def small_dst(k, source):
        if k == 0:
            return col_slice(wo_o, source, wo.shape[1])
        size = wr.shape[0]
        return wr_o.at[pl.ds(pl.multiple_of(source * size, size), size), :]

    def small_copy(k, step):
        return remote(
            small[k][0],
            small_dst(k, row),
            row_s.at[k, step],
            row_r.at[k, step],
            ((row + step) % n_row, col),
        )

    def small_come(k, step):
        source = (row + n_row - step) % n_row
        return remote(
            small[k][0], small_dst(k, source), row_s.at[k, step], row_r.at[k, step], (source, col)
        )

    def small_own(k):
        return pltpu.make_async_copy(small[k][0], small_dst(k, row), own_s.at[3 + k])

    couples = n_row // 2
    couple, side = row // 2, row % 2

    def down_to(where_row, slot):
        return remote(
            wd, col_slice(wd_o, row, shared), down_s.at[slot], down_r.at[slot], (where_row, col)
        )

    def down_come(source_row, slot):
        return remote(
            wd, col_slice(wd_o, source_row, shared), down_s.at[slot], down_r.at[slot], (row, col)
        )

    def down_own():
        return pltpu.make_async_copy(wd, col_slice(wd_o, row, shared), own_s.at[5])

    inner = couple * 2 + 1 - side

    def outer(k):
        return ((couple + k) % couples) * 2 + side

    sources = line_peers() + row_peers()
    targets = [ok for ok, _ in sources]
    for c in range(n_col):
        sources.append((jnp.logical_not(from_self(c)), (col // per, c)))
    for r in range(n_row):
        for j in range(per):
            targets.append(jnp.logical_not(to_self(r, j)))
    shake(sources, targets)
    begin()
    for k in range(2):
        small_own(k).start()
        for step in range(1, n_row):
            small_copy(k, step).start()
    for r in range(n_row):
        for j in range(per):

            @pl.when(to_self(r, j))
            def _():
                for m in range(3):
                    heads_own(m, j).start()

            @pl.when(jnp.logical_not(to_self(r, j)))
            def _():
                for m in range(3):
                    heads(m, r, j).start()

    down_to(inner, 0).start()
    for k in range(1, couples):
        down_to(outer(k), k).start()
    down_own().start()
    middle()
    end()
    for k in range(2):
        small_own(k).wait()
        for step in range(1, n_row):
            small_copy(k, step).wait_send()
            small_come(k, step).wait_recv()
    for r in range(n_row):
        for j in range(per):

            @pl.when(to_self(r, j))
            def _():
                for m in range(3):
                    heads_own(m, j).wait()

            @pl.when(jnp.logical_not(to_self(r, j)))
            def _():
                for m in range(3):
                    heads(m, r, j).wait_send()

    for c in range(n_col):

        @pl.when(jnp.logical_not(from_self(c)))
        def _():
            for m in range(3):
                heads_come(m, c).wait_recv()

    down_own().wait()
    down_to(inner, 0).wait_send()
    down_come(inner, 0).wait_recv()
    for k in range(1, couples):
        down_to(outer(k), k).wait_send()
        down_come(((couple + couples - k) % couples) * 2 + side, k).wait_recv()


ANY = pl.BlockSpec(memory_space=pl.ANY)


def front(tokens, gains, cot, wq, wk, wv, wo, wr, wd, head, ident):
    n_row, n_col = lax.axis_size("row"), lax.axis_size("col")
    rows, part = tokens.shape
    width = part * n_col
    per = wq.shape[1] // head
    local_exp, ff, shared = wd.shape
    dma = pltpu.SemaphoreType.DMA
    shapes = [
        ((rows, width), BF16),
        ((gains.shape[0], width), F32),
        ((rows, width), BF16),
        ((3, width, head), BF16),
        ((wo.shape[0], wo.shape[1] * n_row), BF16),
        ((wr.shape[0] * n_row, part), BF16),
        ((local_exp, ff, width), BF16),
    ]
    return pl.pallas_call(
        front_body,
        in_specs=[ANY] * 9,
        out_specs=[ANY] * 7,
        out_shape=[jax.ShapeDtypeStruct(s, t) for s, t in shapes],
        scratch_shapes=line_sems(3, n_col // 2)
        + [
            dma((3, n_row * per)),
            dma((3, n_col)),
            dma((2, n_row)),
            dma((2, n_row)),
            dma((6,)),
            dma((n_row,)),
            dma((n_row,)),
        ],
        compiler_params=pltpu.CompilerParams(collective_id=ident, has_side_effects=True),
        cost_estimate=pl.CostEstimate(
            flops=0, bytes_accessed=rows * width * 64, transcendentals=0
        ),
        name="front",
    )(tokens, gains, cot, wq, wk, wv, wo, wr, wd)


def middle_body(o, wo, wr, wd_in, o_o, wo_o, wr_o, wd_o, *sems):
    line, (near_s, near_r, far_s, far_r) = sems[:7], sems[7:]
    row, col, n_row, n_col = places()
    begin, middle, end = line_gather((1, 0, 1), [o, wo, wr], [o_o, wo_o, wr_o], line)
    couples = n_row // 2
    couple, side = row // 2, row % 2
    shared = wd_o.shape[2] // n_row
    half = wd_o.shape[0] // 2
    inner = couple * 2 + 1 - side

    def piece(second, source_row):
        return col_slice(wd_o.at[pl.ds(half if second else 0, half)], source_row, shared)

    def near(k):
        block = ((couple + k) % couples) * 2 + side
        return remote(
            piece(False, block), piece(False, block), near_s.at[k], near_r.at[k], (inner, col)
        )

    def near_come(k):
        block = ((couple + k) % couples) * 2 + 1 - side
        return remote(
            piece(False, block), piece(False, block), near_s.at[k], near_r.at[k], (inner, col)
        )

    def far(k):
        where = ((couple + k) % couples) * 2 + side
        return remote(
            piece(True, inner), piece(True, inner), far_s.at[k], far_r.at[k], (where, col)
        )

    def far_come(k):
        source = (couple + couples - k) % couples
        block = source * 2 + 1 - side
        return remote(
            piece(True, block), piece(True, block), far_s.at[k], far_r.at[k], (source * 2 + side, col)
        )

    sources = line_peers() + row_peers()
    shake(sources, [ok for ok, _ in sources])
    begin()
    for k in range(1, couples):
        near(k).start()
        far(k).start()
    middle()
    end()
    for k in range(1, couples):
        near(k).wait_send()
        near_come(k).wait_recv()
        far(k).wait_send()
        far_come(k).wait_recv()


def middle_gather(o, wo, wr, wd, ident):
    n_row, n_col = lax.axis_size("row"), lax.axis_size("col")
    dma = pltpu.SemaphoreType.DMA
    shapes = [
        (o.shape[0], o.shape[1] * n_col),
        (wo.shape[0] * n_col, wo.shape[1]),
        (wr.shape[0], wr.shape[1] * n_col),
        wd.shape,
    ]
    return pl.pallas_call(
        middle_body,
        in_specs=[ANY] * 4,
        out_specs=[ANY] * 4,
        out_shape=[jax.ShapeDtypeStruct(s, BF16) for s in shapes],
        input_output_aliases={3: 3},
        scratch_shapes=line_sems(3, n_col // 2) + [dma((n_row,))] * 4,
        compiler_params=pltpu.CompilerParams(collective_id=ident, has_side_effects=True),
        cost_estimate=pl.CostEstimate(
            flops=0, bytes_accessed=o.shape[0] * o.shape[1] * n_col * 64, transcendentals=0
        ),
        name="middle_gather",
    )(o, wo, wr, wd)


def scatter_body(part, stage, *refs):
    n_in = (1, 4, 4)[stage]
    n_out = (1, 4, 4)[stage]
    x, ins = refs[0], refs[1:n_in]
    out, outs = refs[n_in], refs[n_in + 1 : n_in + n_out]
    rest = refs[n_in + n_out :]
    acc, side, from_left, from_right, load, side_s, side_r = rest[:7]
    right_s, right_r, left_s, left_r = rest[7:11]
    row, col, n_row, n_col = places()
    pairs, pair, core = n_col // 2, col // 2, col % 2
    couples, couple, inside = n_row // 2, row // 2, row % 2
    inner = couple * 2 + 1 - inside
    rows = out.shape[0]
    cuts = load.shape[1]
    height = rows // cuts
    tile = min(256, height)

    def at(pair_index, core_index):
        return (row, pair_index * 2 + core_index)

    def block(owner, q):
        return x.at[
            pl.ds(q * height, height), pl.ds(pl.multiple_of(owner * part, part), part)
        ]

    def cut(ref, d, q):
        return ref.at[d, pl.ds(q * height, height)]

    def fetch(d, q):
        return pltpu.make_async_copy(block(d * 2 + core, q), cut(acc, d, q), load.at[d, q])

    def across(d, q):
        return remote(
            block(d * 2 + 1 - core, q),
            cut(side, d, q),
            side_s.at[d, q],
            side_r.at[d, q],
            at(pair, 1 - core),
        )

    def right(d, q):
        return remote(
            cut(acc, d, q),
            cut(from_left, d, q),
            right_s.at[d, q],
            right_r.at[d, q],
            at(pair + 1, core),
        )

    def left(d, q):
        return remote(
            cut(acc, d, q),
            cut(from_right, d, q),
            left_s.at[d, q],
            left_r.at[d, q],
            at(pair - 1, core),
        )

    copies, arrivals, own = [], [], []
    if stage:
        small_s, small_r, step_s, step_r, own_s = rest[11:]
        extra, extra_o = ins[0], outs[0]
        for k in range(1, n_col):
            where, source = (col + k) % n_col, (col + n_col - k) % n_col
            copies.append(
                remote(extra, extra_o.at[col], small_s.at[k], small_r.at[k], (row, where))
            )
            arrivals.append(
                remote(extra, extra_o.at[source], small_s.at[k], small_r.at[k], (row, where))
            )
        own.append(pltpu.make_async_copy(extra, extra_o.at[col], own_s))
    if stage == 1:
        first, second = ins[1:]
        near_o, far_o = outs[1:]
        shared = first.shape[2] // n_row
        for k in range(couples):
            dst = near_o.at[k]
            there = remote(
                col_slice(first, k * 2 + 1 - inside, shared),
                dst,
                step_s.at[k],
                step_r.at[k],
                (inner, col),
            )
            copies.append(there)
            arrivals.append(there)
        for k in range(1, couples):
            there = remote(
                col_slice(second, (couple + k) % couples, 2 * shared),
                far_o.at[k - 1],
                step_s.at[couples + k],
                step_r.at[couples + k],
                (((couple + k) % couples) * 2 + inside, col),
            )
            copies.append(there)
            arrivals.append(there)
    if stage == 2:
        first, second = ins[1:]
        near_o, far_o = outs[1:]
        for k in range(1, couples):
            there = remote(
                first.at[k - 1],
                far_o.at[k - 1],
                step_s.at[k],
                step_r.at[k],
                (((couple + k) % couples) * 2 + inside, col),
            )
            copies.append(there)
            arrivals.append(there)
        there = remote(second, near_o, step_s.at[0], step_r.at[0], (inner, col))
        copies.append(there)
        arrivals.append(there)

    if stage:
        peers = [(True, (row, (col + k) % n_col)) for k in range(1, n_col)] + row_peers()
    else:
        peers = line_peers()
    shake(peers, [ok for ok, _ in peers])
    order = []
    for t in range(pairs):
        for d in (pairs - 1 - t, t):
            if d not in order:
                order.append(d)
    for d in order:
        for q in range(cuts):
            across(d, q).start()
            fetch(d, q).start()
    for c in copies + own:
        c.start()

    def add(q, into, *sources):
        def step(i, _):
            lines = pl.ds(pl.multiple_of(q * height + i * tile, tile), tile)
            total = sources[0][lines, :].astype(F32)
            for ref in sources[1:]:
                total = total + ref[lines, :].astype(F32)
            into[lines, :] = total.astype(into.dtype)
            return 0

        lax.fori_loop(0, height // tile, step, 0)

    def ready(d, q):
        fetch(d, q).wait()
        across(d, q).wait_recv()

    def go_right(d, q):
        ready(d, q)

        @pl.when(pair > 0)
        def _():
            right(d, q).wait_recv()
            add(q, acc.at[d], acc.at[d], side.at[d], from_left.at[d])

        @pl.when(pair == 0)
        def _():
            add(q, acc.at[d], acc.at[d], side.at[d])

        right(d, q).start()

    def go_left(d, q):
        ready(d, q)

        @pl.when(pair < pairs - 1)
        def _():
            left(d, q).wait_recv()
            add(q, acc.at[d], acc.at[d], side.at[d], from_right.at[d])

        @pl.when(pair == pairs - 1)
        def _():
            add(q, acc.at[d], acc.at[d], side.at[d])

        left(d, q).start()

    for t in range(pairs - 1):
        far, near = pairs - 1 - t, t
        for q in range(cuts):

            @pl.when(far > pair)
            def _():
                go_right(far, q)

            @pl.when(near < pair)
            def _():
                go_left(near, q)

    for q in range(cuts):
        ready(pair, q)

        @pl.when(pair == 0)
        def _():
            left(pair, q).wait_recv()
            add(q, out, acc.at[pair], side.at[pair], from_right.at[pair])

        @pl.when(pair == pairs - 1)
        def _():
            right(pair, q).wait_recv()
            add(q, out, acc.at[pair], side.at[pair], from_left.at[pair])

        @pl.when((pair > 0) & (pair < pairs - 1))
        def _():
            left(pair, q).wait_recv()
            right(pair, q).wait_recv()
            add(q, out, acc.at[pair], side.at[pair], from_left.at[pair], from_right.at[pair])

    for d in range(pairs):
        for q in range(cuts):
            across(d, q).wait_send()

            @pl.when(pair < d)
            def _():
                right(d, q).wait_send()

            @pl.when(pair > d)
            def _():
                left(d, q).wait_send()

    for c in copies:
        c.wait_send()
    for c in arrivals:
        c.wait_recv()
    for c in own:
        c.wait()


def scatter_col(x, ident, stage=0, others=()):
    n_row, n_col = lax.axis_size("row"), lax.axis_size("col")
    pairs, couples = n_col // 2, n_row // 2
    rows, part = x.shape[0], x.shape[1] // n_col
    cuts = 4 if rows % 1024 == 0 else 1
    dma = pltpu.SemaphoreType.DMA
    buffer = pltpu.VMEM((pairs, rows, part), BF16)
    scratch = [buffer] * 4 + [dma((pairs, cuts))] * 7
    out_shape = [jax.ShapeDtypeStruct((rows, part), F32)]
    if stage:
        extra = others[0]
        out_shape.append(jax.ShapeDtypeStruct((n_col,) + extra.shape, extra.dtype))
        scratch += [dma((n_col,)), dma((n_col,)), dma((n_row + 2,)), dma((n_row + 2,)), dma(())]
    if stage == 1:
        half, ff, width = others[1].shape
        shared = width // n_row
        out_shape += [
            jax.ShapeDtypeStruct((couples, half, ff, shared), BF16),
            jax.ShapeDtypeStruct((couples - 1, half, ff, 2 * shared), BF16),
        ]
    if stage == 2:
        out_shape += [
            jax.ShapeDtypeStruct(others[2].shape, BF16),
            jax.ShapeDtypeStruct(others[1].shape, BF16),
        ]
    return pl.pallas_call(
        functools.partial(scatter_body, part, stage),
        in_specs=[ANY] * (1 + len(others)),
        out_specs=[pl.BlockSpec(memory_space=pltpu.VMEM)] + [ANY] * (len(out_shape) - 1),
        out_shape=out_shape,
        scratch_shapes=scratch,
        compiler_params=pltpu.CompilerParams(
            vmem_limit_bytes=VMEM_LIMIT, collective_id=ident, has_side_effects=True
        ),
        cost_estimate=pl.CostEstimate(
            flops=0, bytes_accessed=rows * part * n_col * 40, transcendentals=0
        ),
        name="scatter_col",
    )(x, *others)


def shards(
    tokens,
    gain_attn,
    gain_ffn,
    gain_query,
    gain_key,
    w_query,
    w_key,
    w_value,
    w_out,
    w_router,
    w_gate,
    w_up,
    w_down,
    routes,
    lengths,
    cotangent,
):
    n_col = lax.axis_size("col")
    n_row = lax.axis_size("row")
    col = lax.axis_index("col")
    micro, spans = lengths.shape
    rows, part = tokens.shape
    group = rows // micro
    width = part * n_col
    head = gain_query.shape[0]
    local_exp = w_gate.shape[0]
    experts = local_exp * n_col
    topk = routes.shape[1]
    capacity = 2 * group * topk // experts
    local_heads = w_out.shape[0] // head
    hd = w_out.shape[0] * n_col
    scale = head ** (-0.5)

    def gather(value, axis_name, axis):
        return lax.all_gather(value, axis_name, axis=axis, tiled=True)

    def mine(value, axis):
        size = value.shape[axis] // n_col
        return lax.dynamic_slice_in_dim(value, col * size, size, axis)

    step = max(1, local_exp // 2)
    chunks = [slice(at, at + step) for at in range(0, local_exp, step)]
    full_g = gather(w_gate, "row", 1)
    full_u = gather(w_up, "row", 1)
    inputs_low, gains, upstream_low, w_heads, rows_o, rows_r, half_d = front(
        tokens,
        jnp.stack([gain_attn, gain_ffn]),
        cotangent,
        w_query,
        w_key,
        w_value,
        w_out,
        w_router.T,
        w_down,
        head,
        0,
    )

    segment, position, live = jax.vmap(lambda l: layout(l, group))(lengths)
    position = position.reshape(rows)
    live = live.reshape(rows)
    member = jnp.any(
        routes[:, None, :] == jnp.arange(experts, dtype=jnp.int32)[None, :, None], -1
    )
    member_f = member.astype(F32)
    member_loc = mine(member_f, 1).reshape(micro, group, local_exp)
    lower = (
        jnp.arange(group, dtype=jnp.int32)[:, None] > jnp.arange(group, dtype=jnp.int32)[None, :]
    ).astype(BF16)
    before = jnp.einsum("st,gte->gse", lower, member_loc.astype(BF16), preferred_element_type=F32)
    place = jnp.where(member_loc > 0, before, -1.0).astype(jnp.int32)
    counts = jnp.sum(member_loc, 1).astype(jnp.int32).T
    place_t = place.transpose(2, 0, 1)[:, :, None, :]

    inputs = inputs_low.astype(F32)
    scale_one = inverse_rms(inputs)
    normed = (inputs * scale_one * gains[0]).astype(BF16)
    query_pre, key_pre, value_pre = (nn(normed, w_heads[j]) for j in range(3))
    shape = (rows, local_heads, head)
    cosine, sine = rope_tables(position, head)

    def head_norm(values, gain):
        return rotary(values * inverse_rms(values) * gain, cosine, sine)

    query_rot, query_pull = jax.vjp(head_norm, query_pre.reshape(shape), gain_query)
    key_rot, key_pull = jax.vjp(head_norm, key_pre.reshape(shape), gain_key)
    batch = (micro, group, local_heads, head)
    queries = query_rot.astype(BF16).reshape(batch)
    keys_low = key_rot.astype(BF16).reshape(batch)
    values_low = value_pre.astype(BF16).reshape(batch)
    same = (segment[:, :, None] == segment[:, None, :])[:, None]

    def scores_of():
        raw = jnp.einsum("gqhd,gkhd->ghqk", queries, keys_low, preferred_element_type=F32) * scale
        return jnp.where(same, raw, MASKED)

    scores = scores_of()
    highest = jnp.max(scores, -1, keepdims=True)
    log_total = highest + jnp.log(jnp.sum(jnp.exp(scores - highest), -1, keepdims=True))
    probs_low = jnp.exp(scores - log_total).astype(BF16)
    attended = jnp.einsum(
        "ghqk,gkhd->gqhd", probs_low, values_low, preferred_element_type=F32
    ).astype(BF16)
    attended_full, full_o, full_rt, full_d = middle_gather(
        attended.reshape(rows, local_heads * head), rows_o, rows_r, half_d, 1
    )
    full_r = full_rt.T

    hidden = inputs + nn(attended_full, full_o)
    scale_two = inverse_rms(hidden)
    normed_ffn = (hidden * scale_two * gains[1]).astype(BF16)
    logits = nn(normed_ffn, full_r)
    peak = jnp.max(jnp.where(member, logits, -jnp.inf), -1, keepdims=True)
    raised = jnp.where(member, jnp.exp(jnp.where(member, logits - peak, 0.0)), 0.0)
    gates = raised / jnp.sum(raised, -1, keepdims=True)
    gate_t = mine(gates, 1).reshape(micro, group, local_exp).transpose(2, 0, 1)[:, :, None, :]
    upstream_full = (upstream_low * live[:, None].astype(BF16)).reshape(micro, group, width)
    hn = normed_ffn.reshape(micro, group, width)

    outs, weight_grads = [], []
    for c in chunks:
        xe, dyr, hg, dgp, dup, ye, dxe, tok = expert_pass(
            counts[c],
            place_t[c],
            gate_t[c],
            hn,
            upstream_full,
            full_g,
            full_u,
            full_d,
            capacity,
            c.start,
        )
        gg, gu, gd = expert_grads(xe, dgp, dup, hg, dyr)
        hn, upstream_full, ye, dxe, tok, gg, gu, gd = lax.optimization_barrier(
            (hn, upstream_full, ye, dxe, tok, gg, gu, gd)
        )
        outs.append((ye, dxe, tok))
        weight_grads.append(
            [
                lax.psum_scatter(gg, "row", scatter_dimension=1, tiled=True),
                lax.psum_scatter(gu, "row", scatter_dimension=1, tiled=True),
                gd,
            ]
        )
    def tie(value, c, j):
        value, done = lax.optimization_barrier((value, weight_grads[c][j]))
        weight_grads[c][j] = done
        return value

    row = lax.axis_index("row")
    couples, couple, inside = n_row // 2, row // 2, row % 2
    shared = w_down.shape[2]
    own_tok = jnp.concatenate([o[2] for o in outs], 0)
    back_sum, tok, near, far = scatter_col(
        combine(place, [tie(o[1], 0, 0) if n == 0 else o[1] for n, o in enumerate(outs)]),
        2,
        1,
        (own_tok, weight_grads[0][2], weight_grads[1][2]),
    )
    back_sum = tie(back_sum, 0, 1)

    def down_block(value, block, size):
        return lax.dynamic_slice_in_dim(value, block * size, size, 2).astype(F32)

    down_first = [
        down_block(weight_grads[0][2], ((couple + k) % couples) * 2 + inside, shared)
        + lax.dynamic_index_in_dim(near, (couple + k) % couples, 0, False).astype(F32)
        for k in range(couples)
    ]
    down_second = down_block(weight_grads[1][2], couple, 2 * shared) + jnp.sum(
        far.astype(F32), 0
    )
    down_first_out = jnp.stack(down_first[1:]).astype(BF16)
    down_second_out = lax.dynamic_slice_in_dim(
        down_second, (1 - inside) * shared, shared, 2
    ).astype(BF16)
    down_second = lax.dynamic_slice_in_dim(down_second, inside * shared, shared, 2)
    tok = tok.reshape((experts,) + tok.shape[2:])
    hidden_part = tokens.astype(F32) + nn(attended_full, mine(full_o, 1))
    gate_dots = tok[:, :, 0].reshape(experts, rows).T
    hidden_part = mine(hidden, 1)

    selected = gates * (gate_dots - jnp.sum(gates * gate_dots, -1, keepdims=True))
    logit_grad = selected.astype(BF16)
    router_part = mine(full_r, 0)
    normed_grad = back_sum + nt(logit_grad, router_part)
    grad_router = tn(mine(normed_ffn, 1), logit_grad)
    scaled_two = hidden_part * scale_two
    grad_gain_ffn = jnp.sum(normed_grad * scaled_two, 0)
    dot_two = jnp.sum(tok[:, :, 1].reshape(experts, rows), 0) + jnp.sum(
        logit_grad.astype(F32) * logits, 1
    )
    upstream_part = cotangent.astype(F32) * live[:, None]
    hidden_grad = (
        upstream_part
        + scale_two * (normed_grad * gain_ffn)
        - hidden_part * scale_two**2 * dot_two[:, None] / width
    )

    branch_grad = hidden_grad.astype(BF16)
    (attended_grad,) = scatter_col(nt(branch_grad, mine(full_o, 1)).astype(BF16), 3)
    attended_grad, mixed_slots = lax.optimization_barrier(
        (attended_grad.astype(BF16).reshape(batch), [o[0] for o in outs])
    )
    mixed_sum = lax.psum_scatter(
        combine(place, mixed_slots), "col", scatter_dimension=1, tiled=True
    )
    grad_out = tn(attended_full, branch_grad)
    scores_again = scores_of()
    probs = jnp.exp(scores_again - log_total)
    probs_again = probs.astype(BF16)
    probs_grad = jnp.einsum(
        "gqhd,gkhd->ghqk", attended_grad, values_low, preferred_element_type=F32
    )
    values_grad = jnp.einsum(
        "ghqk,gqhd->gkhd", probs_again, attended_grad, preferred_element_type=F32
    )
    score_grad = (probs * (probs_grad - jnp.sum(probs_grad * probs, -1, keepdims=True))).astype(
        BF16
    )
    query_grad_rot = (
        jnp.einsum("ghqk,gkhd->gqhd", score_grad, keys_low, preferred_element_type=F32) * scale
    )
    key_grad_rot = (
        jnp.einsum("ghqk,gqhd->gkhd", score_grad, queries, preferred_element_type=F32) * scale
    )
    query_grad, gain_query_part = query_pull(query_grad_rot.reshape(shape))
    key_grad, gain_key_part = key_pull(key_grad_rot.reshape(shape))
    flat = (rows, local_heads * head)
    heads_grad = [
        v.reshape(flat).astype(BF16) for v in (query_grad, key_grad, values_grad)
    ]
    back_heads = sum(nt(g, w_heads[j]) for j, g in enumerate(heads_grad))
    pre = (query_pre, key_pre, value_pre)
    dot_part = sum(jnp.sum(g.astype(F32) * p, -1) for g, p in zip(heads_grad, pre))
    sums = jnp.concatenate([dot_part, gain_query_part, gain_key_part])
    sums = jnp.pad(sums, (0, -sums.shape[0] % 1024)).reshape(-1, 128)
    normed_back, sums, down_near, down_far = scatter_col(
        back_heads.astype(BF16), 4, 2, (sums, down_first_out, down_second_out)
    )
    normed_back, mixed_sum = lax.optimization_barrier((normed_back, mixed_sum))
    mixed = (hidden_part + mixed_sum.astype(F32)).astype(BF16)
    sums = jnp.sum(sums, 0).reshape(-1)
    dot_one = sums[:rows]
    gain_query_sum, gain_key_sum = sums[rows : rows + head], sums[rows + head : rows + 2 * head]
    scale_one_part = scale_one
    inputs_part = tokens.astype(F32)
    grad_gain_attn = jnp.sum(normed_back * inputs_part * scale_one_part, 0)
    input_grad = (
        hidden_grad
        + scale_one_part * (normed_back * gain_attn)
        - inputs_part * scale_one_part**2 * dot_one[:, None] / width
    )

    grad_gate, grad_up = (
        jnp.concatenate([w[j] for w in weight_grads], 0).astype(F32) for j in range(2)
    )
    grad_down = jnp.concatenate(
        [
            down_first[0] + jnp.sum(down_far.astype(F32), 0),
            down_second + down_near.astype(F32),
        ],
        0,
    )

    heads_weights = jnp.stack([tn(normed, g) for g in heads_grad]).astype(BF16)
    heads_weights = heads_weights.reshape(3, n_col, part, local_heads * head).transpose(1, 0, 2, 3)
    heads_weights = lax.all_to_all(heads_weights, "col", split_axis=0, concat_axis=0, tiled=True)
    heads_weights = heads_weights.transpose(1, 2, 0, 3).reshape(3 * part, hd)
    heads_weights = lax.psum_scatter(heads_weights, "row", scatter_dimension=1, tiled=True)
    grad_query, grad_key, grad_value = (
        heads_weights[j * part : (j + 1) * part].astype(F32) for j in range(3)
    )
    out_weights = lax.all_to_all(
        grad_out.astype(BF16).reshape(n_col, local_heads * head, part),
        "col",
        split_axis=0,
        concat_axis=0,
        tiled=True,
    )
    out_weights = out_weights.transpose(1, 0, 2).reshape(local_heads * head, width)
    grad_out = lax.psum_scatter(out_weights, "row", scatter_dimension=1, tiled=True).astype(F32)
    smalls = [
        grad_gain_attn,
        grad_gain_ffn,
        gain_query_sum,
        gain_key_sum,
        grad_router.T.reshape(-1),
    ]
    total = lax.psum(jnp.concatenate(smalls).reshape(-1, 128), "row").reshape(-1)
    grad_gain_attn, grad_gain_ffn = total[:part], total[part : 2 * part]
    grad_gain_query = total[2 * part : 2 * part + head]
    grad_gain_key = total[2 * part + head : 2 * part + 2 * head]
    grad_router = lax.dynamic_slice_in_dim(
        total[2 * part + 2 * head :].reshape(experts, part), row * (experts // n_row), experts // n_row, 0
    ).T
    return (
        mixed,
        input_grad,
        grad_gain_attn,
        grad_gain_ffn,
        grad_gain_query,
        grad_gain_key,
        grad_query,
        grad_key,
        grad_value,
        grad_out,
        grad_router,
        grad_gate,
        grad_up,
        grad_down,
    )


def solution(mesh):
    placed = (
        P("row", "col"),
        P("col"),
        P("col"),
        P(),
        P(),
        P("col", "row"),
        P("col", "row"),
        P("col", "row"),
        P("col", "row"),
        P("col", "row"),
        P("col", "row", None),
        P("col", "row", None),
        P("col", None, "row"),
        P("row", None),
        P("row", None),
        P("row", "col"),
    )
    return jax.shard_map(
        shards,
        mesh=mesh,
        in_specs=placed,
        out_specs=(
            P("row", "col"),
            P("row", "col"),
            P("col"),
            P("col"),
            P(),
            P(),
            P("col", "row"),
            P("col", "row"),
            P("col", "row"),
            P("col", "row"),
            P("col", "row"),
            P("col", "row", None),
            P("col", "row", None),
            P("col", None, "row"),
        ),
        check_vma=False,
    )
```

```python
import functools
import math

import jax
import jax.numpy as jnp
from jax import lax
from jax.experimental import pallas as pl
from jax.experimental.pallas import tpu as pltpu
from jax.sharding import PartitionSpec as P

EPSILON = 1e-06
ROPE_BASE = 10000.0
MASKED = -1e30
F32 = jnp.float32
BF16 = jnp.bfloat16
VMEM_LIMIT = 60 * 1024 * 1024
MESH = pl.DeviceIdType.MESH


def inverse_rms(values):
    return lax.rsqrt(jnp.mean(values * values, -1, keepdims=True) + EPSILON)


def rope_tables(position, head):
    half = head // 2
    inverse = jnp.exp(-math.log(ROPE_BASE) * 2.0 / head * jnp.arange(half, dtype=F32))
    angles = position[:, None] * inverse[None, :]
    return jnp.cos(angles)[:, None, :], jnp.sin(angles)[:, None, :]


def rotary(values, cosine, sine):
    half = values.shape[-1] // 2
    first = values[..., :half]
    second = values[..., half:]
    return jnp.concatenate([first * cosine - second * sine, second * cosine + first * sine], -1)


def layout(lengths_row, group):
    ends = jnp.cumsum(lengths_row)
    starts = ends - lengths_row
    row_index = jnp.arange(group, dtype=jnp.int32)
    segment = jnp.sum((row_index[:, None] >= ends[None, :]).astype(jnp.int32), 1)
    member = segment[:, None] == jnp.arange(lengths_row.shape[0], dtype=jnp.int32)[None, :]
    position = (row_index - jnp.sum(jnp.where(member, starts[None, :], 0), 1)).astype(F32)
    live = (segment < lengths_row.shape[0] - 1).astype(F32)
    return (segment, position, live)


def nn(a, b):
    return lax.dot_general(a, b, (((1,), (0,)), ((), ())), preferred_element_type=F32)


def nt(a, b):
    return lax.dot_general(a, b, (((1,), (1,)), ((), ())), preferred_element_type=F32)


def tn(a, b):
    return lax.dot_general(a, b, (((0,), (0,)), ((), ())), preferred_element_type=F32)


def expert_body(shared, counts, place, gate, hn, dy, w, xe_o, dyr_o, hg_o, dgp_o, dup_o, ye_o, dxe_o, tok_o):
    g, i = pl.program_id(0), pl.program_id(1)
    rows = xe_o.shape[1]
    width, ff = w.shape[1:]
    base = i * rows

    @pl.when(i == 0)
    def _():
        tok_o[...] = jnp.zeros_like(tok_o)

    @pl.when(counts[g] <= base)
    def _():
        for ref in (xe_o, dyr_o, hg_o, dgp_o, dup_o, ye_o, dxe_o):
            ref[...] = jnp.zeros_like(ref)

    @pl.when(counts[g] > base)
    def _():
        slot = lax.broadcasted_iota(jnp.int32, (rows, place.shape[2]), 0) + base
        hit = slot == place[0]
        pick = jnp.where(hit, 1.0, 0.0).astype(BF16)
        weight = jnp.sum(jnp.where(hit, gate[0], 0.0), 1, keepdims=True)
        xe = nn(pick, hn[0]).astype(BF16)
        xe_o[0] = xe
        gp = nn(xe, w[0])
        up = nn(xe, w[1])
        sig = jax.nn.sigmoid(gp)
        silu = gp * sig
        hid = silu * up
        hg = (hid * weight).astype(BF16)
        hg_o[0] = hg
        dyr = nn(pick, dy[0]).astype(BF16)
        dyr_o[0] = dyr
        parts = []
        for r in range(width // shared):
            at = r * shared
            total = None
            for b in range(ff // shared):
                low = b * shared
                term = nn(hg[:, low : low + shared], w[2, at : at + shared, low : low + shared])
                total = term if total is None else total + term
            ye_o[0, :, at : at + shared] = total.astype(BF16)
        for b in range(ff // shared):
            low = b * shared
            total = None
            for r in range(width // shared):
                at = r * shared
                term = nt(dyr[:, at : at + shared], w[2, at : at + shared, low : low + shared])
                total = term if total is None else total + term
            parts.append(total)
        back = jnp.concatenate(parts, 1)
        dgate = jnp.sum(back * hid, 1, keepdims=True)
        dhid = back * weight
        dgp = (dhid * up * sig * (1.0 + gp * (1.0 - sig))).astype(BF16)
        dup = (dhid * silu).astype(BF16)
        dgp_o[0] = dgp
        dup_o[0] = dup
        dots = jnp.sum(dgp.astype(F32) * gp + dup.astype(F32) * up, 1, keepdims=True)
        dxe_o[0] = (nt(dgp, w[0]) + nt(dup, w[1])).astype(BF16)
        tok_o[0, 0:1, :] += jnp.sum(jnp.where(hit, dgate, 0.0), 0, keepdims=True)
        tok_o[0, 1:2, :] += jnp.sum(jnp.where(hit, dots, 0.0), 0, keepdims=True)


def expert_pass(counts, place, gate, hn, dy, w, capacity, shared):
    _, width, ff = w.shape
    micro, group, _ = hn.shape
    rows = min(256, capacity)
    blocks = capacity // rows
    tall = lambda g, i, c: (g, i, 0)
    line = lambda g, i, c: (g, 0, 0)
    slots = lambda n: jax.ShapeDtypeStruct((micro, capacity, n), BF16)
    sizes = (width, width, ff, ff, ff, width, width)
    flops = 2 * micro * capacity * width * (6 * ff + 2 * group)
    return pl.pallas_call(
        functools.partial(expert_body, shared),
        grid_spec=pltpu.PrefetchScalarGridSpec(
            num_scalar_prefetch=1,
            grid=(micro, blocks),
            in_specs=[
                pl.BlockSpec((1, 1, group), line),
                pl.BlockSpec((1, 1, group), line),
                pl.BlockSpec((1, group, width), line),
                pl.BlockSpec((1, group, width), line),
                pl.BlockSpec((3, width, ff), lambda g, i, c: (0, 0, 0), pipeline_mode=pl.Buffered(1)),
            ],
            out_specs=[pl.BlockSpec((1, rows, n), tall) for n in sizes]
            + [pl.BlockSpec((1, 2, group), line)],
        ),
        out_shape=[slots(n) for n in sizes] + [jax.ShapeDtypeStruct((micro, 2, group), F32)],
        compiler_params=pltpu.CompilerParams(vmem_limit_bytes=VMEM_LIMIT),
        cost_estimate=pl.CostEstimate(
            flops=flops, bytes_accessed=40 << 20, transcendentals=micro * capacity * ff
        ),
        name="expert_pass",
    )(counts, place, gate, hn, dy, w)


def grads_body(xe, dgp, dup, hg, dyr, out):
    part = xe[...]
    shared = part.shape[1]
    out[0] = tn(part, dgp[...]).astype(BF16)
    out[1] = tn(part, dup[...]).astype(BF16)
    back = dyr[...]
    for b in range(hg.shape[1] // shared):
        low = b * shared
        out[2, :, low : low + shared] = tn(hg[:, low : low + shared], back).astype(BF16)


def expert_grads(xe, dgp, dup, hg, dyr, shared):
    micro, capacity, width = xe.shape
    ff = dgp.shape[2]
    rows = micro * capacity
    xe, dyr = (a.reshape(rows, width) for a in (xe, dyr))
    dgp, dup, hg = (a.reshape(rows, ff) for a in (dgp, dup, hg))
    thin = pl.BlockSpec((rows, shared), lambda r: (0, r))
    whole = pl.BlockSpec((rows, ff), lambda r: (0, 0))
    return pl.pallas_call(
        grads_body,
        grid=(width // shared,),
        in_specs=[thin, whole, whole, whole, thin],
        out_specs=pl.BlockSpec((3, shared, ff), lambda r: (0, r, 0)),
        out_shape=jax.ShapeDtypeStruct((3, width, ff), BF16),
        compiler_params=pltpu.CompilerParams(vmem_limit_bytes=VMEM_LIMIT),
        cost_estimate=pl.CostEstimate(
            flops=6 * rows * width * ff, bytes_accessed=26 << 20, transcendentals=0
        ),
        name="expert_grads",
    )(xe, dgp, dup, hg, dyr)


def pack_body(wg, wu, wd, *rest):
    outs, sem = rest[:-1], rest[-1]
    shared, ff = wg.shape[1:]
    copies = []
    for e, out in enumerate(outs):
        moves = [(wg.at[e], out.at[0]), (wu.at[e], out.at[1])]
        for b in range(ff // shared):
            low = b * shared
            moves.append((wd.at[e, pl.ds(low, shared)], out.at[2, :, pl.ds(low, shared)]))
        for m, (src, dst) in enumerate(moves):
            copies.append(pltpu.make_async_copy(src, dst, sem.at[e, m]))
    for c in copies:
        c.start()
    for c in copies:
        c.wait()


def pack(wg, wu, wd):
    experts, shared, ff = wg.shape
    return pl.pallas_call(
        pack_body,
        in_specs=[pl.BlockSpec(memory_space=pl.ANY)] * 3,
        out_specs=[pl.BlockSpec(memory_space=pl.ANY)] * experts,
        out_shape=[jax.ShapeDtypeStruct((3, shared, ff), BF16)] * experts,
        scratch_shapes=[pltpu.SemaphoreType.DMA((experts, 2 + ff // shared))],
        cost_estimate=pl.CostEstimate(
            flops=0, bytes_accessed=experts * 6 * shared * ff * 2, transcendentals=0
        ),
        name="pack",
    )(wg, wu, wd)


def combine_body(place, *refs):
    out = refs[-1]
    total = jnp.zeros((out.shape[1], out.shape[2]), F32)
    for e, ref in enumerate(refs[:-1]):
        slot = lax.broadcasted_iota(jnp.int32, (out.shape[1], ref.shape[1]), 1)
        pick = jnp.where(slot == place[0, :, e : e + 1], 1.0, 0.0).astype(BF16)
        total = total + nn(pick, ref[0])
    out[0] = total.astype(BF16)


def combine(place, slots):
    micro, group, local = place.shape
    capacity, width = slots[0].shape[1:]
    tile = min(256, group)
    return pl.pallas_call(
        combine_body,
        grid=(micro, group // tile),
        in_specs=[pl.BlockSpec((1, tile, local), lambda g, i: (g, i, 0))]
        + [pl.BlockSpec((1, capacity, width), lambda g, i: (g, 0, 0)) for s in slots],
        out_specs=pl.BlockSpec((1, tile, width), lambda g, i: (g, i, 0)),
        out_shape=jax.ShapeDtypeStruct((micro, group, width), BF16),
        compiler_params=pltpu.CompilerParams(vmem_limit_bytes=VMEM_LIMIT),
        cost_estimate=pl.CostEstimate(
            flops=2 * micro * group * local * capacity * width,
            bytes_accessed=micro * (local * capacity + group) * width * 2,
            transcendentals=0,
        ),
        name="combine",
    )(place, *slots).reshape(micro * group, width)


def places():
    row, col = lax.axis_index("row"), lax.axis_index("col")
    n_row, n_col = lax.axis_size("row"), lax.axis_size("col")
    return row, col, n_row, n_col


def remote(src, dst, send_sem, recv_sem, where):
    return pltpu.make_async_remote_copy(
        src_ref=src,
        dst_ref=dst,
        send_sem=send_sem,
        recv_sem=recv_sem,
        device_id=where,
        device_id_type=MESH,
    )


def shake(sources, targets):
    barrier = pltpu.get_barrier_semaphore()
    for ok, where in sources:
        if ok is True:
            pl.semaphore_signal(barrier, inc=1, device_id=where, device_id_type=MESH)
        else:

            @pl.when(ok)
            def _():
                pl.semaphore_signal(barrier, inc=1, device_id=where, device_id_type=MESH)

    count = 0
    for ok in targets:
        count = count + (1 if ok is True else jnp.where(ok, 1, 0))
    pl.semaphore_wait(barrier, count)


def line_peers():
    row, col, n_row, n_col = places()
    pair, core = col // 2, col % 2
    return [
        (True, (row, pair * 2 + 1 - core)),
        (pair > 0, (row, (pair - 1) * 2 + core)),
        (pair < n_col // 2 - 1, (row, (pair + 1) * 2 + core)),
    ]


def row_peers():
    row, col, n_row, n_col = places()
    return [(True, ((row + k) % n_row, col)) for k in range(1, n_row)]


def col_slice(ref, index, size):
    return ref.at[..., pl.ds(pl.multiple_of(index * size, size), size)]


def line_gather(axes, ins, outs, sems):
    own_sem, right_s, right_r, left_s, left_r, side_s, side_r = sems
    n = len(ins)
    row, col, n_row, n_col = places()
    pairs, pair, core = n_col // 2, col // 2, col % 2

    def at(pair_index, core_index):
        return (row, pair_index * 2 + core_index)

    def block(j, source):
        size = ins[j].shape[axes[j]]
        if axes[j] == 0:
            return outs[j].at[pl.ds(pl.multiple_of(source * size, size), size)]
        return col_slice(outs[j], source, size)

    def right(j, s):
        source = (pair - s) * 2 + core
        src = ins[j] if s == 0 else block(j, source)
        return remote(src, block(j, source), right_s.at[j, s], right_r.at[j, s], at(pair + 1, core))

    def left(j, s):
        source = (pair + s) * 2 + core
        src = ins[j] if s == 0 else block(j, source)
        return remote(src, block(j, source), left_s.at[j, s], left_r.at[j, s], at(pair - 1, core))

    def side(j, source_pair, first=False):
        source = source_pair * 2 + core
        src = ins[j] if first else block(j, source)
        return remote(
            src,
            block(j, source),
            side_s.at[j, source_pair],
            side_r.at[j, source_pair],
            at(pair, 1 - core),
        )

    def arrived(j, recvs, slot, source):
        remote(
            ins[j], block(j, source), recvs.at[j, slot], recvs.at[j, slot], at(pair, 1 - core)
        ).wait_recv()

    def own(j):
        return pltpu.make_async_copy(ins[j], block(j, col), own_sem.at[j])

    def begin():
        for j in range(n):

            @pl.when(pair < pairs - 1)
            def _():
                right(j, 0).start()

            @pl.when(pair > 0)
            def _():
                left(j, 0).start()

        for j in range(n):
            side(j, pair, True).start()
            own(j).start()

    def middle():
        for s in range(1, pairs):
            for j in range(n):

                @pl.when(pair >= s)
                def _():
                    arrived(j, right_r, s - 1, (pair - s) * 2 + core)

                    @pl.when(pair < pairs - 1)
                    def _():
                        right(j, s).start()

                    side(j, pair - s).start()

                @pl.when(pair + s < pairs)
                def _():
                    arrived(j, left_r, s - 1, (pair + s) * 2 + core)

                    @pl.when(pair > 0)
                    def _():
                        left(j, s).start()

                    side(j, pair + s).start()

    def end():
        for j in range(n):
            own(j).wait()
            for p in range(pairs):
                side(j, p).wait_send()
                arrived(j, side_r, p, p * 2 + 1 - core)
            for s in range(pairs):

                @pl.when((pair >= s) & (pair < pairs - 1))
                def _():
                    right(j, s).wait_send()

                @pl.when((pair + s < pairs) & (pair > 0))
                def _():
                    left(j, s).wait_send()

    return begin, middle, end


def line_sems(n, pairs):
    dma = pltpu.SemaphoreType.DMA
    return [dma((n,))] + [dma((n, pairs))] * 6


def front_body(tokens, gains, wq, wk, wv, wo, wr, x_o, gains_o, wh_o, wo_o, wr_o, *sems):
    line, (heads_s, heads_r, row_s, row_r, own_s) = sems[:7], sems[7:]
    row, col, n_row, n_col = places()
    head = wh_o.shape[2]
    part = wq.shape[0]
    per = wq.shape[1] // head
    small = [(wo, wo_o), (wr, wr_o)]
    begin, middle, end = line_gather((1, 1), [tokens, gains], [x_o, gains_o], line)

    def heads_dst(m, source):
        return wh_o.at[m, pl.ds(pl.multiple_of(source * part, part), part), :]

    def heads(m, r, j):
        src = (wq, wk, wv)[m].at[:, pl.ds(j * head, head)]
        return remote(
            src,
            heads_dst(m, col),
            heads_s.at[m, r * per + j],
            heads_r.at[m, col],
            (r, row * per + j),
        )

    def heads_own(m, j):
        src = (wq, wk, wv)[m].at[:, pl.ds(j * head, head)]
        return pltpu.make_async_copy(src, heads_dst(m, col), own_s.at[m])

    def to_self(r, j):
        return (row == r) & (col == row * per + j)

    def heads_come(m, c):
        return remote(
            heads_dst(m, c), heads_dst(m, c), heads_r.at[m, c], heads_r.at[m, c], (row, col)
        )

    def from_self(c):
        return (row == col // per) & (col == c)

    def small_dst(k, source):
        if k == 0:
            return col_slice(wo_o, source, wo.shape[1])
        size = wr.shape[0]
        return wr_o.at[pl.ds(pl.multiple_of(source * size, size), size), :]

    def small_copy(k, step):
        return remote(
            small[k][0],
            small_dst(k, row),
            row_s.at[k, step],
            row_r.at[k, step],
            ((row + step) % n_row, col),
        )

    def small_come(k, step):
        source = (row + n_row - step) % n_row
        return remote(
            small[k][0], small_dst(k, source), row_s.at[k, step], row_r.at[k, step], (source, col)
        )

    def small_own(k):
        return pltpu.make_async_copy(small[k][0], small_dst(k, row), own_s.at[3 + k])

    sources = line_peers() + row_peers()
    targets = [ok for ok, _ in sources]
    for c in range(n_col):
        sources.append((jnp.logical_not(from_self(c)), (col // per, c)))
    for r in range(n_row):
        for j in range(per):
            targets.append(jnp.logical_not(to_self(r, j)))
    shake(sources, targets)
    begin()
    for k in range(2):
        small_own(k).start()
        for step in range(1, n_row):
            small_copy(k, step).start()
    for r in range(n_row):
        for j in range(per):

            @pl.when(to_self(r, j))
            def _():
                for m in range(3):
                    heads_own(m, j).start()

            @pl.when(jnp.logical_not(to_self(r, j)))
            def _():
                for m in range(3):
                    heads(m, r, j).start()

    middle()
    end()
    for k in range(2):
        small_own(k).wait()
        for step in range(1, n_row):
            small_copy(k, step).wait_send()
            small_come(k, step).wait_recv()
    for r in range(n_row):
        for j in range(per):

            @pl.when(to_self(r, j))
            def _():
                for m in range(3):
                    heads_own(m, j).wait()

            @pl.when(jnp.logical_not(to_self(r, j)))
            def _():
                for m in range(3):
                    heads(m, r, j).wait_send()

    for c in range(n_col):

        @pl.when(jnp.logical_not(from_self(c)))
        def _():
            for m in range(3):
                heads_come(m, c).wait_recv()


ANY = pl.BlockSpec(memory_space=pl.ANY)


def front(tokens, gains, wq, wk, wv, wo, wr, head, ident):
    n_row, n_col = lax.axis_size("row"), lax.axis_size("col")
    rows, part = tokens.shape
    width = part * n_col
    per = wq.shape[1] // head
    dma = pltpu.SemaphoreType.DMA
    shapes = [
        ((rows, width), BF16),
        ((gains.shape[0], width), F32),
        ((3, width, head), BF16),
        ((wo.shape[0], wo.shape[1] * n_row), BF16),
        ((wr.shape[0] * n_row, part), BF16),
    ]
    return pl.pallas_call(
        front_body,
        in_specs=[ANY] * 7,
        out_specs=[ANY] * 5,
        out_shape=[jax.ShapeDtypeStruct(s, t) for s, t in shapes],
        scratch_shapes=line_sems(2, n_col // 2)
        + [
            dma((3, n_row * per)),
            dma((3, n_col)),
            dma((2, n_row)),
            dma((2, n_row)),
            dma((6,)),
        ],
        compiler_params=pltpu.CompilerParams(collective_id=ident, has_side_effects=True),
        cost_estimate=pl.CostEstimate(
            flops=0, bytes_accessed=rows * width * 32, transcendentals=0
        ),
        name="front",
    )(tokens, gains, wq, wk, wv, wo, wr)


def middle_body(axes, *refs):
    n = len(axes)
    begin, middle, end = line_gather(axes, refs[:n], refs[n : 2 * n], refs[2 * n :])
    sources = line_peers()
    shake(sources, [ok for ok, _ in sources])
    begin()
    middle()
    end()


def middle_gather(arrays, axes, ident):
    n_col, n = lax.axis_size("col"), len(arrays)
    shapes = [
        tuple(d * n_col if at == axis else d for at, d in enumerate(a.shape))
        for a, axis in zip(arrays, axes)
    ]
    return pl.pallas_call(
        functools.partial(middle_body, axes),
        in_specs=[ANY] * n,
        out_specs=[ANY] * n,
        out_shape=[jax.ShapeDtypeStruct(s, a.dtype) for s, a in zip(shapes, arrays)],
        scratch_shapes=line_sems(n, n_col // 2),
        compiler_params=pltpu.CompilerParams(collective_id=ident, has_side_effects=True),
        cost_estimate=pl.CostEstimate(
            flops=0, bytes_accessed=sum(math.prod(s) for s in shapes) * 32, transcendentals=0
        ),
        name="middle_gather",
    )(*arrays)


def scatter_body(part, stage, *refs):
    n_in = (1, 2, 4)[stage]
    n_out = (1, 2, 4)[stage]
    x, ins = refs[0], refs[1:n_in]
    out, outs = refs[n_in], refs[n_in + 1 : n_in + n_out]
    rest = refs[n_in + n_out :]
    acc, side, from_left, from_right, load, side_s, side_r = rest[:7]
    right_s, right_r, left_s, left_r = rest[7:11]
    row, col, n_row, n_col = places()
    pairs, pair, core = n_col // 2, col // 2, col % 2
    rows = out.shape[0]
    cuts = load.shape[1]
    height = rows // cuts
    tile = min(256, height)

    def at(pair_index, core_index):
        return (row, pair_index * 2 + core_index)

    def block(owner, q):
        return x.at[
            pl.ds(q * height, height), pl.ds(pl.multiple_of(owner * part, part), part)
        ]

    def cut(ref, d, q):
        return ref.at[d, pl.ds(q * height, height)]

    def fetch(d, q):
        return pltpu.make_async_copy(block(d * 2 + core, q), cut(acc, d, q), load.at[d, q])

    def across(d, q):
        return remote(
            block(d * 2 + 1 - core, q),
            cut(side, d, q),
            side_s.at[d, q],
            side_r.at[d, q],
            at(pair, 1 - core),
        )

    def right(d, q):
        return remote(
            cut(acc, d, q),
            cut(from_left, d, q),
            right_s.at[d, q],
            right_r.at[d, q],
            at(pair + 1, core),
        )

    def left(d, q):
        return remote(
            cut(acc, d, q),
            cut(from_right, d, q),
            left_s.at[d, q],
            left_r.at[d, q],
            at(pair - 1, core),
        )

    copies, arrivals, own = [], [], []
    if stage:
        small_s, small_r, own_s = rest[11:14]
        extra, extra_o = ins[0], outs[0]
        for k in range(1, n_col):
            where, source = (col + k) % n_col, (col + n_col - k) % n_col
            copies.append(
                remote(extra, extra_o.at[col], small_s.at[k], small_r.at[k], (row, where))
            )
            arrivals.append(
                remote(extra, extra_o.at[source], small_s.at[k], small_r.at[k], (row, where))
            )
        own.append(pltpu.make_async_copy(extra, extra_o.at[col], own_s))
    guarded = []
    if stage == 2:
        give_s, give_r, keep_s = rest[14:]
        per = n_col // n_row
        heads, branch = ins[1:]
        heads_o, branch_o = outs[1:]
        part_h = heads.shape[1] // n_col
        rows_b = branch.shape[0] // n_col
        target = col // per
        for k in range(n_col):
            pieces = [
                (heads.at[:, pl.ds(k * part_h, part_h), :], heads_o.at[row, col % per]),
                (branch.at[pl.ds(k * rows_b, rows_b), :], branch_o.at[row, col % per]),
            ]
            self_here = (row == target) & (col == k)
            for m, (src, dst) in enumerate(pieces):
                guarded.append(
                    (
                        self_here,
                        pltpu.make_async_copy(src, dst, keep_s.at[m]),
                        remote(
                            src, dst, give_s.at[m, k], give_r.at[m, row * per + col % per], (target, k)
                        ),
                    )
                )
        takes = []
        for r in range(n_row):
            for j in range(per):
                mine_here = (row == r) & (col == row * per + j)
                for m, (ref, src) in enumerate(
                    ((heads_o, heads.at[:, pl.ds(0, part_h), :]), (branch_o, branch.at[pl.ds(0, rows_b), :]))
                ):
                    takes.append(
                        (
                            jnp.logical_not(mine_here),
                            remote(
                                src,
                                ref.at[r, j],
                                give_s.at[m, 0],
                                give_r.at[m, r * per + j],
                                (r, row * per + j),
                            ),
                        )
                    )
    if stage:
        peers = [(True, (row, (col + k) % n_col)) for k in range(1, n_col)]
    else:
        peers = line_peers()
    targets = [ok for ok, _ in peers]
    if stage == 2:
        for r in range(n_row):
            for j in range(per):
                here = (row == r) & (col == row * per + j)
                peers.append((jnp.logical_not(here), (r, row * per + j)))
        for k in range(n_col):
            targets.append(jnp.logical_not((row == target) & (col == k)))
    shake(peers, targets)
    order = []
    for t in range(pairs):
        for d in (pairs - 1 - t, t):
            if d not in order:
                order.append(d)
    for d in order:
        for q in range(cuts):
            across(d, q).start()
            fetch(d, q).start()
    for c in copies + own:
        c.start()
    for here, keep, give in guarded:

        @pl.when(here)
        def _():
            keep.start()

        @pl.when(jnp.logical_not(here))
        def _():
            give.start()

    def add(q, into, *sources):
        def step(i, _):
            lines = pl.ds(pl.multiple_of(q * height + i * tile, tile), tile)
            total = sources[0][lines, :].astype(F32)
            for ref in sources[1:]:
                total = total + ref[lines, :].astype(F32)
            into[lines, :] = total.astype(into.dtype)
            return 0

        lax.fori_loop(0, height // tile, step, 0)

    def ready(d, q):
        fetch(d, q).wait()
        across(d, q).wait_recv()

    def go_right(d, q):
        ready(d, q)

        @pl.when(pair > 0)
        def _():
            right(d, q).wait_recv()
            add(q, acc.at[d], acc.at[d], side.at[d], from_left.at[d])

        @pl.when(pair == 0)
        def _():
            add(q, acc.at[d], acc.at[d], side.at[d])

        right(d, q).start()

    def go_left(d, q):
        ready(d, q)

        @pl.when(pair < pairs - 1)
        def _():
            left(d, q).wait_recv()
            add(q, acc.at[d], acc.at[d], side.at[d], from_right.at[d])

        @pl.when(pair == pairs - 1)
        def _():
            add(q, acc.at[d], acc.at[d], side.at[d])

        left(d, q).start()

    for t in range(pairs - 1):
        far, near = pairs - 1 - t, t
        for q in range(cuts):

            @pl.when(far > pair)
            def _():
                go_right(far, q)

            @pl.when(near < pair)
            def _():
                go_left(near, q)

    for q in range(cuts):
        ready(pair, q)

        @pl.when(pair == 0)
        def _():
            left(pair, q).wait_recv()
            add(q, out, acc.at[pair], side.at[pair], from_right.at[pair])

        @pl.when(pair == pairs - 1)
        def _():
            right(pair, q).wait_recv()
            add(q, out, acc.at[pair], side.at[pair], from_left.at[pair])

        @pl.when((pair > 0) & (pair < pairs - 1))
        def _():
            left(pair, q).wait_recv()
            right(pair, q).wait_recv()
            add(q, out, acc.at[pair], side.at[pair], from_left.at[pair], from_right.at[pair])

    for d in range(pairs):
        for q in range(cuts):
            across(d, q).wait_send()

            @pl.when(pair < d)
            def _():
                right(d, q).wait_send()

            @pl.when(pair > d)
            def _():
                left(d, q).wait_send()

    for c in copies:
        c.wait_send()
    for c in arrivals:
        c.wait_recv()
    for c in own:
        c.wait()
    for here, keep, give in guarded:

        @pl.when(here)
        def _():
            keep.wait()

        @pl.when(jnp.logical_not(here))
        def _():
            give.wait_send()

    if stage == 2:
        for away, take in takes:

            @pl.when(away)
            def _():
                take.wait_recv()


def scatter_col(x, ident, stage=0, others=()):
    n_row, n_col = lax.axis_size("row"), lax.axis_size("col")
    pairs, per = n_col // 2, n_col // n_row
    rows, part = x.shape[0], x.shape[1] // n_col
    cuts = 4 if rows % 1024 == 0 else 1
    dma = pltpu.SemaphoreType.DMA
    buffer = pltpu.VMEM((pairs, rows, part), BF16)
    scratch = [buffer] * 4 + [dma((pairs, cuts))] * 7
    out_shape = [jax.ShapeDtypeStruct((rows, part), F32)]
    if stage:
        extra = others[0]
        out_shape.append(jax.ShapeDtypeStruct((n_col,) + extra.shape, extra.dtype))
        scratch += [dma((n_col,)), dma((n_col,)), dma(())]
    if stage == 2:
        heads, branch = others[1:]
        scratch += [dma((2, n_col)), dma((2, n_row * per)), dma((2,))]
        out_shape += [
            jax.ShapeDtypeStruct((n_row, per, 3, heads.shape[1] // n_col, heads.shape[2]), BF16),
            jax.ShapeDtypeStruct((n_row, per, branch.shape[0] // n_col, branch.shape[1]), BF16),
        ]
    return pl.pallas_call(
        functools.partial(scatter_body, part, stage),
        in_specs=[ANY] * (1 + len(others)),
        out_specs=[pl.BlockSpec(memory_space=pltpu.VMEM)] + [ANY] * (len(out_shape) - 1),
        out_shape=out_shape,
        scratch_shapes=scratch,
        compiler_params=pltpu.CompilerParams(
            vmem_limit_bytes=VMEM_LIMIT, collective_id=ident, has_side_effects=True
        ),
        cost_estimate=pl.CostEstimate(
            flops=0, bytes_accessed=rows * part * n_col * 40, transcendentals=0
        ),
        name="scatter_col",
    )(x, *others)


def shards(
    tokens,
    gain_attn,
    gain_ffn,
    gain_query,
    gain_key,
    w_query,
    w_key,
    w_value,
    w_out,
    w_router,
    w_gate,
    w_up,
    w_down,
    routes,
    lengths,
    cotangent,
):
    n_col = lax.axis_size("col")
    n_row = lax.axis_size("row")
    col = lax.axis_index("col")
    micro, spans = lengths.shape
    rows, part = tokens.shape
    group = rows // micro
    width = part * n_col
    head = gain_query.shape[0]
    local_exp = w_gate.shape[0]
    experts = local_exp * n_col
    topk = routes.shape[1]
    capacity = 2 * group * topk // experts
    local_heads = w_out.shape[0] // head
    hd = w_out.shape[0] * n_col
    scale = head ** (-0.5)

    def gather(value, axis_name, axis):
        return lax.all_gather(value, axis_name, axis=axis, tiled=True)

    def mine(value, axis):
        size = value.shape[axis] // n_col
        return lax.dynamic_slice_in_dim(value, col * size, size, axis)

    shared = w_down.shape[2]
    big = [gather(w, "row", 1) for w in pack(w_gate, w_up, w_down)]
    inputs_low, gains, w_heads, rows_o, rows_r = front(
        tokens,
        jnp.stack([gain_attn, gain_ffn]),
        w_query,
        w_key,
        w_value,
        w_out,
        w_router.T,
        head,
        0,
    )

    segment, position, live = jax.vmap(lambda l: layout(l, group))(lengths)
    position = position.reshape(rows)
    live = live.reshape(rows)
    member = jnp.any(
        routes[:, None, :] == jnp.arange(experts, dtype=jnp.int32)[None, :, None], -1
    )
    member_f = member.astype(F32)
    member_loc = mine(member_f, 1).reshape(micro, group, local_exp)
    lower = (
        jnp.arange(group, dtype=jnp.int32)[:, None] > jnp.arange(group, dtype=jnp.int32)[None, :]
    ).astype(BF16)
    before = jnp.einsum("st,gte->gse", lower, member_loc.astype(BF16), preferred_element_type=F32)
    place = jnp.where(member_loc > 0, before, -1.0).astype(jnp.int32)
    counts = jnp.sum(member_loc, 1).astype(jnp.int32).T
    place_t = place.transpose(2, 0, 1)[:, :, None, :]

    inputs = inputs_low.astype(F32)
    scale_one = inverse_rms(inputs)
    normed = (inputs * scale_one * gains[0]).astype(BF16)
    query_pre, key_pre, value_pre = (nn(normed, w_heads[j]) for j in range(3))
    shape = (rows, local_heads, head)
    cosine, sine = rope_tables(position, head)

    def head_norm(values, gain):
        return rotary(values * inverse_rms(values) * gain, cosine, sine)

    query_rot, query_pull = jax.vjp(head_norm, query_pre.reshape(shape), gain_query)
    key_rot, key_pull = jax.vjp(head_norm, key_pre.reshape(shape), gain_key)
    batch = (micro, group, local_heads, head)
    queries = query_rot.astype(BF16).reshape(batch)
    keys_low = key_rot.astype(BF16).reshape(batch)
    values_low = value_pre.astype(BF16).reshape(batch)
    same = (segment[:, :, None] == segment[:, None, :])[:, None]

    def scores_of():
        raw = jnp.einsum("gqhd,gkhd->ghqk", queries, keys_low, preferred_element_type=F32) * scale
        return jnp.where(same, raw, MASKED)

    scores = scores_of()
    highest = jnp.max(scores, -1, keepdims=True)
    log_total = highest + jnp.log(jnp.sum(jnp.exp(scores - highest), -1, keepdims=True))
    probs_low = jnp.exp(scores - log_total).astype(BF16)
    attended = jnp.einsum(
        "ghqk,gkhd->gqhd", probs_low, values_low, preferred_element_type=F32
    ).astype(BF16)
    attended_full, full_o, full_rt, upstream_low = middle_gather(
        [attended.reshape(rows, local_heads * head), rows_o, rows_r, cotangent], (1, 0, 1, 1), 1
    )
    full_r = full_rt.T

    hidden = inputs + nn(attended_full, full_o)
    scale_two = inverse_rms(hidden)
    normed_ffn = (hidden * scale_two * gains[1]).astype(BF16)
    logits = nn(normed_ffn, full_r)
    peak = jnp.max(jnp.where(member, logits, -jnp.inf), -1, keepdims=True)
    raised = jnp.where(member, jnp.exp(jnp.where(member, logits - peak, 0.0)), 0.0)
    gates = raised / jnp.sum(raised, -1, keepdims=True)
    gate_t = mine(gates, 1).reshape(micro, group, local_exp).transpose(2, 0, 1)[:, :, None, :]
    upstream_full = (upstream_low * live[:, None].astype(BF16)).reshape(micro, group, width)
    hn = normed_ffn.reshape(micro, group, width)

    outs, weight_grads = [], []
    for e in range(local_exp):
        xe, dyr, hg, dgp, dup, ye, dxe, tok = expert_pass(
            counts[e], place_t[e], gate_t[e], hn, upstream_full, big[e], capacity, shared
        )
        grad = expert_grads(xe, dgp, dup, hg, dyr, shared)
        hn, upstream_full, ye, dxe, tok, grad = lax.optimization_barrier(
            (hn, upstream_full, ye, dxe, tok, grad)
        )
        outs.append((ye, dxe, tok))
        weight_grads.append(lax.psum_scatter(grad, "row", scatter_dimension=1, tiled=True))

    def tie(value, e):
        value, weight_grads[e] = lax.optimization_barrier((value, weight_grads[e]))
        return value

    row = lax.axis_index("row")
    back_sum, tok = scatter_col(
        combine(place, [o[1] for o in outs]), 2, 1, (jnp.stack([o[2] for o in outs]),)
    )
    back_sum = tie(back_sum, 0)
    tok = tok.reshape((experts,) + tok.shape[2:])
    hidden_part = tokens.astype(F32) + nn(attended_full, mine(full_o, 1))
    gate_dots = tok[:, :, 0].reshape(experts, rows).T
    hidden_part = mine(hidden, 1)

    selected = gates * (gate_dots - jnp.sum(gates * gate_dots, -1, keepdims=True))
    logit_grad = selected.astype(BF16)
    router_part = mine(full_r, 0)
    normed_grad = back_sum + nt(logit_grad, router_part)
    grad_router = tn(mine(normed_ffn, 1), logit_grad)
    scaled_two = hidden_part * scale_two
    grad_gain_ffn = jnp.sum(normed_grad * scaled_two, 0)
    dot_two = jnp.sum(tok[:, :, 1].reshape(experts, rows), 0) + jnp.sum(
        logit_grad.astype(F32) * logits, 1
    )
    upstream_part = cotangent.astype(F32) * live[:, None]
    hidden_grad = (
        upstream_part
        + scale_two * (normed_grad * gain_ffn)
        - hidden_part * scale_two**2 * dot_two[:, None] / width
    )

    branch_grad = hidden_grad.astype(BF16)
    (attended_grad,) = scatter_col(nt(branch_grad, mine(full_o, 1)).astype(BF16), 3)
    attended_grad = attended_grad.astype(BF16).reshape(batch)
    grad_out = tn(attended_full, branch_grad)
    scores_again = scores_of()
    probs = jnp.exp(scores_again - log_total)
    probs_again = probs.astype(BF16)
    probs_grad = jnp.einsum(
        "gqhd,gkhd->ghqk", attended_grad, values_low, preferred_element_type=F32
    )
    values_grad = jnp.einsum(
        "ghqk,gqhd->gkhd", probs_again, attended_grad, preferred_element_type=F32
    )
    score_grad = (probs * (probs_grad - jnp.sum(probs_grad * probs, -1, keepdims=True))).astype(
        BF16
    )
    query_grad_rot = (
        jnp.einsum("ghqk,gkhd->gqhd", score_grad, keys_low, preferred_element_type=F32) * scale
    )
    key_grad_rot = (
        jnp.einsum("ghqk,gqhd->gkhd", score_grad, queries, preferred_element_type=F32) * scale
    )
    query_grad, gain_query_part = query_pull(query_grad_rot.reshape(shape))
    key_grad, gain_key_part = key_pull(key_grad_rot.reshape(shape))
    flat = (rows, local_heads * head)
    heads_grad = [
        v.reshape(flat).astype(BF16) for v in (query_grad, key_grad, values_grad)
    ]
    back_heads = sum(nt(g, w_heads[j]) for j, g in enumerate(heads_grad))
    pre = (query_pre, key_pre, value_pre)
    dot_part = sum(jnp.sum(g.astype(F32) * p, -1) for g, p in zip(heads_grad, pre))
    sums = jnp.concatenate([dot_part, gain_query_part, gain_key_part])
    sums = jnp.pad(sums, (0, -sums.shape[0] % 1024)).reshape(-1, 128)
    heads_weights = jnp.stack([tn(normed, g) for g in heads_grad]).astype(BF16)
    back_heads, mixed_slots = lax.optimization_barrier(
        (back_heads.astype(BF16), [o[0] for o in outs])
    )
    (mixed_sum,) = scatter_col(combine(place, mixed_slots), 4)
    mixed = (hidden_part + mixed_sum).astype(BF16)
    back_heads, mixed = lax.optimization_barrier((back_heads, mixed))
    normed_back, sums, heads_terms, out_terms = scatter_col(
        tie(back_heads, 1), 5, 2, (sums, heads_weights, grad_out.astype(BF16))
    )
    sums = jnp.sum(sums, 0).reshape(-1)
    dot_one = sums[:rows]
    gain_query_sum, gain_key_sum = sums[rows : rows + head], sums[rows + head : rows + 2 * head]
    scale_one_part = scale_one
    inputs_part = tokens.astype(F32)
    grad_gain_attn = jnp.sum(normed_back * inputs_part * scale_one_part, 0)
    input_grad = (
        hidden_grad
        + scale_one_part * (normed_back * gain_attn)
        - inputs_part * scale_one_part**2 * dot_one[:, None] / width
    )

    weight_grads = jnp.stack(weight_grads, 1).astype(F32)
    grad_gate, grad_up = weight_grads[0], weight_grads[1]
    grad_down = jnp.concatenate(
        [weight_grads[2][..., b * shared : (b + 1) * shared] for b in range(w_down.shape[1] // shared)],
        1,
    )

    heads_terms = jnp.sum(heads_terms.astype(F32), 0)
    heads_sum = jnp.concatenate([heads_terms[j] for j in range(heads_terms.shape[0])], -1)
    grad_query, grad_key, grad_value = heads_sum[0], heads_sum[1], heads_sum[2]
    out_terms = jnp.sum(out_terms.astype(F32), 0)
    grad_out = jnp.concatenate([out_terms[j] for j in range(out_terms.shape[0])], -1)
    smalls = [
        grad_gain_attn,
        grad_gain_ffn,
        gain_query_sum,
        gain_key_sum,
        grad_router.T.reshape(-1),
    ]
    total = lax.psum(jnp.concatenate(smalls).reshape(-1, 128), "row").reshape(-1)
    grad_gain_attn, grad_gain_ffn = total[:part], total[part : 2 * part]
    grad_gain_query = total[2 * part : 2 * part + head]
    grad_gain_key = total[2 * part + head : 2 * part + 2 * head]
    grad_router = lax.dynamic_slice_in_dim(
        total[2 * part + 2 * head :].reshape(experts, part), row * (experts // n_row), experts // n_row, 0
    ).T
    return (
        mixed,
        input_grad,
        grad_gain_attn,
        grad_gain_ffn,
        grad_gain_query,
        grad_gain_key,
        grad_query,
        grad_key,
        grad_value,
        grad_out,
        grad_router,
        grad_gate,
        grad_up,
        grad_down,
    )


def solution(mesh):
    placed = (
        P("row", "col"),
        P("col"),
        P("col"),
        P(),
        P(),
        P("col", "row"),
        P("col", "row"),
        P("col", "row"),
        P("col", "row"),
        P("col", "row"),
        P("col", "row", None),
        P("col", "row", None),
        P("col", None, "row"),
        P("row", None),
        P("row", None),
        P("row", "col"),
    )
    return jax.shard_map(
        shards,
        mesh=mesh,
        in_specs=placed,
        out_specs=(
            P("row", "col"),
            P("row", "col"),
            P("col"),
            P("col"),
            P(),
            P(),
            P("col", "row"),
            P("col", "row"),
            P("col", "row"),
            P("col", "row"),
            P("col", "row"),
            P("col", "row", None),
            P("col", "row", None),
            P("col", None, "row"),
        ),
        check_vma=False,
    )
```

```python
import functools
import math

import jax
import jax.numpy as jnp
from jax import lax
from jax.experimental import pallas as pl
from jax.experimental.pallas import tpu as pltpu
from jax.sharding import PartitionSpec as P

EPSILON = 1e-06
ROPE_BASE = 10000.0
MASKED = -1e30
F32 = jnp.float32
BF16 = jnp.bfloat16
VMEM_LIMIT = 60 * 1024 * 1024
MESH = pl.DeviceIdType.MESH
ANY = pl.BlockSpec(memory_space=pl.ANY)


def inverse_rms(values):
    return lax.rsqrt(jnp.mean(values * values, -1, keepdims=True) + EPSILON)


def rope_tables(position, head):
    half = head // 2
    inverse = jnp.exp(-math.log(ROPE_BASE) * 2.0 / head * jnp.arange(half, dtype=F32))
    angles = position[:, None] * inverse[None, :]
    return jnp.cos(angles)[:, None, :], jnp.sin(angles)[:, None, :]


def rotary(values, cosine, sine):
    half = values.shape[-1] // 2
    first = values[..., :half]
    second = values[..., half:]
    return jnp.concatenate([first * cosine - second * sine, second * cosine + first * sine], -1)


def layout(lengths_row, group):
    ends = jnp.cumsum(lengths_row)
    starts = ends - lengths_row
    row_index = jnp.arange(group, dtype=jnp.int32)
    segment = jnp.sum((row_index[:, None] >= ends[None, :]).astype(jnp.int32), 1)
    member = segment[:, None] == jnp.arange(lengths_row.shape[0], dtype=jnp.int32)[None, :]
    position = (row_index - jnp.sum(jnp.where(member, starts[None, :], 0), 1)).astype(F32)
    live = (segment < lengths_row.shape[0] - 1).astype(F32)
    return (segment, position, live)


def nn(a, b):
    return lax.dot_general(a, b, (((1,), (0,)), ((), ())), preferred_element_type=F32)


def nt(a, b):
    return lax.dot_general(a, b, (((1,), (1,)), ((), ())), preferred_element_type=F32)


def tn(a, b):
    return lax.dot_general(a, b, (((0,), (0,)), ((), ())), preferred_element_type=F32)


def expert_body(shared, counts, place, gate, hn, dy, w, xe_o, dyr_o, hg_o, dgp_o, dup_o, ye_o, dxe_o, tok_o):
    g, i = pl.program_id(0), pl.program_id(1)
    rows = xe_o.shape[1]
    width, ff = w.shape[1:]
    base = i * rows

    @pl.when(i == 0)
    def _():
        tok_o[...] = jnp.zeros_like(tok_o)

    @pl.when(counts[g] <= base)
    def _():
        for ref in (xe_o, dyr_o, hg_o, dgp_o, dup_o, ye_o, dxe_o):
            ref[...] = jnp.zeros_like(ref)

    @pl.when(counts[g] > base)
    def _():
        slot = lax.broadcasted_iota(jnp.int32, (rows, place.shape[2]), 0) + base
        hit = slot == place[0]
        pick = jnp.where(hit, 1.0, 0.0).astype(BF16)
        weight = jnp.sum(jnp.where(hit, gate[0], 0.0), 1, keepdims=True)
        xe = nn(pick, hn[0]).astype(BF16)
        xe_o[0] = xe
        gp = nn(xe, w[0])
        up = nn(xe, w[1])
        sig = jax.nn.sigmoid(gp)
        silu = gp * sig
        hid = silu * up
        hg = (hid * weight).astype(BF16)
        hg_o[0] = hg
        dyr = nn(pick, dy[0]).astype(BF16)
        dyr_o[0] = dyr
        parts = []
        for r in range(width // shared):
            at = r * shared
            total = None
            for b in range(ff // shared):
                low = b * shared
                term = nn(hg[:, low : low + shared], w[2, at : at + shared, low : low + shared])
                total = term if total is None else total + term
            ye_o[0, :, at : at + shared] = total.astype(BF16)
        for b in range(ff // shared):
            low = b * shared
            total = None
            for r in range(width // shared):
                at = r * shared
                term = nt(dyr[:, at : at + shared], w[2, at : at + shared, low : low + shared])
                total = term if total is None else total + term
            parts.append(total)
        back = jnp.concatenate(parts, 1)
        dgate = jnp.sum(back * hid, 1, keepdims=True)
        dhid = back * weight
        dgp = (dhid * up * sig * (1.0 + gp * (1.0 - sig))).astype(BF16)
        dup = (dhid * silu).astype(BF16)
        dgp_o[0] = dgp
        dup_o[0] = dup
        dots = jnp.sum(dgp.astype(F32) * gp + dup.astype(F32) * up, 1, keepdims=True)
        dxe_o[0] = (nt(dgp, w[0]) + nt(dup, w[1])).astype(BF16)
        tok_o[0, 0:1, :] += jnp.sum(jnp.where(hit, dgate, 0.0), 0, keepdims=True)
        tok_o[0, 1:2, :] += jnp.sum(jnp.where(hit, dots, 0.0), 0, keepdims=True)


def expert_pass(counts, place, gate, hn, dy, w, capacity, shared):
    _, width, ff = w.shape
    micro, group, _ = hn.shape
    rows = min(256, capacity)
    blocks = capacity // rows
    tall = lambda g, i, c: (g, i, 0)
    line = lambda g, i, c: (g, 0, 0)
    slots = lambda n: jax.ShapeDtypeStruct((micro, capacity, n), BF16)
    sizes = (width, width, ff, ff, ff, width, width)
    flops = 2 * micro * capacity * width * (6 * ff + 2 * group)
    return pl.pallas_call(
        functools.partial(expert_body, shared),
        grid_spec=pltpu.PrefetchScalarGridSpec(
            num_scalar_prefetch=1,
            grid=(micro, blocks),
            in_specs=[
                pl.BlockSpec((1, 1, group), line),
                pl.BlockSpec((1, 1, group), line),
                pl.BlockSpec((1, group, width), line),
                pl.BlockSpec((1, group, width), line),
                pl.BlockSpec((3, width, ff), lambda g, i, c: (0, 0, 0), pipeline_mode=pl.Buffered(1)),
            ],
            out_specs=[pl.BlockSpec((1, rows, n), tall) for n in sizes]
            + [pl.BlockSpec((1, 2, group), line)],
        ),
        out_shape=[slots(n) for n in sizes] + [jax.ShapeDtypeStruct((micro, 2, group), F32)],
        compiler_params=pltpu.CompilerParams(vmem_limit_bytes=VMEM_LIMIT),
        cost_estimate=pl.CostEstimate(
            flops=flops, bytes_accessed=40 << 20, transcendentals=micro * capacity * ff
        ),
        name="expert_pass",
    )(counts, place, gate, hn, dy, w)


def grads_body(xe, dgp, dup, hg, dyr, out):
    part = xe[...]
    shared = part.shape[1]
    out[0] = tn(part, dgp[...]).astype(BF16)
    out[1] = tn(part, dup[...]).astype(BF16)
    back = dyr[...]
    for b in range(hg.shape[1] // shared):
        low = b * shared
        out[2, :, low : low + shared] = tn(hg[:, low : low + shared], back).astype(BF16)


def expert_grads(xe, dgp, dup, hg, dyr, shared):
    micro, capacity, width = xe.shape
    ff = dgp.shape[2]
    rows = micro * capacity
    xe, dyr = (a.reshape(rows, width) for a in (xe, dyr))
    dgp, dup, hg = (a.reshape(rows, ff) for a in (dgp, dup, hg))
    thin = pl.BlockSpec((rows, shared), lambda r: (0, r))
    whole = pl.BlockSpec((rows, ff), lambda r: (0, 0))
    return pl.pallas_call(
        grads_body,
        grid=(width // shared,),
        in_specs=[thin, whole, whole, whole, thin],
        out_specs=pl.BlockSpec((3, shared, ff), lambda r: (0, r, 0)),
        out_shape=jax.ShapeDtypeStruct((3, width, ff), BF16),
        compiler_params=pltpu.CompilerParams(vmem_limit_bytes=VMEM_LIMIT),
        cost_estimate=pl.CostEstimate(
            flops=6 * rows * width * ff, bytes_accessed=26 << 20, transcendentals=0
        ),
        name="expert_grads",
    )(xe, dgp, dup, hg, dyr)


def pack_body(wg, wu, wd, out):
    shared = out.shape[1]
    out[0] = wg[0]
    out[1] = wu[0]
    for b in range(out.shape[2] // shared):
        low = b * shared
        out[2, :, low : low + shared] = wd[0, low : low + shared, :]


def pack(wg, wu, wd, e):
    _, shared, ff = wg.shape
    block = pl.BlockSpec((1, shared, ff), lambda i: (e, 0, 0))
    return pl.pallas_call(
        pack_body,
        grid=(1,),
        in_specs=[block, block, pl.BlockSpec((1, ff, shared), lambda i: (e, 0, 0))],
        out_specs=pl.BlockSpec((3, shared, ff), lambda i: (0, 0, 0)),
        out_shape=jax.ShapeDtypeStruct((3, shared, ff), BF16),
        cost_estimate=pl.CostEstimate(
            flops=0, bytes_accessed=12 * shared * ff, transcendentals=0
        ),
        name="pack",
    )(wg, wu, wd)


def unpack_body(x, *refs):
    gg, gu, gd = refs[-3:]
    shared = x.shape[1]
    gg[0] = x[0].astype(F32)
    gu[0] = x[1].astype(F32)
    for b in range(x.shape[2] // shared):
        low = b * shared
        gd[0, low : low + shared, :] = x[2, :, low : low + shared].astype(F32)


def unpack(x, held, e, experts):
    _, shared, ff = x.shape
    block = pl.BlockSpec((1, shared, ff), lambda i: (e, 0, 0))
    held = list(held)
    return pl.pallas_call(
        unpack_body,
        grid=(1,),
        in_specs=[pl.BlockSpec((3, shared, ff), lambda i: (0, 0, 0))] + [ANY] * len(held),
        out_specs=[block, block, pl.BlockSpec((1, ff, shared), lambda i: (e, 0, 0))],
        out_shape=[
            jax.ShapeDtypeStruct((experts, shared, ff), F32),
            jax.ShapeDtypeStruct((experts, shared, ff), F32),
            jax.ShapeDtypeStruct((experts, ff, shared), F32),
        ],
        input_output_aliases={1 + j: j for j in range(len(held))},
        compiler_params=pltpu.CompilerParams(vmem_limit_bytes=VMEM_LIMIT),
        cost_estimate=pl.CostEstimate(
            flops=0, bytes_accessed=18 * shared * ff, transcendentals=0
        ),
        name="unpack",
    )(x, *held)


def combine_body(place, *refs):
    out = refs[-1]
    total = jnp.zeros((out.shape[1], out.shape[2]), F32)
    for e, ref in enumerate(refs[:-1]):
        slot = lax.broadcasted_iota(jnp.int32, (out.shape[1], ref.shape[1]), 1)
        pick = jnp.where(slot == place[0, :, e : e + 1], 1.0, 0.0).astype(BF16)
        total = total + nn(pick, ref[0])
    out[0] = total.astype(BF16)


def combine(place, slots):
    micro, group, local = place.shape
    capacity, width = slots[0].shape[1:]
    tile = min(256, group)
    return pl.pallas_call(
        combine_body,
        grid=(micro, group // tile),
        in_specs=[pl.BlockSpec((1, tile, local), lambda g, i: (g, i, 0))]
        + [pl.BlockSpec((1, capacity, width), lambda g, i: (g, 0, 0)) for s in slots],
        out_specs=pl.BlockSpec((1, tile, width), lambda g, i: (g, i, 0)),
        out_shape=jax.ShapeDtypeStruct((micro, group, width), BF16),
        compiler_params=pltpu.CompilerParams(vmem_limit_bytes=VMEM_LIMIT),
        cost_estimate=pl.CostEstimate(
            flops=2 * micro * group * local * capacity * width,
            bytes_accessed=micro * (local * capacity + group) * width * 2,
            transcendentals=0,
        ),
        name="combine",
    )(place, *slots).reshape(micro * group, width)


def places():
    row, col = lax.axis_index("row"), lax.axis_index("col")
    n_row, n_col = lax.axis_size("row"), lax.axis_size("col")
    return row, col, n_row, n_col


def remote(src, dst, send_sem, recv_sem, where):
    return pltpu.make_async_remote_copy(
        src_ref=src,
        dst_ref=dst,
        send_sem=send_sem,
        recv_sem=recv_sem,
        device_id=where,
        device_id_type=MESH,
    )


def shake(sources, targets):
    barrier = pltpu.get_barrier_semaphore()
    for ok, where in sources:
        if ok is True:
            pl.semaphore_signal(barrier, inc=1, device_id=where, device_id_type=MESH)
        else:

            @pl.when(ok)
            def _():
                pl.semaphore_signal(barrier, inc=1, device_id=where, device_id_type=MESH)

    count = 0
    for ok in targets:
        count = count + (1 if ok is True else jnp.where(ok, 1, 0))
    pl.semaphore_wait(barrier, count)


def line_peers():
    row, col, n_row, n_col = places()
    pair, core = col // 2, col % 2
    return [
        (True, (row, pair * 2 + 1 - core)),
        (pair > 0, (row, (pair - 1) * 2 + core)),
        (pair < n_col // 2 - 1, (row, (pair + 1) * 2 + core)),
    ]


def row_peers():
    row, col, n_row, n_col = places()
    return [(True, ((row + k) % n_row, col)) for k in range(1, n_row)]


def col_slice(ref, index, size):
    return ref.at[..., pl.ds(pl.multiple_of(index * size, size), size)]


def line_gather(axes, ins, outs, sems):
    own_sem, right_s, right_r, left_s, left_r, side_s, side_r = sems
    n = len(ins)
    row, col, n_row, n_col = places()
    pairs, pair, core = n_col // 2, col // 2, col % 2

    def at(pair_index, core_index):
        return (row, pair_index * 2 + core_index)

    def block(j, source):
        size = ins[j].shape[axes[j]]
        if axes[j] == 0:
            return outs[j].at[pl.ds(pl.multiple_of(source * size, size), size)]
        return col_slice(outs[j], source, size)

    def right(j, s):
        source = (pair - s) * 2 + core
        src = ins[j] if s == 0 else block(j, source)
        return remote(src, block(j, source), right_s.at[j, s], right_r.at[j, s], at(pair + 1, core))

    def left(j, s):
        source = (pair + s) * 2 + core
        src = ins[j] if s == 0 else block(j, source)
        return remote(src, block(j, source), left_s.at[j, s], left_r.at[j, s], at(pair - 1, core))

    def side(j, source_pair, first=False):
        source = source_pair * 2 + core
        src = ins[j] if first else block(j, source)
        return remote(
            src,
            block(j, source),
            side_s.at[j, source_pair],
            side_r.at[j, source_pair],
            at(pair, 1 - core),
        )

    def arrived(j, recvs, slot, source):
        remote(
            ins[j], block(j, source), recvs.at[j, slot], recvs.at[j, slot], at(pair, 1 - core)
        ).wait_recv()

    def own(j):
        return pltpu.make_async_copy(ins[j], block(j, col), own_sem.at[j])

    def begin():
        for j in range(n):

            @pl.when(pair < pairs - 1)
            def _():
                right(j, 0).start()

            @pl.when(pair > 0)
            def _():
                left(j, 0).start()

        for j in range(n):
            side(j, pair, True).start()
            own(j).start()

    def middle():
        for s in range(1, pairs):
            for j in range(n):

                @pl.when(pair >= s)
                def _():
                    arrived(j, right_r, s - 1, (pair - s) * 2 + core)

                    @pl.when(pair < pairs - 1)
                    def _():
                        right(j, s).start()

                    side(j, pair - s).start()

                @pl.when(pair + s < pairs)
                def _():
                    arrived(j, left_r, s - 1, (pair + s) * 2 + core)

                    @pl.when(pair > 0)
                    def _():
                        left(j, s).start()

                    side(j, pair + s).start()

    def end():
        for j in range(n):
            own(j).wait()
            for p in range(pairs):
                side(j, p).wait_send()
                arrived(j, side_r, p, p * 2 + 1 - core)
            for s in range(pairs):

                @pl.when((pair >= s) & (pair < pairs - 1))
                def _():
                    right(j, s).wait_send()

                @pl.when((pair + s < pairs) & (pair > 0))
                def _():
                    left(j, s).wait_send()

    return begin, middle, end


def line_sems(n, pairs):
    dma = pltpu.SemaphoreType.DMA
    return [dma((n,))] + [dma((n, pairs))] * 6


def front_body(tokens, gains, wq, wk, wv, wo, wr, *refs):
    x_o, gains_o, wh_o, wo_o, wr_o = refs[:5]
    wide = refs[5:8]
    line, (heads_s, heads_r, row_s, row_r, own_s) = refs[8:15], refs[15:]
    row, col, n_row, n_col = places()
    head = wh_o.shape[2]
    part = wq.shape[0]
    begin, middle, end = line_gather((1, 1), [tokens, gains], [x_o, gains_o], line)
    small = [(wq, wide[0]), (wk, wide[1]), (wv, wide[2]), (wo, wo_o), (wr, wr_o)]

    def small_dst(k, source):
        src, dst = small[k]
        if k < 4:
            return col_slice(dst, source, src.shape[1])
        return dst.at[pl.ds(pl.multiple_of(source * src.shape[0], src.shape[0]), src.shape[0]), :]

    def small_copy(k, step):
        return remote(
            small[k][0],
            small_dst(k, row),
            row_s.at[k, step],
            row_r.at[k, step],
            ((row + step) % n_row, col),
        )

    def small_come(k, step):
        source = (row + n_row - step) % n_row
        return remote(
            small[k][0], small_dst(k, source), row_s.at[k, step], row_r.at[k, step], (source, col)
        )

    def small_own(k):
        return pltpu.make_async_copy(small[k][0], small_dst(k, row), own_s.at[k])

    def heads_dst(m, source):
        return wh_o.at[m, pl.ds(pl.multiple_of(source * part, part), part), :]

    def heads(m, step):
        where = (col + step) % n_col
        return remote(
            col_slice(wide[m], where, head),
            heads_dst(m, col),
            heads_s.at[m, step],
            heads_r.at[m, step],
            (row, where),
        )

    def heads_come(m, step):
        source = (col + n_col - step) % n_col
        return remote(
            heads_dst(m, source),
            heads_dst(m, source),
            heads_s.at[m, step],
            heads_r.at[m, step],
            (row, source),
        )

    def heads_own(m):
        return pltpu.make_async_copy(
            col_slice(wide[m], col, head), heads_dst(m, col), own_s.at[5 + m]
        )

    peers = [(True, (row, (col + k) % n_col)) for k in range(1, n_col)] + row_peers()
    shake(peers, [ok for ok, _ in peers])
    for k in range(5):
        for step in range(1, n_row):
            small_copy(k, step).start()
        small_own(k).start()
    begin()
    for k in range(3):
        small_own(k).wait()
        for step in range(1, n_row):
            small_come(k, step).wait_recv()
    for m in range(3):
        heads_own(m).start()
        for step in range(1, n_col):
            heads(m, step).start()
    middle()
    end()
    for k in range(5):
        if k >= 3:
            small_own(k).wait()
        for step in range(1, n_row):
            small_copy(k, step).wait_send()
            if k >= 3:
                small_come(k, step).wait_recv()
    for m in range(3):
        heads_own(m).wait()
        for step in range(1, n_col):
            heads(m, step).wait_send()
            heads_come(m, step).wait_recv()


def front(tokens, gains, wq, wk, wv, wo, wr, head, ident):
    n_row, n_col = lax.axis_size("row"), lax.axis_size("col")
    rows, part = tokens.shape
    width = part * n_col
    dma = pltpu.SemaphoreType.DMA
    shapes = [
        ((rows, width), BF16),
        ((gains.shape[0], width), F32),
        ((3, width, head), BF16),
        ((wo.shape[0], wo.shape[1] * n_row), BF16),
        ((wr.shape[0] * n_row, part), BF16),
    ] + [((part, wq.shape[1] * n_row), BF16)] * 3
    return pl.pallas_call(
        front_body,
        in_specs=[ANY] * 7,
        out_specs=[ANY] * 8,
        out_shape=[jax.ShapeDtypeStruct(s, t) for s, t in shapes],
        scratch_shapes=line_sems(2, n_col // 2)
        + [
            dma((3, n_col)),
            dma((3, n_col)),
            dma((5, n_row)),
            dma((5, n_row)),
            dma((8,)),
        ],
        compiler_params=pltpu.CompilerParams(collective_id=ident, has_side_effects=True),
        cost_estimate=pl.CostEstimate(
            flops=0, bytes_accessed=rows * width * 32, transcendentals=0
        ),
        name="front",
    )(tokens, gains, wq, wk, wv, wo, wr)[:5]


def middle_body(axes, *refs):
    n = len(axes)
    begin, middle, end = line_gather(axes, refs[:n], refs[n : 2 * n], refs[2 * n :])
    sources = line_peers()
    shake(sources, [ok for ok, _ in sources])
    begin()
    middle()
    end()


def middle_gather(arrays, axes, ident):
    n_col, n = lax.axis_size("col"), len(arrays)
    shapes = [
        tuple(d * n_col if at == axis else d for at, d in enumerate(a.shape))
        for a, axis in zip(arrays, axes)
    ]
    return pl.pallas_call(
        functools.partial(middle_body, axes),
        in_specs=[ANY] * n,
        out_specs=[ANY] * n,
        out_shape=[jax.ShapeDtypeStruct(s, a.dtype) for s, a in zip(shapes, arrays)],
        scratch_shapes=line_sems(n, n_col // 2),
        compiler_params=pltpu.CompilerParams(collective_id=ident, has_side_effects=True),
        cost_estimate=pl.CostEstimate(
            flops=0, bytes_accessed=sum(math.prod(s) for s in shapes) * 32, transcendentals=0
        ),
        name="middle_gather",
    )(*arrays)


def scatter_body(part, stage, *refs):
    n_in = (1, 2, 4, 3)[stage]
    n_out = (1, 2, 4, 3)[stage]
    x, ins = refs[0], refs[1:n_in]
    out, outs = refs[n_in], refs[n_in + 1 : n_in + n_out]
    rest = refs[n_in + n_out :]
    acc, side, from_left, from_right, load, side_s, side_r = rest[:7]
    right_s, right_r, left_s, left_r = rest[7:11]
    row, col, n_row, n_col = places()
    pairs, pair, core = n_col // 2, col // 2, col % 2
    rows = out.shape[0]
    cuts = load.shape[1]
    height = rows // cuts
    tile = min(256, height)

    def at(pair_index, core_index):
        return (row, pair_index * 2 + core_index)

    def block(owner, q):
        return x.at[
            pl.ds(q * height, height), pl.ds(pl.multiple_of(owner * part, part), part)
        ]

    def cut(ref, d, q):
        return ref.at[d, pl.ds(q * height, height)]

    def fetch(d, q):
        return pltpu.make_async_copy(block(d * 2 + core, q), cut(acc, d, q), load.at[d, q])

    def across(d, q):
        return remote(
            block(d * 2 + 1 - core, q),
            cut(side, d, q),
            side_s.at[d, q],
            side_r.at[d, q],
            at(pair, 1 - core),
        )

    def right(d, q):
        return remote(
            cut(acc, d, q),
            cut(from_left, d, q),
            right_s.at[d, q],
            right_r.at[d, q],
            at(pair + 1, core),
        )

    def left(d, q):
        return remote(
            cut(acc, d, q),
            cut(from_right, d, q),
            left_s.at[d, q],
            left_r.at[d, q],
            at(pair - 1, core),
        )

    copies, arrivals, own = [], [], []
    if stage in (1, 2):
        small_s, small_r, own_s = rest[11:14]
        extra, extra_o = ins[0], outs[0]
        for k in range(1, n_col):
            where, source = (col + k) % n_col, (col + n_col - k) % n_col
            copies.append(
                remote(extra, extra_o.at[col], small_s.at[k], small_r.at[k], (row, where))
            )
            arrivals.append(
                remote(extra, extra_o.at[source], small_s.at[k], small_r.at[k], (row, where))
            )
        own.append(pltpu.make_async_copy(extra, extra_o.at[col], own_s))
    if stage == 2:
        give_s, give_r, keep_s = rest[14:]
        per = n_col // n_row
        for m in range(2):
            src, dst = ins[1 + m], outs[1 + m]

            def block_of(r):
                return src.at[pl.ds(r * per, per)]

            for step in range(1, n_row):
                where, source = (row + step) % n_row, (row + n_row - step) % n_row
                sems = (give_s.at[m, step], give_r.at[m, step])
                copies.append(remote(block_of(where), dst.at[row], *sems, (where, col)))
                arrivals.append(remote(block_of(where), dst.at[source], *sems, (where, col)))
            own.append(pltpu.make_async_copy(block_of(row), dst.at[row], keep_s.at[m]))
    if stage == 3:
        give_s, give_r, keep_s = rest[11:]
        for m in range(2):
            src, dst = ins[m], outs[m]
            size = src.shape[1 - m] // n_col

            def block_for(c):
                at_c = pl.ds(pl.multiple_of(c * size, size), size)
                return src.at[:, at_c, :] if m == 0 else src.at[at_c, :]

            for step in range(1, n_col):
                where, source = (col + step) % n_col, (col + n_col - step) % n_col
                sems = (give_s.at[m, step], give_r.at[m, step])
                copies.append(remote(block_for(where), dst.at[col], *sems, (row, where)))
                arrivals.append(remote(block_for(where), dst.at[source], *sems, (row, where)))
            own.append(pltpu.make_async_copy(block_for(col), dst.at[col], keep_s.at[m]))
    if stage:
        peers = [(True, (row, (col + k) % n_col)) for k in range(1, n_col)]
    else:
        peers = line_peers()
    if stage == 2:
        peers += row_peers()
    shake(peers, [ok for ok, _ in peers])
    order = []
    for t in range(pairs):
        for d in (pairs - 1 - t, t):
            if d not in order:
                order.append(d)
    for d in order:
        for q in range(cuts):
            across(d, q).start()
            fetch(d, q).start()
    for c in copies + own:
        c.start()

    def add(q, into, *sources):
        def step(i, _):
            lines = pl.ds(pl.multiple_of(q * height + i * tile, tile), tile)
            total = sources[0][lines, :].astype(F32)
            for ref in sources[1:]:
                total = total + ref[lines, :].astype(F32)
            into[lines, :] = total.astype(into.dtype)
            return 0

        lax.fori_loop(0, height // tile, step, 0)

    def ready(d, q):
        fetch(d, q).wait()
        across(d, q).wait_recv()

    def go_right(d, q):
        ready(d, q)

        @pl.when(pair > 0)
        def _():
            right(d, q).wait_recv()
            add(q, acc.at[d], acc.at[d], side.at[d], from_left.at[d])

        @pl.when(pair == 0)
        def _():
            add(q, acc.at[d], acc.at[d], side.at[d])

        right(d, q).start()

    def go_left(d, q):
        ready(d, q)

        @pl.when(pair < pairs - 1)
        def _():
            left(d, q).wait_recv()
            add(q, acc.at[d], acc.at[d], side.at[d], from_right.at[d])

        @pl.when(pair == pairs - 1)
        def _():
            add(q, acc.at[d], acc.at[d], side.at[d])

        left(d, q).start()

    for t in range(pairs - 1):
        far, near = pairs - 1 - t, t
        for q in range(cuts):

            @pl.when(far > pair)
            def _():
                go_right(far, q)

            @pl.when(near < pair)
            def _():
                go_left(near, q)

    for q in range(cuts):
        ready(pair, q)

        @pl.when(pair == 0)
        def _():
            left(pair, q).wait_recv()
            add(q, out, acc.at[pair], side.at[pair], from_right.at[pair])

        @pl.when(pair == pairs - 1)
        def _():
            right(pair, q).wait_recv()
            add(q, out, acc.at[pair], side.at[pair], from_left.at[pair])

        @pl.when((pair > 0) & (pair < pairs - 1))
        def _():
            left(pair, q).wait_recv()
            right(pair, q).wait_recv()
            add(q, out, acc.at[pair], side.at[pair], from_left.at[pair], from_right.at[pair])

    for d in range(pairs):
        for q in range(cuts):
            across(d, q).wait_send()

            @pl.when(pair < d)
            def _():
                right(d, q).wait_send()

            @pl.when(pair > d)
            def _():
                left(d, q).wait_send()

    for c in copies:
        c.wait_send()
    for c in arrivals:
        c.wait_recv()
    for c in own:
        c.wait()


def scatter_col(x, ident, stage=0, others=()):
    n_row, n_col = lax.axis_size("row"), lax.axis_size("col")
    pairs, per = n_col // 2, n_col // n_row
    rows, part = x.shape[0], x.shape[1] // n_col
    cuts = 4 if rows % 1024 == 0 else 1
    dma = pltpu.SemaphoreType.DMA
    buffer = pltpu.VMEM((pairs, rows, part), BF16)
    scratch = [buffer] * 4 + [dma((pairs, cuts))] * 7
    out_shape = [jax.ShapeDtypeStruct((rows, part), F32)]
    if stage in (1, 2):
        extra = others[0]
        out_shape.append(jax.ShapeDtypeStruct((n_col,) + extra.shape, extra.dtype))
        scratch += [dma((n_col,)), dma((n_col,)), dma(())]
    if stage == 2:
        scratch += [dma((2, n_row)), dma((2, n_row)), dma((2,))]
        for value in others[1:]:
            out_shape.append(jax.ShapeDtypeStruct((n_row, per) + value.shape[1:], BF16))
    if stage == 3:
        heads, branch = others
        scratch += [dma((2, n_col)), dma((2, n_col)), dma((2,))]
        out_shape += [
            jax.ShapeDtypeStruct((n_col, 3, heads.shape[1] // n_col, heads.shape[2]), BF16),
            jax.ShapeDtypeStruct((n_col, branch.shape[0] // n_col, branch.shape[1]), BF16),
        ]
    return pl.pallas_call(
        functools.partial(scatter_body, part, stage),
        in_specs=[ANY] * (1 + len(others)),
        out_specs=[pl.BlockSpec(memory_space=pltpu.VMEM)] + [ANY] * (len(out_shape) - 1),
        out_shape=out_shape,
        scratch_shapes=scratch,
        compiler_params=pltpu.CompilerParams(
            vmem_limit_bytes=VMEM_LIMIT, collective_id=ident, has_side_effects=True
        ),
        cost_estimate=pl.CostEstimate(
            flops=0, bytes_accessed=rows * part * n_col * 40, transcendentals=0
        ),
        name="scatter_col",
    )(x, *others)


def shards(
    tokens,
    gain_attn,
    gain_ffn,
    gain_query,
    gain_key,
    w_query,
    w_key,
    w_value,
    w_out,
    w_router,
    w_gate,
    w_up,
    w_down,
    routes,
    lengths,
    cotangent,
):
    n_col = lax.axis_size("col")
    n_row = lax.axis_size("row")
    col = lax.axis_index("col")
    micro, spans = lengths.shape
    rows, part = tokens.shape
    group = rows // micro
    width = part * n_col
    head = gain_query.shape[0]
    local_exp = w_gate.shape[0]
    experts = local_exp * n_col
    topk = routes.shape[1]
    capacity = 2 * group * topk // experts
    local_heads = w_out.shape[0] // head
    hd = w_out.shape[0] * n_col
    scale = head ** (-0.5)

    def gather(value, axis_name, axis):
        return lax.all_gather(value, axis_name, axis=axis, tiled=True)

    def mine(value, axis):
        size = value.shape[axis] // n_col
        return lax.dynamic_slice_in_dim(value, col * size, size, axis)

    shared = w_down.shape[2]
    big = [gather(pack(w_gate, w_up, w_down, e), "row", 1) for e in range(local_exp)]
    inputs_low, gains, w_heads, rows_o, rows_r = front(
        tokens,
        jnp.stack([gain_attn, gain_ffn]),
        w_query,
        w_key,
        w_value,
        w_out,
        w_router.T,
        head,
        0,
    )

    segment, position, live = jax.vmap(lambda l: layout(l, group))(lengths)
    position = position.reshape(rows)
    live = live.reshape(rows)
    member = jnp.any(
        routes[:, None, :] == jnp.arange(experts, dtype=jnp.int32)[None, :, None], -1
    )
    member_f = member.astype(F32)
    member_loc = mine(member_f, 1).reshape(micro, group, local_exp)
    lower = (
        jnp.arange(group, dtype=jnp.int32)[:, None] > jnp.arange(group, dtype=jnp.int32)[None, :]
    ).astype(BF16)
    before = jnp.einsum("st,gte->gse", lower, member_loc.astype(BF16), preferred_element_type=F32)
    place = jnp.where(member_loc > 0, before, -1.0).astype(jnp.int32)
    counts = jnp.sum(member_loc, 1).astype(jnp.int32).T
    place_t = place.transpose(2, 0, 1)[:, :, None, :]

    inputs = inputs_low.astype(F32)
    scale_one = inverse_rms(inputs)
    normed = (inputs * scale_one * gains[0]).astype(BF16)
    query_pre, key_pre, value_pre = (nn(normed, w_heads[j]) for j in range(3))
    shape = (rows, local_heads, head)
    cosine, sine = rope_tables(position, head)

    def head_norm(values, gain):
        return rotary(values * inverse_rms(values) * gain, cosine, sine)

    query_rot, query_pull = jax.vjp(head_norm, query_pre.reshape(shape), gain_query)
    key_rot, key_pull = jax.vjp(head_norm, key_pre.reshape(shape), gain_key)
    batch = (micro, group, local_heads, head)
    queries = query_rot.astype(BF16).reshape(batch)
    keys_low = key_rot.astype(BF16).reshape(batch)
    values_low = value_pre.astype(BF16).reshape(batch)
    same = (segment[:, :, None] == segment[:, None, :])[:, None]

    def scores_of():
        raw = jnp.einsum("gqhd,gkhd->ghqk", queries, keys_low, preferred_element_type=F32) * scale
        return jnp.where(same, raw, MASKED)

    scores = scores_of()
    highest = jnp.max(scores, -1, keepdims=True)
    log_total = highest + jnp.log(jnp.sum(jnp.exp(scores - highest), -1, keepdims=True))
    probs_low = jnp.exp(scores - log_total).astype(BF16)
    attended = jnp.einsum(
        "ghqk,gkhd->gqhd", probs_low, values_low, preferred_element_type=F32
    ).astype(BF16)
    attended_full, full_o, full_rt, upstream_low = middle_gather(
        [attended.reshape(rows, local_heads * head), rows_o, rows_r, cotangent], (1, 0, 1, 1), 1
    )
    full_r = full_rt.T

    hidden = inputs + nn(attended_full, full_o)
    scale_two = inverse_rms(hidden)
    normed_ffn = (hidden * scale_two * gains[1]).astype(BF16)
    logits = nn(normed_ffn, full_r)
    peak = jnp.max(jnp.where(member, logits, -jnp.inf), -1, keepdims=True)
    raised = jnp.where(member, jnp.exp(jnp.where(member, logits - peak, 0.0)), 0.0)
    gates = raised / jnp.sum(raised, -1, keepdims=True)
    gate_t = mine(gates, 1).reshape(micro, group, local_exp).transpose(2, 0, 1)[:, :, None, :]
    upstream_full = (upstream_low * live[:, None].astype(BF16)).reshape(micro, group, width)
    hn = normed_ffn.reshape(micro, group, width)

    outs, weight_grads = [], []
    for e in range(local_exp):
        xe, dyr, hg, dgp, dup, ye, dxe, tok = expert_pass(
            counts[e], place_t[e], gate_t[e], hn, upstream_full, big[e], capacity, shared
        )
        grad = expert_grads(xe, dgp, dup, hg, dyr, shared)
        hn, upstream_full, ye, dxe, tok, grad = lax.optimization_barrier(
            (hn, upstream_full, ye, dxe, tok, grad)
        )
        outs.append((ye, dxe, tok))
        weight_grads.append(lax.psum_scatter(grad, "row", scatter_dimension=1, tiled=True))

    def tie(value, e):
        value, weight_grads[e] = lax.optimization_barrier((value, weight_grads[e]))
        return value

    row = lax.axis_index("row")
    back_sum, tok = scatter_col(
        combine(place, [o[1] for o in outs]), 2, 1, (jnp.stack([o[2] for o in outs]),)
    )
    back_sum = tie(back_sum, 0)
    tok = tok.reshape((experts,) + tok.shape[2:])
    hidden_part = tokens.astype(F32) + nn(attended_full, mine(full_o, 1))
    gate_dots = tok[:, :, 0].reshape(experts, rows).T
    hidden_part = mine(hidden, 1)

    selected = gates * (gate_dots - jnp.sum(gates * gate_dots, -1, keepdims=True))
    logit_grad = selected.astype(BF16)
    router_part = mine(full_r, 0)
    normed_grad = back_sum + nt(logit_grad, router_part)
    grad_router = tn(mine(normed_ffn, 1), logit_grad)
    scaled_two = hidden_part * scale_two
    grad_gain_ffn = jnp.sum(normed_grad * scaled_two, 0)
    dot_two = jnp.sum(tok[:, :, 1].reshape(experts, rows), 0) + jnp.sum(
        logit_grad.astype(F32) * logits, 1
    )
    upstream_part = cotangent.astype(F32) * live[:, None]
    hidden_grad = (
        upstream_part
        + scale_two * (normed_grad * gain_ffn)
        - hidden_part * scale_two**2 * dot_two[:, None] / width
    )

    branch_grad = hidden_grad.astype(BF16)
    (attended_grad,) = scatter_col(nt(branch_grad, mine(full_o, 1)).astype(BF16), 3)
    attended_grad = attended_grad.astype(BF16).reshape(batch)
    grad_out = tn(attended_full, branch_grad)
    scores_again = scores_of()
    probs = jnp.exp(scores_again - log_total)
    probs_again = probs.astype(BF16)
    probs_grad = jnp.einsum(
        "gqhd,gkhd->ghqk", attended_grad, values_low, preferred_element_type=F32
    )
    values_grad = jnp.einsum(
        "ghqk,gqhd->gkhd", probs_again, attended_grad, preferred_element_type=F32
    )
    score_grad = (probs * (probs_grad - jnp.sum(probs_grad * probs, -1, keepdims=True))).astype(
        BF16
    )
    query_grad_rot = (
        jnp.einsum("ghqk,gkhd->gqhd", score_grad, keys_low, preferred_element_type=F32) * scale
    )
    key_grad_rot = (
        jnp.einsum("ghqk,gqhd->gkhd", score_grad, queries, preferred_element_type=F32) * scale
    )
    query_grad, gain_query_part = query_pull(query_grad_rot.reshape(shape))
    key_grad, gain_key_part = key_pull(key_grad_rot.reshape(shape))
    flat = (rows, local_heads * head)
    heads_grad = [
        v.reshape(flat).astype(BF16) for v in (query_grad, key_grad, values_grad)
    ]
    back_heads = sum(nt(g, w_heads[j]) for j, g in enumerate(heads_grad))
    pre = (query_pre, key_pre, value_pre)
    dot_part = sum(jnp.sum(g.astype(F32) * p, -1) for g, p in zip(heads_grad, pre))
    sums = jnp.concatenate([dot_part, gain_query_part, gain_key_part])
    sums = jnp.pad(sums, (0, -sums.shape[0] % 1024)).reshape(-1, 128)
    heads_weights = jnp.stack([tn(normed, g) for g in heads_grad]).astype(BF16)
    back_heads, mixed_slots = lax.optimization_barrier(
        (back_heads.astype(BF16), [o[0] for o in outs])
    )
    mixed_sum, heads_terms, out_terms = scatter_col(
        combine(place, mixed_slots), 4, 3, (heads_weights, grad_out.astype(BF16))
    )
    mixed = (hidden_part + mixed_sum).astype(BF16)
    back_heads, mixed = lax.optimization_barrier((back_heads, mixed))
    normed_back, sums, heads_terms, out_terms = scatter_col(
        tie(back_heads, 1), 5, 2, (sums, heads_terms, out_terms)
    )
    sums = jnp.sum(sums, 0).reshape(-1)
    dot_one = sums[:rows]
    gain_query_sum, gain_key_sum = sums[rows : rows + head], sums[rows + head : rows + 2 * head]
    scale_one_part = scale_one
    inputs_part = tokens.astype(F32)
    grad_gain_attn = jnp.sum(normed_back * inputs_part * scale_one_part, 0)
    input_grad = (
        hidden_grad
        + scale_one_part * (normed_back * gain_attn)
        - inputs_part * scale_one_part**2 * dot_one[:, None] / width
    )

    held = ()
    for e, grad in enumerate(weight_grads):
        held = unpack(grad, held, e, local_exp)
    grad_gate, grad_up, grad_down = held

    heads_terms = jnp.sum(heads_terms.astype(F32), 0)
    heads_sum = jnp.concatenate([heads_terms[j] for j in range(heads_terms.shape[0])], -1)
    grad_query, grad_key, grad_value = heads_sum[0], heads_sum[1], heads_sum[2]
    out_terms = jnp.sum(out_terms.astype(F32), 0)
    grad_out = jnp.concatenate([out_terms[j] for j in range(out_terms.shape[0])], -1)
    smalls = [
        grad_gain_attn,
        grad_gain_ffn,
        gain_query_sum,
        gain_key_sum,
        grad_router.T.reshape(-1),
    ]
    total = lax.psum(jnp.concatenate(smalls).reshape(-1, 128), "row").reshape(-1)
    grad_gain_attn, grad_gain_ffn = total[:part], total[part : 2 * part]
    grad_gain_query = total[2 * part : 2 * part + head]
    grad_gain_key = total[2 * part + head : 2 * part + 2 * head]
    grad_router = lax.dynamic_slice_in_dim(
        total[2 * part + 2 * head :].reshape(experts, part), row * (experts // n_row), experts // n_row, 0
    ).T
    return (
        mixed,
        input_grad,
        grad_gain_attn,
        grad_gain_ffn,
        grad_gain_query,
        grad_gain_key,
        grad_query,
        grad_key,
        grad_value,
        grad_out,
        grad_router,
        grad_gate,
        grad_up,
        grad_down,
    )


def solution(mesh):
    placed = (
        P("row", "col"),
        P("col"),
        P("col"),
        P(),
        P(),
        P("col", "row"),
        P("col", "row"),
        P("col", "row"),
        P("col", "row"),
        P("col", "row"),
        P("col", "row", None),
        P("col", "row", None),
        P("col", None, "row"),
        P("row", None),
        P("row", None),
        P("row", "col"),
    )
    return jax.shard_map(
        shards,
        mesh=mesh,
        in_specs=placed,
        out_specs=(
            P("row", "col"),
            P("row", "col"),
            P("col"),
            P("col"),
            P(),
            P(),
            P("col", "row"),
            P("col", "row"),
            P("col", "row"),
            P("col", "row"),
            P("col", "row"),
            P("col", "row", None),
            P("col", "row", None),
            P("col", None, "row"),
        ),
        check_vma=False,
    )
```

```python
import functools
import math

import jax
import jax.numpy as jnp
from jax import lax
from jax.experimental import pallas as pl
from jax.experimental.pallas import tpu as pltpu
from jax.sharding import PartitionSpec as P

EPSILON = 1e-06
ROPE_BASE = 10000.0
MASKED = -1e30
F32 = jnp.float32
BF16 = jnp.bfloat16
VMEM_LIMIT = 60 * 1024 * 1024
MESH = pl.DeviceIdType.MESH
ANY = pl.BlockSpec(memory_space=pl.ANY)


def inverse_rms(values):
    return lax.rsqrt(jnp.mean(values * values, -1, keepdims=True) + EPSILON)


def rope_tables(position, head):
    half = head // 2
    inverse = jnp.exp(-math.log(ROPE_BASE) * 2.0 / head * jnp.arange(half, dtype=F32))
    angles = position[:, None] * inverse[None, :]
    return jnp.cos(angles)[:, None, :], jnp.sin(angles)[:, None, :]


def rotary(values, cosine, sine):
    half = values.shape[-1] // 2
    first = values[..., :half]
    second = values[..., half:]
    return jnp.concatenate([first * cosine - second * sine, second * cosine + first * sine], -1)


def layout(lengths_row, group):
    ends = jnp.cumsum(lengths_row)
    starts = ends - lengths_row
    row_index = jnp.arange(group, dtype=jnp.int32)
    segment = jnp.sum((row_index[:, None] >= ends[None, :]).astype(jnp.int32), 1)
    member = segment[:, None] == jnp.arange(lengths_row.shape[0], dtype=jnp.int32)[None, :]
    position = (row_index - jnp.sum(jnp.where(member, starts[None, :], 0), 1)).astype(F32)
    live = (segment < lengths_row.shape[0] - 1).astype(F32)
    return (segment, position, live)


def nn(a, b):
    return lax.dot_general(a, b, (((1,), (0,)), ((), ())), preferred_element_type=F32)


def nt(a, b):
    return lax.dot_general(a, b, (((1,), (1,)), ((), ())), preferred_element_type=F32)


def tn(a, b):
    return lax.dot_general(a, b, (((0,), (0,)), ((), ())), preferred_element_type=F32)


def expert_body(shared, counts, place, gate, hn, dy, w, xe_o, dyr_o, hg_o, dgp_o, dup_o, ye_o, dxe_o, tok_o):
    g, i = pl.program_id(0), pl.program_id(1)
    rows = xe_o.shape[1]
    width, ff = w.shape[1:]
    base = i * rows

    @pl.when(i == 0)
    def _():
        tok_o[...] = jnp.zeros_like(tok_o)

    @pl.when(counts[g] <= base)
    def _():
        for ref in (xe_o, dyr_o, hg_o, dgp_o, dup_o, ye_o, dxe_o):
            ref[...] = jnp.zeros_like(ref)

    @pl.when(counts[g] > base)
    def _():
        slot = lax.broadcasted_iota(jnp.int32, (rows, place.shape[2]), 0) + base
        hit = slot == place[0]
        pick = jnp.where(hit, 1.0, 0.0).astype(BF16)
        weight = jnp.sum(jnp.where(hit, gate[0], 0.0), 1, keepdims=True)
        xe = nn(pick, hn[0]).astype(BF16)
        xe_o[0] = xe
        gp = nn(xe, w[0])
        up = nn(xe, w[1])
        sig = jax.nn.sigmoid(gp)
        silu = gp * sig
        hid = silu * up
        hg = (hid * weight).astype(BF16)
        hg_o[0] = hg
        dyr = nn(pick, dy[0]).astype(BF16)
        dyr_o[0] = dyr
        parts = []
        for r in range(width // shared):
            at = r * shared
            total = None
            for b in range(ff // shared):
                low = b * shared
                term = nn(hg[:, low : low + shared], w[2, at : at + shared, low : low + shared])
                total = term if total is None else total + term
            ye_o[0, :, at : at + shared] = total.astype(BF16)
        for b in range(ff // shared):
            low = b * shared
            total = None
            for r in range(width // shared):
                at = r * shared
                term = nt(dyr[:, at : at + shared], w[2, at : at + shared, low : low + shared])
                total = term if total is None else total + term
            parts.append(total)
        back = jnp.concatenate(parts, 1)
        dgate = jnp.sum(back * hid, 1, keepdims=True)
        dhid = back * weight
        dgp = (dhid * up * sig * (1.0 + gp * (1.0 - sig))).astype(BF16)
        dup = (dhid * silu).astype(BF16)
        dgp_o[0] = dgp
        dup_o[0] = dup
        dots = jnp.sum(dgp.astype(F32) * gp + dup.astype(F32) * up, 1, keepdims=True)
        dxe_o[0] = (nt(dgp, w[0]) + nt(dup, w[1])).astype(BF16)
        tok_o[0, 0:1, :] += jnp.sum(jnp.where(hit, dgate, 0.0), 0, keepdims=True)
        tok_o[0, 1:2, :] += jnp.sum(jnp.where(hit, dots, 0.0), 0, keepdims=True)


def expert_pass(counts, place, gate, hn, dy, w, capacity, shared):
    _, width, ff = w.shape
    micro, group, _ = hn.shape
    rows = min(256, capacity)
    blocks = capacity // rows
    tall = lambda g, i, c: (g, i, 0)
    line = lambda g, i, c: (g, 0, 0)
    slots = lambda n: jax.ShapeDtypeStruct((micro, capacity, n), BF16)
    sizes = (width, width, ff, ff, ff, width, width)
    flops = 2 * micro * capacity * width * (6 * ff + 2 * group)
    return pl.pallas_call(
        functools.partial(expert_body, shared),
        grid_spec=pltpu.PrefetchScalarGridSpec(
            num_scalar_prefetch=1,
            grid=(micro, blocks),
            in_specs=[
                pl.BlockSpec((1, 1, group), line),
                pl.BlockSpec((1, 1, group), line),
                pl.BlockSpec((1, group, width), line),
                pl.BlockSpec((1, group, width), line),
                pl.BlockSpec((3, width, ff), lambda g, i, c: (0, 0, 0), pipeline_mode=pl.Buffered(1)),
            ],
            out_specs=[pl.BlockSpec((1, rows, n), tall) for n in sizes]
            + [pl.BlockSpec((1, 2, group), line)],
        ),
        out_shape=[slots(n) for n in sizes] + [jax.ShapeDtypeStruct((micro, 2, group), F32)],
        compiler_params=pltpu.CompilerParams(vmem_limit_bytes=VMEM_LIMIT),
        cost_estimate=pl.CostEstimate(
            flops=flops, bytes_accessed=40 << 20, transcendentals=micro * capacity * ff
        ),
        name="expert_pass",
    )(counts, place, gate, hn, dy, w)


def grads_body(xe, dgp, dup, hg, dyr, out):
    part = xe[...]
    shared = part.shape[1]
    out[0] = tn(part, dgp[...]).astype(BF16)
    out[1] = tn(part, dup[...]).astype(BF16)
    back = dyr[...]
    for b in range(hg.shape[1] // shared):
        low = b * shared
        out[2, :, low : low + shared] = tn(hg[:, low : low + shared], back).astype(BF16)


def expert_grads(xe, dgp, dup, hg, dyr, shared):
    micro, capacity, width = xe.shape
    ff = dgp.shape[2]
    rows = micro * capacity
    xe, dyr = (a.reshape(rows, width) for a in (xe, dyr))
    dgp, dup, hg = (a.reshape(rows, ff) for a in (dgp, dup, hg))
    thin = pl.BlockSpec((rows, shared), lambda r: (0, r))
    whole = pl.BlockSpec((rows, ff), lambda r: (0, 0))
    return pl.pallas_call(
        grads_body,
        grid=(width // shared,),
        in_specs=[thin, whole, whole, whole, thin],
        out_specs=pl.BlockSpec((3, shared, ff), lambda r: (0, r, 0)),
        out_shape=jax.ShapeDtypeStruct((3, width, ff), BF16),
        compiler_params=pltpu.CompilerParams(vmem_limit_bytes=VMEM_LIMIT),
        cost_estimate=pl.CostEstimate(
            flops=6 * rows * width * ff, bytes_accessed=26 << 20, transcendentals=0
        ),
        name="expert_grads",
    )(xe, dgp, dup, hg, dyr)


def pack_body(wg, wu, wd, out):
    shared = out.shape[1]
    out[0] = wg[0]
    out[1] = wu[0]
    for b in range(out.shape[2] // shared):
        low = b * shared
        out[2, :, low : low + shared] = wd[0, low : low + shared, :]


def pack(wg, wu, wd, e):
    _, shared, ff = wg.shape
    block = pl.BlockSpec((1, shared, ff), lambda i: (e, 0, 0))
    return pl.pallas_call(
        pack_body,
        grid=(1,),
        in_specs=[block, block, pl.BlockSpec((1, ff, shared), lambda i: (e, 0, 0))],
        out_specs=pl.BlockSpec((3, shared, ff), lambda i: (0, 0, 0)),
        out_shape=jax.ShapeDtypeStruct((3, shared, ff), BF16),
        cost_estimate=pl.CostEstimate(
            flops=0, bytes_accessed=12 * shared * ff, transcendentals=0
        ),
        name="pack",
    )(wg, wu, wd)


def unpack_body(x, *refs):
    gg, gu, gd = refs[-3:]
    shared = x.shape[1]
    gg[0] = x[0].astype(F32)
    gu[0] = x[1].astype(F32)
    for b in range(x.shape[2] // shared):
        low = b * shared
        gd[0, low : low + shared, :] = x[2, :, low : low + shared].astype(F32)


def unpack(x, held, e, experts):
    _, shared, ff = x.shape
    block = pl.BlockSpec((1, shared, ff), lambda i: (e, 0, 0))
    held = list(held)
    return pl.pallas_call(
        unpack_body,
        grid=(1,),
        in_specs=[pl.BlockSpec((3, shared, ff), lambda i: (0, 0, 0))] + [ANY] * len(held),
        out_specs=[block, block, pl.BlockSpec((1, ff, shared), lambda i: (e, 0, 0))],
        out_shape=[
            jax.ShapeDtypeStruct((experts, shared, ff), F32),
            jax.ShapeDtypeStruct((experts, shared, ff), F32),
            jax.ShapeDtypeStruct((experts, ff, shared), F32),
        ],
        input_output_aliases={1 + j: j for j in range(len(held))},
        compiler_params=pltpu.CompilerParams(vmem_limit_bytes=VMEM_LIMIT),
        cost_estimate=pl.CostEstimate(
            flops=0, bytes_accessed=18 * shared * ff, transcendentals=0
        ),
        name="unpack",
    )(x, *held)


def places():
    row, col = lax.axis_index("row"), lax.axis_index("col")
    n_row, n_col = lax.axis_size("row"), lax.axis_size("col")
    return row, col, n_row, n_col


def remote(src, dst, send_sem, recv_sem, where):
    return pltpu.make_async_remote_copy(
        src_ref=src,
        dst_ref=dst,
        send_sem=send_sem,
        recv_sem=recv_sem,
        device_id=where,
        device_id_type=MESH,
    )


def shake(sources, targets):
    barrier = pltpu.get_barrier_semaphore()
    for ok, where in sources:
        if ok is True:
            pl.semaphore_signal(barrier, inc=1, device_id=where, device_id_type=MESH)
        else:

            @pl.when(ok)
            def _():
                pl.semaphore_signal(barrier, inc=1, device_id=where, device_id_type=MESH)

    count = 0
    for ok in targets:
        count = count + (1 if ok is True else jnp.where(ok, 1, 0))
    pl.semaphore_wait(barrier, count)


def line_peers():
    row, col, n_row, n_col = places()
    pair, core = col // 2, col % 2
    return [
        (True, (row, pair * 2 + 1 - core)),
        (pair > 0, (row, (pair - 1) * 2 + core)),
        (pair < n_col // 2 - 1, (row, (pair + 1) * 2 + core)),
    ]


def row_peers():
    row, col, n_row, n_col = places()
    return [(True, ((row + k) % n_row, col)) for k in range(1, n_row)]


def col_slice(ref, index, size):
    return ref.at[..., pl.ds(pl.multiple_of(index * size, size), size)]


def line_gather(axes, ins, outs, sems):
    own_sem, right_s, right_r, left_s, left_r, side_s, side_r = sems
    n = len(ins)
    row, col, n_row, n_col = places()
    pairs, pair, core = n_col // 2, col // 2, col % 2

    def at(pair_index, core_index):
        return (row, pair_index * 2 + core_index)

    def block(j, source):
        size = ins[j].shape[axes[j]]
        if axes[j] == 0:
            return outs[j].at[pl.ds(pl.multiple_of(source * size, size), size)]
        return col_slice(outs[j], source, size)

    def right(j, s):
        source = (pair - s) * 2 + core
        src = ins[j] if s == 0 else block(j, source)
        return remote(src, block(j, source), right_s.at[j, s], right_r.at[j, s], at(pair + 1, core))

    def left(j, s):
        source = (pair + s) * 2 + core
        src = ins[j] if s == 0 else block(j, source)
        return remote(src, block(j, source), left_s.at[j, s], left_r.at[j, s], at(pair - 1, core))

    def side(j, source_pair, first=False):
        source = source_pair * 2 + core
        src = ins[j] if first else block(j, source)
        return remote(
            src,
            block(j, source),
            side_s.at[j, source_pair],
            side_r.at[j, source_pair],
            at(pair, 1 - core),
        )

    def arrived(j, recvs, slot, source):
        remote(
            ins[j], block(j, source), recvs.at[j, slot], recvs.at[j, slot], at(pair, 1 - core)
        ).wait_recv()

    def own(j):
        return pltpu.make_async_copy(ins[j], block(j, col), own_sem.at[j])

    def begin():
        for j in range(n):

            @pl.when(pair < pairs - 1)
            def _():
                right(j, 0).start()

            @pl.when(pair > 0)
            def _():
                left(j, 0).start()

        for j in range(n):
            side(j, pair, True).start()
            own(j).start()

    def middle():
        for s in range(1, pairs):
            for j in range(n):

                @pl.when(pair >= s)
                def _():
                    arrived(j, right_r, s - 1, (pair - s) * 2 + core)

                    @pl.when(pair < pairs - 1)
                    def _():
                        right(j, s).start()

                    side(j, pair - s).start()

                @pl.when(pair + s < pairs)
                def _():
                    arrived(j, left_r, s - 1, (pair + s) * 2 + core)

                    @pl.when(pair > 0)
                    def _():
                        left(j, s).start()

                    side(j, pair + s).start()

    def end():
        for j in range(n):
            own(j).wait()
            for p in range(pairs):
                side(j, p).wait_send()
                arrived(j, side_r, p, p * 2 + 1 - core)
            for s in range(pairs):

                @pl.when((pair >= s) & (pair < pairs - 1))
                def _():
                    right(j, s).wait_send()

                @pl.when((pair + s < pairs) & (pair > 0))
                def _():
                    left(j, s).wait_send()

    return begin, middle, end


def line_sems(n, pairs):
    dma = pltpu.SemaphoreType.DMA
    return [dma((n,))] + [dma((n, pairs))] * 6


def front_body(tokens, gains, wq, wk, wv, wo, wr, *refs):
    x_o, gains_o, wh_o, wo_o, wr_o = refs[:5]
    wide = refs[5:8]
    line, (heads_s, heads_r, row_s, row_r, own_s) = refs[8:15], refs[15:]
    row, col, n_row, n_col = places()
    head = wh_o.shape[2]
    part = wq.shape[0]
    begin, middle, end = line_gather((1, 1), [tokens, gains], [x_o, gains_o], line)
    small = [(wq, wide[0]), (wk, wide[1]), (wv, wide[2]), (wo, wo_o), (wr, wr_o)]

    def small_dst(k, source):
        src, dst = small[k]
        if k < 4:
            return col_slice(dst, source, src.shape[1])
        return dst.at[pl.ds(pl.multiple_of(source * src.shape[0], src.shape[0]), src.shape[0]), :]

    def small_copy(k, step):
        return remote(
            small[k][0],
            small_dst(k, row),
            row_s.at[k, step],
            row_r.at[k, step],
            ((row + step) % n_row, col),
        )

    def small_come(k, step):
        source = (row + n_row - step) % n_row
        return remote(
            small[k][0], small_dst(k, source), row_s.at[k, step], row_r.at[k, step], (source, col)
        )

    def small_own(k):
        return pltpu.make_async_copy(small[k][0], small_dst(k, row), own_s.at[k])

    def heads_dst(m, source):
        return wh_o.at[m, pl.ds(pl.multiple_of(source * part, part), part), :]

    def heads(m, step):
        where = (col + step) % n_col
        return remote(
            col_slice(wide[m], where, head),
            heads_dst(m, col),
            heads_s.at[m, step],
            heads_r.at[m, step],
            (row, where),
        )

    def heads_come(m, step):
        source = (col + n_col - step) % n_col
        return remote(
            heads_dst(m, source),
            heads_dst(m, source),
            heads_s.at[m, step],
            heads_r.at[m, step],
            (row, source),
        )

    def heads_own(m):
        return pltpu.make_async_copy(
            col_slice(wide[m], col, head), heads_dst(m, col), own_s.at[5 + m]
        )

    peers = [(True, (row, (col + k) % n_col)) for k in range(1, n_col)] + row_peers()
    shake(peers, [ok for ok, _ in peers])
    for k in range(5):
        for step in range(1, n_row):
            small_copy(k, step).start()
        small_own(k).start()
    begin()
    for k in range(3):
        small_own(k).wait()
        for step in range(1, n_row):
            small_come(k, step).wait_recv()
    for m in range(3):
        heads_own(m).start()
        for step in range(1, n_col):
            heads(m, step).start()
    middle()
    end()
    for k in range(5):
        if k >= 3:
            small_own(k).wait()
        for step in range(1, n_row):
            small_copy(k, step).wait_send()
            if k >= 3:
                small_come(k, step).wait_recv()
    for m in range(3):
        heads_own(m).wait()
        for step in range(1, n_col):
            heads(m, step).wait_send()
            heads_come(m, step).wait_recv()


def front(tokens, gains, wq, wk, wv, wo, wr, head, ident):
    n_row, n_col = lax.axis_size("row"), lax.axis_size("col")
    rows, part = tokens.shape
    width = part * n_col
    dma = pltpu.SemaphoreType.DMA
    shapes = [
        ((rows, width), BF16),
        ((gains.shape[0], width), F32),
        ((3, width, head), BF16),
        ((wo.shape[0], wo.shape[1] * n_row), BF16),
        ((wr.shape[0] * n_row, part), BF16),
    ] + [((part, wq.shape[1] * n_row), BF16)] * 3
    return pl.pallas_call(
        front_body,
        in_specs=[ANY] * 7,
        out_specs=[ANY] * 8,
        out_shape=[jax.ShapeDtypeStruct(s, t) for s, t in shapes],
        scratch_shapes=line_sems(2, n_col // 2)
        + [
            dma((3, n_col)),
            dma((3, n_col)),
            dma((5, n_row)),
            dma((5, n_row)),
            dma((8,)),
        ],
        compiler_params=pltpu.CompilerParams(collective_id=ident, has_side_effects=True),
        cost_estimate=pl.CostEstimate(
            flops=0, bytes_accessed=rows * width * 32, transcendentals=0
        ),
        name="front",
    )(tokens, gains, wq, wk, wv, wo, wr)[:5]


def middle_body(axes, *refs):
    n = len(axes)
    begin, middle, end = line_gather(axes, refs[:n], refs[n : 2 * n], refs[2 * n :])
    sources = line_peers()
    shake(sources, [ok for ok, _ in sources])
    begin()
    middle()
    end()


def middle_gather(arrays, axes, ident):
    n_col, n = lax.axis_size("col"), len(arrays)
    shapes = [
        tuple(d * n_col if at == axis else d for at, d in enumerate(a.shape))
        for a, axis in zip(arrays, axes)
    ]
    return pl.pallas_call(
        functools.partial(middle_body, axes),
        in_specs=[ANY] * n,
        out_specs=[ANY] * n,
        out_shape=[jax.ShapeDtypeStruct(s, a.dtype) for s, a in zip(shapes, arrays)],
        scratch_shapes=line_sems(n, n_col // 2),
        compiler_params=pltpu.CompilerParams(collective_id=ident, has_side_effects=True),
        cost_estimate=pl.CostEstimate(
            flops=0, bytes_accessed=sum(math.prod(s) for s in shapes) * 32, transcendentals=0
        ),
        name="middle_gather",
    )(*arrays)


def scatter_body(part, stage, local, *refs):
    n_in = (1, 2, 4, 3)[stage]
    n_out = (1, 2, 4, 3)[stage]
    if local:
        place, slots, refs = refs[0], refs[1 : 1 + local], refs[local:]
    x, ins = refs[0], refs[1:n_in]
    out, outs = refs[n_in], refs[n_in + 1 : n_in + n_out]
    rest = refs[n_in + n_out :]
    acc, side, from_left, from_right, load, side_s, side_r = rest[:7]
    right_s, right_r, left_s, left_r = rest[7:11]
    if local:
        give, chosen, held, held_s = rest[11:15]
        rest = rest[4:]
    row, col, n_row, n_col = places()
    pairs, pair, core = n_col // 2, col // 2, col % 2
    rows = out.shape[0]
    cuts = load.shape[1]
    height = rows // cuts
    tile = min(256, height)

    def at(pair_index, core_index):
        return (row, pair_index * 2 + core_index)

    def block(owner, q):
        return x.at[
            pl.ds(q * height, height), pl.ds(pl.multiple_of(owner * part, part), part)
        ]

    def cut(ref, d, q):
        return ref.at[d, pl.ds(q * height, height)]

    def fetch(d, q):
        return pltpu.make_async_copy(block(d * 2 + core, q), cut(acc, d, q), load.at[d, q])

    def across(d, q):
        return remote(
            cut(give, d, q) if local else block(d * 2 + 1 - core, q),
            cut(side, d, q),
            side_s.at[d, q],
            side_r.at[d, q],
            at(pair, 1 - core),
        )

    def right(d, q):
        return remote(
            cut(acc, d, q),
            cut(from_left, d, q),
            right_s.at[d, q],
            right_r.at[d, q],
            at(pair + 1, core),
        )

    def left(d, q):
        return remote(
            cut(acc, d, q),
            cut(from_right, d, q),
            left_s.at[d, q],
            left_r.at[d, q],
            at(pair - 1, core),
        )

    copies, arrivals, own = [], [], []
    if stage in (1, 2):
        small_s, small_r, own_s = rest[11:14]
        extra, extra_o = ins[0], outs[0]
        for k in range(1, n_col):
            where, source = (col + k) % n_col, (col + n_col - k) % n_col
            copies.append(
                remote(extra, extra_o.at[col], small_s.at[k], small_r.at[k], (row, where))
            )
            arrivals.append(
                remote(extra, extra_o.at[source], small_s.at[k], small_r.at[k], (row, where))
            )
        own.append(pltpu.make_async_copy(extra, extra_o.at[col], own_s))
    if stage == 2:
        give_s, give_r, keep_s = rest[14:]
        per = n_col // n_row
        for m in range(2):
            src, dst = ins[1 + m], outs[1 + m]

            def block_of(r):
                return src.at[pl.ds(r * per, per)]

            for step in range(1, n_row):
                where, source = (row + step) % n_row, (row + n_row - step) % n_row
                sems = (give_s.at[m, step], give_r.at[m, step])
                copies.append(remote(block_of(where), dst.at[row], *sems, (where, col)))
                arrivals.append(remote(block_of(where), dst.at[source], *sems, (where, col)))
            own.append(pltpu.make_async_copy(block_of(row), dst.at[row], keep_s.at[m]))
    if stage == 3:
        give_s, give_r, keep_s = rest[11:]
        for m in range(2):
            src, dst = ins[m], outs[m]
            size = src.shape[1 - m] // n_col

            def block_for(c):
                at_c = pl.ds(pl.multiple_of(c * size, size), size)
                return src.at[:, at_c, :] if m == 0 else src.at[at_c, :]

            for step in range(1, n_col):
                where, source = (col + step) % n_col, (col + n_col - step) % n_col
                sems = (give_s.at[m, step], give_r.at[m, step])
                copies.append(remote(block_for(where), dst.at[col], *sems, (row, where)))
                arrivals.append(remote(block_for(where), dst.at[source], *sems, (row, where)))
            own.append(pltpu.make_async_copy(block_for(col), dst.at[col], keep_s.at[m]))
    if stage:
        peers = [(True, (row, (col + k) % n_col)) for k in range(1, n_col)]
    else:
        peers = line_peers()
    if stage == 2:
        peers += row_peers()
    shake(peers, [ok for ok, _ in peers])
    order = []
    for t in range(pairs):
        for d in (pairs - 1 - t, t):
            if d not in order:
                order.append(d)
    if local:
        micro, capacity = held.shape[2], held.shape[3]
        group = chosen.shape[1]
        owners = []
        for d in order:
            owners += [d * 2 + 1 - core, d * 2 + core]

        def bring(n):
            return [
                pltpu.make_async_copy(
                    slots[e].at[:, :, pl.ds(pl.multiple_of(owners[n] * part, part), part)],
                    held.at[n % 2, e],
                    held_s.at[n % 2, e],
                )
                for e in range(local)
            ]

        def make(n, into):
            for c in bring(n):
                c.wait()
            if n + 1 < len(owners):
                for c in bring(n + 1):
                    c.start()
            steps = group // tile

            def step(i, _):
                g, at_row = i // steps, pl.multiple_of((i % steps) * tile, tile)
                total = None
                for e in range(local):
                    term = nn(
                        chosen[g, pl.ds(at_row, tile), e * capacity : (e + 1) * capacity],
                        held[n % 2, e, g],
                    )
                    total = term if total is None else total + term
                into[pl.ds(pl.multiple_of(i * tile, tile), tile), :] = total.astype(BF16)
                return 0

            lax.fori_loop(0, micro * steps, step, 0)

        def make_pair(m):
            d = order[m]
            make(2 * m, give.at[d])
            for q in range(cuts):
                across(d, q).start()
            make(2 * m + 1, acc.at[d])

        for c in bring(0):
            c.start()

        def choose(i, _):
            steps = group // tile
            g, at_row = i // steps, pl.multiple_of((i % steps) * tile, tile)
            for e in range(local):
                slot = lax.broadcasted_iota(jnp.int32, (tile, capacity), 1)
                hit = slot == place[g, pl.ds(at_row, tile), e : e + 1]
                chosen[g, pl.ds(at_row, tile), e * capacity : (e + 1) * capacity] = jnp.where(
                    hit, 1.0, 0.0
                ).astype(BF16)
            return 0

        lax.fori_loop(0, micro * (group // tile), choose, 0)
    else:
        for d in order:
            for q in range(cuts):
                across(d, q).start()
                fetch(d, q).start()
    for c in copies + own:
        c.start()

    def add(q, into, *sources):
        def step(i, _):
            lines = pl.ds(pl.multiple_of(q * height + i * tile, tile), tile)
            total = sources[0][lines, :].astype(F32)
            for ref in sources[1:]:
                total = total + ref[lines, :].astype(F32)
            into[lines, :] = total.astype(into.dtype)
            return 0

        lax.fori_loop(0, height // tile, step, 0)

    def ready(d, q):
        if not local:
            fetch(d, q).wait()
        across(d, q).wait_recv()

    def go_right(d, q):
        ready(d, q)

        @pl.when(pair > 0)
        def _():
            right(d, q).wait_recv()
            add(q, acc.at[d], acc.at[d], side.at[d], from_left.at[d])

        @pl.when(pair == 0)
        def _():
            add(q, acc.at[d], acc.at[d], side.at[d])

        right(d, q).start()

    def go_left(d, q):
        ready(d, q)

        @pl.when(pair < pairs - 1)
        def _():
            left(d, q).wait_recv()
            add(q, acc.at[d], acc.at[d], side.at[d], from_right.at[d])

        @pl.when(pair == pairs - 1)
        def _():
            add(q, acc.at[d], acc.at[d], side.at[d])

        left(d, q).start()

    if local:
        for m in range(2):
            make_pair(m)
        for q in range(cuts):

            @pl.when(pair == 0)
            def _():
                go_right(pairs - 1, q)

            @pl.when(pair == pairs - 1)
            def _():
                go_left(0, q)

        for m in range(2, pairs):
            make_pair(m)
    for t in range(pairs - 1):
        far, near = pairs - 1 - t, t
        go_far, go_near = far > pair, near < pair
        if local and t == 0:
            go_far, go_near = go_far & (pair > 0), go_near & (pair < pairs - 1)
        for q in range(cuts):

            @pl.when(go_far)
            def _():
                go_right(far, q)

            @pl.when(go_near)
            def _():
                go_left(near, q)

    for q in range(cuts):
        ready(pair, q)

        @pl.when(pair == 0)
        def _():
            left(pair, q).wait_recv()
            add(q, out, acc.at[pair], side.at[pair], from_right.at[pair])

        @pl.when(pair == pairs - 1)
        def _():
            right(pair, q).wait_recv()
            add(q, out, acc.at[pair], side.at[pair], from_left.at[pair])

        @pl.when((pair > 0) & (pair < pairs - 1))
        def _():
            left(pair, q).wait_recv()
            right(pair, q).wait_recv()
            add(q, out, acc.at[pair], side.at[pair], from_left.at[pair], from_right.at[pair])

    for d in range(pairs):
        for q in range(cuts):
            across(d, q).wait_send()

            @pl.when(pair < d)
            def _():
                right(d, q).wait_send()

            @pl.when(pair > d)
            def _():
                left(d, q).wait_send()

    for c in copies:
        c.wait_send()
    for c in arrivals:
        c.wait_recv()
    for c in own:
        c.wait()


def scatter_col(x, ident, stage=0, others=(), place=None):
    n_row, n_col = lax.axis_size("row"), lax.axis_size("col")
    pairs, per = n_col // 2, n_col // n_row
    local = 0 if place is None else len(x)
    if local:
        micro, group, _ = place.shape
        capacity = x[0].shape[1]
        rows, part = micro * group, x[0].shape[2] // n_col
    else:
        rows, part = x.shape[0], x.shape[1] // n_col
    cuts = 4 if rows % 1024 == 0 else 1
    dma = pltpu.SemaphoreType.DMA
    buffer = pltpu.VMEM((pairs, rows, part), BF16)
    scratch = [buffer] * 4 + [dma((pairs, cuts))] * 7
    if local:
        scratch += [
            buffer,
            pltpu.VMEM((micro, group, local * capacity), BF16),
            pltpu.VMEM((2, local, micro, capacity, part), BF16),
            dma((2, local)),
        ]
    out_shape = [jax.ShapeDtypeStruct((rows, part), F32)]
    if stage in (1, 2):
        extra = others[0]
        out_shape.append(jax.ShapeDtypeStruct((n_col,) + extra.shape, extra.dtype))
        scratch += [dma((n_col,)), dma((n_col,)), dma(())]
    if stage == 2:
        scratch += [dma((2, n_row)), dma((2, n_row)), dma((2,))]
        for value in others[1:]:
            out_shape.append(jax.ShapeDtypeStruct((n_row, per) + value.shape[1:], BF16))
    if stage == 3:
        heads, branch = others
        scratch += [dma((2, n_col)), dma((2, n_col)), dma((2,))]
        out_shape += [
            jax.ShapeDtypeStruct((n_col, 3, heads.shape[1] // n_col, heads.shape[2]), BF16),
            jax.ShapeDtypeStruct((n_col, branch.shape[0] // n_col, branch.shape[1]), BF16),
        ]
    first = [pl.BlockSpec(memory_space=pltpu.VMEM)] + [ANY] * local if local else [ANY]
    values = (place, *x) if local else (x,)
    return pl.pallas_call(
        functools.partial(scatter_body, part, stage, local),
        in_specs=first + [ANY] * len(others),
        out_specs=[pl.BlockSpec(memory_space=pltpu.VMEM)] + [ANY] * (len(out_shape) - 1),
        out_shape=out_shape,
        scratch_shapes=scratch,
        compiler_params=pltpu.CompilerParams(
            vmem_limit_bytes=VMEM_LIMIT, collective_id=ident, has_side_effects=True
        ),
        cost_estimate=pl.CostEstimate(
            flops=0, bytes_accessed=rows * part * n_col * 40, transcendentals=0
        ),
        name="scatter_col",
    )(*values, *others)


def shards(
    tokens,
    gain_attn,
    gain_ffn,
    gain_query,
    gain_key,
    w_query,
    w_key,
    w_value,
    w_out,
    w_router,
    w_gate,
    w_up,
    w_down,
    routes,
    lengths,
    cotangent,
):
    n_col = lax.axis_size("col")
    n_row = lax.axis_size("row")
    col = lax.axis_index("col")
    micro, spans = lengths.shape
    rows, part = tokens.shape
    group = rows // micro
    width = part * n_col
    head = gain_query.shape[0]
    local_exp = w_gate.shape[0]
    experts = local_exp * n_col
    topk = routes.shape[1]
    capacity = 2 * group * topk // experts
    local_heads = w_out.shape[0] // head
    hd = w_out.shape[0] * n_col
    scale = head ** (-0.5)

    def gather(value, axis_name, axis):
        return lax.all_gather(value, axis_name, axis=axis, tiled=True)

    def mine(value, axis):
        size = value.shape[axis] // n_col
        return lax.dynamic_slice_in_dim(value, col * size, size, axis)

    shared = w_down.shape[2]
    packed = [pack(w_gate, w_up, w_down, e) for e in range(local_exp)]
    big = [gather(p, "row", 1) for p in packed]
    inputs_low, gains, w_heads, rows_o, rows_r = front(
        tokens,
        jnp.stack([gain_attn, gain_ffn]),
        w_query,
        w_key,
        w_value,
        w_out,
        w_router.T,
        head,
        0,
    )

    segment, position, live = jax.vmap(lambda l: layout(l, group))(lengths)
    position = position.reshape(rows)
    live = live.reshape(rows)
    upstream_part = cotangent.astype(F32) * live[:, None]
    member = jnp.any(
        routes[:, None, :] == jnp.arange(experts, dtype=jnp.int32)[None, :, None], -1
    )
    member_f = member.astype(F32)
    member_loc = mine(member_f, 1).reshape(micro, group, local_exp)
    lower = (
        jnp.arange(group, dtype=jnp.int32)[:, None] > jnp.arange(group, dtype=jnp.int32)[None, :]
    ).astype(BF16)
    before = jnp.einsum("st,gte->gse", lower, member_loc.astype(BF16), preferred_element_type=F32)
    place = jnp.where(member_loc > 0, before, -1.0).astype(jnp.int32)
    counts = jnp.sum(member_loc, 1).astype(jnp.int32).T
    place_t = place.transpose(2, 0, 1)[:, :, None, :]

    inputs = inputs_low.astype(F32)
    scale_one = inverse_rms(inputs)
    normed = (inputs * scale_one * gains[0]).astype(BF16)
    all_heads = jnp.concatenate([w_heads[j] for j in range(3)], 1)
    query_pre, key_pre, value_pre = jnp.split(nn(normed, all_heads), 3, 1)
    shape = (rows, local_heads, head)
    cosine, sine = rope_tables(position, head)

    def head_norm(values, gain):
        return rotary(values * inverse_rms(values) * gain, cosine, sine)

    query_rot, query_pull = jax.vjp(head_norm, query_pre.reshape(shape), gain_query)
    key_rot, key_pull = jax.vjp(head_norm, key_pre.reshape(shape), gain_key)
    batch = (micro, group, local_heads, head)
    queries = query_rot.astype(BF16).reshape(batch)
    keys_low = key_rot.astype(BF16).reshape(batch)
    values_low = value_pre.astype(BF16).reshape(batch)
    same = (segment[:, :, None] == segment[:, None, :])[:, None]

    def scores_of():
        raw = jnp.einsum("gqhd,gkhd->ghqk", queries, keys_low, preferred_element_type=F32) * scale
        return jnp.where(same, raw, MASKED)

    scores = scores_of()
    highest = jnp.max(scores, -1, keepdims=True)
    log_total = highest + jnp.log(jnp.sum(jnp.exp(scores - highest), -1, keepdims=True))
    probs_low = jnp.exp(scores - log_total).astype(BF16)
    attended = jnp.einsum(
        "ghqk,gkhd->gqhd", probs_low, values_low, preferred_element_type=F32
    ).astype(BF16)
    attended_full, full_o, full_rt, upstream_low = middle_gather(
        [attended.reshape(rows, local_heads * head), rows_o, rows_r, upstream_part.astype(BF16)],
        (1, 0, 1, 1),
        1,
    )
    full_r = full_rt.T

    hidden = inputs + nn(attended_full, full_o)
    scale_two = inverse_rms(hidden)
    normed_ffn = (hidden * scale_two * gains[1]).astype(BF16)
    logits = nn(normed_ffn, full_r)
    peak = jnp.max(jnp.where(member, logits, -jnp.inf), -1, keepdims=True)
    raised = jnp.where(member, jnp.exp(jnp.where(member, logits - peak, 0.0)), 0.0)
    gates = raised / jnp.sum(raised, -1, keepdims=True)
    gate_t = mine(gates, 1).reshape(micro, group, local_exp).transpose(2, 0, 1)[:, :, None, :]
    upstream_full = upstream_low.reshape(micro, group, width)
    hn = normed_ffn.reshape(micro, group, width)

    outs, weight_grads = [], []
    for e in range(local_exp):
        xe, dyr, hg, dgp, dup, ye, dxe, tok = expert_pass(
            counts[e], place_t[e], gate_t[e], hn, upstream_full, big[e], capacity, shared
        )
        grad = expert_grads(xe, dgp, dup, hg, dyr, shared)
        hn, upstream_full, ye, dxe, tok, grad = lax.optimization_barrier(
            (hn, upstream_full, ye, dxe, tok, grad)
        )
        outs.append((ye, dxe, tok))
        weight_grads.append(lax.psum_scatter(grad, "row", scatter_dimension=1, tiled=True))

    def tie(value, e):
        value, weight_grads[e] = lax.optimization_barrier((value, weight_grads[e]))
        return value

    row = lax.axis_index("row")
    back_sum, tok = scatter_col(
        [o[1] for o in outs], 2, 1, (jnp.stack([o[2] for o in outs]),), place
    )
    back_sum = tie(back_sum, 0)
    tok = tok.reshape((experts,) + tok.shape[2:])
    hidden_part = tokens.astype(F32) + nn(attended_full, mine(full_o, 1))
    gate_dots = tok[:, :, 0].reshape(experts, rows).T
    hidden_part = mine(hidden, 1)

    selected = gates * (gate_dots - jnp.sum(gates * gate_dots, -1, keepdims=True))
    logit_grad = selected.astype(BF16)
    router_part = mine(full_r, 0)
    normed_grad = back_sum + nt(logit_grad, router_part)
    grad_router = tn(mine(normed_ffn, 1), logit_grad)
    scaled_two = hidden_part * scale_two
    grad_gain_ffn = jnp.sum(normed_grad * scaled_two, 0)
    dot_two = jnp.sum(tok[:, :, 1].reshape(experts, rows), 0) + jnp.sum(
        logit_grad.astype(F32) * logits, 1
    )
    hidden_grad = (
        upstream_part
        + scale_two * (normed_grad * gain_ffn)
        - hidden_part * scale_two**2 * dot_two[:, None] / width
    )

    branch_grad = hidden_grad.astype(BF16)
    (attended_grad,) = scatter_col(nt(branch_grad, mine(full_o, 1)).astype(BF16), 3)
    attended_grad = attended_grad.astype(BF16).reshape(batch)
    grad_out = tn(attended_full, branch_grad)
    scores_again = scores_of()
    probs = jnp.exp(scores_again - log_total)
    probs_again = probs.astype(BF16)
    probs_grad = jnp.einsum(
        "gqhd,gkhd->ghqk", attended_grad, values_low, preferred_element_type=F32
    )
    values_grad = jnp.einsum(
        "ghqk,gqhd->gkhd", probs_again, attended_grad, preferred_element_type=F32
    )
    score_grad = (probs * (probs_grad - jnp.sum(probs_grad * probs, -1, keepdims=True))).astype(
        BF16
    )
    query_grad_rot = (
        jnp.einsum("ghqk,gkhd->gqhd", score_grad, keys_low, preferred_element_type=F32) * scale
    )
    key_grad_rot = (
        jnp.einsum("ghqk,gqhd->gkhd", score_grad, queries, preferred_element_type=F32) * scale
    )
    query_grad, gain_query_part = query_pull(query_grad_rot.reshape(shape))
    key_grad, gain_key_part = key_pull(key_grad_rot.reshape(shape))
    flat = (rows, local_heads * head)
    heads_grad = [
        v.reshape(flat).astype(BF16) for v in (query_grad, key_grad, values_grad)
    ]
    all_grads = jnp.concatenate(heads_grad, 1)
    back_heads = nt(all_grads, all_heads)
    pre = (query_pre, key_pre, value_pre)
    dot_part = sum(jnp.sum(g.astype(F32) * p, -1) for g, p in zip(heads_grad, pre))
    sums = jnp.concatenate([dot_part, gain_query_part, gain_key_part])
    sums = jnp.pad(sums, (0, -sums.shape[0] % 1024)).reshape(-1, 128)
    heads_weights = tn(normed, all_grads).astype(BF16)
    heads_weights = jnp.stack(jnp.split(heads_weights, 3, 1))
    back_heads, mixed_slots = lax.optimization_barrier(
        (back_heads.astype(BF16), [o[0] for o in outs])
    )
    mixed_sum, heads_terms, out_terms = scatter_col(
        mixed_slots, 4, 3, (heads_weights, grad_out.astype(BF16)), place
    )
    mixed = (hidden_part + mixed_sum).astype(BF16)
    back_heads, mixed = lax.optimization_barrier((back_heads, mixed))
    normed_back, sums, heads_terms, out_terms = scatter_col(
        tie(back_heads, 1), 5, 2, (sums, heads_terms, out_terms)
    )
    sums = jnp.sum(sums, 0).reshape(-1)
    dot_one = sums[:rows]
    gain_query_sum, gain_key_sum = sums[rows : rows + head], sums[rows + head : rows + 2 * head]
    scale_one_part = scale_one
    inputs_part = tokens.astype(F32)
    grad_gain_attn = jnp.sum(normed_back * inputs_part * scale_one_part, 0)
    input_grad = (
        hidden_grad
        + scale_one_part * (normed_back * gain_attn)
        - inputs_part * scale_one_part**2 * dot_one[:, None] / width
    )

    held = ()
    for e, grad in enumerate(weight_grads):
        held = unpack(grad, held, e, local_exp)
    grad_gate, grad_up, grad_down = held

    heads_terms = jnp.sum(heads_terms.astype(F32), 0)
    heads_sum = jnp.concatenate([heads_terms[j] for j in range(heads_terms.shape[0])], -1)
    grad_query, grad_key, grad_value = heads_sum[0], heads_sum[1], heads_sum[2]
    out_terms = jnp.sum(out_terms.astype(F32), 0)
    grad_out = jnp.concatenate([out_terms[j] for j in range(out_terms.shape[0])], -1)
    smalls = [
        grad_gain_attn,
        grad_gain_ffn,
        gain_query_sum,
        gain_key_sum,
        grad_router.T.reshape(-1),
    ]
    total = lax.psum(jnp.concatenate(smalls).reshape(-1, 128), "row").reshape(-1)
    grad_gain_attn, grad_gain_ffn = total[:part], total[part : 2 * part]
    grad_gain_query = total[2 * part : 2 * part + head]
    grad_gain_key = total[2 * part + head : 2 * part + 2 * head]
    grad_router = lax.dynamic_slice_in_dim(
        total[2 * part + 2 * head :].reshape(experts, part), row * (experts // n_row), experts // n_row, 0
    ).T
    return (
        mixed,
        input_grad,
        grad_gain_attn,
        grad_gain_ffn,
        grad_gain_query,
        grad_gain_key,
        grad_query,
        grad_key,
        grad_value,
        grad_out,
        grad_router,
        grad_gate,
        grad_up,
        grad_down,
    )


def solution(mesh):
    placed = (
        P("row", "col"),
        P("col"),
        P("col"),
        P(),
        P(),
        P("col", "row"),
        P("col", "row"),
        P("col", "row"),
        P("col", "row"),
        P("col", "row"),
        P("col", "row", None),
        P("col", "row", None),
        P("col", None, "row"),
        P("row", None),
        P("row", None),
        P("row", "col"),
    )
    return jax.shard_map(
        shards,
        mesh=mesh,
        in_specs=placed,
        out_specs=(
            P("row", "col"),
            P("row", "col"),
            P("col"),
            P("col"),
            P(),
            P(),
            P("col", "row"),
            P("col", "row"),
            P("col", "row"),
            P("col", "row"),
            P("col", "row"),
            P("col", "row", None),
            P("col", "row", None),
            P("col", None, "row"),
        ),
        check_vma=False,
    )
```

```python
import functools
import math

import jax
import jax.numpy as jnp
from jax import lax
from jax.experimental import pallas as pl
from jax.experimental.pallas import tpu as pltpu
from jax.sharding import PartitionSpec as P

EPSILON = 1e-06
ROPE_BASE = 10000.0
MASKED = -1e30
F32 = jnp.float32
BF16 = jnp.bfloat16
VMEM_LIMIT = 60 * 1024 * 1024
MESH = pl.DeviceIdType.MESH
ANY = pl.BlockSpec(memory_space=pl.ANY)


def inverse_rms(values):
    return lax.rsqrt(jnp.mean(values * values, -1, keepdims=True) + EPSILON)


def rope_tables(position, head):
    half = head // 2
    inverse = jnp.exp(-math.log(ROPE_BASE) * 2.0 / head * jnp.arange(half, dtype=F32))
    angles = position[:, None] * inverse[None, :]
    return jnp.cos(angles)[:, None, :], jnp.sin(angles)[:, None, :]


def rotary(values, cosine, sine):
    half = values.shape[-1] // 2
    first = values[..., :half]
    second = values[..., half:]
    return jnp.concatenate([first * cosine - second * sine, second * cosine + first * sine], -1)


def layout(lengths_row, group):
    ends = jnp.cumsum(lengths_row)
    starts = ends - lengths_row
    row_index = jnp.arange(group, dtype=jnp.int32)
    segment = jnp.sum((row_index[:, None] >= ends[None, :]).astype(jnp.int32), 1)
    member = segment[:, None] == jnp.arange(lengths_row.shape[0], dtype=jnp.int32)[None, :]
    position = (row_index - jnp.sum(jnp.where(member, starts[None, :], 0), 1)).astype(F32)
    live = (segment < lengths_row.shape[0] - 1).astype(F32)
    return (segment, position, live)


def nn(a, b):
    return lax.dot_general(a, b, (((1,), (0,)), ((), ())), preferred_element_type=F32)


def nt(a, b):
    return lax.dot_general(a, b, (((1,), (1,)), ((), ())), preferred_element_type=F32)


def tn(a, b):
    return lax.dot_general(a, b, (((0,), (0,)), ((), ())), preferred_element_type=F32)


def expert_body(shared, counts, place, gate, hn, dy, w, xe_o, dyr_o, hg_o, dgp_o, dup_o, ye_o, dxe_o, tok_o):
    g = pl.program_id(0)
    full = xe_o.shape[1]
    half = full // 2
    width, ff = w.shape[2:]

    def clear(low):
        for ref in (xe_o, dyr_o, hg_o, dgp_o, dup_o, ye_o, dxe_o):
            ref[0, low:] = jnp.zeros((full - low, ref.shape[2]), BF16)

    def run(rows):
        slot = lax.broadcasted_iota(jnp.int32, (rows, place.shape[2]), 0)
        hit = slot == place[0]
        pick = jnp.where(hit, 1.0, 0.0).astype(BF16)
        weight = jnp.sum(jnp.where(hit, gate[0], 0.0), 1, keepdims=True)
        xe = nn(pick, hn[0]).astype(BF16)
        xe_o[0, :rows] = xe
        gp = nn(xe, w[0, 0])
        up = nn(xe, w[0, 1])
        sig = jax.nn.sigmoid(gp)
        silu = gp * sig
        hid = silu * up
        hg = (hid * weight).astype(BF16)
        hg_o[0, :rows] = hg
        dyr = nn(pick, dy[0]).astype(BF16)
        dyr_o[0, :rows] = dyr
        parts = []
        for r in range(width // shared):
            at = r * shared
            total = None
            for b in range(ff // shared):
                low = b * shared
                term = nn(hg[:, low : low + shared], w[0, 2, at : at + shared, low : low + shared])
                total = term if total is None else total + term
            ye_o[0, :rows, at : at + shared] = total.astype(BF16)
        for b in range(ff // shared):
            low = b * shared
            total = None
            for r in range(width // shared):
                at = r * shared
                term = nt(dyr[:, at : at + shared], w[0, 2, at : at + shared, low : low + shared])
                total = term if total is None else total + term
            parts.append(total)
        back = jnp.concatenate(parts, 1)
        dgate = jnp.sum(back * hid, 1, keepdims=True)
        dhid = back * weight
        dgp = (dhid * up * sig * (1.0 + gp * (1.0 - sig))).astype(BF16)
        dup = (dhid * silu).astype(BF16)
        dgp_o[0, :rows] = dgp
        dup_o[0, :rows] = dup
        dots = jnp.sum(dgp.astype(F32) * gp + dup.astype(F32) * up, 1, keepdims=True)
        dxe_o[0, :rows] = (nt(dgp, w[0, 0]) + nt(dup, w[0, 1])).astype(BF16)
        tok_o[0, 0:1, :] = jnp.sum(jnp.where(hit, dgate, 0.0), 0, keepdims=True)
        tok_o[0, 1:2, :] = jnp.sum(jnp.where(hit, dots, 0.0), 0, keepdims=True)

    @pl.when(counts[g] == 0)
    def _():
        clear(0)
        tok_o[...] = jnp.zeros_like(tok_o)

    @pl.when((counts[g] > 0) & (counts[g] <= half))
    def _():
        run(half)
        clear(half)

    @pl.when(counts[g] > half)
    def _():
        run(full)


def expert_pass(counts, place, gate, hn, dy, w, at, capacity, shared):
    width, ff = w.shape[2:]
    micro, group, _ = hn.shape
    line = lambda g, c: (g, 0, 0)
    slots = lambda n: jax.ShapeDtypeStruct((micro, capacity, n), BF16)
    sizes = (width, width, ff, ff, ff, width, width)
    flops = 2 * micro * capacity * width * (6 * ff + 2 * group)
    once = pl.Buffered(1)
    return pl.pallas_call(
        functools.partial(expert_body, shared),
        grid_spec=pltpu.PrefetchScalarGridSpec(
            num_scalar_prefetch=1,
            grid=(micro,),
            in_specs=[
                pl.BlockSpec((1, 1, group), line),
                pl.BlockSpec((1, 1, group), line),
                pl.BlockSpec((1, group, width), line, pipeline_mode=once),
                pl.BlockSpec((1, group, width), line, pipeline_mode=once),
                pl.BlockSpec((1, 3, width, ff), lambda g, c: (at, 0, 0, 0), pipeline_mode=once),
            ],
            out_specs=[pl.BlockSpec((1, capacity, n), line, pipeline_mode=once) for n in sizes]
            + [pl.BlockSpec((1, 2, group), line)],
        ),
        out_shape=[slots(n) for n in sizes] + [jax.ShapeDtypeStruct((micro, 2, group), F32)],
        compiler_params=pltpu.CompilerParams(vmem_limit_bytes=VMEM_LIMIT),
        cost_estimate=pl.CostEstimate(
            flops=flops, bytes_accessed=40 << 20, transcendentals=micro * capacity * ff
        ),
        name="expert_pass",
    )(counts, place, gate, hn, dy, w)


def grads_body(xe, dgp, dup, hg, dyr, *rest):
    out = rest[-1]
    part = xe[...]
    shared = part.shape[1]
    out[0, 0] = tn(part, dgp[...]).astype(BF16)
    out[0, 1] = tn(part, dup[...]).astype(BF16)
    back = dyr[...]
    for b in range(hg.shape[1] // shared):
        low = b * shared
        out[0, 2, :, low : low + shared] = tn(hg[:, low : low + shared], back).astype(BF16)


def expert_grads(xe, dgp, dup, hg, dyr, shared, at, pair, held):
    micro, capacity, width = xe.shape
    ff = dgp.shape[2]
    rows = micro * capacity
    xe, dyr = (a.reshape(rows, width) for a in (xe, dyr))
    dgp, dup, hg = (a.reshape(rows, ff) for a in (dgp, dup, hg))
    thin = pl.BlockSpec((rows, shared), lambda r: (0, r))
    whole = pl.BlockSpec((rows, ff), lambda r: (0, 0))
    return pl.pallas_call(
        grads_body,
        grid=(width // shared,),
        in_specs=[thin, whole, whole, whole, thin] + [ANY] * len(held),
        out_specs=pl.BlockSpec((1, 3, shared, ff), lambda r: (at, 0, r, 0)),
        out_shape=jax.ShapeDtypeStruct((pair, 3, width, ff), BF16),
        input_output_aliases={5: 0} if held else {},
        compiler_params=pltpu.CompilerParams(vmem_limit_bytes=VMEM_LIMIT),
        cost_estimate=pl.CostEstimate(
            flops=6 * rows * width * ff, bytes_accessed=26 << 20, transcendentals=0
        ),
        name="expert_grads",
    )(xe, dgp, dup, hg, dyr, *held)


def pack_body(wg, wu, wd, out):
    shared = out.shape[2]
    out[0, 0] = wg[0]
    out[0, 1] = wu[0]
    for b in range(out.shape[3] // shared):
        low = b * shared
        out[0, 2, :, low : low + shared] = wd[0, low : low + shared, :]


def pack(wg, wu, wd, first, pair):
    _, shared, ff = wg.shape
    block = pl.BlockSpec((1, shared, ff), lambda i: (first + i, 0, 0))
    return pl.pallas_call(
        pack_body,
        grid=(pair,),
        in_specs=[block, block, pl.BlockSpec((1, ff, shared), lambda i: (first + i, 0, 0))],
        out_specs=pl.BlockSpec((1, 3, shared, ff), lambda i: (i, 0, 0, 0)),
        out_shape=jax.ShapeDtypeStruct((pair, 3, shared, ff), BF16),
        cost_estimate=pl.CostEstimate(
            flops=0, bytes_accessed=pair * 12 * shared * ff, transcendentals=0
        ),
        name="pack",
    )(wg, wu, wd)


def unpack_body(x, *refs):
    gg, gu, gd = refs[-3:]
    shared = x.shape[2]
    gg[0] = x[0, 0].astype(F32)
    gu[0] = x[0, 1].astype(F32)
    for b in range(x.shape[3] // shared):
        low = b * shared
        gd[0, low : low + shared, :] = x[0, 2, :, low : low + shared].astype(F32)


def unpack(x, held, first, experts):
    pair, _, shared, ff = x.shape
    block = pl.BlockSpec((1, shared, ff), lambda i: (first + i, 0, 0))
    return pl.pallas_call(
        unpack_body,
        grid=(pair,),
        in_specs=[pl.BlockSpec((1, 3, shared, ff), lambda i: (i, 0, 0, 0))] + [ANY] * len(held),
        out_specs=[block, block, pl.BlockSpec((1, ff, shared), lambda i: (first + i, 0, 0))],
        out_shape=[
            jax.ShapeDtypeStruct((experts, shared, ff), F32),
            jax.ShapeDtypeStruct((experts, shared, ff), F32),
            jax.ShapeDtypeStruct((experts, ff, shared), F32),
        ],
        input_output_aliases={1 + j: j for j in range(len(held))},
        compiler_params=pltpu.CompilerParams(vmem_limit_bytes=VMEM_LIMIT),
        cost_estimate=pl.CostEstimate(
            flops=0, bytes_accessed=pair * 18 * shared * ff, transcendentals=0
        ),
        name="unpack",
    )(x, *held)


def places():
    row, col = lax.axis_index("row"), lax.axis_index("col")
    n_row, n_col = lax.axis_size("row"), lax.axis_size("col")
    return row, col, n_row, n_col


def remote(src, dst, send_sem, recv_sem, where):
    return pltpu.make_async_remote_copy(
        src_ref=src,
        dst_ref=dst,
        send_sem=send_sem,
        recv_sem=recv_sem,
        device_id=where,
        device_id_type=MESH,
    )


def shake(sources, targets):
    barrier = pltpu.get_barrier_semaphore()
    for ok, where in sources:
        if ok is True:
            pl.semaphore_signal(barrier, inc=1, device_id=where, device_id_type=MESH)
        else:

            @pl.when(ok)
            def _():
                pl.semaphore_signal(barrier, inc=1, device_id=where, device_id_type=MESH)

    count = 0
    for ok in targets:
        count = count + (1 if ok is True else jnp.where(ok, 1, 0))
    pl.semaphore_wait(barrier, count)


def line_peers():
    row, col, n_row, n_col = places()
    pair, core = col // 2, col % 2
    return [
        (True, (row, pair * 2 + 1 - core)),
        (pair > 0, (row, (pair - 1) * 2 + core)),
        (pair < n_col // 2 - 1, (row, (pair + 1) * 2 + core)),
    ]


def row_peers():
    row, col, n_row, n_col = places()
    return [(True, ((row + k) % n_row, col)) for k in range(1, n_row)]


def col_slice(ref, index, size):
    return ref.at[..., pl.ds(pl.multiple_of(index * size, size), size)]


def line_gather(axes, ins, outs, sems):
    own_sem, right_s, right_r, left_s, left_r, side_s, side_r = sems
    n = len(ins)
    row, col, n_row, n_col = places()
    pairs, pair, core = n_col // 2, col // 2, col % 2

    def at(pair_index, core_index):
        return (row, pair_index * 2 + core_index)

    def block(j, source):
        size = ins[j].shape[axes[j]]
        if axes[j] == 0:
            return outs[j].at[pl.ds(pl.multiple_of(source * size, size), size)]
        return col_slice(outs[j], source, size)

    def right(j, s):
        source = (pair - s) * 2 + core
        src = ins[j] if s == 0 else block(j, source)
        return remote(src, block(j, source), right_s.at[j, s], right_r.at[j, s], at(pair + 1, core))

    def left(j, s):
        source = (pair + s) * 2 + core
        src = ins[j] if s == 0 else block(j, source)
        return remote(src, block(j, source), left_s.at[j, s], left_r.at[j, s], at(pair - 1, core))

    def side(j, source_pair, first=False):
        source = source_pair * 2 + core
        src = ins[j] if first else block(j, source)
        return remote(
            src,
            block(j, source),
            side_s.at[j, source_pair],
            side_r.at[j, source_pair],
            at(pair, 1 - core),
        )

    def arrived(j, recvs, slot, source):
        remote(
            ins[j], block(j, source), recvs.at[j, slot], recvs.at[j, slot], at(pair, 1 - core)
        ).wait_recv()

    def own(j):
        return pltpu.make_async_copy(ins[j], block(j, col), own_sem.at[j])

    def begin():
        for j in range(n):

            @pl.when(pair < pairs - 1)
            def _():
                right(j, 0).start()

            @pl.when(pair > 0)
            def _():
                left(j, 0).start()

        for j in range(n):
            side(j, pair, True).start()
            own(j).start()

    def middle():
        for s in range(1, pairs):
            for j in range(n):

                @pl.when(pair >= s)
                def _():
                    arrived(j, right_r, s - 1, (pair - s) * 2 + core)

                    @pl.when(pair < pairs - 1)
                    def _():
                        right(j, s).start()

                    side(j, pair - s).start()

                @pl.when(pair + s < pairs)
                def _():
                    arrived(j, left_r, s - 1, (pair + s) * 2 + core)

                    @pl.when(pair > 0)
                    def _():
                        left(j, s).start()

                    side(j, pair + s).start()

    def end():
        for j in range(n):
            own(j).wait()
            for p in range(pairs):
                side(j, p).wait_send()
                arrived(j, side_r, p, p * 2 + 1 - core)
            for s in range(pairs):

                @pl.when((pair >= s) & (pair < pairs - 1))
                def _():
                    right(j, s).wait_send()

                @pl.when((pair + s < pairs) & (pair > 0))
                def _():
                    left(j, s).wait_send()

    return begin, middle, end


def line_sems(n, pairs):
    dma = pltpu.SemaphoreType.DMA
    return [dma((n,))] + [dma((n, pairs))] * 6


def front_body(tokens, gains, wq, wk, wv, wo, wr, *refs):
    x_o, gains_o, wh_o, wo_o, wr_o = refs[:5]
    wide = refs[5:8]
    line, (heads_s, heads_r, row_s, row_r, own_s) = refs[8:15], refs[15:]
    row, col, n_row, n_col = places()
    head = wh_o.shape[2]
    part = wq.shape[0]
    begin, middle, end = line_gather((1, 1), [tokens, gains], [x_o, gains_o], line)
    small = [(wq, wide[0]), (wk, wide[1]), (wv, wide[2]), (wo, wo_o), (wr, wr_o)]

    def small_dst(k, source):
        src, dst = small[k]
        if k < 4:
            return col_slice(dst, source, src.shape[1])
        return dst.at[pl.ds(pl.multiple_of(source * src.shape[0], src.shape[0]), src.shape[0]), :]

    def small_copy(k, step):
        return remote(
            small[k][0],
            small_dst(k, row),
            row_s.at[k, step],
            row_r.at[k, step],
            ((row + step) % n_row, col),
        )

    def small_come(k, step):
        source = (row + n_row - step) % n_row
        return remote(
            small[k][0], small_dst(k, source), row_s.at[k, step], row_r.at[k, step], (source, col)
        )

    def small_own(k):
        return pltpu.make_async_copy(small[k][0], small_dst(k, row), own_s.at[k])

    def heads_dst(m, source):
        return wh_o.at[m, pl.ds(pl.multiple_of(source * part, part), part), :]

    def heads(m, step):
        where = (col + step) % n_col
        return remote(
            col_slice(wide[m], where, head),
            heads_dst(m, col),
            heads_s.at[m, step],
            heads_r.at[m, step],
            (row, where),
        )

    def heads_come(m, step):
        source = (col + n_col - step) % n_col
        return remote(
            heads_dst(m, source),
            heads_dst(m, source),
            heads_s.at[m, step],
            heads_r.at[m, step],
            (row, source),
        )

    def heads_own(m):
        return pltpu.make_async_copy(
            col_slice(wide[m], col, head), heads_dst(m, col), own_s.at[5 + m]
        )

    peers = [(True, (row, (col + k) % n_col)) for k in range(1, n_col)] + row_peers()
    shake(peers, [ok for ok, _ in peers])
    for k in range(5):
        for step in range(1, n_row):
            small_copy(k, step).start()
        small_own(k).start()
    begin()
    for k in range(3):
        small_own(k).wait()
        for step in range(1, n_row):
            small_come(k, step).wait_recv()
    for m in range(3):
        heads_own(m).start()
        for step in range(1, n_col):
            heads(m, step).start()
    middle()
    end()
    for k in range(5):
        if k >= 3:
            small_own(k).wait()
        for step in range(1, n_row):
            small_copy(k, step).wait_send()
            if k >= 3:
                small_come(k, step).wait_recv()
    for m in range(3):
        heads_own(m).wait()
        for step in range(1, n_col):
            heads(m, step).wait_send()
            heads_come(m, step).wait_recv()


def front(tokens, gains, wq, wk, wv, wo, wr, head, ident):
    n_row, n_col = lax.axis_size("row"), lax.axis_size("col")
    rows, part = tokens.shape
    width = part * n_col
    dma = pltpu.SemaphoreType.DMA
    shapes = [
        ((rows, width), BF16),
        ((gains.shape[0], width), F32),
        ((3, width, head), BF16),
        ((wo.shape[0], wo.shape[1] * n_row), BF16),
        ((wr.shape[0] * n_row, part), BF16),
    ] + [((part, wq.shape[1] * n_row), BF16)] * 3
    return pl.pallas_call(
        front_body,
        in_specs=[ANY] * 7,
        out_specs=[ANY] * 8,
        out_shape=[jax.ShapeDtypeStruct(s, t) for s, t in shapes],
        scratch_shapes=line_sems(2, n_col // 2)
        + [
            dma((3, n_col)),
            dma((3, n_col)),
            dma((5, n_row)),
            dma((5, n_row)),
            dma((8,)),
        ],
        compiler_params=pltpu.CompilerParams(collective_id=ident, has_side_effects=True),
        cost_estimate=pl.CostEstimate(
            flops=0, bytes_accessed=rows * width * 32, transcendentals=0
        ),
        name="front",
    )(tokens, gains, wq, wk, wv, wo, wr)


def middle_body(axes, *refs):
    n = len(axes)
    begin, middle, end = line_gather(axes, refs[:n], refs[n : 2 * n], refs[2 * n :])
    sources = line_peers()
    shake(sources, [ok for ok, _ in sources])
    begin()
    middle()
    end()


def middle_gather(arrays, axes, ident):
    n_col, n = lax.axis_size("col"), len(arrays)
    shapes = [
        tuple(d * n_col if at == axis else d for at, d in enumerate(a.shape))
        for a, axis in zip(arrays, axes)
    ]
    return pl.pallas_call(
        functools.partial(middle_body, axes),
        in_specs=[ANY] * n,
        out_specs=[ANY] * n,
        out_shape=[jax.ShapeDtypeStruct(s, a.dtype) for s, a in zip(shapes, arrays)],
        scratch_shapes=line_sems(n, n_col // 2),
        compiler_params=pltpu.CompilerParams(collective_id=ident, has_side_effects=True),
        cost_estimate=pl.CostEstimate(
            flops=0, bytes_accessed=sum(math.prod(s) for s in shapes) * 32, transcendentals=0
        ),
        name="middle_gather",
    )(*arrays)


def scatter_body(part, stage, local, *refs):
    n_in = (1, 2, 4, 4)[stage]
    n_out = (1, 2, 4, 4)[stage]
    if local:
        place, slots, refs = refs[0], refs[1 : 1 + local], refs[local:]
    x, ins = refs[0], refs[1:n_in]
    out, outs = refs[n_in], refs[n_in + 1 : n_in + n_out]
    rest = refs[n_in + n_out :]
    acc, side, from_left, from_right, load, side_s, side_r = rest[:7]
    right_s, right_r, left_s, left_r = rest[7:11]
    if local:
        give, chosen, held, held_s = rest[11:15]
        rest = rest[4:]
    row, col, n_row, n_col = places()
    pairs, pair, core = n_col // 2, col // 2, col % 2
    rows = out.shape[0]
    cuts = load.shape[1]
    height = rows // cuts
    tile = min(256, height)

    def at(pair_index, core_index):
        return (row, pair_index * 2 + core_index)

    def block(owner, q):
        return x.at[
            pl.ds(q * height, height), pl.ds(pl.multiple_of(owner * part, part), part)
        ]

    def cut(ref, d, q):
        return ref.at[d, pl.ds(q * height, height)]

    def fetch(d, q):
        return pltpu.make_async_copy(block(d * 2 + core, q), cut(acc, d, q), load.at[d, q])

    def across(d, q):
        return remote(
            cut(give, d, q) if local else block(d * 2 + 1 - core, q),
            cut(side, d, q),
            side_s.at[d, q],
            side_r.at[d, q],
            at(pair, 1 - core),
        )

    def right(d, q):
        return remote(
            cut(acc, d, q),
            cut(from_left, d, q),
            right_s.at[d, q],
            right_r.at[d, q],
            at(pair + 1, core),
        )

    def left(d, q):
        return remote(
            cut(acc, d, q),
            cut(from_right, d, q),
            left_s.at[d, q],
            left_r.at[d, q],
            at(pair - 1, core),
        )

    copies, arrivals, own = [], [], []
    if stage:
        small_s, small_r, own_s = rest[11:14]
        extra, extra_o = ins[0], outs[0]
        here, ring = (row, n_row) if stage == 2 else (col, n_col)
        for k in range(1, ring):
            where, source = (here + k) % ring, (here + ring - k) % ring
            to = (where, col) if stage == 2 else (row, where)
            copies.append(remote(extra, extra_o.at[here], small_s.at[k], small_r.at[k], to))
            arrivals.append(remote(extra, extra_o.at[source], small_s.at[k], small_r.at[k], to))
        own.append(pltpu.make_async_copy(extra, extra_o.at[here], own_s))
    if stage == 2:
        give_s, give_r, keep_s = rest[14:]
        per = n_col // n_row
        for m in range(2):
            src, dst = ins[1 + m], outs[1 + m]

            def block_of(r):
                return src.at[pl.ds(r * per, per)]

            for step in range(1, n_row):
                where, source = (row + step) % n_row, (row + n_row - step) % n_row
                sems = (give_s.at[m, step], give_r.at[m, step])
                copies.append(remote(block_of(where), dst.at[row], *sems, (where, col)))
                arrivals.append(remote(block_of(where), dst.at[source], *sems, (where, col)))
            own.append(pltpu.make_async_copy(block_of(row), dst.at[row], keep_s.at[m]))
    if stage == 3:
        give_s, give_r, keep_s = rest[14:]
        for m in range(2):
            src, dst = ins[1 + m], outs[1 + m]
            size = src.shape[1 - m] // n_col

            def block_for(c):
                at_c = pl.ds(pl.multiple_of(c * size, size), size)
                return src.at[:, at_c, :] if m == 0 else src.at[at_c, :]

            for step in range(1, n_col):
                where, source = (col + step) % n_col, (col + n_col - step) % n_col
                sems = (give_s.at[m, step], give_r.at[m, step])
                copies.append(remote(block_for(where), dst.at[col], *sems, (row, where)))
                arrivals.append(remote(block_for(where), dst.at[source], *sems, (row, where)))
            own.append(pltpu.make_async_copy(block_for(col), dst.at[col], keep_s.at[m]))
    if stage:
        peers = [(True, (row, (col + k) % n_col)) for k in range(1, n_col)]
    else:
        peers = line_peers()
    if stage == 2:
        peers += row_peers()
    shake(peers, [ok for ok, _ in peers])
    order = []
    for t in range(pairs):
        for d in (pairs - 1 - t, t):
            if d not in order:
                order.append(d)
    if local:
        micro, capacity = held.shape[2], held.shape[3]
        group = chosen.shape[1]
        owners = []
        for d in order:
            owners += [d * 2 + 1 - core, d * 2 + core]

        def bring(n):
            return [
                pltpu.make_async_copy(
                    slots[e].at[:, :, pl.ds(pl.multiple_of(owners[n] * part, part), part)],
                    held.at[n % 2, e],
                    held_s.at[n % 2, e],
                )
                for e in range(local)
            ]

        def make(n, into):
            for c in bring(n):
                c.wait()
            if n + 1 < len(owners):
                for c in bring(n + 1):
                    c.start()
            steps = group // tile

            def step(i, _):
                g, at_row = i // steps, pl.multiple_of((i % steps) * tile, tile)
                total = None
                for e in range(local):
                    term = nn(
                        chosen[g, pl.ds(at_row, tile), e * capacity : (e + 1) * capacity],
                        held[n % 2, e, g],
                    )
                    total = term if total is None else total + term
                into[pl.ds(pl.multiple_of(i * tile, tile), tile), :] = total.astype(BF16)
                return 0

            lax.fori_loop(0, micro * steps, step, 0)

        def make_pair(m):
            d = order[m]
            make(2 * m, give.at[d])
            for q in range(cuts):
                across(d, q).start()
            make(2 * m + 1, acc.at[d])

        for c in bring(0):
            c.start()

        def choose(i, _):
            steps = group // tile
            g, at_row = i // steps, pl.multiple_of((i % steps) * tile, tile)
            for e in range(local):
                slot = lax.broadcasted_iota(jnp.int32, (tile, capacity), 1)
                hit = slot == place[g, pl.ds(at_row, tile), e : e + 1]
                chosen[g, pl.ds(at_row, tile), e * capacity : (e + 1) * capacity] = jnp.where(
                    hit, 1.0, 0.0
                ).astype(BF16)
            return 0

        lax.fori_loop(0, micro * (group // tile), choose, 0)
    else:
        for d in order:
            for q in range(cuts):
                across(d, q).start()
                fetch(d, q).start()
    for c in copies + own:
        c.start()

    def add(q, into, *sources):
        def step(i, _):
            lines = pl.ds(pl.multiple_of(q * height + i * tile, tile), tile)
            total = sources[0][lines, :].astype(F32)
            for ref in sources[1:]:
                total = total + ref[lines, :].astype(F32)
            into[lines, :] = total.astype(into.dtype)
            return 0

        lax.fori_loop(0, height // tile, step, 0)

    def ready(d, q):
        if not local:
            fetch(d, q).wait()
        across(d, q).wait_recv()

    def go_right(d, q):
        ready(d, q)

        @pl.when(pair > 0)
        def _():
            right(d, q).wait_recv()
            add(q, acc.at[d], acc.at[d], side.at[d], from_left.at[d])

        @pl.when(pair == 0)
        def _():
            add(q, acc.at[d], acc.at[d], side.at[d])

        right(d, q).start()

    def go_left(d, q):
        ready(d, q)

        @pl.when(pair < pairs - 1)
        def _():
            left(d, q).wait_recv()
            add(q, acc.at[d], acc.at[d], side.at[d], from_right.at[d])

        @pl.when(pair == pairs - 1)
        def _():
            add(q, acc.at[d], acc.at[d], side.at[d])

        left(d, q).start()

    if local:
        for m in range(2):
            make_pair(m)
        for q in range(cuts):

            @pl.when(pair == 0)
            def _():
                go_right(pairs - 1, q)

            @pl.when(pair == pairs - 1)
            def _():
                go_left(0, q)

        for m in range(2, pairs):
            make_pair(m)
    for t in range(pairs - 1):
        far, near = pairs - 1 - t, t
        go_far, go_near = far > pair, near < pair
        if local and t == 0:
            go_far, go_near = go_far & (pair > 0), go_near & (pair < pairs - 1)
        for q in range(cuts):

            @pl.when(go_far)
            def _():
                go_right(far, q)

            @pl.when(go_near)
            def _():
                go_left(near, q)

    for q in range(cuts):
        ready(pair, q)

        @pl.when(pair == 0)
        def _():
            left(pair, q).wait_recv()
            add(q, out, acc.at[pair], side.at[pair], from_right.at[pair])

        @pl.when(pair == pairs - 1)
        def _():
            right(pair, q).wait_recv()
            add(q, out, acc.at[pair], side.at[pair], from_left.at[pair])

        @pl.when((pair > 0) & (pair < pairs - 1))
        def _():
            left(pair, q).wait_recv()
            right(pair, q).wait_recv()
            add(q, out, acc.at[pair], side.at[pair], from_left.at[pair], from_right.at[pair])

    for d in range(pairs):
        for q in range(cuts):
            across(d, q).wait_send()

            @pl.when(pair < d)
            def _():
                right(d, q).wait_send()

            @pl.when(pair > d)
            def _():
                left(d, q).wait_send()

    for c in copies:
        c.wait_send()
    for c in arrivals:
        c.wait_recv()
    for c in own:
        c.wait()


def scatter_col(x, ident, stage=0, others=(), place=None):
    n_row, n_col = lax.axis_size("row"), lax.axis_size("col")
    pairs, per = n_col // 2, n_col // n_row
    local = 0 if place is None else len(x)
    if local:
        micro, group, _ = place.shape
        capacity = x[0].shape[1]
        rows, part = micro * group, x[0].shape[2] // n_col
    else:
        rows, part = x.shape[0], x.shape[1] // n_col
    cuts = 4 if rows % 1024 == 0 else 1
    dma = pltpu.SemaphoreType.DMA
    buffer = pltpu.VMEM((pairs, rows, part), BF16)
    scratch = [buffer] * 4 + [dma((pairs, cuts))] * 7
    if local:
        scratch += [
            buffer,
            pltpu.VMEM((micro, group, local * capacity), BF16),
            pltpu.VMEM((2, local, micro, capacity, part), BF16),
            dma((2, local)),
        ]
    out_shape = [jax.ShapeDtypeStruct((rows, part), F32)]
    if stage:
        extra, ring = others[0], n_row if stage == 2 else n_col
        out_shape.append(jax.ShapeDtypeStruct((ring,) + extra.shape, extra.dtype))
        scratch += [dma((ring,)), dma((ring,)), dma(())]
    if stage == 2:
        scratch += [dma((2, n_row)), dma((2, n_row)), dma((2,))]
        for value in others[1:]:
            out_shape.append(jax.ShapeDtypeStruct((n_row, per) + value.shape[1:], BF16))
    if stage == 3:
        heads, branch = others[1:]
        scratch += [dma((2, n_col)), dma((2, n_col)), dma((2,))]
        out_shape += [
            jax.ShapeDtypeStruct((n_col, 3, heads.shape[1] // n_col, heads.shape[2]), BF16),
            jax.ShapeDtypeStruct((n_col, branch.shape[0] // n_col, branch.shape[1]), BF16),
        ]
    first = [pl.BlockSpec(memory_space=pltpu.VMEM)] + [ANY] * local if local else [ANY]
    values = (place, *x) if local else (x,)
    return pl.pallas_call(
        functools.partial(scatter_body, part, stage, local),
        in_specs=first + [ANY] * len(others),
        out_specs=[pl.BlockSpec(memory_space=pltpu.VMEM)] + [ANY] * (len(out_shape) - 1),
        out_shape=out_shape,
        scratch_shapes=scratch,
        compiler_params=pltpu.CompilerParams(
            vmem_limit_bytes=VMEM_LIMIT, collective_id=ident, has_side_effects=True
        ),
        cost_estimate=pl.CostEstimate(
            flops=0, bytes_accessed=rows * part * n_col * 40, transcendentals=0
        ),
        name="scatter_col",
    )(*values, *others)


def shards(
    tokens,
    gain_attn,
    gain_ffn,
    gain_query,
    gain_key,
    w_query,
    w_key,
    w_value,
    w_out,
    w_router,
    w_gate,
    w_up,
    w_down,
    routes,
    lengths,
    cotangent,
):
    n_col = lax.axis_size("col")
    n_row = lax.axis_size("row")
    col = lax.axis_index("col")
    micro, spans = lengths.shape
    rows, part = tokens.shape
    group = rows // micro
    width = part * n_col
    head = gain_query.shape[0]
    local_exp = w_gate.shape[0]
    experts = local_exp * n_col
    topk = routes.shape[1]
    capacity = 2 * group * topk // experts
    local_heads = w_out.shape[0] // head
    hd = w_out.shape[0] * n_col
    scale = head ** (-0.5)

    def gather(value, axis_name, axis):
        return lax.all_gather(value, axis_name, axis=axis, tiled=True)

    def mine(value, axis):
        size = value.shape[axis] // n_col
        return lax.dynamic_slice_in_dim(value, col * size, size, axis)

    shared = w_down.shape[2]
    pair = 2 if local_exp % 2 == 0 else 1
    big = [
        gather(pack(w_gate, w_up, w_down, at, pair), "row", 2) for at in range(0, local_exp, pair)
    ]
    inputs_low, gains, w_heads, rows_o, rows_r, *wide = front(
        tokens,
        jnp.stack([gain_attn, gain_ffn]),
        w_query,
        w_key,
        w_value,
        w_out,
        w_router.T,
        head,
        0,
    )

    segment, position, live = jax.vmap(lambda l: layout(l, group))(lengths)
    position = position.reshape(rows)
    live = live.reshape(rows)
    upstream_part = cotangent.astype(F32) * live[:, None]
    member = jnp.any(
        routes[:, None, :] == jnp.arange(experts, dtype=jnp.int32)[None, :, None], -1
    )
    member_f = member.astype(F32)
    member_loc = mine(member_f, 1).reshape(micro, group, local_exp)
    lower = (
        jnp.arange(group, dtype=jnp.int32)[:, None] > jnp.arange(group, dtype=jnp.int32)[None, :]
    ).astype(BF16)
    before = jnp.einsum("st,gte->gse", lower, member_loc.astype(BF16), preferred_element_type=F32)
    place = jnp.where(member_loc > 0, before, -1.0).astype(jnp.int32)
    counts = jnp.sum(member_loc, 1).astype(jnp.int32).T
    place_t = place.transpose(2, 0, 1)[:, :, None, :]

    inputs = inputs_low.astype(F32)
    scale_one = inverse_rms(inputs)
    normed = (inputs * scale_one * gains[0]).astype(BF16)
    all_heads = jnp.concatenate([w_heads[j] for j in range(3)], 1)
    query_pre, key_pre, value_pre = jnp.split(nn(normed, all_heads), 3, 1)
    shape = (rows, local_heads, head)
    cosine, sine = rope_tables(position, head)

    def head_norm(values, gain):
        return rotary(values * inverse_rms(values) * gain, cosine, sine)

    query_rot, query_pull = jax.vjp(head_norm, query_pre.reshape(shape), gain_query)
    key_rot, key_pull = jax.vjp(head_norm, key_pre.reshape(shape), gain_key)
    batch = (micro, group, local_heads, head)
    queries = query_rot.astype(BF16).reshape(batch)
    keys_low = key_rot.astype(BF16).reshape(batch)
    values_low = value_pre.astype(BF16).reshape(batch)
    same = (segment[:, :, None] == segment[:, None, :])[:, None]

    def scores_of():
        raw = jnp.einsum("gqhd,gkhd->ghqk", queries, keys_low, preferred_element_type=F32) * scale
        return jnp.where(same, raw, MASKED)

    scores = scores_of()
    highest = jnp.max(scores, -1, keepdims=True)
    log_total = highest + jnp.log(jnp.sum(jnp.exp(scores - highest), -1, keepdims=True))
    probs_low = jnp.exp(scores - log_total).astype(BF16)
    attended = jnp.einsum(
        "ghqk,gkhd->gqhd", probs_low, values_low, preferred_element_type=F32
    ).astype(BF16)
    attended_full, full_o, full_rt, upstream_low = middle_gather(
        [attended.reshape(rows, local_heads * head), rows_o, rows_r, upstream_part.astype(BF16)],
        (1, 0, 1, 1),
        1,
    )
    full_r = full_rt.T

    hidden = inputs + nn(attended_full, full_o)
    scale_two = inverse_rms(hidden)
    normed_ffn = (hidden * scale_two * gains[1]).astype(BF16)
    logits = nn(normed_ffn, full_r)
    peak = jnp.max(jnp.where(member, logits, -jnp.inf), -1, keepdims=True)
    raised = jnp.where(member, jnp.exp(jnp.where(member, logits - peak, 0.0)), 0.0)
    gates = raised / jnp.sum(raised, -1, keepdims=True)
    gate_t = mine(gates, 1).reshape(micro, group, local_exp).transpose(2, 0, 1)[:, :, None, :]
    upstream_full = upstream_low.reshape(micro, group, width)
    hn = normed_ffn.reshape(micro, group, width)

    outs, weight_grads, grad = [], [], None
    for e in range(local_exp):
        xe, dyr, hg, dgp, dup, ye, dxe, tok = expert_pass(
            counts[e],
            place_t[e],
            gate_t[e],
            hn,
            upstream_full,
            big[e // pair],
            e % pair,
            capacity,
            shared,
        )
        held = () if e % pair == 0 else (grad,)
        grad = expert_grads(xe, dgp, dup, hg, dyr, shared, e % pair, pair, held)
        hn, upstream_full, ye, dxe, tok, grad = lax.optimization_barrier(
            (hn, upstream_full, ye, dxe, tok, grad)
        )
        outs.append((ye, dxe, tok))
        if e % pair == pair - 1:
            weight_grads.append(lax.psum_scatter(grad, "row", scatter_dimension=2, tiled=True))

    def tie(value, e):
        value, weight_grads[e] = lax.optimization_barrier((value, weight_grads[e]))
        return value

    row = lax.axis_index("row")
    back_sum, tok = scatter_col(
        [o[1] for o in outs], 2, 1, (jnp.stack([o[2] for o in outs]),), place
    )
    tok = tok.reshape((experts,) + tok.shape[2:])
    hidden_part = tokens.astype(F32) + nn(attended_full, mine(full_o, 1))
    gate_dots = tok[:, :, 0].reshape(experts, rows).T
    hidden_part = mine(hidden, 1)

    selected = gates * (gate_dots - jnp.sum(gates * gate_dots, -1, keepdims=True))
    logit_grad = selected.astype(BF16)
    router_part = mine(full_r, 0)
    normed_grad = back_sum + nt(logit_grad, router_part)
    grad_router = tn(mine(normed_ffn, 1), logit_grad)
    scaled_two = hidden_part * scale_two
    grad_gain_ffn = jnp.sum(normed_grad * scaled_two, 0)
    dot_two = jnp.sum(tok[:, :, 1].reshape(experts, rows), 0) + jnp.sum(
        logit_grad.astype(F32) * logits, 1
    )
    hidden_grad = (
        upstream_part
        + scale_two * (normed_grad * gain_ffn)
        - hidden_part * scale_two**2 * dot_two[:, None] / width
    )

    branch_grad = hidden_grad.astype(BF16)
    (attended_grad,) = scatter_col(nt(branch_grad, mine(full_o, 1)).astype(BF16), 3)
    attended_grad = attended_grad.astype(BF16).reshape(batch)
    grad_out = tn(attended_full, branch_grad)
    scores_again = scores_of()
    probs = jnp.exp(scores_again - log_total)
    probs_again = probs.astype(BF16)
    probs_grad = jnp.einsum(
        "gqhd,gkhd->ghqk", attended_grad, values_low, preferred_element_type=F32
    )
    values_grad = jnp.einsum(
        "ghqk,gqhd->gkhd", probs_again, attended_grad, preferred_element_type=F32
    )
    score_grad = (probs * (probs_grad - jnp.sum(probs_grad * probs, -1, keepdims=True))).astype(
        BF16
    )
    query_grad_rot = (
        jnp.einsum("ghqk,gkhd->gqhd", score_grad, keys_low, preferred_element_type=F32) * scale
    )
    key_grad_rot = (
        jnp.einsum("ghqk,gqhd->gkhd", score_grad, queries, preferred_element_type=F32) * scale
    )
    query_grad, gain_query_part = query_pull(query_grad_rot.reshape(shape))
    key_grad, gain_key_part = key_pull(key_grad_rot.reshape(shape))
    flat = (rows, local_heads * head)
    heads_grad = [
        v.reshape(flat).astype(BF16) for v in (query_grad, key_grad, values_grad)
    ]
    all_grads = jnp.concatenate(heads_grad, 1)
    back_heads = nt(all_grads, all_heads)
    pre = (query_pre, key_pre, value_pre)
    dot_part = sum(jnp.sum(g.astype(F32) * p, -1) for g, p in zip(heads_grad, pre))
    sums = jnp.concatenate([dot_part, gain_query_part, gain_key_part])
    sums = jnp.pad(sums, (0, -sums.shape[0] % 1024)).reshape(-1, 128)
    heads_weights = tn(normed, all_grads).astype(BF16)
    heads_weights = jnp.stack(jnp.split(heads_weights, 3, 1))
    back_heads, mixed_slots = lax.optimization_barrier(
        (back_heads.astype(BF16), [o[0] for o in outs])
    )
    mixed_sum, sums, heads_terms, out_terms = scatter_col(
        mixed_slots, 4, 3, (sums, heads_weights, grad_out.astype(BF16)), place
    )
    mixed = (hidden_part + mixed_sum).astype(BF16)
    sums = jnp.sum(sums, 0).reshape(-1)
    dot_one = sums[:rows]
    gain_attn_part = 0.0
    for m in range(3):
        for c in range(n_col):
            columns = wide[m][:, c * local_heads * head : (c + 1) * local_heads * head]
            gain_attn_part = gain_attn_part + jnp.sum(
                columns.astype(F32) * heads_terms[c, m].astype(F32), -1
            )
    smalls = jnp.concatenate(
        [
            gain_attn_part,
            grad_gain_ffn,
            sums[rows : rows + 2 * head],
            grad_router.T.reshape(-1),
        ]
    ).reshape(-1, 128)
    back_heads, mixed = lax.optimization_barrier((back_heads, mixed))
    normed_back, smalls, heads_terms, out_terms = scatter_col(
        tie(back_heads, 0), 5, 2, (smalls, heads_terms, out_terms)
    )
    scale_one_part = scale_one
    inputs_part = tokens.astype(F32)
    input_grad = (
        hidden_grad
        + scale_one_part * (normed_back * gain_attn)
        - inputs_part * scale_one_part**2 * dot_one[:, None] / width
    )

    held = ()
    for e, grad in enumerate(weight_grads):
        held = unpack(grad, held, e * pair, local_exp)
    grad_gate, grad_up, grad_down = held

    heads_terms = jnp.sum(heads_terms.astype(F32), 0)
    heads_sum = jnp.concatenate([heads_terms[j] for j in range(heads_terms.shape[0])], -1)
    grad_query, grad_key, grad_value = heads_sum[0], heads_sum[1], heads_sum[2]
    out_terms = jnp.sum(out_terms.astype(F32), 0)
    grad_out = jnp.concatenate([out_terms[j] for j in range(out_terms.shape[0])], -1)
    row = lax.axis_index("row")
    total = jnp.sum(smalls, 0).reshape(-1)
    grad_gain_attn, grad_gain_ffn = total[:part] / gain_attn, total[part : 2 * part]
    grad_gain_query = total[2 * part : 2 * part + head]
    grad_gain_key = total[2 * part + head : 2 * part + 2 * head]
    grad_router = lax.dynamic_slice_in_dim(
        total[2 * part + 2 * head :].reshape(experts, part), row * (experts // n_row), experts // n_row, 0
    ).T
    return (
        mixed,
        input_grad,
        grad_gain_attn,
        grad_gain_ffn,
        grad_gain_query,
        grad_gain_key,
        grad_query,
        grad_key,
        grad_value,
        grad_out,
        grad_router,
        grad_gate,
        grad_up,
        grad_down,
    )


def solution(mesh):
    placed = (
        P("row", "col"),
        P("col"),
        P("col"),
        P(),
        P(),
        P("col", "row"),
        P("col", "row"),
        P("col", "row"),
        P("col", "row"),
        P("col", "row"),
        P("col", "row", None),
        P("col", "row", None),
        P("col", None, "row"),
        P("row", None),
        P("row", None),
        P("row", "col"),
    )
    return jax.shard_map(
        shards,
        mesh=mesh,
        in_specs=placed,
        out_specs=(
            P("row", "col"),
            P("row", "col"),
            P("col"),
            P("col"),
            P(),
            P(),
            P("col", "row"),
            P("col", "row"),
            P("col", "row"),
            P("col", "row"),
            P("col", "row"),
            P("col", "row", None),
            P("col", "row", None),
            P("col", None, "row"),
        ),
        check_vma=False,
    )
```

```python
import functools
import math

import jax
import jax.numpy as jnp
from jax import lax
from jax.experimental import pallas as pl
from jax.experimental.pallas import tpu as pltpu
from jax.sharding import PartitionSpec as P

EPSILON = 1e-06
ROPE_BASE = 10000.0
MASKED = -1e30
F32 = jnp.float32
BF16 = jnp.bfloat16
VMEM_LIMIT = 60 * 1024 * 1024
MESH = pl.DeviceIdType.MESH
ANY = pl.BlockSpec(memory_space=pl.ANY)


def inverse_rms(values):
    return lax.rsqrt(jnp.mean(values * values, -1, keepdims=True) + EPSILON)


def rope_tables(position, head):
    half = head // 2
    inverse = jnp.exp(-math.log(ROPE_BASE) * 2.0 / head * jnp.arange(half, dtype=F32))
    angles = position[:, None] * inverse[None, :]
    return jnp.cos(angles)[:, None, :], jnp.sin(angles)[:, None, :]


def rotary(values, cosine, sine):
    half = values.shape[-1] // 2
    first = values[..., :half]
    second = values[..., half:]
    return jnp.concatenate([first * cosine - second * sine, second * cosine + first * sine], -1)


def layout(lengths_row, group):
    ends = jnp.cumsum(lengths_row)
    starts = ends - lengths_row
    row_index = jnp.arange(group, dtype=jnp.int32)
    segment = jnp.sum((row_index[:, None] >= ends[None, :]).astype(jnp.int32), 1)
    member = segment[:, None] == jnp.arange(lengths_row.shape[0], dtype=jnp.int32)[None, :]
    position = (row_index - jnp.sum(jnp.where(member, starts[None, :], 0), 1)).astype(F32)
    live = (segment < lengths_row.shape[0] - 1).astype(F32)
    return (segment, position, live)


def nn(a, b):
    return lax.dot_general(a, b, (((1,), (0,)), ((), ())), preferred_element_type=F32)


def nt(a, b):
    return lax.dot_general(a, b, (((1,), (1,)), ((), ())), preferred_element_type=F32)


def tn(a, b):
    return lax.dot_general(a, b, (((0,), (0,)), ((), ())), preferred_element_type=F32)


def expert_body(shared, counts, place, gate, hn, dy, w, xe_o, dyr_o, hg_o, dgp_o, dup_o, ye_o, dxe_o, tok_o):
    g, i = pl.program_id(0), pl.program_id(1)
    rows = xe_o.shape[1]
    width, ff = w.shape[2:]
    base = i * rows

    @pl.when(i == 0)
    def _():
        tok_o[...] = jnp.zeros_like(tok_o)

    @pl.when(counts[g] <= base)
    def _():
        for ref in (xe_o, dyr_o, hg_o, dgp_o, dup_o, ye_o, dxe_o):
            ref[...] = jnp.zeros_like(ref)

    @pl.when(counts[g] > base)
    def _():
        slot = lax.broadcasted_iota(jnp.int32, (rows, place.shape[2]), 0) + base
        hit = slot == place[0]
        pick = jnp.where(hit, 1.0, 0.0).astype(BF16)
        weight = jnp.sum(jnp.where(hit, gate[0], 0.0), 1, keepdims=True)
        xe = nn(pick, hn[0]).astype(BF16)
        xe_o[0] = xe
        gp = nn(xe, w[0, 0])
        up = nn(xe, w[0, 1])
        sig = jax.nn.sigmoid(gp)
        silu = gp * sig
        hid = silu * up
        hg = (hid * weight).astype(BF16)
        hg_o[0] = hg
        dyr = nn(pick, dy[0]).astype(BF16)
        dyr_o[0] = dyr
        parts = []
        for r in range(width // shared):
            at = r * shared
            total = None
            for b in range(ff // shared):
                low = b * shared
                term = nn(hg[:, low : low + shared], w[0, 2, at : at + shared, low : low + shared])
                total = term if total is None else total + term
            ye_o[0, :, at : at + shared] = total.astype(BF16)
        for b in range(ff // shared):
            low = b * shared
            total = None
            for r in range(width // shared):
                at = r * shared
                term = nt(dyr[:, at : at + shared], w[0, 2, at : at + shared, low : low + shared])
                total = term if total is None else total + term
            parts.append(total)
        back = jnp.concatenate(parts, 1)
        dgate = jnp.sum(back * hid, 1, keepdims=True)
        dhid = back * weight
        dgp = (dhid * up * sig * (1.0 + gp * (1.0 - sig))).astype(BF16)
        dup = (dhid * silu).astype(BF16)
        dgp_o[0] = dgp
        dup_o[0] = dup
        dots = jnp.sum(dgp.astype(F32) * gp + dup.astype(F32) * up, 1, keepdims=True)
        dxe_o[0] = (nt(dgp, w[0, 0]) + nt(dup, w[0, 1])).astype(BF16)
        tok_o[0, 0:1, :] += jnp.sum(jnp.where(hit, dgate, 0.0), 0, keepdims=True)
        tok_o[0, 1:2, :] += jnp.sum(jnp.where(hit, dots, 0.0), 0, keepdims=True)


def expert_pass(counts, place, gate, hn, dy, w, at, capacity, shared):
    width, ff = w.shape[2:]
    micro, group, _ = hn.shape
    rows = min(256, capacity)
    blocks = capacity // rows
    tall = lambda g, i, c: (g, i, 0)
    line = lambda g, i, c: (g, 0, 0)
    slots = lambda n: jax.ShapeDtypeStruct((micro, capacity, n), BF16)
    sizes = (width, width, ff, ff, ff, width, width)
    flops = 2 * micro * capacity * width * (6 * ff + 2 * group)
    return pl.pallas_call(
        functools.partial(expert_body, shared),
        grid_spec=pltpu.PrefetchScalarGridSpec(
            num_scalar_prefetch=1,
            grid=(micro, blocks),
            in_specs=[
                pl.BlockSpec((1, 1, group), line),
                pl.BlockSpec((1, 1, group), line),
                pl.BlockSpec((1, group, width), line),
                pl.BlockSpec((1, group, width), line),
                pl.BlockSpec(
                    (1, 3, width, ff), lambda g, i, c: (at, 0, 0, 0), pipeline_mode=pl.Buffered(1)
                ),
            ],
            out_specs=[pl.BlockSpec((1, rows, n), tall) for n in sizes]
            + [pl.BlockSpec((1, 2, group), line)],
        ),
        out_shape=[slots(n) for n in sizes] + [jax.ShapeDtypeStruct((micro, 2, group), F32)],
        compiler_params=pltpu.CompilerParams(vmem_limit_bytes=VMEM_LIMIT),
        cost_estimate=pl.CostEstimate(
            flops=flops, bytes_accessed=40 << 20, transcendentals=micro * capacity * ff
        ),
        name="expert_pass",
    )(counts, place, gate, hn, dy, w)


def grads_body(xe, dgp, dup, hg, dyr, *rest):
    out = rest[-1]
    part = xe[...]
    shared = part.shape[1]
    out[0, 0] = tn(part, dgp[...]).astype(BF16)
    out[0, 1] = tn(part, dup[...]).astype(BF16)
    back = dyr[...]
    for b in range(hg.shape[1] // shared):
        low = b * shared
        out[0, 2, :, low : low + shared] = tn(hg[:, low : low + shared], back).astype(BF16)


def expert_grads(xe, dgp, dup, hg, dyr, shared, at, pair, held):
    micro, capacity, width = xe.shape
    ff = dgp.shape[2]
    rows = micro * capacity
    xe, dyr = (a.reshape(rows, width) for a in (xe, dyr))
    dgp, dup, hg = (a.reshape(rows, ff) for a in (dgp, dup, hg))
    thin = pl.BlockSpec((rows, shared), lambda r: (0, r))
    whole = pl.BlockSpec((rows, ff), lambda r: (0, 0))
    return pl.pallas_call(
        grads_body,
        grid=(width // shared,),
        in_specs=[thin, whole, whole, whole, thin] + [ANY] * len(held),
        out_specs=pl.BlockSpec((1, 3, shared, ff), lambda r: (at, 0, r, 0)),
        out_shape=jax.ShapeDtypeStruct((pair, 3, width, ff), BF16),
        input_output_aliases={5: 0} if held else {},
        compiler_params=pltpu.CompilerParams(vmem_limit_bytes=VMEM_LIMIT),
        cost_estimate=pl.CostEstimate(
            flops=6 * rows * width * ff, bytes_accessed=26 << 20, transcendentals=0
        ),
        name="expert_grads",
    )(xe, dgp, dup, hg, dyr, *held)


def pack_body(wg, wu, wd, out):
    shared = out.shape[2]
    out[0, 0] = wg[0]
    out[0, 1] = wu[0]
    for b in range(out.shape[3] // shared):
        low = b * shared
        out[0, 2, :, low : low + shared] = wd[0, low : low + shared, :]


def pack(wg, wu, wd, first, pair):
    _, shared, ff = wg.shape
    block = pl.BlockSpec((1, shared, ff), lambda i: (first + i, 0, 0))
    return pl.pallas_call(
        pack_body,
        grid=(pair,),
        in_specs=[block, block, pl.BlockSpec((1, ff, shared), lambda i: (first + i, 0, 0))],
        out_specs=pl.BlockSpec((1, 3, shared, ff), lambda i: (i, 0, 0, 0)),
        out_shape=jax.ShapeDtypeStruct((pair, 3, shared, ff), BF16),
        cost_estimate=pl.CostEstimate(
            flops=0, bytes_accessed=pair * 12 * shared * ff, transcendentals=0
        ),
        name="pack",
    )(wg, wu, wd)


def unpack_body(x, *refs):
    gg, gu, gd = refs[-3:]
    shared = x.shape[2]
    gg[0] = x[0, 0].astype(F32)
    gu[0] = x[0, 1].astype(F32)
    for b in range(x.shape[3] // shared):
        low = b * shared
        gd[0, low : low + shared, :] = x[0, 2, :, low : low + shared].astype(F32)


def unpack(x, held, first, experts):
    pair, _, shared, ff = x.shape
    block = pl.BlockSpec((1, shared, ff), lambda i: (first + i, 0, 0))
    return pl.pallas_call(
        unpack_body,
        grid=(pair,),
        in_specs=[pl.BlockSpec((1, 3, shared, ff), lambda i: (i, 0, 0, 0))] + [ANY] * len(held),
        out_specs=[block, block, pl.BlockSpec((1, ff, shared), lambda i: (first + i, 0, 0))],
        out_shape=[
            jax.ShapeDtypeStruct((experts, shared, ff), F32),
            jax.ShapeDtypeStruct((experts, shared, ff), F32),
            jax.ShapeDtypeStruct((experts, ff, shared), F32),
        ],
        input_output_aliases={1 + j: j for j in range(len(held))},
        compiler_params=pltpu.CompilerParams(vmem_limit_bytes=VMEM_LIMIT),
        cost_estimate=pl.CostEstimate(
            flops=0, bytes_accessed=pair * 18 * shared * ff, transcendentals=0
        ),
        name="unpack",
    )(x, *held)


def places():
    row, col = lax.axis_index("row"), lax.axis_index("col")
    n_row, n_col = lax.axis_size("row"), lax.axis_size("col")
    return row, col, n_row, n_col


def remote(src, dst, send_sem, recv_sem, where):
    return pltpu.make_async_remote_copy(
        src_ref=src,
        dst_ref=dst,
        send_sem=send_sem,
        recv_sem=recv_sem,
        device_id=where,
        device_id_type=MESH,
    )


def shake(sources, targets):
    barrier = pltpu.get_barrier_semaphore()
    for ok, where in sources:
        if ok is True:
            pl.semaphore_signal(barrier, inc=1, device_id=where, device_id_type=MESH)
        else:

            @pl.when(ok)
            def _():
                pl.semaphore_signal(barrier, inc=1, device_id=where, device_id_type=MESH)

    count = 0
    for ok in targets:
        count = count + (1 if ok is True else jnp.where(ok, 1, 0))
    pl.semaphore_wait(barrier, count)


def line_peers():
    row, col, n_row, n_col = places()
    pair, core = col // 2, col % 2
    return [
        (True, (row, pair * 2 + 1 - core)),
        (pair > 0, (row, (pair - 1) * 2 + core)),
        (pair < n_col // 2 - 1, (row, (pair + 1) * 2 + core)),
    ]


def row_peers():
    row, col, n_row, n_col = places()
    return [(True, ((row + k) % n_row, col)) for k in range(1, n_row)]


def col_slice(ref, index, size):
    return ref.at[..., pl.ds(pl.multiple_of(index * size, size), size)]


def line_gather(axes, ins, outs, sems):
    own_sem, right_s, right_r, left_s, left_r, side_s, side_r = sems
    n = len(ins)
    row, col, n_row, n_col = places()
    pairs, pair, core = n_col // 2, col // 2, col % 2

    def at(pair_index, core_index):
        return (row, pair_index * 2 + core_index)

    def block(j, source):
        size = ins[j].shape[axes[j]]
        if axes[j] == 0:
            return outs[j].at[pl.ds(pl.multiple_of(source * size, size), size)]
        return col_slice(outs[j], source, size)

    def right(j, s):
        source = (pair - s) * 2 + core
        src = ins[j] if s == 0 else block(j, source)
        return remote(src, block(j, source), right_s.at[j, s], right_r.at[j, s], at(pair + 1, core))

    def left(j, s):
        source = (pair + s) * 2 + core
        src = ins[j] if s == 0 else block(j, source)
        return remote(src, block(j, source), left_s.at[j, s], left_r.at[j, s], at(pair - 1, core))

    def side(j, source_pair, first=False):
        source = source_pair * 2 + core
        src = ins[j] if first else block(j, source)
        return remote(
            src,
            block(j, source),
            side_s.at[j, source_pair],
            side_r.at[j, source_pair],
            at(pair, 1 - core),
        )

    def arrived(j, recvs, slot, source):
        remote(
            ins[j], block(j, source), recvs.at[j, slot], recvs.at[j, slot], at(pair, 1 - core)
        ).wait_recv()

    def own(j):
        return pltpu.make_async_copy(ins[j], block(j, col), own_sem.at[j])

    def begin():
        for j in range(n):

            @pl.when(pair < pairs - 1)
            def _():
                right(j, 0).start()

            @pl.when(pair > 0)
            def _():
                left(j, 0).start()

        for j in range(n):
            side(j, pair, True).start()
            own(j).start()

    def middle():
        for s in range(1, pairs):
            for j in range(n):

                @pl.when(pair >= s)
                def _():
                    arrived(j, right_r, s - 1, (pair - s) * 2 + core)

                    @pl.when(pair < pairs - 1)
                    def _():
                        right(j, s).start()

                    side(j, pair - s).start()

                @pl.when(pair + s < pairs)
                def _():
                    arrived(j, left_r, s - 1, (pair + s) * 2 + core)

                    @pl.when(pair > 0)
                    def _():
                        left(j, s).start()

                    side(j, pair + s).start()

    def end():
        for j in range(n):
            own(j).wait()
            for p in range(pairs):
                side(j, p).wait_send()
                arrived(j, side_r, p, p * 2 + 1 - core)
            for s in range(pairs):

                @pl.when((pair >= s) & (pair < pairs - 1))
                def _():
                    right(j, s).wait_send()

                @pl.when((pair + s < pairs) & (pair > 0))
                def _():
                    left(j, s).wait_send()

    return begin, middle, end


def line_sems(n, pairs):
    dma = pltpu.SemaphoreType.DMA
    return [dma((n,))] + [dma((n, pairs))] * 6


def front_body(tokens, gains, wq, wk, wv, wo, wr, *refs):
    x_o, gains_o, wh_o, wo_o, wr_o = refs[:5]
    wide = refs[5:8]
    line, (heads_s, heads_r, row_s, row_r, own_s) = refs[8:15], refs[15:]
    row, col, n_row, n_col = places()
    head = wh_o.shape[2]
    part = wq.shape[0]
    begin, middle, end = line_gather((1, 1), [tokens, gains], [x_o, gains_o], line)
    small = [(wq, wide[0]), (wk, wide[1]), (wv, wide[2]), (wo, wo_o), (wr, wr_o)]

    def small_dst(k, source):
        src, dst = small[k]
        if k < 4:
            return col_slice(dst, source, src.shape[1])
        return dst.at[pl.ds(pl.multiple_of(source * src.shape[0], src.shape[0]), src.shape[0]), :]

    def small_copy(k, step):
        return remote(
            small[k][0],
            small_dst(k, row),
            row_s.at[k, step],
            row_r.at[k, step],
            ((row + step) % n_row, col),
        )

    def small_come(k, step):
        source = (row + n_row - step) % n_row
        return remote(
            small[k][0], small_dst(k, source), row_s.at[k, step], row_r.at[k, step], (source, col)
        )

    def small_own(k):
        return pltpu.make_async_copy(small[k][0], small_dst(k, row), own_s.at[k])

    def heads_dst(m, source):
        return wh_o.at[m, pl.ds(pl.multiple_of(source * part, part), part), :]

    def heads(m, step):
        where = (col + step) % n_col
        return remote(
            col_slice(wide[m], where, head),
            heads_dst(m, col),
            heads_s.at[m, step],
            heads_r.at[m, step],
            (row, where),
        )

    def heads_come(m, step):
        source = (col + n_col - step) % n_col
        return remote(
            heads_dst(m, source),
            heads_dst(m, source),
            heads_s.at[m, step],
            heads_r.at[m, step],
            (row, source),
        )

    def heads_own(m):
        return pltpu.make_async_copy(
            col_slice(wide[m], col, head), heads_dst(m, col), own_s.at[5 + m]
        )

    peers = [(True, (row, (col + k) % n_col)) for k in range(1, n_col)] + row_peers()
    shake(peers, [ok for ok, _ in peers])
    for k in range(5):
        for step in range(1, n_row):
            small_copy(k, step).start()
        small_own(k).start()
    begin()
    for k in range(3):
        small_own(k).wait()
        for step in range(1, n_row):
            small_come(k, step).wait_recv()
    for m in range(3):
        heads_own(m).start()
        for step in range(1, n_col):
            heads(m, step).start()
    middle()
    end()
    for k in range(5):
        if k >= 3:
            small_own(k).wait()
        for step in range(1, n_row):
            small_copy(k, step).wait_send()
            if k >= 3:
                small_come(k, step).wait_recv()
    for m in range(3):
        heads_own(m).wait()
        for step in range(1, n_col):
            heads(m, step).wait_send()
            heads_come(m, step).wait_recv()


def front(tokens, gains, wq, wk, wv, wo, wr, head, ident):
    n_row, n_col = lax.axis_size("row"), lax.axis_size("col")
    rows, part = tokens.shape
    width = part * n_col
    dma = pltpu.SemaphoreType.DMA
    shapes = [
        ((rows, width), BF16),
        ((gains.shape[0], width), F32),
        ((3, width, head), BF16),
        ((wo.shape[0], wo.shape[1] * n_row), BF16),
        ((wr.shape[0] * n_row, part), BF16),
    ] + [((part, wq.shape[1] * n_row), BF16)] * 3
    return pl.pallas_call(
        front_body,
        in_specs=[ANY] * 7,
        out_specs=[ANY] * 8,
        out_shape=[jax.ShapeDtypeStruct(s, t) for s, t in shapes],
        scratch_shapes=line_sems(2, n_col // 2)
        + [
            dma((3, n_col)),
            dma((3, n_col)),
            dma((5, n_row)),
            dma((5, n_row)),
            dma((8,)),
        ],
        compiler_params=pltpu.CompilerParams(collective_id=ident, has_side_effects=True),
        cost_estimate=pl.CostEstimate(
            flops=0, bytes_accessed=rows * width * 32, transcendentals=0
        ),
        name="front",
    )(tokens, gains, wq, wk, wv, wo, wr)


def middle_body(axes, *refs):
    n = len(axes)
    begin, middle, end = line_gather(axes, refs[:n], refs[n : 2 * n], refs[2 * n :])
    sources = line_peers()
    shake(sources, [ok for ok, _ in sources])
    begin()
    middle()
    end()


def middle_gather(arrays, axes, ident):
    n_col, n = lax.axis_size("col"), len(arrays)
    shapes = [
        tuple(d * n_col if at == axis else d for at, d in enumerate(a.shape))
        for a, axis in zip(arrays, axes)
    ]
    return pl.pallas_call(
        functools.partial(middle_body, axes),
        in_specs=[ANY] * n,
        out_specs=[ANY] * n,
        out_shape=[jax.ShapeDtypeStruct(s, a.dtype) for s, a in zip(shapes, arrays)],
        scratch_shapes=line_sems(n, n_col // 2),
        compiler_params=pltpu.CompilerParams(collective_id=ident, has_side_effects=True),
        cost_estimate=pl.CostEstimate(
            flops=0, bytes_accessed=sum(math.prod(s) for s in shapes) * 32, transcendentals=0
        ),
        name="middle_gather",
    )(*arrays)


def scatter_body(part, stage, local, *refs):
    n_in = (1, 2, 4, 4)[stage]
    n_out = (1, 2, 4, 4)[stage]
    if local:
        place, slots, refs = refs[0], refs[1 : 1 + local], refs[local:]
    x, ins = refs[0], refs[1:n_in]
    out, outs = refs[n_in], refs[n_in + 1 : n_in + n_out]
    rest = refs[n_in + n_out :]
    acc, side, from_left, from_right, load, side_s, side_r = rest[:7]
    right_s, right_r, left_s, left_r = rest[7:11]
    if local:
        give, chosen, held, held_s = rest[11:15]
        rest = rest[4:]
    row, col, n_row, n_col = places()
    pairs, pair, core = n_col // 2, col // 2, col % 2
    rows = out.shape[0]
    cuts = load.shape[1]
    height = rows // cuts
    tile = min(256, height)

    def at(pair_index, core_index):
        return (row, pair_index * 2 + core_index)

    def block(owner, q):
        return x.at[
            pl.ds(q * height, height), pl.ds(pl.multiple_of(owner * part, part), part)
        ]

    def cut(ref, d, q):
        return ref.at[d, pl.ds(q * height, height)]

    def fetch(d, q):
        return pltpu.make_async_copy(block(d * 2 + core, q), cut(acc, d, q), load.at[d, q])

    def across(d, q):
        return remote(
            cut(give, d, q) if local else block(d * 2 + 1 - core, q),
            cut(side, d, q),
            side_s.at[d, q],
            side_r.at[d, q],
            at(pair, 1 - core),
        )

    def right(d, q):
        return remote(
            cut(acc, d, q),
            cut(from_left, d, q),
            right_s.at[d, q],
            right_r.at[d, q],
            at(pair + 1, core),
        )

    def left(d, q):
        return remote(
            cut(acc, d, q),
            cut(from_right, d, q),
            left_s.at[d, q],
            left_r.at[d, q],
            at(pair - 1, core),
        )

    copies, arrivals, own = [], [], []
    if stage:
        small_s, small_r, own_s = rest[11:14]
        extra, extra_o = ins[0], outs[0]
        here, ring = (row, n_row) if stage == 2 else (col, n_col)
        for k in range(1, ring):
            where, source = (here + k) % ring, (here + ring - k) % ring
            to = (where, col) if stage == 2 else (row, where)
            copies.append(remote(extra, extra_o.at[here], small_s.at[k], small_r.at[k], to))
            arrivals.append(remote(extra, extra_o.at[source], small_s.at[k], small_r.at[k], to))
        own.append(pltpu.make_async_copy(extra, extra_o.at[here], own_s))
    if stage == 2:
        give_s, give_r, keep_s = rest[14:]
        per = n_col // n_row
        for m in range(2):
            src, dst = ins[1 + m], outs[1 + m]

            def block_of(r):
                return src.at[pl.ds(r * per, per)]

            for step in range(1, n_row):
                where, source = (row + step) % n_row, (row + n_row - step) % n_row
                sems = (give_s.at[m, step], give_r.at[m, step])
                copies.append(remote(block_of(where), dst.at[row], *sems, (where, col)))
                arrivals.append(remote(block_of(where), dst.at[source], *sems, (where, col)))
            own.append(pltpu.make_async_copy(block_of(row), dst.at[row], keep_s.at[m]))
    if stage == 3:
        give_s, give_r, keep_s = rest[14:]
        for m in range(2):
            src, dst = ins[1 + m], outs[1 + m]
            size = src.shape[1 - m] // n_col

            def block_for(c):
                at_c = pl.ds(pl.multiple_of(c * size, size), size)
                return src.at[:, at_c, :] if m == 0 else src.at[at_c, :]

            for step in range(1, n_col):
                where, source = (col + step) % n_col, (col + n_col - step) % n_col
                sems = (give_s.at[m, step], give_r.at[m, step])
                copies.append(remote(block_for(where), dst.at[col], *sems, (row, where)))
                arrivals.append(remote(block_for(where), dst.at[source], *sems, (row, where)))
            own.append(pltpu.make_async_copy(block_for(col), dst.at[col], keep_s.at[m]))
    if stage:
        peers = [(True, (row, (col + k) % n_col)) for k in range(1, n_col)]
    else:
        peers = line_peers()
    if stage == 2:
        peers += row_peers()
    shake(peers, [ok for ok, _ in peers])
    order = []
    for t in range(pairs):
        for d in (pairs - 1 - t, t):
            if d not in order:
                order.append(d)
    if local:
        micro, capacity = held.shape[2], held.shape[3]
        group = chosen.shape[1]
        owners = []
        for d in order:
            owners += [d * 2 + 1 - core, d * 2 + core]

        def bring(n):
            return [
                pltpu.make_async_copy(
                    slots[e].at[:, :, pl.ds(pl.multiple_of(owners[n] * part, part), part)],
                    held.at[n % 2, e],
                    held_s.at[n % 2, e],
                )
                for e in range(local)
            ]

        def make(n, into):
            for c in bring(n):
                c.wait()
            if n + 1 < len(owners):
                for c in bring(n + 1):
                    c.start()
            steps = group // tile

            def step(i, _):
                g, at_row = i // steps, pl.multiple_of((i % steps) * tile, tile)
                total = None
                for e in range(local):
                    term = nn(
                        chosen[g, pl.ds(at_row, tile), e * capacity : (e + 1) * capacity],
                        held[n % 2, e, g],
                    )
                    total = term if total is None else total + term
                into[pl.ds(pl.multiple_of(i * tile, tile), tile), :] = total.astype(BF16)
                return 0

            lax.fori_loop(0, micro * steps, step, 0)

        def make_pair(m):
            d = order[m]
            make(2 * m, give.at[d])
            for q in range(cuts):
                across(d, q).start()
            make(2 * m + 1, acc.at[d])

        for c in bring(0):
            c.start()

        def choose(i, _):
            steps = group // tile
            g, at_row = i // steps, pl.multiple_of((i % steps) * tile, tile)
            for e in range(local):
                slot = lax.broadcasted_iota(jnp.int32, (tile, capacity), 1)
                hit = slot == place[g, pl.ds(at_row, tile), e : e + 1]
                chosen[g, pl.ds(at_row, tile), e * capacity : (e + 1) * capacity] = jnp.where(
                    hit, 1.0, 0.0
                ).astype(BF16)
            return 0

        lax.fori_loop(0, micro * (group // tile), choose, 0)
    else:
        for d in order:
            for q in range(cuts):
                across(d, q).start()
                fetch(d, q).start()
    for c in copies + own:
        c.start()

    def add(q, into, *sources):
        def step(i, _):
            lines = pl.ds(pl.multiple_of(q * height + i * tile, tile), tile)
            total = sources[0][lines, :].astype(F32)
            for ref in sources[1:]:
                total = total + ref[lines, :].astype(F32)
            into[lines, :] = total.astype(into.dtype)
            return 0

        lax.fori_loop(0, height // tile, step, 0)

    def ready(d, q):
        if not local:
            fetch(d, q).wait()
        across(d, q).wait_recv()

    def go_right(d, q):
        ready(d, q)

        @pl.when(pair > 0)
        def _():
            right(d, q).wait_recv()
            add(q, acc.at[d], acc.at[d], side.at[d], from_left.at[d])

        @pl.when(pair == 0)
        def _():
            add(q, acc.at[d], acc.at[d], side.at[d])

        right(d, q).start()

    def go_left(d, q):
        ready(d, q)

        @pl.when(pair < pairs - 1)
        def _():
            left(d, q).wait_recv()
            add(q, acc.at[d], acc.at[d], side.at[d], from_right.at[d])

        @pl.when(pair == pairs - 1)
        def _():
            add(q, acc.at[d], acc.at[d], side.at[d])

        left(d, q).start()

    if local:
        for m in range(2):
            make_pair(m)
        for q in range(cuts):

            @pl.when(pair == 0)
            def _():
                go_right(pairs - 1, q)

            @pl.when(pair == pairs - 1)
            def _():
                go_left(0, q)

        for m in range(2, pairs):
            make_pair(m)
    for t in range(pairs - 1):
        far, near = pairs - 1 - t, t
        go_far, go_near = far > pair, near < pair
        if local and t == 0:
            go_far, go_near = go_far & (pair > 0), go_near & (pair < pairs - 1)
        for q in range(cuts):

            @pl.when(go_far)
            def _():
                go_right(far, q)

            @pl.when(go_near)
            def _():
                go_left(near, q)

    for q in range(cuts):
        ready(pair, q)

        @pl.when(pair == 0)
        def _():
            left(pair, q).wait_recv()
            add(q, out, acc.at[pair], side.at[pair], from_right.at[pair])

        @pl.when(pair == pairs - 1)
        def _():
            right(pair, q).wait_recv()
            add(q, out, acc.at[pair], side.at[pair], from_left.at[pair])

        @pl.when((pair > 0) & (pair < pairs - 1))
        def _():
            left(pair, q).wait_recv()
            right(pair, q).wait_recv()
            add(q, out, acc.at[pair], side.at[pair], from_left.at[pair], from_right.at[pair])

    for d in range(pairs):
        for q in range(cuts):
            across(d, q).wait_send()

            @pl.when(pair < d)
            def _():
                right(d, q).wait_send()

            @pl.when(pair > d)
            def _():
                left(d, q).wait_send()

    for c in copies:
        c.wait_send()
    for c in arrivals:
        c.wait_recv()
    for c in own:
        c.wait()


def scatter_col(x, ident, stage=0, others=(), place=None):
    n_row, n_col = lax.axis_size("row"), lax.axis_size("col")
    pairs, per = n_col // 2, n_col // n_row
    local = 0 if place is None else len(x)
    if local:
        micro, group, _ = place.shape
        capacity = x[0].shape[1]
        rows, part = micro * group, x[0].shape[2] // n_col
    else:
        rows, part = x.shape[0], x.shape[1] // n_col
    cuts = 4 if rows % 1024 == 0 else 1
    dma = pltpu.SemaphoreType.DMA
    buffer = pltpu.VMEM((pairs, rows, part), BF16)
    scratch = [buffer] * 4 + [dma((pairs, cuts))] * 7
    if local:
        scratch += [
            buffer,
            pltpu.VMEM((micro, group, local * capacity), BF16),
            pltpu.VMEM((2, local, micro, capacity, part), BF16),
            dma((2, local)),
        ]
    out_shape = [jax.ShapeDtypeStruct((rows, part), F32)]
    if stage:
        extra, ring = others[0], n_row if stage == 2 else n_col
        out_shape.append(jax.ShapeDtypeStruct((ring,) + extra.shape, extra.dtype))
        scratch += [dma((ring,)), dma((ring,)), dma(())]
    if stage == 2:
        scratch += [dma((2, n_row)), dma((2, n_row)), dma((2,))]
        for value in others[1:]:
            out_shape.append(jax.ShapeDtypeStruct((n_row, per) + value.shape[1:], BF16))
    if stage == 3:
        heads, branch = others[1:]
        scratch += [dma((2, n_col)), dma((2, n_col)), dma((2,))]
        out_shape += [
            jax.ShapeDtypeStruct((n_col, 3, heads.shape[1] // n_col, heads.shape[2]), BF16),
            jax.ShapeDtypeStruct((n_col, branch.shape[0] // n_col, branch.shape[1]), BF16),
        ]
    first = [pl.BlockSpec(memory_space=pltpu.VMEM)] + [ANY] * local if local else [ANY]
    values = (place, *x) if local else (x,)
    return pl.pallas_call(
        functools.partial(scatter_body, part, stage, local),
        in_specs=first + [ANY] * len(others),
        out_specs=[pl.BlockSpec(memory_space=pltpu.VMEM)] + [ANY] * (len(out_shape) - 1),
        out_shape=out_shape,
        scratch_shapes=scratch,
        compiler_params=pltpu.CompilerParams(
            vmem_limit_bytes=VMEM_LIMIT, collective_id=ident, has_side_effects=True
        ),
        cost_estimate=pl.CostEstimate(
            flops=0, bytes_accessed=rows * part * n_col * 40, transcendentals=0
        ),
        name="scatter_col",
    )(*values, *others)


def shards(
    tokens,
    gain_attn,
    gain_ffn,
    gain_query,
    gain_key,
    w_query,
    w_key,
    w_value,
    w_out,
    w_router,
    w_gate,
    w_up,
    w_down,
    routes,
    lengths,
    cotangent,
):
    n_col = lax.axis_size("col")
    n_row = lax.axis_size("row")
    col = lax.axis_index("col")
    micro, spans = lengths.shape
    rows, part = tokens.shape
    group = rows // micro
    width = part * n_col
    head = gain_query.shape[0]
    local_exp = w_gate.shape[0]
    experts = local_exp * n_col
    topk = routes.shape[1]
    capacity = 2 * group * topk // experts
    local_heads = w_out.shape[0] // head
    hd = w_out.shape[0] * n_col
    scale = head ** (-0.5)

    def gather(value, axis_name, axis):
        return lax.all_gather(value, axis_name, axis=axis, tiled=True)

    def mine(value, axis):
        size = value.shape[axis] // n_col
        return lax.dynamic_slice_in_dim(value, col * size, size, axis)

    shared = w_down.shape[2]
    pair = 2 if local_exp % 2 == 0 else 1
    big = [
        gather(pack(w_gate, w_up, w_down, at, pair), "row", 2) for at in range(0, local_exp, pair)
    ]
    inputs_low, gains, w_heads, rows_o, rows_r, *wide = front(
        tokens,
        jnp.stack([gain_attn, gain_ffn]),
        w_query,
        w_key,
        w_value,
        w_out,
        w_router.T,
        head,
        0,
    )

    segment, position, live = jax.vmap(lambda l: layout(l, group))(lengths)
    position = position.reshape(rows)
    live = live.reshape(rows)
    upstream_part = cotangent.astype(F32) * live[:, None]
    member = jnp.any(
        routes[:, None, :] == jnp.arange(experts, dtype=jnp.int32)[None, :, None], -1
    )
    member_f = member.astype(F32)
    member_loc = mine(member_f, 1).reshape(micro, group, local_exp)
    lower = (
        jnp.arange(group, dtype=jnp.int32)[:, None] > jnp.arange(group, dtype=jnp.int32)[None, :]
    ).astype(BF16)
    before = jnp.einsum("st,gte->gse", lower, member_loc.astype(BF16), preferred_element_type=F32)
    place = jnp.where(member_loc > 0, before, -1.0).astype(jnp.int32)
    counts = jnp.sum(member_loc, 1).astype(jnp.int32).T
    place_t = place.transpose(2, 0, 1)[:, :, None, :]

    inputs = inputs_low.astype(F32)
    scale_one = inverse_rms(inputs)
    normed = (inputs * scale_one * gains[0]).astype(BF16)
    all_heads = jnp.concatenate([w_heads[j] for j in range(3)], 1)
    query_pre, key_pre, value_pre = jnp.split(nn(normed, all_heads), 3, 1)
    shape = (rows, local_heads, head)
    cosine, sine = rope_tables(position, head)

    def head_norm(values, gain):
        return rotary(values * inverse_rms(values) * gain, cosine, sine)

    query_rot, query_pull = jax.vjp(head_norm, query_pre.reshape(shape), gain_query)
    key_rot, key_pull = jax.vjp(head_norm, key_pre.reshape(shape), gain_key)
    batch = (micro, group, local_heads, head)
    queries = query_rot.astype(BF16).reshape(batch)
    keys_low = key_rot.astype(BF16).reshape(batch)
    values_low = value_pre.astype(BF16).reshape(batch)
    same = (segment[:, :, None] == segment[:, None, :])[:, None]

    def scores_of():
        raw = jnp.einsum("gqhd,gkhd->ghqk", queries, keys_low, preferred_element_type=F32) * scale
        return jnp.where(same, raw, MASKED)

    scores = scores_of()
    highest = jnp.max(scores, -1, keepdims=True)
    log_total = highest + jnp.log(jnp.sum(jnp.exp(scores - highest), -1, keepdims=True))
    probs_low = jnp.exp(scores - log_total).astype(BF16)
    attended = jnp.einsum(
        "ghqk,gkhd->gqhd", probs_low, values_low, preferred_element_type=F32
    ).astype(BF16)
    attended_full, full_o, full_rt, upstream_low = middle_gather(
        [attended.reshape(rows, local_heads * head), rows_o, rows_r, upstream_part.astype(BF16)],
        (1, 0, 1, 1),
        1,
    )
    full_r = full_rt.T

    hidden = inputs + nn(attended_full, full_o)
    scale_two = inverse_rms(hidden)
    normed_ffn = (hidden * scale_two * gains[1]).astype(BF16)
    logits = nn(normed_ffn, full_r)
    peak = jnp.max(jnp.where(member, logits, -jnp.inf), -1, keepdims=True)
    raised = jnp.where(member, jnp.exp(jnp.where(member, logits - peak, 0.0)), 0.0)
    gates = raised / jnp.sum(raised, -1, keepdims=True)
    gate_t = mine(gates, 1).reshape(micro, group, local_exp).transpose(2, 0, 1)[:, :, None, :]
    upstream_full = upstream_low.reshape(micro, group, width)
    hn = normed_ffn.reshape(micro, group, width)

    outs, weight_grads, grad = [], [], None
    for e in range(local_exp):
        xe, dyr, hg, dgp, dup, ye, dxe, tok = expert_pass(
            counts[e],
            place_t[e],
            gate_t[e],
            hn,
            upstream_full,
            big[e // pair],
            e % pair,
            capacity,
            shared,
        )
        held = () if e % pair == 0 else (grad,)
        grad = expert_grads(xe, dgp, dup, hg, dyr, shared, e % pair, pair, held)
        hn, upstream_full, ye, dxe, tok, grad = lax.optimization_barrier(
            (hn, upstream_full, ye, dxe, tok, grad)
        )
        outs.append((ye, dxe, tok))
        if e % pair == pair - 1:
            weight_grads.append(lax.psum_scatter(grad, "row", scatter_dimension=2, tiled=True))

    def tie(value, e):
        value, weight_grads[e] = lax.optimization_barrier((value, weight_grads[e]))
        return value

    row = lax.axis_index("row")
    back_sum, tok = scatter_col(
        [o[1] for o in outs], 2, 1, (jnp.stack([o[2] for o in outs]),), place
    )
    tok = tok.reshape((experts,) + tok.shape[2:])
    hidden_part = tokens.astype(F32) + nn(attended_full, mine(full_o, 1))
    gate_dots = tok[:, :, 0].reshape(experts, rows).T
    hidden_part = mine(hidden, 1)

    selected = gates * (gate_dots - jnp.sum(gates * gate_dots, -1, keepdims=True))
    logit_grad = selected.astype(BF16)
    router_part = mine(full_r, 0)
    normed_grad = back_sum + nt(logit_grad, router_part)
    grad_router = tn(mine(normed_ffn, 1), logit_grad)
    scaled_two = hidden_part * scale_two
    grad_gain_ffn = jnp.sum(normed_grad * scaled_two, 0)
    dot_two = jnp.sum(tok[:, :, 1].reshape(experts, rows), 0) + jnp.sum(
        logit_grad.astype(F32) * logits, 1
    )
    hidden_grad = (
        upstream_part
        + scale_two * (normed_grad * gain_ffn)
        - hidden_part * scale_two**2 * dot_two[:, None] / width
    )

    branch_grad = hidden_grad.astype(BF16)
    (attended_grad,) = scatter_col(nt(branch_grad, mine(full_o, 1)).astype(BF16), 3)
    attended_grad = attended_grad.astype(BF16).reshape(batch)
    grad_out = tn(attended_full, branch_grad)
    scores_again = scores_of()
    probs = jnp.exp(scores_again - log_total)
    probs_again = probs.astype(BF16)
    probs_grad = jnp.einsum(
        "gqhd,gkhd->ghqk", attended_grad, values_low, preferred_element_type=F32
    )
    values_grad = jnp.einsum(
        "ghqk,gqhd->gkhd", probs_again, attended_grad, preferred_element_type=F32
    )
    score_grad = (probs * (probs_grad - jnp.sum(probs_grad * probs, -1, keepdims=True))).astype(
        BF16
    )
    query_grad_rot = (
        jnp.einsum("ghqk,gkhd->gqhd", score_grad, keys_low, preferred_element_type=F32) * scale
    )
    key_grad_rot = (
        jnp.einsum("ghqk,gqhd->gkhd", score_grad, queries, preferred_element_type=F32) * scale
    )
    query_grad, gain_query_part = query_pull(query_grad_rot.reshape(shape))
    key_grad, gain_key_part = key_pull(key_grad_rot.reshape(shape))
    flat = (rows, local_heads * head)
    heads_grad = [
        v.reshape(flat).astype(BF16) for v in (query_grad, key_grad, values_grad)
    ]
    all_grads = jnp.concatenate(heads_grad, 1)
    back_heads = nt(all_grads, all_heads)
    pre = (query_pre, key_pre, value_pre)
    dot_part = sum(jnp.sum(g.astype(F32) * p, -1) for g, p in zip(heads_grad, pre))
    sums = jnp.concatenate([dot_part, gain_query_part, gain_key_part])
    sums = jnp.pad(sums, (0, -sums.shape[0] % 1024)).reshape(-1, 128)
    heads_weights = tn(normed, all_grads).astype(BF16)
    heads_weights = jnp.stack(jnp.split(heads_weights, 3, 1))
    back_heads, mixed_slots = lax.optimization_barrier(
        (back_heads.astype(BF16), [o[0] for o in outs])
    )
    mixed_sum, sums, heads_terms, out_terms = scatter_col(
        mixed_slots, 4, 3, (sums, heads_weights, grad_out.astype(BF16)), place
    )
    mixed = (hidden_part + mixed_sum).astype(BF16)
    sums = jnp.sum(sums, 0).reshape(-1)
    dot_one = sums[:rows]
    gain_attn_part = 0.0
    for m in range(3):
        for c in range(n_col):
            columns = wide[m][:, c * local_heads * head : (c + 1) * local_heads * head]
            gain_attn_part = gain_attn_part + jnp.sum(
                columns.astype(F32) * heads_terms[c, m].astype(F32), -1
            )
    smalls = jnp.concatenate(
        [
            gain_attn_part,
            grad_gain_ffn,
            sums[rows : rows + 2 * head],
            grad_router.T.reshape(-1),
        ]
    ).reshape(-1, 128)
    back_heads, mixed = lax.optimization_barrier((back_heads, mixed))
    normed_back, smalls, heads_terms, out_terms = scatter_col(
        tie(back_heads, 0), 5, 2, (smalls, heads_terms, out_terms)
    )
    scale_one_part = scale_one
    inputs_part = tokens.astype(F32)
    input_grad = (
        hidden_grad
        + scale_one_part * (normed_back * gain_attn)
        - inputs_part * scale_one_part**2 * dot_one[:, None] / width
    )

    held = ()
    for e, grad in enumerate(weight_grads):
        held = unpack(grad, held, e * pair, local_exp)
    grad_gate, grad_up, grad_down = held

    heads_terms = jnp.sum(heads_terms.astype(F32), 0)
    heads_sum = jnp.concatenate([heads_terms[j] for j in range(heads_terms.shape[0])], -1)
    grad_query, grad_key, grad_value = heads_sum[0], heads_sum[1], heads_sum[2]
    out_terms = jnp.sum(out_terms.astype(F32), 0)
    grad_out = jnp.concatenate([out_terms[j] for j in range(out_terms.shape[0])], -1)
    row = lax.axis_index("row")
    total = jnp.sum(smalls, 0).reshape(-1)
    grad_gain_attn, grad_gain_ffn = total[:part] / gain_attn, total[part : 2 * part]
    grad_gain_query = total[2 * part : 2 * part + head]
    grad_gain_key = total[2 * part + head : 2 * part + 2 * head]
    grad_router = lax.dynamic_slice_in_dim(
        total[2 * part + 2 * head :].reshape(experts, part), row * (experts // n_row), experts // n_row, 0
    ).T
    return (
        mixed,
        input_grad,
        grad_gain_attn,
        grad_gain_ffn,
        grad_gain_query,
        grad_gain_key,
        grad_query,
        grad_key,
        grad_value,
        grad_out,
        grad_router,
        grad_gate,
        grad_up,
        grad_down,
    )


def solution(mesh):
    placed = (
        P("row", "col"),
        P("col"),
        P("col"),
        P(),
        P(),
        P("col", "row"),
        P("col", "row"),
        P("col", "row"),
        P("col", "row"),
        P("col", "row"),
        P("col", "row", None),
        P("col", "row", None),
        P("col", None, "row"),
        P("row", None),
        P("row", None),
        P("row", "col"),
    )
    return jax.shard_map(
        shards,
        mesh=mesh,
        in_specs=placed,
        out_specs=(
            P("row", "col"),
            P("row", "col"),
            P("col"),
            P("col"),
            P(),
            P(),
            P("col", "row"),
            P("col", "row"),
            P("col", "row"),
            P("col", "row"),
            P("col", "row"),
            P("col", "row", None),
            P("col", "row", None),
            P("col", None, "row"),
        ),
        check_vma=False,
    )
```

```python
import functools
import math

import jax
import jax.numpy as jnp
from jax import lax
from jax.experimental import pallas as pl
from jax.experimental.pallas import tpu as pltpu
from jax.sharding import PartitionSpec as P

EPSILON = 1e-06
ROPE_BASE = 10000.0
MASKED = -1e30
F32 = jnp.float32
BF16 = jnp.bfloat16
VMEM_LIMIT = 60 * 1024 * 1024
MESH = pl.DeviceIdType.MESH
ANY = pl.BlockSpec(memory_space=pl.ANY)


def inverse_rms(values):
    return lax.rsqrt(jnp.mean(values * values, -1, keepdims=True) + EPSILON)


def rope_tables(position, head):
    half = head // 2
    inverse = jnp.exp(-math.log(ROPE_BASE) * 2.0 / head * jnp.arange(half, dtype=F32))
    angles = position[:, None] * inverse[None, :]
    return jnp.cos(angles)[:, None, :], jnp.sin(angles)[:, None, :]


def rotary(values, cosine, sine):
    half = values.shape[-1] // 2
    first = values[..., :half]
    second = values[..., half:]
    return jnp.concatenate([first * cosine - second * sine, second * cosine + first * sine], -1)


def layout(lengths_row, group):
    ends = jnp.cumsum(lengths_row)
    starts = ends - lengths_row
    row_index = jnp.arange(group, dtype=jnp.int32)
    segment = jnp.sum((row_index[:, None] >= ends[None, :]).astype(jnp.int32), 1)
    member = segment[:, None] == jnp.arange(lengths_row.shape[0], dtype=jnp.int32)[None, :]
    position = (row_index - jnp.sum(jnp.where(member, starts[None, :], 0), 1)).astype(F32)
    live = (segment < lengths_row.shape[0] - 1).astype(F32)
    return (segment, position, live)


def nn(a, b):
    return lax.dot_general(a, b, (((1,), (0,)), ((), ())), preferred_element_type=F32)


def nt(a, b):
    return lax.dot_general(a, b, (((1,), (1,)), ((), ())), preferred_element_type=F32)


def tn(a, b):
    return lax.dot_general(a, b, (((0,), (0,)), ((), ())), preferred_element_type=F32)


def expert_body(shared, counts, place, gate, hn, dy, w, xe_o, dyr_o, hg_o, dgp_o, dup_o, ye_o, dxe_o, tok_o):
    g, i = pl.program_id(0), pl.program_id(1)
    rows = xe_o.shape[1]
    width, ff = w.shape[2:]
    base = i * rows

    @pl.when(i == 0)
    def _():
        tok_o[...] = jnp.zeros_like(tok_o)

    @pl.when(counts[g] <= base)
    def _():
        for ref in (xe_o, dyr_o, hg_o, dgp_o, dup_o, ye_o, dxe_o):
            ref[...] = jnp.zeros_like(ref)

    @pl.when(counts[g] > base)
    def _():
        slot = lax.broadcasted_iota(jnp.int32, (rows, place.shape[2]), 0) + base
        hit = slot == place[0]
        pick = jnp.where(hit, 1.0, 0.0).astype(BF16)
        weight = jnp.sum(jnp.where(hit, gate[0], 0.0), 1, keepdims=True)
        xe = nn(pick, hn[0]).astype(BF16)
        xe_o[0] = xe
        gp = nn(xe, w[0, 0])
        up = nn(xe, w[0, 1])
        sig = jax.nn.sigmoid(gp)
        silu = gp * sig
        hid = silu * up
        hg = (hid * weight).astype(BF16)
        hg_o[0] = hg
        dyr = nn(pick, dy[0]).astype(BF16)
        dyr_o[0] = dyr
        parts = []
        for r in range(width // shared):
            at = r * shared
            total = None
            for b in range(ff // shared):
                low = b * shared
                term = nn(hg[:, low : low + shared], w[0, 2, at : at + shared, low : low + shared])
                total = term if total is None else total + term
            ye_o[0, :, at : at + shared] = total.astype(BF16)
        for b in range(ff // shared):
            low = b * shared
            total = None
            for r in range(width // shared):
                at = r * shared
                term = nt(dyr[:, at : at + shared], w[0, 2, at : at + shared, low : low + shared])
                total = term if total is None else total + term
            parts.append(total)
        back = jnp.concatenate(parts, 1)
        dgate = jnp.sum(back * hid, 1, keepdims=True)
        dhid = back * weight
        dgp = (dhid * up * sig * (1.0 + gp * (1.0 - sig))).astype(BF16)
        dup = (dhid * silu).astype(BF16)
        dgp_o[0] = dgp
        dup_o[0] = dup
        dots = jnp.sum(dgp.astype(F32) * gp + dup.astype(F32) * up, 1, keepdims=True)
        dxe_o[0] = (nt(dgp, w[0, 0]) + nt(dup, w[0, 1])).astype(BF16)
        tok_o[0, 0:1, :] += jnp.sum(jnp.where(hit, dgate, 0.0), 0, keepdims=True)
        tok_o[0, 1:2, :] += jnp.sum(jnp.where(hit, dots, 0.0), 0, keepdims=True)


def expert_pass(counts, place, gate, hn, dy, w, at, capacity, shared):
    width, ff = w.shape[2:]
    micro, group, _ = hn.shape
    rows = min(256, capacity)
    blocks = capacity // rows
    tall = lambda g, i, c: (g, i, 0)
    line = lambda g, i, c: (g, 0, 0)
    slots = lambda n: jax.ShapeDtypeStruct((micro, capacity, n), BF16)
    sizes = (width, width, ff, ff, ff, width, width)
    flops = 2 * micro * capacity * width * (6 * ff + 2 * group)
    return pl.pallas_call(
        functools.partial(expert_body, shared),
        grid_spec=pltpu.PrefetchScalarGridSpec(
            num_scalar_prefetch=1,
            grid=(micro, blocks),
            in_specs=[
                pl.BlockSpec((1, 1, group), line),
                pl.BlockSpec((1, 1, group), line),
                pl.BlockSpec((1, group, width), line),
                pl.BlockSpec((1, group, width), line),
                pl.BlockSpec(
                    (1, 3, width, ff), lambda g, i, c: (at, 0, 0, 0), pipeline_mode=pl.Buffered(1)
                ),
            ],
            out_specs=[pl.BlockSpec((1, rows, n), tall) for n in sizes]
            + [pl.BlockSpec((1, 2, group), line)],
        ),
        out_shape=[slots(n) for n in sizes] + [jax.ShapeDtypeStruct((micro, 2, group), F32)],
        compiler_params=pltpu.CompilerParams(vmem_limit_bytes=VMEM_LIMIT),
        cost_estimate=pl.CostEstimate(
            flops=flops, bytes_accessed=40 << 20, transcendentals=micro * capacity * ff
        ),
        name="expert_pass",
    )(counts, place, gate, hn, dy, w)


def grads_body(xe, dgp, dup, hg, dyr, *rest):
    out = rest[-1]
    part = xe[...]
    shared = part.shape[1]
    out[0, 0] = tn(part, dgp[...]).astype(BF16)
    out[0, 1] = tn(part, dup[...]).astype(BF16)
    back = dyr[...]
    for b in range(hg.shape[1] // shared):
        low = b * shared
        out[0, 2, :, low : low + shared] = tn(hg[:, low : low + shared], back).astype(BF16)


def expert_grads(xe, dgp, dup, hg, dyr, shared, at, pair, held):
    micro, capacity, width = xe.shape
    ff = dgp.shape[2]
    rows = micro * capacity
    xe, dyr = (a.reshape(rows, width) for a in (xe, dyr))
    dgp, dup, hg = (a.reshape(rows, ff) for a in (dgp, dup, hg))
    thin = pl.BlockSpec((rows, shared), lambda r: (0, r))
    whole = pl.BlockSpec((rows, ff), lambda r: (0, 0))
    return pl.pallas_call(
        grads_body,
        grid=(width // shared,),
        in_specs=[thin, whole, whole, whole, thin] + [ANY] * len(held),
        out_specs=pl.BlockSpec((1, 3, shared, ff), lambda r: (at, 0, r, 0)),
        out_shape=jax.ShapeDtypeStruct((pair, 3, width, ff), BF16),
        input_output_aliases={5: 0} if held else {},
        compiler_params=pltpu.CompilerParams(vmem_limit_bytes=VMEM_LIMIT),
        cost_estimate=pl.CostEstimate(
            flops=6 * rows * width * ff, bytes_accessed=26 << 20, transcendentals=0
        ),
        name="expert_grads",
    )(xe, dgp, dup, hg, dyr, *held)


def pack_body(wg, wu, wd, out):
    shared = out.shape[2]
    out[0, 0] = wg[0]
    out[0, 1] = wu[0]
    for b in range(out.shape[3] // shared):
        low = b * shared
        out[0, 2, :, low : low + shared] = wd[0, low : low + shared, :]


def pack(wg, wu, wd, first, pair):
    _, shared, ff = wg.shape
    block = pl.BlockSpec((1, shared, ff), lambda i: (first + i, 0, 0))
    return pl.pallas_call(
        pack_body,
        grid=(pair,),
        in_specs=[block, block, pl.BlockSpec((1, ff, shared), lambda i: (first + i, 0, 0))],
        out_specs=pl.BlockSpec((1, 3, shared, ff), lambda i: (i, 0, 0, 0)),
        out_shape=jax.ShapeDtypeStruct((pair, 3, shared, ff), BF16),
        cost_estimate=pl.CostEstimate(
            flops=0, bytes_accessed=pair * 12 * shared * ff, transcendentals=0
        ),
        name="pack",
    )(wg, wu, wd)


def unpack_body(x, *refs):
    gg, gu, gd = refs[-3:]
    shared = x.shape[2]
    gg[0] = x[0, 0].astype(F32)
    gu[0] = x[0, 1].astype(F32)
    for b in range(x.shape[3] // shared):
        low = b * shared
        gd[0, low : low + shared, :] = x[0, 2, :, low : low + shared].astype(F32)


def unpack(x, held, first, experts):
    pair, _, shared, ff = x.shape
    block = pl.BlockSpec((1, shared, ff), lambda i: (first + i, 0, 0))
    return pl.pallas_call(
        unpack_body,
        grid=(pair,),
        in_specs=[pl.BlockSpec((1, 3, shared, ff), lambda i: (i, 0, 0, 0))] + [ANY] * len(held),
        out_specs=[block, block, pl.BlockSpec((1, ff, shared), lambda i: (first + i, 0, 0))],
        out_shape=[
            jax.ShapeDtypeStruct((experts, shared, ff), F32),
            jax.ShapeDtypeStruct((experts, shared, ff), F32),
            jax.ShapeDtypeStruct((experts, ff, shared), F32),
        ],
        input_output_aliases={1 + j: j for j in range(len(held))},
        compiler_params=pltpu.CompilerParams(vmem_limit_bytes=VMEM_LIMIT),
        cost_estimate=pl.CostEstimate(
            flops=0, bytes_accessed=pair * 18 * shared * ff, transcendentals=0
        ),
        name="unpack",
    )(x, *held)


def combine_body(place, *refs):
    out = refs[-1]
    total = jnp.zeros((out.shape[1], out.shape[2]), F32)
    for e, ref in enumerate(refs[:-1]):
        slot = lax.broadcasted_iota(jnp.int32, (out.shape[1], ref.shape[1]), 1)
        pick = jnp.where(slot == place[0, :, e : e + 1], 1.0, 0.0).astype(BF16)
        total = total + nn(pick, ref[0])
    out[0] = total.astype(BF16)


def combine(place, slots):
    micro, group, local = place.shape
    capacity, width = slots[0].shape[1:]
    tile = min(256, group)
    return pl.pallas_call(
        combine_body,
        grid=(micro, group // tile),
        in_specs=[pl.BlockSpec((1, tile, local), lambda g, i: (g, i, 0))]
        + [pl.BlockSpec((1, capacity, width), lambda g, i: (g, 0, 0)) for s in slots],
        out_specs=pl.BlockSpec((1, tile, width), lambda g, i: (g, i, 0)),
        out_shape=jax.ShapeDtypeStruct((micro, group, width), BF16),
        compiler_params=pltpu.CompilerParams(vmem_limit_bytes=VMEM_LIMIT),
        cost_estimate=pl.CostEstimate(
            flops=2 * micro * group * local * capacity * width,
            bytes_accessed=micro * (local * capacity + group) * width * 2,
            transcendentals=0,
        ),
        name="combine",
    )(place, *slots).reshape(micro * group, width)


def places():
    row, col = lax.axis_index("row"), lax.axis_index("col")
    n_row, n_col = lax.axis_size("row"), lax.axis_size("col")
    return row, col, n_row, n_col


def remote(src, dst, send_sem, recv_sem, where):
    return pltpu.make_async_remote_copy(
        src_ref=src,
        dst_ref=dst,
        send_sem=send_sem,
        recv_sem=recv_sem,
        device_id=where,
        device_id_type=MESH,
    )


def shake(sources, targets):
    barrier = pltpu.get_barrier_semaphore()
    for ok, where in sources:
        if ok is True:
            pl.semaphore_signal(barrier, inc=1, device_id=where, device_id_type=MESH)
        else:

            @pl.when(ok)
            def _():
                pl.semaphore_signal(barrier, inc=1, device_id=where, device_id_type=MESH)

    count = 0
    for ok in targets:
        count = count + (1 if ok is True else jnp.where(ok, 1, 0))
    pl.semaphore_wait(barrier, count)


def line_peers():
    row, col, n_row, n_col = places()
    pair, core = col // 2, col % 2
    return [
        (True, (row, pair * 2 + 1 - core)),
        (pair > 0, (row, (pair - 1) * 2 + core)),
        (pair < n_col // 2 - 1, (row, (pair + 1) * 2 + core)),
    ]


def row_peers():
    row, col, n_row, n_col = places()
    return [(True, ((row + k) % n_row, col)) for k in range(1, n_row)]


def col_slice(ref, index, size):
    return ref.at[..., pl.ds(pl.multiple_of(index * size, size), size)]


def line_gather(axes, ins, outs, sems):
    own_sem, right_s, right_r, left_s, left_r, side_s, side_r = sems
    n = len(ins)
    row, col, n_row, n_col = places()
    pairs, pair, core = n_col // 2, col // 2, col % 2

    def at(pair_index, core_index):
        return (row, pair_index * 2 + core_index)

    def block(j, source):
        size = ins[j].shape[axes[j]]
        if axes[j] == 0:
            return outs[j].at[pl.ds(pl.multiple_of(source * size, size), size)]
        return col_slice(outs[j], source, size)

    def right(j, s):
        source = (pair - s) * 2 + core
        src = ins[j] if s == 0 else block(j, source)
        return remote(src, block(j, source), right_s.at[j, s], right_r.at[j, s], at(pair + 1, core))

    def left(j, s):
        source = (pair + s) * 2 + core
        src = ins[j] if s == 0 else block(j, source)
        return remote(src, block(j, source), left_s.at[j, s], left_r.at[j, s], at(pair - 1, core))

    def side(j, source_pair, first=False):
        source = source_pair * 2 + core
        src = ins[j] if first else block(j, source)
        return remote(
            src,
            block(j, source),
            side_s.at[j, source_pair],
            side_r.at[j, source_pair],
            at(pair, 1 - core),
        )

    def arrived(j, recvs, slot, source):
        remote(
            ins[j], block(j, source), recvs.at[j, slot], recvs.at[j, slot], at(pair, 1 - core)
        ).wait_recv()

    def own(j):
        return pltpu.make_async_copy(ins[j], block(j, col), own_sem.at[j])

    def begin():
        for j in range(n):

            @pl.when(pair < pairs - 1)
            def _():
                right(j, 0).start()

            @pl.when(pair > 0)
            def _():
                left(j, 0).start()

        for j in range(n):
            side(j, pair, True).start()
            own(j).start()

    def middle():
        for s in range(1, pairs):
            for j in range(n):

                @pl.when(pair >= s)
                def _():
                    arrived(j, right_r, s - 1, (pair - s) * 2 + core)

                    @pl.when(pair < pairs - 1)
                    def _():
                        right(j, s).start()

                    side(j, pair - s).start()

                @pl.when(pair + s < pairs)
                def _():
                    arrived(j, left_r, s - 1, (pair + s) * 2 + core)

                    @pl.when(pair > 0)
                    def _():
                        left(j, s).start()

                    side(j, pair + s).start()

    def end():
        for j in range(n):
            own(j).wait()
            for p in range(pairs):
                side(j, p).wait_send()
                arrived(j, side_r, p, p * 2 + 1 - core)
            for s in range(pairs):

                @pl.when((pair >= s) & (pair < pairs - 1))
                def _():
                    right(j, s).wait_send()

                @pl.when((pair + s < pairs) & (pair > 0))
                def _():
                    left(j, s).wait_send()

    return begin, middle, end


def line_sems(n, pairs):
    dma = pltpu.SemaphoreType.DMA
    return [dma((n,))] + [dma((n, pairs))] * 6


def front_body(tokens, gains, wq, wk, wv, wo, wr, *refs):
    x_o, gains_o, wh_o, wo_o, wr_o = refs[:5]
    wide = refs[5:8]
    line, (heads_s, heads_r, row_s, row_r, own_s) = refs[8:15], refs[15:]
    row, col, n_row, n_col = places()
    head = wh_o.shape[2]
    part = wq.shape[0]
    begin, middle, end = line_gather((1, 1), [tokens, gains], [x_o, gains_o], line)
    small = [(wq, wide[0]), (wk, wide[1]), (wv, wide[2]), (wo, wo_o), (wr, wr_o)]

    def small_dst(k, source):
        src, dst = small[k]
        if k < 4:
            return col_slice(dst, source, src.shape[1])
        return dst.at[pl.ds(pl.multiple_of(source * src.shape[0], src.shape[0]), src.shape[0]), :]

    def small_copy(k, step):
        return remote(
            small[k][0],
            small_dst(k, row),
            row_s.at[k, step],
            row_r.at[k, step],
            ((row + step) % n_row, col),
        )

    def small_come(k, step):
        source = (row + n_row - step) % n_row
        return remote(
            small[k][0], small_dst(k, source), row_s.at[k, step], row_r.at[k, step], (source, col)
        )

    def small_own(k):
        return pltpu.make_async_copy(small[k][0], small_dst(k, row), own_s.at[k])

    def heads_dst(m, source):
        return wh_o.at[m, pl.ds(pl.multiple_of(source * part, part), part), :]

    def heads(m, step):
        where = (col + step) % n_col
        return remote(
            col_slice(wide[m], where, head),
            heads_dst(m, col),
            heads_s.at[m, step],
            heads_r.at[m, step],
            (row, where),
        )

    def heads_come(m, step):
        source = (col + n_col - step) % n_col
        return remote(
            heads_dst(m, source),
            heads_dst(m, source),
            heads_s.at[m, step],
            heads_r.at[m, step],
            (row, source),
        )

    def heads_own(m):
        return pltpu.make_async_copy(
            col_slice(wide[m], col, head), heads_dst(m, col), own_s.at[5 + m]
        )

    peers = [(True, (row, (col + k) % n_col)) for k in range(1, n_col)] + row_peers()
    shake(peers, [ok for ok, _ in peers])
    for k in range(5):
        for step in range(1, n_row):
            small_copy(k, step).start()
        small_own(k).start()
    begin()
    for k in range(3):
        small_own(k).wait()
        for step in range(1, n_row):
            small_come(k, step).wait_recv()
    for m in range(3):
        heads_own(m).start()
        for step in range(1, n_col):
            heads(m, step).start()
    middle()
    end()
    for k in range(5):
        if k >= 3:
            small_own(k).wait()
        for step in range(1, n_row):
            small_copy(k, step).wait_send()
            if k >= 3:
                small_come(k, step).wait_recv()
    for m in range(3):
        heads_own(m).wait()
        for step in range(1, n_col):
            heads(m, step).wait_send()
            heads_come(m, step).wait_recv()


def front(tokens, gains, wq, wk, wv, wo, wr, head, ident):
    n_row, n_col = lax.axis_size("row"), lax.axis_size("col")
    rows, part = tokens.shape
    width = part * n_col
    dma = pltpu.SemaphoreType.DMA
    shapes = [
        ((rows, width), BF16),
        ((gains.shape[0], width), F32),
        ((3, width, head), BF16),
        ((wo.shape[0], wo.shape[1] * n_row), BF16),
        ((wr.shape[0] * n_row, part), BF16),
    ] + [((part, wq.shape[1] * n_row), BF16)] * 3
    return pl.pallas_call(
        front_body,
        in_specs=[ANY] * 7,
        out_specs=[ANY] * 8,
        out_shape=[jax.ShapeDtypeStruct(s, t) for s, t in shapes],
        scratch_shapes=line_sems(2, n_col // 2)
        + [
            dma((3, n_col)),
            dma((3, n_col)),
            dma((5, n_row)),
            dma((5, n_row)),
            dma((8,)),
        ],
        compiler_params=pltpu.CompilerParams(collective_id=ident, has_side_effects=True),
        cost_estimate=pl.CostEstimate(
            flops=0, bytes_accessed=rows * width * 32, transcendentals=0
        ),
        name="front",
    )(tokens, gains, wq, wk, wv, wo, wr)


def middle_body(axes, *refs):
    n = len(axes)
    begin, middle, end = line_gather(axes, refs[:n], refs[n : 2 * n], refs[2 * n :])
    sources = line_peers()
    shake(sources, [ok for ok, _ in sources])
    begin()
    middle()
    end()


def middle_gather(arrays, axes, ident):
    n_col, n = lax.axis_size("col"), len(arrays)
    shapes = [
        tuple(d * n_col if at == axis else d for at, d in enumerate(a.shape))
        for a, axis in zip(arrays, axes)
    ]
    return pl.pallas_call(
        functools.partial(middle_body, axes),
        in_specs=[ANY] * n,
        out_specs=[ANY] * n,
        out_shape=[jax.ShapeDtypeStruct(s, a.dtype) for s, a in zip(shapes, arrays)],
        scratch_shapes=line_sems(n, n_col // 2),
        compiler_params=pltpu.CompilerParams(collective_id=ident, has_side_effects=True),
        cost_estimate=pl.CostEstimate(
            flops=0, bytes_accessed=sum(math.prod(s) for s in shapes) * 32, transcendentals=0
        ),
        name="middle_gather",
    )(*arrays)


def scatter_body(part, stage, local, *refs):
    n_in = (1, 2, 4, 4)[stage]
    n_out = (1, 2, 4, 4)[stage]
    if local:
        place, slots, refs = refs[0], refs[1 : 1 + local], refs[local:]
    x, ins = refs[0], refs[1:n_in]
    out, outs = refs[n_in], refs[n_in + 1 : n_in + n_out]
    rest = refs[n_in + n_out :]
    acc, side, from_left, from_right, load, side_s, side_r = rest[:7]
    right_s, right_r, left_s, left_r = rest[7:11]
    if local:
        give, chosen, held, held_s = rest[11:15]
        rest = rest[4:]
    row, col, n_row, n_col = places()
    pairs, pair, core = n_col // 2, col // 2, col % 2
    rows = out.shape[0]
    cuts = load.shape[1]
    height = rows // cuts
    tile = min(256, height)

    def at(pair_index, core_index):
        return (row, pair_index * 2 + core_index)

    def block(owner, q):
        return x.at[
            pl.ds(q * height, height), pl.ds(pl.multiple_of(owner * part, part), part)
        ]

    def cut(ref, d, q):
        return ref.at[d, pl.ds(q * height, height)]

    def fetch(d, q):
        return pltpu.make_async_copy(block(d * 2 + core, q), cut(acc, d, q), load.at[d, q])

    def across(d, q):
        return remote(
            cut(give, d, q) if local else block(d * 2 + 1 - core, q),
            cut(side, d, q),
            side_s.at[d, q],
            side_r.at[d, q],
            at(pair, 1 - core),
        )

    def right(d, q):
        return remote(
            cut(acc, d, q),
            cut(from_left, d, q),
            right_s.at[d, q],
            right_r.at[d, q],
            at(pair + 1, core),
        )

    def left(d, q):
        return remote(
            cut(acc, d, q),
            cut(from_right, d, q),
            left_s.at[d, q],
            left_r.at[d, q],
            at(pair - 1, core),
        )

    copies, arrivals, own = [], [], []
    if stage:
        small_s, small_r, own_s = rest[11:14]
        extra, extra_o = ins[0], outs[0]
        here, ring = (row, n_row) if stage == 2 else (col, n_col)
        for k in range(1, ring):
            where, source = (here + k) % ring, (here + ring - k) % ring
            to = (where, col) if stage == 2 else (row, where)
            copies.append(remote(extra, extra_o.at[here], small_s.at[k], small_r.at[k], to))
            arrivals.append(remote(extra, extra_o.at[source], small_s.at[k], small_r.at[k], to))
        own.append(pltpu.make_async_copy(extra, extra_o.at[here], own_s))
    if stage == 2:
        give_s, give_r, keep_s = rest[14:]
        per = n_col // n_row
        for m in range(2):
            src, dst = ins[1 + m], outs[1 + m]

            def block_of(r):
                return src.at[pl.ds(r * per, per)]

            for step in range(1, n_row):
                where, source = (row + step) % n_row, (row + n_row - step) % n_row
                sems = (give_s.at[m, step], give_r.at[m, step])
                copies.append(remote(block_of(where), dst.at[row], *sems, (where, col)))
                arrivals.append(remote(block_of(where), dst.at[source], *sems, (where, col)))
            own.append(pltpu.make_async_copy(block_of(row), dst.at[row], keep_s.at[m]))
    if stage == 3:
        give_s, give_r, keep_s = rest[14:]
        for m in range(2):
            src, dst = ins[1 + m], outs[1 + m]
            size = src.shape[1 - m] // n_col

            def block_for(c):
                at_c = pl.ds(pl.multiple_of(c * size, size), size)
                return src.at[:, at_c, :] if m == 0 else src.at[at_c, :]

            for step in range(1, n_col):
                where, source = (col + step) % n_col, (col + n_col - step) % n_col
                sems = (give_s.at[m, step], give_r.at[m, step])
                copies.append(remote(block_for(where), dst.at[col], *sems, (row, where)))
                arrivals.append(remote(block_for(where), dst.at[source], *sems, (row, where)))
            own.append(pltpu.make_async_copy(block_for(col), dst.at[col], keep_s.at[m]))
    if stage:
        peers = [(True, (row, (col + k) % n_col)) for k in range(1, n_col)]
    else:
        peers = line_peers()
    if stage == 2:
        peers += row_peers()
    shake(peers, [ok for ok, _ in peers])
    order = []
    for t in range(pairs):
        for d in (pairs - 1 - t, t):
            if d not in order:
                order.append(d)
    if local:
        micro, capacity = held.shape[2], held.shape[3]
        group = chosen.shape[1]
        owners = []
        for d in order:
            owners += [d * 2 + 1 - core, d * 2 + core]

        def bring(n):
            return [
                pltpu.make_async_copy(
                    slots[e].at[:, :, pl.ds(pl.multiple_of(owners[n] * part, part), part)],
                    held.at[n % 2, e],
                    held_s.at[n % 2, e],
                )
                for e in range(local)
            ]

        def make(n, into):
            for c in bring(n):
                c.wait()
            if n + 1 < len(owners):
                for c in bring(n + 1):
                    c.start()
            steps = group // tile

            def step(i, _):
                g, at_row = i // steps, pl.multiple_of((i % steps) * tile, tile)
                total = None
                for e in range(local):
                    term = nn(
                        chosen[g, pl.ds(at_row, tile), e * capacity : (e + 1) * capacity],
                        held[n % 2, e, g],
                    )
                    total = term if total is None else total + term
                into[pl.ds(pl.multiple_of(i * tile, tile), tile), :] = total.astype(BF16)
                return 0

            lax.fori_loop(0, micro * steps, step, 0)

        def make_pair(m):
            d = order[m]
            make(2 * m, give.at[d])
            for q in range(cuts):
                across(d, q).start()
            make(2 * m + 1, acc.at[d])

        for c in bring(0):
            c.start()

        def choose(i, _):
            steps = group // tile
            g, at_row = i // steps, pl.multiple_of((i % steps) * tile, tile)
            for e in range(local):
                slot = lax.broadcasted_iota(jnp.int32, (tile, capacity), 1)
                hit = slot == place[g, pl.ds(at_row, tile), e : e + 1]
                chosen[g, pl.ds(at_row, tile), e * capacity : (e + 1) * capacity] = jnp.where(
                    hit, 1.0, 0.0
                ).astype(BF16)
            return 0

        lax.fori_loop(0, micro * (group // tile), choose, 0)
    else:
        for d in order:
            for q in range(cuts):
                across(d, q).start()
                fetch(d, q).start()
    for c in copies + own:
        c.start()

    def add(q, into, *sources):
        def step(i, _):
            lines = pl.ds(pl.multiple_of(q * height + i * tile, tile), tile)
            total = sources[0][lines, :].astype(F32)
            for ref in sources[1:]:
                total = total + ref[lines, :].astype(F32)
            into[lines, :] = total.astype(into.dtype)
            return 0

        lax.fori_loop(0, height // tile, step, 0)

    def ready(d, q):
        if not local:
            fetch(d, q).wait()
        across(d, q).wait_recv()

    def go_right(d, q):
        ready(d, q)

        @pl.when(pair > 0)
        def _():
            right(d, q).wait_recv()
            add(q, acc.at[d], acc.at[d], side.at[d], from_left.at[d])

        @pl.when(pair == 0)
        def _():
            add(q, acc.at[d], acc.at[d], side.at[d])

        right(d, q).start()

    def go_left(d, q):
        ready(d, q)

        @pl.when(pair < pairs - 1)
        def _():
            left(d, q).wait_recv()
            add(q, acc.at[d], acc.at[d], side.at[d], from_right.at[d])

        @pl.when(pair == pairs - 1)
        def _():
            add(q, acc.at[d], acc.at[d], side.at[d])

        left(d, q).start()

    if local:
        for m in range(2):
            make_pair(m)
        for q in range(cuts):

            @pl.when(pair == 0)
            def _():
                go_right(pairs - 1, q)

            @pl.when(pair == pairs - 1)
            def _():
                go_left(0, q)

        for m in range(2, pairs):
            make_pair(m)
    for t in range(pairs - 1):
        far, near = pairs - 1 - t, t
        go_far, go_near = far > pair, near < pair
        if local and t == 0:
            go_far, go_near = go_far & (pair > 0), go_near & (pair < pairs - 1)
        for q in range(cuts):

            @pl.when(go_far)
            def _():
                go_right(far, q)

            @pl.when(go_near)
            def _():
                go_left(near, q)

    for q in range(cuts):
        ready(pair, q)

        @pl.when(pair == 0)
        def _():
            left(pair, q).wait_recv()
            add(q, out, acc.at[pair], side.at[pair], from_right.at[pair])

        @pl.when(pair == pairs - 1)
        def _():
            right(pair, q).wait_recv()
            add(q, out, acc.at[pair], side.at[pair], from_left.at[pair])

        @pl.when((pair > 0) & (pair < pairs - 1))
        def _():
            left(pair, q).wait_recv()
            right(pair, q).wait_recv()
            add(q, out, acc.at[pair], side.at[pair], from_left.at[pair], from_right.at[pair])

    for d in range(pairs):
        for q in range(cuts):
            across(d, q).wait_send()

            @pl.when(pair < d)
            def _():
                right(d, q).wait_send()

            @pl.when(pair > d)
            def _():
                left(d, q).wait_send()

    for c in copies:
        c.wait_send()
    for c in arrivals:
        c.wait_recv()
    for c in own:
        c.wait()


def scatter_col(x, ident, stage=0, others=(), place=None):
    n_row, n_col = lax.axis_size("row"), lax.axis_size("col")
    pairs, per = n_col // 2, n_col // n_row
    local = 0 if place is None else len(x)
    if local:
        micro, group, _ = place.shape
        capacity = x[0].shape[1]
        rows, part = micro * group, x[0].shape[2] // n_col
    else:
        rows, part = x.shape[0], x.shape[1] // n_col
    cuts = 4 if rows % 1024 == 0 else 1
    dma = pltpu.SemaphoreType.DMA
    buffer = pltpu.VMEM((pairs, rows, part), BF16)
    scratch = [buffer] * 4 + [dma((pairs, cuts))] * 7
    if local:
        scratch += [
            buffer,
            pltpu.VMEM((micro, group, local * capacity), BF16),
            pltpu.VMEM((2, local, micro, capacity, part), BF16),
            dma((2, local)),
        ]
    out_shape = [jax.ShapeDtypeStruct((rows, part), F32)]
    if stage:
        extra, ring = others[0], n_row if stage == 2 else n_col
        out_shape.append(jax.ShapeDtypeStruct((ring,) + extra.shape, extra.dtype))
        scratch += [dma((ring,)), dma((ring,)), dma(())]
    if stage == 2:
        scratch += [dma((2, n_row)), dma((2, n_row)), dma((2,))]
        for value in others[1:]:
            out_shape.append(jax.ShapeDtypeStruct((n_row, per) + value.shape[1:], BF16))
    if stage == 3:
        heads, branch = others[1:]
        scratch += [dma((2, n_col)), dma((2, n_col)), dma((2,))]
        out_shape += [
            jax.ShapeDtypeStruct((n_col, 3, heads.shape[1] // n_col, heads.shape[2]), BF16),
            jax.ShapeDtypeStruct((n_col, branch.shape[0] // n_col, branch.shape[1]), BF16),
        ]
    first = [pl.BlockSpec(memory_space=pltpu.VMEM)] + [ANY] * local if local else [ANY]
    values = (place, *x) if local else (x,)
    return pl.pallas_call(
        functools.partial(scatter_body, part, stage, local),
        in_specs=first + [ANY] * len(others),
        out_specs=[pl.BlockSpec(memory_space=pltpu.VMEM)] + [ANY] * (len(out_shape) - 1),
        out_shape=out_shape,
        scratch_shapes=scratch,
        compiler_params=pltpu.CompilerParams(
            vmem_limit_bytes=VMEM_LIMIT, collective_id=ident, has_side_effects=True
        ),
        cost_estimate=pl.CostEstimate(
            flops=0, bytes_accessed=rows * part * n_col * 40, transcendentals=0
        ),
        name="scatter_col",
    )(*values, *others)


def exchange_body(extra, heads, branch, extra_o, heads_o, branch_o, sends, recvs, keep):
    row, col, n_row, n_col = places()
    part, rows = heads.shape[1] // n_col, branch.shape[0] // n_col

    def pieces(c):
        at_part = pl.ds(pl.multiple_of(c * part, part), part)
        at_rows = pl.ds(pl.multiple_of(c * rows, rows), rows)
        return heads.at[:, at_part, :], branch.at[at_rows, :], extra

    peers = [(True, (row, (col + k) % n_col)) for k in range(1, n_col)]
    shake(peers, [ok for ok, _ in peers])
    outs = (heads_o, branch_o, extra_o)
    copies, arrivals = [], []
    for k in range(1, n_col):
        where, source = (col + k) % n_col, (col + n_col - k) % n_col
        for m, src in enumerate(pieces(where)):
            sems = (sends.at[m, k], recvs.at[m, k])
            copies.append(remote(src, outs[m].at[col], *sems, (row, where)))
            arrivals.append(remote(src, outs[m].at[source], *sems, (row, where)))
    own = [
        pltpu.make_async_copy(src, outs[m].at[col], keep.at[m])
        for m, src in enumerate(pieces(col))
    ]
    for c in copies + own:
        c.start()
    for c in copies:
        c.wait_send()
    for c in arrivals:
        c.wait_recv()
    for c in own:
        c.wait()


def exchange_col(extra, heads, branch, ident):
    n_col = lax.axis_size("col")
    dma = pltpu.SemaphoreType.DMA
    return pl.pallas_call(
        exchange_body,
        in_specs=[ANY] * 3,
        out_specs=[ANY] * 3,
        out_shape=[
            jax.ShapeDtypeStruct((n_col,) + extra.shape, F32),
            jax.ShapeDtypeStruct((n_col, 3, heads.shape[1] // n_col, heads.shape[2]), BF16),
            jax.ShapeDtypeStruct((n_col, branch.shape[0] // n_col, branch.shape[1]), BF16),
        ],
        scratch_shapes=[dma((3, n_col)), dma((3, n_col)), dma((3,))],
        compiler_params=pltpu.CompilerParams(collective_id=ident, has_side_effects=True),
        cost_estimate=pl.CostEstimate(flops=0, bytes_accessed=64 << 20, transcendentals=0),
        name="exchange_col",
    )(extra, heads, branch)


def shards(
    tokens,
    gain_attn,
    gain_ffn,
    gain_query,
    gain_key,
    w_query,
    w_key,
    w_value,
    w_out,
    w_router,
    w_gate,
    w_up,
    w_down,
    routes,
    lengths,
    cotangent,
):
    n_col = lax.axis_size("col")
    n_row = lax.axis_size("row")
    col = lax.axis_index("col")
    micro, spans = lengths.shape
    rows, part = tokens.shape
    group = rows // micro
    width = part * n_col
    head = gain_query.shape[0]
    local_exp = w_gate.shape[0]
    experts = local_exp * n_col
    topk = routes.shape[1]
    capacity = 2 * group * topk // experts
    local_heads = w_out.shape[0] // head
    hd = w_out.shape[0] * n_col
    scale = head ** (-0.5)

    def gather(value, axis_name, axis):
        return lax.all_gather(value, axis_name, axis=axis, tiled=True)

    def mine(value, axis):
        size = value.shape[axis] // n_col
        return lax.dynamic_slice_in_dim(value, col * size, size, axis)

    shared = w_down.shape[2]
    pair = 2 if local_exp % 2 == 0 else 1
    big = [
        gather(pack(w_gate, w_up, w_down, at, pair), "row", 2) for at in range(0, local_exp, pair)
    ]
    inputs_low, gains, w_heads, rows_o, rows_r, *wide = front(
        tokens,
        jnp.stack([gain_attn, gain_ffn]),
        w_query,
        w_key,
        w_value,
        w_out,
        w_router.T,
        head,
        0,
    )

    segment, position, live = jax.vmap(lambda l: layout(l, group))(lengths)
    position = position.reshape(rows)
    live = live.reshape(rows)
    upstream_part = cotangent.astype(F32) * live[:, None]
    member = jnp.any(
        routes[:, None, :] == jnp.arange(experts, dtype=jnp.int32)[None, :, None], -1
    )
    member_f = member.astype(F32)
    member_loc = mine(member_f, 1).reshape(micro, group, local_exp)
    lower = (
        jnp.arange(group, dtype=jnp.int32)[:, None] > jnp.arange(group, dtype=jnp.int32)[None, :]
    ).astype(BF16)
    before = jnp.einsum("st,gte->gse", lower, member_loc.astype(BF16), preferred_element_type=F32)
    place = jnp.where(member_loc > 0, before, -1.0).astype(jnp.int32)
    counts = jnp.sum(member_loc, 1).astype(jnp.int32).T
    place_t = place.transpose(2, 0, 1)[:, :, None, :]

    inputs = inputs_low.astype(F32)
    scale_one = inverse_rms(inputs)
    normed = (inputs * scale_one * gains[0]).astype(BF16)
    all_heads = jnp.concatenate([w_heads[j] for j in range(3)], 1)
    query_pre, key_pre, value_pre = jnp.split(nn(normed, all_heads), 3, 1)
    shape = (rows, local_heads, head)
    cosine, sine = rope_tables(position, head)

    def head_norm(values, gain):
        return rotary(values * inverse_rms(values) * gain, cosine, sine)

    query_rot, query_pull = jax.vjp(head_norm, query_pre.reshape(shape), gain_query)
    key_rot, key_pull = jax.vjp(head_norm, key_pre.reshape(shape), gain_key)
    batch = (micro, group, local_heads, head)
    queries = query_rot.astype(BF16).reshape(batch)
    keys_low = key_rot.astype(BF16).reshape(batch)
    values_low = value_pre.astype(BF16).reshape(batch)
    same = (segment[:, :, None] == segment[:, None, :])[:, None]

    def scores_of():
        raw = jnp.einsum("gqhd,gkhd->ghqk", queries, keys_low, preferred_element_type=F32) * scale
        return jnp.where(same, raw, MASKED)

    scores = scores_of()
    highest = jnp.max(scores, -1, keepdims=True)
    log_total = highest + jnp.log(jnp.sum(jnp.exp(scores - highest), -1, keepdims=True))
    probs_low = jnp.exp(scores - log_total).astype(BF16)
    attended = jnp.einsum(
        "ghqk,gkhd->gqhd", probs_low, values_low, preferred_element_type=F32
    ).astype(BF16)
    attended_full, full_o, full_rt, upstream_low = middle_gather(
        [attended.reshape(rows, local_heads * head), rows_o, rows_r, upstream_part.astype(BF16)],
        (1, 0, 1, 1),
        1,
    )
    full_r = full_rt.T

    hidden = inputs + nn(attended_full, full_o)
    scale_two = inverse_rms(hidden)
    normed_ffn = (hidden * scale_two * gains[1]).astype(BF16)
    logits = nn(normed_ffn, full_r)
    peak = jnp.max(jnp.where(member, logits, -jnp.inf), -1, keepdims=True)
    raised = jnp.where(member, jnp.exp(jnp.where(member, logits - peak, 0.0)), 0.0)
    gates = raised / jnp.sum(raised, -1, keepdims=True)
    gate_t = mine(gates, 1).reshape(micro, group, local_exp).transpose(2, 0, 1)[:, :, None, :]
    upstream_full = upstream_low.reshape(micro, group, width)
    hn = normed_ffn.reshape(micro, group, width)

    outs, weight_grads, grad = [], [], None
    for e in range(local_exp):
        xe, dyr, hg, dgp, dup, ye, dxe, tok = expert_pass(
            counts[e],
            place_t[e],
            gate_t[e],
            hn,
            upstream_full,
            big[e // pair],
            e % pair,
            capacity,
            shared,
        )
        held = () if e % pair == 0 else (grad,)
        grad = expert_grads(xe, dgp, dup, hg, dyr, shared, e % pair, pair, held)
        hn, upstream_full, ye, dxe, tok, grad = lax.optimization_barrier(
            (hn, upstream_full, ye, dxe, tok, grad)
        )
        outs.append((ye, dxe, tok))
        if e % pair == pair - 1:
            weight_grads.append(lax.psum_scatter(grad, "row", scatter_dimension=2, tiled=True))

    def tie(value, e):
        value, weight_grads[e] = lax.optimization_barrier((value, weight_grads[e]))
        return value

    row = lax.axis_index("row")
    back_sum, tok = scatter_col(
        [o[1] for o in outs], 2, 1, (jnp.stack([o[2] for o in outs]),), place
    )
    tok = tok.reshape((experts,) + tok.shape[2:])
    hidden_part = tokens.astype(F32) + nn(attended_full, mine(full_o, 1))
    gate_dots = tok[:, :, 0].reshape(experts, rows).T
    hidden_part = mine(hidden, 1)

    selected = gates * (gate_dots - jnp.sum(gates * gate_dots, -1, keepdims=True))
    logit_grad = selected.astype(BF16)
    router_part = mine(full_r, 0)
    normed_grad = back_sum + nt(logit_grad, router_part)
    grad_router = tn(mine(normed_ffn, 1), logit_grad)
    scaled_two = hidden_part * scale_two
    grad_gain_ffn = jnp.sum(normed_grad * scaled_two, 0)
    dot_two = jnp.sum(tok[:, :, 1].reshape(experts, rows), 0) + jnp.sum(
        logit_grad.astype(F32) * logits, 1
    )
    hidden_grad = (
        upstream_part
        + scale_two * (normed_grad * gain_ffn)
        - hidden_part * scale_two**2 * dot_two[:, None] / width
    )

    branch_grad = hidden_grad.astype(BF16)
    (attended_grad,) = scatter_col(nt(branch_grad, mine(full_o, 1)).astype(BF16), 3)
    attended_grad = tie(attended_grad.astype(BF16).reshape(batch), 0)
    grad_out = tn(attended_full, branch_grad)
    scores_again = scores_of()
    probs = jnp.exp(scores_again - log_total)
    probs_again = probs.astype(BF16)
    probs_grad = jnp.einsum(
        "gqhd,gkhd->ghqk", attended_grad, values_low, preferred_element_type=F32
    )
    values_grad = jnp.einsum(
        "ghqk,gqhd->gkhd", probs_again, attended_grad, preferred_element_type=F32
    )
    score_grad = (probs * (probs_grad - jnp.sum(probs_grad * probs, -1, keepdims=True))).astype(
        BF16
    )
    query_grad_rot = (
        jnp.einsum("ghqk,gkhd->gqhd", score_grad, keys_low, preferred_element_type=F32) * scale
    )
    key_grad_rot = (
        jnp.einsum("ghqk,gqhd->gkhd", score_grad, queries, preferred_element_type=F32) * scale
    )
    query_grad, gain_query_part = query_pull(query_grad_rot.reshape(shape))
    key_grad, gain_key_part = key_pull(key_grad_rot.reshape(shape))
    flat = (rows, local_heads * head)
    heads_grad = [
        v.reshape(flat).astype(BF16) for v in (query_grad, key_grad, values_grad)
    ]
    all_grads = jnp.concatenate(heads_grad, 1)
    back_heads = nt(all_grads, all_heads)
    pre = (query_pre, key_pre, value_pre)
    dot_part = sum(jnp.sum(g.astype(F32) * p, -1) for g, p in zip(heads_grad, pre))
    sums = jnp.concatenate([dot_part, gain_query_part, gain_key_part])
    sums = jnp.pad(sums, (0, -sums.shape[0] % 1024)).reshape(-1, 128)
    heads_weights = tn(normed, all_grads).astype(BF16)
    heads_weights = jnp.stack(jnp.split(heads_weights, 3, 1))
    sums, heads_terms, out_terms = exchange_col(sums, heads_weights, grad_out.astype(BF16), 4)
    sums, mixed_slots = lax.optimization_barrier((sums, [o[0] for o in outs]))
    mixed_sum = lax.psum_scatter(
        combine(place, mixed_slots), "col", scatter_dimension=1, tiled=True
    )
    sums = jnp.sum(sums, 0).reshape(-1)
    dot_one = sums[:rows]
    gain_attn_part = 0.0
    for m in range(3):
        for c in range(n_col):
            columns = wide[m][:, c * local_heads * head : (c + 1) * local_heads * head]
            gain_attn_part = gain_attn_part + jnp.sum(
                columns.astype(F32) * heads_terms[c, m].astype(F32), -1
            )
    smalls = jnp.concatenate(
        [
            gain_attn_part,
            grad_gain_ffn,
            sums[rows : rows + 2 * head],
            grad_router.T.reshape(-1),
        ]
    ).reshape(-1, 128)
    normed_back, smalls, heads_terms, out_terms = scatter_col(
        back_heads.astype(BF16), 5, 2, (smalls, heads_terms, out_terms)
    )
    normed_back, mixed_sum = lax.optimization_barrier((normed_back, mixed_sum))
    mixed = (hidden_part + mixed_sum.astype(F32)).astype(BF16)
    scale_one_part = scale_one
    inputs_part = tokens.astype(F32)
    input_grad = (
        hidden_grad
        + scale_one_part * (normed_back * gain_attn)
        - inputs_part * scale_one_part**2 * dot_one[:, None] / width
    )

    held = ()
    for e, grad in enumerate(weight_grads):
        held = unpack(grad, held, e * pair, local_exp)
    grad_gate, grad_up, grad_down = held

    heads_terms = jnp.sum(heads_terms.astype(F32), 0)
    heads_sum = jnp.concatenate([heads_terms[j] for j in range(heads_terms.shape[0])], -1)
    grad_query, grad_key, grad_value = heads_sum[0], heads_sum[1], heads_sum[2]
    out_terms = jnp.sum(out_terms.astype(F32), 0)
    grad_out = jnp.concatenate([out_terms[j] for j in range(out_terms.shape[0])], -1)
    row = lax.axis_index("row")
    total = jnp.sum(smalls, 0).reshape(-1)
    grad_gain_attn, grad_gain_ffn = total[:part] / gain_attn, total[part : 2 * part]
    grad_gain_query = total[2 * part : 2 * part + head]
    grad_gain_key = total[2 * part + head : 2 * part + 2 * head]
    grad_router = lax.dynamic_slice_in_dim(
        total[2 * part + 2 * head :].reshape(experts, part), row * (experts // n_row), experts // n_row, 0
    ).T
    return (
        mixed,
        input_grad,
        grad_gain_attn,
        grad_gain_ffn,
        grad_gain_query,
        grad_gain_key,
        grad_query,
        grad_key,
        grad_value,
        grad_out,
        grad_router,
        grad_gate,
        grad_up,
        grad_down,
    )


def solution(mesh):
    placed = (
        P("row", "col"),
        P("col"),
        P("col"),
        P(),
        P(),
        P("col", "row"),
        P("col", "row"),
        P("col", "row"),
        P("col", "row"),
        P("col", "row"),
        P("col", "row", None),
        P("col", "row", None),
        P("col", None, "row"),
        P("row", None),
        P("row", None),
        P("row", "col"),
    )
    return jax.shard_map(
        shards,
        mesh=mesh,
        in_specs=placed,
        out_specs=(
            P("row", "col"),
            P("row", "col"),
            P("col"),
            P("col"),
            P(),
            P(),
            P("col", "row"),
            P("col", "row"),
            P("col", "row"),
            P("col", "row"),
            P("col", "row"),
            P("col", "row", None),
            P("col", "row", None),
            P("col", None, "row"),
        ),
        check_vma=False,
    )
```

```python
import functools
import math

import jax
import jax.numpy as jnp
from jax import lax
from jax.experimental import pallas as pl
from jax.experimental.pallas import tpu as pltpu
from jax.sharding import PartitionSpec as P

EPSILON = 1e-06
ROPE_BASE = 10000.0
MASKED = -1e30
F32 = jnp.float32
BF16 = jnp.bfloat16
VMEM_LIMIT = 60 * 1024 * 1024
MESH = pl.DeviceIdType.MESH
ANY = pl.BlockSpec(memory_space=pl.ANY)


def inverse_rms(values):
    return lax.rsqrt(jnp.mean(values * values, -1, keepdims=True) + EPSILON)


def rope_tables(position, head):
    half = head // 2
    inverse = jnp.exp(-math.log(ROPE_BASE) * 2.0 / head * jnp.arange(half, dtype=F32))
    angles = position[:, None] * inverse[None, :]
    return jnp.cos(angles)[:, None, :], jnp.sin(angles)[:, None, :]


def rotary(values, cosine, sine):
    half = values.shape[-1] // 2
    first = values[..., :half]
    second = values[..., half:]
    return jnp.concatenate([first * cosine - second * sine, second * cosine + first * sine], -1)


def layout(lengths_row, group):
    ends = jnp.cumsum(lengths_row)
    starts = ends - lengths_row
    row_index = jnp.arange(group, dtype=jnp.int32)
    segment = jnp.sum((row_index[:, None] >= ends[None, :]).astype(jnp.int32), 1)
    member = segment[:, None] == jnp.arange(lengths_row.shape[0], dtype=jnp.int32)[None, :]
    position = (row_index - jnp.sum(jnp.where(member, starts[None, :], 0), 1)).astype(F32)
    live = (segment < lengths_row.shape[0] - 1).astype(F32)
    return (segment, position, live)


def nn(a, b):
    return lax.dot_general(a, b, (((1,), (0,)), ((), ())), preferred_element_type=F32)


def nt(a, b):
    return lax.dot_general(a, b, (((1,), (1,)), ((), ())), preferred_element_type=F32)


def tn(a, b):
    return lax.dot_general(a, b, (((0,), (0,)), ((), ())), preferred_element_type=F32)


def expert_body(shared, counts, place, gate, hn, dy, w, xe_o, dyr_o, hg_o, dgp_o, dup_o, ye_o, dxe_o, tok_o):
    g, i = pl.program_id(0), pl.program_id(1)
    rows = xe_o.shape[1]
    width, ff = w.shape[2:]
    base = i * rows

    @pl.when(i == 0)
    def _():
        tok_o[...] = jnp.zeros_like(tok_o)

    @pl.when(counts[g] <= base)
    def _():
        for ref in (xe_o, dyr_o, hg_o, dgp_o, dup_o, ye_o, dxe_o):
            ref[...] = jnp.zeros_like(ref)

    @pl.when(counts[g] > base)
    def _():
        slot = lax.broadcasted_iota(jnp.int32, (rows, place.shape[2]), 0) + base
        hit = slot == place[0]
        pick = jnp.where(hit, 1.0, 0.0).astype(BF16)
        weight = jnp.sum(jnp.where(hit, gate[0], 0.0), 1, keepdims=True)
        xe = nn(pick, hn[0]).astype(BF16)
        xe_o[0] = xe
        gp = nn(xe, w[0, 0])
        up = nn(xe, w[0, 1])
        sig = jax.nn.sigmoid(gp)
        silu = gp * sig
        hid = silu * up
        hg = (hid * weight).astype(BF16)
        hg_o[0] = hg
        dyr = nn(pick, dy[0]).astype(BF16)
        dyr_o[0] = dyr
        parts = []
        for r in range(width // shared):
            at = r * shared
            total = None
            for b in range(ff // shared):
                low = b * shared
                term = nn(hg[:, low : low + shared], w[0, 2, at : at + shared, low : low + shared])
                total = term if total is None else total + term
            ye_o[0, :, at : at + shared] = total.astype(BF16)
        for b in range(ff // shared):
            low = b * shared
            total = None
            for r in range(width // shared):
                at = r * shared
                term = nt(dyr[:, at : at + shared], w[0, 2, at : at + shared, low : low + shared])
                total = term if total is None else total + term
            parts.append(total)
        back = jnp.concatenate(parts, 1)
        dgate = jnp.sum(back * hid, 1, keepdims=True)
        dhid = back * weight
        dgp = (dhid * up * sig * (1.0 + gp * (1.0 - sig))).astype(BF16)
        dup = (dhid * silu).astype(BF16)
        dgp_o[0] = dgp
        dup_o[0] = dup
        dots = jnp.sum(dgp.astype(F32) * gp + dup.astype(F32) * up, 1, keepdims=True)
        dxe_o[0] = (nt(dgp, w[0, 0]) + nt(dup, w[0, 1])).astype(BF16)
        tok_o[0, 0:1, :] += jnp.sum(jnp.where(hit, dgate, 0.0), 0, keepdims=True)
        tok_o[0, 1:2, :] += jnp.sum(jnp.where(hit, dots, 0.0), 0, keepdims=True)


def expert_pass(counts, place, gate, hn, dy, w, at, capacity, shared):
    width, ff = w.shape[2:]
    micro, group, _ = hn.shape
    rows = min(256, capacity)
    blocks = capacity // rows
    tall = lambda g, i, c: (g, i, 0)
    line = lambda g, i, c: (g, 0, 0)
    slots = lambda n: jax.ShapeDtypeStruct((micro, capacity, n), BF16)
    sizes = (width, width, ff, ff, ff, width, width)
    flops = 2 * micro * capacity * width * (6 * ff + 2 * group)
    return pl.pallas_call(
        functools.partial(expert_body, shared),
        grid_spec=pltpu.PrefetchScalarGridSpec(
            num_scalar_prefetch=1,
            grid=(micro, blocks),
            in_specs=[
                pl.BlockSpec((1, 1, group), line),
                pl.BlockSpec((1, 1, group), line),
                pl.BlockSpec((1, group, width), line),
                pl.BlockSpec((1, group, width), line),
                pl.BlockSpec(
                    (1, 3, width, ff), lambda g, i, c: (at, 0, 0, 0), pipeline_mode=pl.Buffered(1)
                ),
            ],
            out_specs=[pl.BlockSpec((1, rows, n), tall) for n in sizes]
            + [pl.BlockSpec((1, 2, group), line)],
        ),
        out_shape=[slots(n) for n in sizes] + [jax.ShapeDtypeStruct((micro, 2, group), F32)],
        compiler_params=pltpu.CompilerParams(vmem_limit_bytes=VMEM_LIMIT),
        cost_estimate=pl.CostEstimate(
            flops=flops, bytes_accessed=40 << 20, transcendentals=micro * capacity * ff
        ),
        name="expert_pass",
    )(counts, place, gate, hn, dy, w)


def grads_body(xe, dgp, dup, hg, dyr, *rest):
    out = rest[-1]
    part = xe[...]
    shared = part.shape[1]
    out[0, 0] = tn(part, dgp[...]).astype(BF16)
    out[0, 1] = tn(part, dup[...]).astype(BF16)
    back = dyr[...]
    for b in range(hg.shape[1] // shared):
        low = b * shared
        out[0, 2, :, low : low + shared] = tn(hg[:, low : low + shared], back).astype(BF16)


def expert_grads(xe, dgp, dup, hg, dyr, shared, at, pair, held):
    micro, capacity, width = xe.shape
    ff = dgp.shape[2]
    rows = micro * capacity
    xe, dyr = (a.reshape(rows, width) for a in (xe, dyr))
    dgp, dup, hg = (a.reshape(rows, ff) for a in (dgp, dup, hg))
    thin = pl.BlockSpec((rows, shared), lambda r: (0, r))
    whole = pl.BlockSpec((rows, ff), lambda r: (0, 0))
    return pl.pallas_call(
        grads_body,
        grid=(width // shared,),
        in_specs=[thin, whole, whole, whole, thin] + [ANY] * len(held),
        out_specs=pl.BlockSpec((1, 3, shared, ff), lambda r: (at, 0, r, 0)),
        out_shape=jax.ShapeDtypeStruct((pair, 3, width, ff), BF16),
        input_output_aliases={5: 0} if held else {},
        compiler_params=pltpu.CompilerParams(vmem_limit_bytes=VMEM_LIMIT),
        cost_estimate=pl.CostEstimate(
            flops=6 * rows * width * ff, bytes_accessed=26 << 20, transcendentals=0
        ),
        name="expert_grads",
    )(xe, dgp, dup, hg, dyr, *held)


def pack_body(wg, wu, wd, out):
    shared = out.shape[2]
    out[0, 0] = wg[0]
    out[0, 1] = wu[0]
    for b in range(out.shape[3] // shared):
        low = b * shared
        out[0, 2, :, low : low + shared] = wd[0, low : low + shared, :]


def pack(wg, wu, wd, first, pair):
    _, shared, ff = wg.shape
    block = pl.BlockSpec((1, shared, ff), lambda i: (first + i, 0, 0))
    return pl.pallas_call(
        pack_body,
        grid=(pair,),
        in_specs=[block, block, pl.BlockSpec((1, ff, shared), lambda i: (first + i, 0, 0))],
        out_specs=pl.BlockSpec((1, 3, shared, ff), lambda i: (i, 0, 0, 0)),
        out_shape=jax.ShapeDtypeStruct((pair, 3, shared, ff), BF16),
        cost_estimate=pl.CostEstimate(
            flops=0, bytes_accessed=pair * 12 * shared * ff, transcendentals=0
        ),
        name="pack",
    )(wg, wu, wd)


def unpack_body(x, *refs):
    gg, gu, gd = refs[-3:]
    shared = x.shape[2]
    gg[0] = x[0, 0].astype(F32)
    gu[0] = x[0, 1].astype(F32)
    for b in range(x.shape[3] // shared):
        low = b * shared
        gd[0, low : low + shared, :] = x[0, 2, :, low : low + shared].astype(F32)


def unpack(x, held, first, experts):
    pair, _, shared, ff = x.shape
    block = pl.BlockSpec((1, shared, ff), lambda i: (first + i, 0, 0))
    return pl.pallas_call(
        unpack_body,
        grid=(pair,),
        in_specs=[pl.BlockSpec((1, 3, shared, ff), lambda i: (i, 0, 0, 0))] + [ANY] * len(held),
        out_specs=[block, block, pl.BlockSpec((1, ff, shared), lambda i: (first + i, 0, 0))],
        out_shape=[
            jax.ShapeDtypeStruct((experts, shared, ff), F32),
            jax.ShapeDtypeStruct((experts, shared, ff), F32),
            jax.ShapeDtypeStruct((experts, ff, shared), F32),
        ],
        input_output_aliases={1 + j: j for j in range(len(held))},
        compiler_params=pltpu.CompilerParams(vmem_limit_bytes=VMEM_LIMIT),
        cost_estimate=pl.CostEstimate(
            flops=0, bytes_accessed=pair * 18 * shared * ff, transcendentals=0
        ),
        name="unpack",
    )(x, *held)


def places():
    row, col = lax.axis_index("row"), lax.axis_index("col")
    n_row, n_col = lax.axis_size("row"), lax.axis_size("col")
    return row, col, n_row, n_col


def remote(src, dst, send_sem, recv_sem, where):
    return pltpu.make_async_remote_copy(
        src_ref=src,
        dst_ref=dst,
        send_sem=send_sem,
        recv_sem=recv_sem,
        device_id=where,
        device_id_type=MESH,
    )


def shake(sources, targets):
    barrier = pltpu.get_barrier_semaphore()
    for ok, where in sources:
        if ok is True:
            pl.semaphore_signal(barrier, inc=1, device_id=where, device_id_type=MESH)
        else:

            @pl.when(ok)
            def _():
                pl.semaphore_signal(barrier, inc=1, device_id=where, device_id_type=MESH)

    count = 0
    for ok in targets:
        count = count + (1 if ok is True else jnp.where(ok, 1, 0))
    pl.semaphore_wait(barrier, count)


def line_peers():
    row, col, n_row, n_col = places()
    pair, core = col // 2, col % 2
    return [
        (True, (row, pair * 2 + 1 - core)),
        (pair > 0, (row, (pair - 1) * 2 + core)),
        (pair < n_col // 2 - 1, (row, (pair + 1) * 2 + core)),
    ]


def row_peers():
    row, col, n_row, n_col = places()
    return [(True, ((row + k) % n_row, col)) for k in range(1, n_row)]


def col_slice(ref, index, size):
    return ref.at[..., pl.ds(pl.multiple_of(index * size, size), size)]


def line_gather(axes, ins, outs, sems):
    own_sem, right_s, right_r, left_s, left_r, side_s, side_r = sems
    n = len(ins)
    row, col, n_row, n_col = places()
    pairs, pair, core = n_col // 2, col // 2, col % 2

    def at(pair_index, core_index):
        return (row, pair_index * 2 + core_index)

    def block(j, source):
        size = ins[j].shape[axes[j]]
        if axes[j] == 0:
            return outs[j].at[pl.ds(pl.multiple_of(source * size, size), size)]
        return col_slice(outs[j], source, size)

    def right(j, s):
        source = (pair - s) * 2 + core
        src = ins[j] if s == 0 else block(j, source)
        return remote(src, block(j, source), right_s.at[j, s], right_r.at[j, s], at(pair + 1, core))

    def left(j, s):
        source = (pair + s) * 2 + core
        src = ins[j] if s == 0 else block(j, source)
        return remote(src, block(j, source), left_s.at[j, s], left_r.at[j, s], at(pair - 1, core))

    def side(j, source_pair, first=False):
        source = source_pair * 2 + core
        src = ins[j] if first else block(j, source)
        return remote(
            src,
            block(j, source),
            side_s.at[j, source_pair],
            side_r.at[j, source_pair],
            at(pair, 1 - core),
        )

    def arrived(j, recvs, slot, source):
        remote(
            ins[j], block(j, source), recvs.at[j, slot], recvs.at[j, slot], at(pair, 1 - core)
        ).wait_recv()

    def own(j):
        return pltpu.make_async_copy(ins[j], block(j, col), own_sem.at[j])

    def begin():
        for j in range(n):

            @pl.when(pair < pairs - 1)
            def _():
                right(j, 0).start()

            @pl.when(pair > 0)
            def _():
                left(j, 0).start()

        for j in range(n):
            side(j, pair, True).start()
            own(j).start()

    def middle():
        for s in range(1, pairs):
            for j in range(n):

                @pl.when(pair >= s)
                def _():
                    arrived(j, right_r, s - 1, (pair - s) * 2 + core)

                    @pl.when(pair < pairs - 1)
                    def _():
                        right(j, s).start()

                    side(j, pair - s).start()

                @pl.when(pair + s < pairs)
                def _():
                    arrived(j, left_r, s - 1, (pair + s) * 2 + core)

                    @pl.when(pair > 0)
                    def _():
                        left(j, s).start()

                    side(j, pair + s).start()

    def end():
        for j in range(n):
            own(j).wait()
            for p in range(pairs):
                side(j, p).wait_send()
                arrived(j, side_r, p, p * 2 + 1 - core)
            for s in range(pairs):

                @pl.when((pair >= s) & (pair < pairs - 1))
                def _():
                    right(j, s).wait_send()

                @pl.when((pair + s < pairs) & (pair > 0))
                def _():
                    left(j, s).wait_send()

    return begin, middle, end


def line_sems(n, pairs):
    dma = pltpu.SemaphoreType.DMA
    return [dma((n,))] + [dma((n, pairs))] * 6


def front_body(tokens, gains, wq, wk, wv, wo, wr, *refs):
    x_o, gains_o, wh_o, wo_o, wr_o = refs[:5]
    wide = refs[5:8]
    line, (heads_s, heads_r, row_s, row_r, own_s) = refs[8:15], refs[15:]
    row, col, n_row, n_col = places()
    head = wh_o.shape[2]
    part = wq.shape[0]
    begin, middle, end = line_gather((1, 1), [tokens, gains], [x_o, gains_o], line)
    small = [(wq, wide[0]), (wk, wide[1]), (wv, wide[2]), (wo, wo_o), (wr, wr_o)]

    def small_dst(k, source):
        src, dst = small[k]
        if k < 4:
            return col_slice(dst, source, src.shape[1])
        return dst.at[pl.ds(pl.multiple_of(source * src.shape[0], src.shape[0]), src.shape[0]), :]

    def small_copy(k, step):
        return remote(
            small[k][0],
            small_dst(k, row),
            row_s.at[k, step],
            row_r.at[k, step],
            ((row + step) % n_row, col),
        )

    def small_come(k, step):
        source = (row + n_row - step) % n_row
        return remote(
            small[k][0], small_dst(k, source), row_s.at[k, step], row_r.at[k, step], (source, col)
        )

    def small_own(k):
        return pltpu.make_async_copy(small[k][0], small_dst(k, row), own_s.at[k])

    def heads_dst(m, source):
        return wh_o.at[m, pl.ds(pl.multiple_of(source * part, part), part), :]

    def heads(m, step):
        where = (col + step) % n_col
        return remote(
            col_slice(wide[m], where, head),
            heads_dst(m, col),
            heads_s.at[m, step],
            heads_r.at[m, step],
            (row, where),
        )

    def heads_come(m, step):
        source = (col + n_col - step) % n_col
        return remote(
            heads_dst(m, source),
            heads_dst(m, source),
            heads_s.at[m, step],
            heads_r.at[m, step],
            (row, source),
        )

    def heads_own(m):
        return pltpu.make_async_copy(
            col_slice(wide[m], col, head), heads_dst(m, col), own_s.at[5 + m]
        )

    peers = [(True, (row, (col + k) % n_col)) for k in range(1, n_col)] + row_peers()
    shake(peers, [ok for ok, _ in peers])
    for k in range(5):
        for step in range(1, n_row):
            small_copy(k, step).start()
        small_own(k).start()
    begin()
    for k in range(3):
        small_own(k).wait()
        for step in range(1, n_row):
            small_come(k, step).wait_recv()
    for m in range(3):
        heads_own(m).start()
        for step in range(1, n_col):
            heads(m, step).start()
    middle()
    end()
    for k in range(5):
        if k >= 3:
            small_own(k).wait()
        for step in range(1, n_row):
            small_copy(k, step).wait_send()
            if k >= 3:
                small_come(k, step).wait_recv()
    for m in range(3):
        heads_own(m).wait()
        for step in range(1, n_col):
            heads(m, step).wait_send()
            heads_come(m, step).wait_recv()


def front(tokens, gains, wq, wk, wv, wo, wr, head, ident):
    n_row, n_col = lax.axis_size("row"), lax.axis_size("col")
    rows, part = tokens.shape
    width = part * n_col
    dma = pltpu.SemaphoreType.DMA
    shapes = [
        ((rows, width), BF16),
        ((gains.shape[0], width), F32),
        ((3, width, head), BF16),
        ((wo.shape[0], wo.shape[1] * n_row), BF16),
        ((wr.shape[0] * n_row, part), BF16),
    ] + [((part, wq.shape[1] * n_row), BF16)] * 3
    return pl.pallas_call(
        front_body,
        in_specs=[ANY] * 7,
        out_specs=[ANY] * 8,
        out_shape=[jax.ShapeDtypeStruct(s, t) for s, t in shapes],
        scratch_shapes=line_sems(2, n_col // 2)
        + [
            dma((3, n_col)),
            dma((3, n_col)),
            dma((5, n_row)),
            dma((5, n_row)),
            dma((8,)),
        ],
        compiler_params=pltpu.CompilerParams(collective_id=ident, has_side_effects=True),
        cost_estimate=pl.CostEstimate(
            flops=0, bytes_accessed=rows * width * 32, transcendentals=0
        ),
        name="front",
    )(tokens, gains, wq, wk, wv, wo, wr)


def middle_body(axes, *refs):
    n = len(axes)
    begin, middle, end = line_gather(axes, refs[:n], refs[n : 2 * n], refs[2 * n :])
    sources = line_peers()
    shake(sources, [ok for ok, _ in sources])
    begin()
    middle()
    end()


def middle_gather(arrays, axes, ident):
    n_col, n = lax.axis_size("col"), len(arrays)
    shapes = [
        tuple(d * n_col if at == axis else d for at, d in enumerate(a.shape))
        for a, axis in zip(arrays, axes)
    ]
    return pl.pallas_call(
        functools.partial(middle_body, axes),
        in_specs=[ANY] * n,
        out_specs=[ANY] * n,
        out_shape=[jax.ShapeDtypeStruct(s, a.dtype) for s, a in zip(shapes, arrays)],
        scratch_shapes=line_sems(n, n_col // 2),
        compiler_params=pltpu.CompilerParams(collective_id=ident, has_side_effects=True),
        cost_estimate=pl.CostEstimate(
            flops=0, bytes_accessed=sum(math.prod(s) for s in shapes) * 32, transcendentals=0
        ),
        name="middle_gather",
    )(*arrays)


def scatter_body(part, stage, local, *refs):
    n_in = (1, 2, 4, 4)[stage]
    n_out = (1, 2, 4, 4)[stage]
    if local:
        place, slots, refs = refs[0], refs[1 : 1 + local], refs[local:]
    x, ins = refs[0], refs[1:n_in]
    out, outs = refs[n_in], refs[n_in + 1 : n_in + n_out]
    rest = refs[n_in + n_out :]
    acc, side, from_left, from_right, load, side_s, side_r = rest[:7]
    right_s, right_r, left_s, left_r = rest[7:11]
    if local:
        give, chosen, held, held_s = rest[11:15]
        rest = rest[4:]
    row, col, n_row, n_col = places()
    pairs, pair, core = n_col // 2, col // 2, col % 2
    rows = out.shape[0]
    cuts = load.shape[1]
    height = rows // cuts
    tile = min(256, height)

    def at(pair_index, core_index):
        return (row, pair_index * 2 + core_index)

    def block(owner, q):
        return x.at[
            pl.ds(q * height, height), pl.ds(pl.multiple_of(owner * part, part), part)
        ]

    def cut(ref, d, q):
        return ref.at[d, pl.ds(q * height, height)]

    def fetch(d, q):
        return pltpu.make_async_copy(block(d * 2 + core, q), cut(acc, d, q), load.at[d, q])

    def across(d, q):
        return remote(
            cut(give, d, q) if local else block(d * 2 + 1 - core, q),
            cut(side, d, q),
            side_s.at[d, q],
            side_r.at[d, q],
            at(pair, 1 - core),
        )

    def right(d, q):
        return remote(
            cut(acc, d, q),
            cut(from_left, d, q),
            right_s.at[d, q],
            right_r.at[d, q],
            at(pair + 1, core),
        )

    def left(d, q):
        return remote(
            cut(acc, d, q),
            cut(from_right, d, q),
            left_s.at[d, q],
            left_r.at[d, q],
            at(pair - 1, core),
        )

    copies, arrivals, own = [], [], []
    if stage:
        small_s, small_r, own_s = rest[11:14]
        extra, extra_o = ins[0], outs[0]
        here, ring = (row, n_row) if stage == 2 else (col, n_col)
        for k in range(1, ring):
            where, source = (here + k) % ring, (here + ring - k) % ring
            to = (where, col) if stage == 2 else (row, where)
            copies.append(remote(extra, extra_o.at[here], small_s.at[k], small_r.at[k], to))
            arrivals.append(remote(extra, extra_o.at[source], small_s.at[k], small_r.at[k], to))
        own.append(pltpu.make_async_copy(extra, extra_o.at[here], own_s))
    if stage == 2:
        give_s, give_r, keep_s = rest[14:]
        per = n_col // n_row
        for m in range(2):
            src, dst = ins[1 + m], outs[1 + m]

            def block_of(r):
                return src.at[pl.ds(r * per, per)]

            for step in range(1, n_row):
                where, source = (row + step) % n_row, (row + n_row - step) % n_row
                sems = (give_s.at[m, step], give_r.at[m, step])
                copies.append(remote(block_of(where), dst.at[row], *sems, (where, col)))
                arrivals.append(remote(block_of(where), dst.at[source], *sems, (where, col)))
            own.append(pltpu.make_async_copy(block_of(row), dst.at[row], keep_s.at[m]))
    if stage == 3:
        give_s, give_r, keep_s = rest[14:]
        for m in range(2):
            src, dst = ins[1 + m], outs[1 + m]
            size = src.shape[1 - m] // n_col

            def block_for(c):
                at_c = pl.ds(pl.multiple_of(c * size, size), size)
                return src.at[:, at_c, :] if m == 0 else src.at[at_c, :]

            for step in range(1, n_col):
                where, source = (col + step) % n_col, (col + n_col - step) % n_col
                sems = (give_s.at[m, step], give_r.at[m, step])
                copies.append(remote(block_for(where), dst.at[col], *sems, (row, where)))
                arrivals.append(remote(block_for(where), dst.at[source], *sems, (row, where)))
            own.append(pltpu.make_async_copy(block_for(col), dst.at[col], keep_s.at[m]))
    if stage:
        peers = [(True, (row, (col + k) % n_col)) for k in range(1, n_col)]
    else:
        peers = line_peers()
    if stage == 2:
        peers += row_peers()
    shake(peers, [ok for ok, _ in peers])
    order = []
    for t in range(pairs):
        for d in (pairs - 1 - t, t):
            if d not in order:
                order.append(d)
    if local:
        micro, capacity = held.shape[2], held.shape[3]
        group = chosen.shape[1]
        owners = []
        for d in order:
            owners += [d * 2 + 1 - core, d * 2 + core]

        def bring(n):
            return [
                pltpu.make_async_copy(
                    slots[e].at[:, :, pl.ds(pl.multiple_of(owners[n] * part, part), part)],
                    held.at[n % 2, e],
                    held_s.at[n % 2, e],
                )
                for e in range(local)
            ]

        def make(n, into):
            for c in bring(n):
                c.wait()
            if n + 1 < len(owners):
                for c in bring(n + 1):
                    c.start()
            steps = group // tile

            def step(i, _):
                g, at_row = i // steps, pl.multiple_of((i % steps) * tile, tile)
                total = None
                for e in range(local):
                    term = nn(
                        chosen[g, pl.ds(at_row, tile), e * capacity : (e + 1) * capacity],
                        held[n % 2, e, g],
                    )
                    total = term if total is None else total + term
                into[pl.ds(pl.multiple_of(i * tile, tile), tile), :] = total.astype(BF16)
                return 0

            lax.fori_loop(0, micro * steps, step, 0)

        def make_pair(m):
            d = order[m]
            make(2 * m, give.at[d])
            for q in range(cuts):
                across(d, q).start()
            make(2 * m + 1, acc.at[d])

        for c in bring(0):
            c.start()

        def choose(i, _):
            steps = group // tile
            g, at_row = i // steps, pl.multiple_of((i % steps) * tile, tile)
            for e in range(local):
                slot = lax.broadcasted_iota(jnp.int32, (tile, capacity), 1)
                hit = slot == place[g, pl.ds(at_row, tile), e : e + 1]
                chosen[g, pl.ds(at_row, tile), e * capacity : (e + 1) * capacity] = jnp.where(
                    hit, 1.0, 0.0
                ).astype(BF16)
            return 0

        lax.fori_loop(0, micro * (group // tile), choose, 0)
    else:
        for d in order:
            for q in range(cuts):
                across(d, q).start()
                fetch(d, q).start()
    for c in copies + own:
        c.start()

    def add(q, into, *sources):
        def step(i, _):
            lines = pl.ds(pl.multiple_of(q * height + i * tile, tile), tile)
            total = sources[0][lines, :].astype(F32)
            for ref in sources[1:]:
                total = total + ref[lines, :].astype(F32)
            into[lines, :] = total.astype(into.dtype)
            return 0

        lax.fori_loop(0, height // tile, step, 0)

    def ready(d, q):
        if not local:
            fetch(d, q).wait()
        across(d, q).wait_recv()

    def go_right(d, q):
        ready(d, q)

        @pl.when(pair > 0)
        def _():
            right(d, q).wait_recv()
            add(q, acc.at[d], acc.at[d], side.at[d], from_left.at[d])

        @pl.when(pair == 0)
        def _():
            add(q, acc.at[d], acc.at[d], side.at[d])

        right(d, q).start()

    def go_left(d, q):
        ready(d, q)

        @pl.when(pair < pairs - 1)
        def _():
            left(d, q).wait_recv()
            add(q, acc.at[d], acc.at[d], side.at[d], from_right.at[d])

        @pl.when(pair == pairs - 1)
        def _():
            add(q, acc.at[d], acc.at[d], side.at[d])

        left(d, q).start()

    if local:
        for m in range(2):
            make_pair(m)
        for q in range(cuts):

            @pl.when(pair == 0)
            def _():
                go_right(pairs - 1, q)

            @pl.when(pair == pairs - 1)
            def _():
                go_left(0, q)

        for m in range(2, pairs):
            make_pair(m)
    for t in range(pairs - 1):
        far, near = pairs - 1 - t, t
        go_far, go_near = far > pair, near < pair
        if local and t == 0:
            go_far, go_near = go_far & (pair > 0), go_near & (pair < pairs - 1)
        for q in range(cuts):

            @pl.when(go_far)
            def _():
                go_right(far, q)

            @pl.when(go_near)
            def _():
                go_left(near, q)

    for q in range(cuts):
        ready(pair, q)

        @pl.when(pair == 0)
        def _():
            left(pair, q).wait_recv()
            add(q, out, acc.at[pair], side.at[pair], from_right.at[pair])

        @pl.when(pair == pairs - 1)
        def _():
            right(pair, q).wait_recv()
            add(q, out, acc.at[pair], side.at[pair], from_left.at[pair])

        @pl.when((pair > 0) & (pair < pairs - 1))
        def _():
            left(pair, q).wait_recv()
            right(pair, q).wait_recv()
            add(q, out, acc.at[pair], side.at[pair], from_left.at[pair], from_right.at[pair])

    for d in range(pairs):
        for q in range(cuts):
            across(d, q).wait_send()

            @pl.when(pair < d)
            def _():
                right(d, q).wait_send()

            @pl.when(pair > d)
            def _():
                left(d, q).wait_send()

    for c in copies:
        c.wait_send()
    for c in arrivals:
        c.wait_recv()
    for c in own:
        c.wait()


def scatter_col(x, ident, stage=0, others=(), place=None):
    n_row, n_col = lax.axis_size("row"), lax.axis_size("col")
    pairs, per = n_col // 2, n_col // n_row
    local = 0 if place is None else len(x)
    if local:
        micro, group, _ = place.shape
        capacity = x[0].shape[1]
        rows, part = micro * group, x[0].shape[2] // n_col
    else:
        rows, part = x.shape[0], x.shape[1] // n_col
    cuts = 4 if rows % 1024 == 0 else 1
    dma = pltpu.SemaphoreType.DMA
    buffer = pltpu.VMEM((pairs, rows, part), BF16)
    scratch = [buffer] * 4 + [dma((pairs, cuts))] * 7
    if local:
        scratch += [
            buffer,
            pltpu.VMEM((micro, group, local * capacity), BF16),
            pltpu.VMEM((2, local, micro, capacity, part), BF16),
            dma((2, local)),
        ]
    out_shape = [jax.ShapeDtypeStruct((rows, part), F32)]
    if stage:
        extra, ring = others[0], n_row if stage == 2 else n_col
        out_shape.append(jax.ShapeDtypeStruct((ring,) + extra.shape, extra.dtype))
        scratch += [dma((ring,)), dma((ring,)), dma(())]
    if stage == 2:
        scratch += [dma((2, n_row)), dma((2, n_row)), dma((2,))]
        for value in others[1:]:
            out_shape.append(jax.ShapeDtypeStruct((n_row, per) + value.shape[1:], BF16))
    if stage == 3:
        heads, branch = others[1:]
        scratch += [dma((2, n_col)), dma((2, n_col)), dma((2,))]
        out_shape += [
            jax.ShapeDtypeStruct((n_col, 3, heads.shape[1] // n_col, heads.shape[2]), BF16),
            jax.ShapeDtypeStruct((n_col, branch.shape[0] // n_col, branch.shape[1]), BF16),
        ]
    first = [pl.BlockSpec(memory_space=pltpu.VMEM)] + [ANY] * local if local else [ANY]
    values = (place, *x) if local else (x,)
    return pl.pallas_call(
        functools.partial(scatter_body, part, stage, local),
        in_specs=first + [ANY] * len(others),
        out_specs=[pl.BlockSpec(memory_space=pltpu.VMEM)] + [ANY] * (len(out_shape) - 1),
        out_shape=out_shape,
        scratch_shapes=scratch,
        compiler_params=pltpu.CompilerParams(
            vmem_limit_bytes=VMEM_LIMIT, collective_id=ident, has_side_effects=True
        ),
        cost_estimate=pl.CostEstimate(
            flops=0, bytes_accessed=rows * part * n_col * 40, transcendentals=0
        ),
        name="scatter_col",
    )(*values, *others)


def shards(
    tokens,
    gain_attn,
    gain_ffn,
    gain_query,
    gain_key,
    w_query,
    w_key,
    w_value,
    w_out,
    w_router,
    w_gate,
    w_up,
    w_down,
    routes,
    lengths,
    cotangent,
):
    n_col = lax.axis_size("col")
    n_row = lax.axis_size("row")
    col = lax.axis_index("col")
    micro, spans = lengths.shape
    rows, part = tokens.shape
    group = rows // micro
    width = part * n_col
    head = gain_query.shape[0]
    local_exp = w_gate.shape[0]
    experts = local_exp * n_col
    topk = routes.shape[1]
    capacity = 2 * group * topk // experts
    local_heads = w_out.shape[0] // head
    hd = w_out.shape[0] * n_col
    scale = head ** (-0.5)

    def gather(value, axis_name, axis):
        return lax.all_gather(value, axis_name, axis=axis, tiled=True)

    def mine(value, axis):
        size = value.shape[axis] // n_col
        return lax.dynamic_slice_in_dim(value, col * size, size, axis)

    shared = w_down.shape[2]
    pair = 2 if local_exp % 2 == 0 else 1
    spans = [(0, pair)] + [(at, 1) for at in range(pair, local_exp)]
    big = {}
    for first, count in spans:
        whole = gather(pack(w_gate, w_up, w_down, first, count), "row", 2)
        for e in range(count):
            big[first + e] = (whole, e)
    inputs_low, gains, w_heads, rows_o, rows_r, *wide = front(
        tokens,
        jnp.stack([gain_attn, gain_ffn]),
        w_query,
        w_key,
        w_value,
        w_out,
        w_router.T,
        head,
        0,
    )

    segment, position, live = jax.vmap(lambda l: layout(l, group))(lengths)
    position = position.reshape(rows)
    live = live.reshape(rows)
    upstream_part = cotangent.astype(F32) * live[:, None]
    member = jnp.any(
        routes[:, None, :] == jnp.arange(experts, dtype=jnp.int32)[None, :, None], -1
    )
    member_f = member.astype(F32)
    member_loc = mine(member_f, 1).reshape(micro, group, local_exp)
    lower = (
        jnp.arange(group, dtype=jnp.int32)[:, None] > jnp.arange(group, dtype=jnp.int32)[None, :]
    ).astype(BF16)
    before = jnp.einsum("st,gte->gse", lower, member_loc.astype(BF16), preferred_element_type=F32)
    place = jnp.where(member_loc > 0, before, -1.0).astype(jnp.int32)
    counts = jnp.sum(member_loc, 1).astype(jnp.int32).T
    place_t = place.transpose(2, 0, 1)[:, :, None, :]

    inputs = inputs_low.astype(F32)
    scale_one = inverse_rms(inputs)
    normed = (inputs * scale_one * gains[0]).astype(BF16)
    all_heads = jnp.concatenate([w_heads[j] for j in range(3)], 1)
    query_pre, key_pre, value_pre = jnp.split(nn(normed, all_heads), 3, 1)
    shape = (rows, local_heads, head)
    cosine, sine = rope_tables(position, head)

    def head_norm(values, gain):
        return rotary(values * inverse_rms(values) * gain, cosine, sine)

    query_rot, query_pull = jax.vjp(head_norm, query_pre.reshape(shape), gain_query)
    key_rot, key_pull = jax.vjp(head_norm, key_pre.reshape(shape), gain_key)
    batch = (micro, group, local_heads, head)
    queries = query_rot.astype(BF16).reshape(batch)
    keys_low = key_rot.astype(BF16).reshape(batch)
    values_low = value_pre.astype(BF16).reshape(batch)
    same = (segment[:, :, None] == segment[:, None, :])[:, None]

    def scores_of():
        raw = jnp.einsum("gqhd,gkhd->ghqk", queries, keys_low, preferred_element_type=F32) * scale
        return jnp.where(same, raw, MASKED)

    scores = scores_of()
    highest = jnp.max(scores, -1, keepdims=True)
    log_total = highest + jnp.log(jnp.sum(jnp.exp(scores - highest), -1, keepdims=True))
    probs_low = jnp.exp(scores - log_total).astype(BF16)
    attended = jnp.einsum(
        "ghqk,gkhd->gqhd", probs_low, values_low, preferred_element_type=F32
    ).astype(BF16)
    attended_full, full_o, full_rt, upstream_low = middle_gather(
        [attended.reshape(rows, local_heads * head), rows_o, rows_r, upstream_part.astype(BF16)],
        (1, 0, 1, 1),
        1,
    )
    full_r = full_rt.T

    hidden = inputs + nn(attended_full, full_o)
    scale_two = inverse_rms(hidden)
    normed_ffn = (hidden * scale_two * gains[1]).astype(BF16)
    logits = nn(normed_ffn, full_r)
    peak = jnp.max(jnp.where(member, logits, -jnp.inf), -1, keepdims=True)
    raised = jnp.where(member, jnp.exp(jnp.where(member, logits - peak, 0.0)), 0.0)
    gates = raised / jnp.sum(raised, -1, keepdims=True)
    gate_t = mine(gates, 1).reshape(micro, group, local_exp).transpose(2, 0, 1)[:, :, None, :]
    upstream_full = upstream_low.reshape(micro, group, width)
    hn = normed_ffn.reshape(micro, group, width)

    outs, weight_grads, grad = [], [], None
    for e in range(local_exp):
        xe, dyr, hg, dgp, dup, ye, dxe, tok = expert_pass(
            counts[e],
            place_t[e],
            gate_t[e],
            hn,
            upstream_full,
            *big[e],
            capacity,
            shared,
        )
        held = () if e % pair == 0 else (grad,)
        grad = expert_grads(xe, dgp, dup, hg, dyr, shared, e % pair, pair, held)
        hn, upstream_full, ye, dxe, tok, grad = lax.optimization_barrier(
            (hn, upstream_full, ye, dxe, tok, grad)
        )
        outs.append((ye, dxe, tok))
        if e % pair == pair - 1:
            weight_grads.append(lax.psum_scatter(grad, "row", scatter_dimension=2, tiled=True))

    def tie(value, e):
        value, weight_grads[e] = lax.optimization_barrier((value, weight_grads[e]))
        return value

    row = lax.axis_index("row")
    back_sum, tok = scatter_col(
        [o[1] for o in outs], 2, 1, (jnp.stack([o[2] for o in outs]),), place
    )
    tok = tok.reshape((experts,) + tok.shape[2:])
    hidden_part = tokens.astype(F32) + nn(attended_full, mine(full_o, 1))
    gate_dots = tok[:, :, 0].reshape(experts, rows).T
    hidden_part = mine(hidden, 1)

    selected = gates * (gate_dots - jnp.sum(gates * gate_dots, -1, keepdims=True))
    logit_grad = selected.astype(BF16)
    router_part = mine(full_r, 0)
    normed_grad = back_sum + nt(logit_grad, router_part)
    grad_router = tn(mine(normed_ffn, 1), logit_grad)
    scaled_two = hidden_part * scale_two
    grad_gain_ffn = jnp.sum(normed_grad * scaled_two, 0)
    dot_two = jnp.sum(tok[:, :, 1].reshape(experts, rows), 0) + jnp.sum(
        logit_grad.astype(F32) * logits, 1
    )
    hidden_grad = (
        upstream_part
        + scale_two * (normed_grad * gain_ffn)
        - hidden_part * scale_two**2 * dot_two[:, None] / width
    )

    branch_grad = hidden_grad.astype(BF16)
    (attended_grad,) = scatter_col(nt(branch_grad, mine(full_o, 1)).astype(BF16), 3)
    attended_grad = attended_grad.astype(BF16).reshape(batch)
    grad_out = tn(attended_full, branch_grad)
    scores_again = scores_of()
    probs = jnp.exp(scores_again - log_total)
    probs_again = probs.astype(BF16)
    probs_grad = jnp.einsum(
        "gqhd,gkhd->ghqk", attended_grad, values_low, preferred_element_type=F32
    )
    values_grad = jnp.einsum(
        "ghqk,gqhd->gkhd", probs_again, attended_grad, preferred_element_type=F32
    )
    score_grad = (probs * (probs_grad - jnp.sum(probs_grad * probs, -1, keepdims=True))).astype(
        BF16
    )
    query_grad_rot = (
        jnp.einsum("ghqk,gkhd->gqhd", score_grad, keys_low, preferred_element_type=F32) * scale
    )
    key_grad_rot = (
        jnp.einsum("ghqk,gqhd->gkhd", score_grad, queries, preferred_element_type=F32) * scale
    )
    query_grad, gain_query_part = query_pull(query_grad_rot.reshape(shape))
    key_grad, gain_key_part = key_pull(key_grad_rot.reshape(shape))
    flat = (rows, local_heads * head)
    heads_grad = [
        v.reshape(flat).astype(BF16) for v in (query_grad, key_grad, values_grad)
    ]
    all_grads = jnp.concatenate(heads_grad, 1)
    back_heads = nt(all_grads, all_heads)
    pre = (query_pre, key_pre, value_pre)
    dot_part = sum(jnp.sum(g.astype(F32) * p, -1) for g, p in zip(heads_grad, pre))
    sums = jnp.concatenate([dot_part, gain_query_part, gain_key_part])
    sums = jnp.pad(sums, (0, -sums.shape[0] % 1024)).reshape(-1, 128)
    heads_weights = tn(normed, all_grads).astype(BF16)
    heads_weights = jnp.stack(jnp.split(heads_weights, 3, 1))
    back_heads, mixed_slots = lax.optimization_barrier(
        (back_heads.astype(BF16), [o[0] for o in outs])
    )
    mixed_sum, sums, heads_terms, out_terms = scatter_col(
        mixed_slots, 4, 3, (sums, heads_weights, grad_out.astype(BF16)), place
    )
    mixed = (hidden_part + mixed_sum).astype(BF16)
    sums = jnp.sum(sums, 0).reshape(-1)
    dot_one = sums[:rows]
    gain_attn_part = 0.0
    for m in range(3):
        for c in range(n_col):
            columns = wide[m][:, c * local_heads * head : (c + 1) * local_heads * head]
            gain_attn_part = gain_attn_part + jnp.sum(
                columns.astype(F32) * heads_terms[c, m].astype(F32), -1
            )
    smalls = jnp.concatenate(
        [
            gain_attn_part,
            grad_gain_ffn,
            sums[rows : rows + 2 * head],
            grad_router.T.reshape(-1),
        ]
    ).reshape(-1, 128)
    back_heads, mixed = lax.optimization_barrier((back_heads, mixed))
    normed_back, smalls, heads_terms, out_terms = scatter_col(
        tie(back_heads, 0), 5, 2, (smalls, heads_terms, out_terms)
    )
    scale_one_part = scale_one
    inputs_part = tokens.astype(F32)
    input_grad = (
        hidden_grad
        + scale_one_part * (normed_back * gain_attn)
        - inputs_part * scale_one_part**2 * dot_one[:, None] / width
    )

    held = ()
    for e, grad in enumerate(weight_grads):
        held = unpack(grad, held, e * pair, local_exp)
    grad_gate, grad_up, grad_down = held

    heads_terms = jnp.sum(heads_terms.astype(F32), 0)
    heads_sum = jnp.concatenate([heads_terms[j] for j in range(heads_terms.shape[0])], -1)
    grad_query, grad_key, grad_value = heads_sum[0], heads_sum[1], heads_sum[2]
    out_terms = jnp.sum(out_terms.astype(F32), 0)
    grad_out = jnp.concatenate([out_terms[j] for j in range(out_terms.shape[0])], -1)
    row = lax.axis_index("row")
    total = jnp.sum(smalls, 0).reshape(-1)
    grad_gain_attn, grad_gain_ffn = total[:part] / gain_attn, total[part : 2 * part]
    grad_gain_query = total[2 * part : 2 * part + head]
    grad_gain_key = total[2 * part + head : 2 * part + 2 * head]
    grad_router = lax.dynamic_slice_in_dim(
        total[2 * part + 2 * head :].reshape(experts, part), row * (experts // n_row), experts // n_row, 0
    ).T
    return (
        mixed,
        input_grad,
        grad_gain_attn,
        grad_gain_ffn,
        grad_gain_query,
        grad_gain_key,
        grad_query,
        grad_key,
        grad_value,
        grad_out,
        grad_router,
        grad_gate,
        grad_up,
        grad_down,
    )


def solution(mesh):
    placed = (
        P("row", "col"),
        P("col"),
        P("col"),
        P(),
        P(),
        P("col", "row"),
        P("col", "row"),
        P("col", "row"),
        P("col", "row"),
        P("col", "row"),
        P("col", "row", None),
        P("col", "row", None),
        P("col", None, "row"),
        P("row", None),
        P("row", None),
        P("row", "col"),
    )
    return jax.shard_map(
        shards,
        mesh=mesh,
        in_specs=placed,
        out_specs=(
            P("row", "col"),
            P("row", "col"),
            P("col"),
            P("col"),
            P(),
            P(),
            P("col", "row"),
            P("col", "row"),
            P("col", "row"),
            P("col", "row"),
            P("col", "row"),
            P("col", "row", None),
            P("col", "row", None),
            P("col", None, "row"),
        ),
        check_vma=False,
    )
```

```python
import functools
import math

import jax
import jax.numpy as jnp
from jax import lax
from jax.experimental import pallas as pl
from jax.experimental.pallas import tpu as pltpu
from jax.sharding import PartitionSpec as P

EPSILON = 1e-06
ROPE_BASE = 10000.0
MASKED = -1e30
F32 = jnp.float32
BF16 = jnp.bfloat16
VMEM_LIMIT = 60 * 1024 * 1024
MESH = pl.DeviceIdType.MESH
ANY = pl.BlockSpec(memory_space=pl.ANY)


def inverse_rms(values):
    return lax.rsqrt(jnp.mean(values * values, -1, keepdims=True) + EPSILON)


def rope_tables(position, head):
    half = head // 2
    inverse = jnp.exp(-math.log(ROPE_BASE) * 2.0 / head * jnp.arange(half, dtype=F32))
    angles = position[:, None] * inverse[None, :]
    return jnp.cos(angles)[:, None, :], jnp.sin(angles)[:, None, :]


def rotary(values, cosine, sine):
    half = values.shape[-1] // 2
    first = values[..., :half]
    second = values[..., half:]
    return jnp.concatenate([first * cosine - second * sine, second * cosine + first * sine], -1)


def layout(lengths_row, group):
    ends = jnp.cumsum(lengths_row)
    starts = ends - lengths_row
    row_index = jnp.arange(group, dtype=jnp.int32)
    segment = jnp.sum((row_index[:, None] >= ends[None, :]).astype(jnp.int32), 1)
    member = segment[:, None] == jnp.arange(lengths_row.shape[0], dtype=jnp.int32)[None, :]
    position = (row_index - jnp.sum(jnp.where(member, starts[None, :], 0), 1)).astype(F32)
    live = (segment < lengths_row.shape[0] - 1).astype(F32)
    return (segment, position, live)


def nn(a, b):
    return lax.dot_general(a, b, (((1,), (0,)), ((), ())), preferred_element_type=F32)


def nt(a, b):
    return lax.dot_general(a, b, (((1,), (1,)), ((), ())), preferred_element_type=F32)


def tn(a, b):
    return lax.dot_general(a, b, (((0,), (0,)), ((), ())), preferred_element_type=F32)


def expert_body(shared, counts, place, gate, hn, dy, w, xe_o, dyr_o, hg_o, dgp_o, dup_o, ye_o, dxe_o, tok_o):
    g, i = pl.program_id(0), pl.program_id(1)
    rows = xe_o.shape[1]
    width, ff = w.shape[2:]
    base = i * rows

    @pl.when(i == 0)
    def _():
        tok_o[...] = jnp.zeros_like(tok_o)

    @pl.when(counts[g] <= base)
    def _():
        for ref in (xe_o, dyr_o, hg_o, dgp_o, dup_o, ye_o, dxe_o):
            ref[...] = jnp.zeros_like(ref)

    @pl.when(counts[g] > base)
    def _():
        slot = lax.broadcasted_iota(jnp.int32, (rows, place.shape[2]), 0) + base
        hit = slot == place[0]
        pick = jnp.where(hit, 1.0, 0.0).astype(BF16)
        weight = jnp.sum(jnp.where(hit, gate[0], 0.0), 1, keepdims=True)
        xe = nn(pick, hn[0]).astype(BF16)
        xe_o[0] = xe
        gp = nn(xe, w[0, 0])
        up = nn(xe, w[0, 1])
        sig = jax.nn.sigmoid(gp)
        silu = gp * sig
        hid = silu * up
        hg = (hid * weight).astype(BF16)
        hg_o[0] = hg
        dyr = nn(pick, dy[0]).astype(BF16)
        dyr_o[0] = dyr
        parts = []
        for r in range(width // shared):
            at = r * shared
            total = None
            for b in range(ff // shared):
                low = b * shared
                term = nn(hg[:, low : low + shared], w[0, 2, at : at + shared, low : low + shared])
                total = term if total is None else total + term
            ye_o[0, :, at : at + shared] = total.astype(BF16)
        for b in range(ff // shared):
            low = b * shared
            total = None
            for r in range(width // shared):
                at = r * shared
                term = nt(dyr[:, at : at + shared], w[0, 2, at : at + shared, low : low + shared])
                total = term if total is None else total + term
            parts.append(total)
        back = jnp.concatenate(parts, 1)
        dgate = jnp.sum(back * hid, 1, keepdims=True)
        dhid = back * weight
        dgp = (dhid * up * sig * (1.0 + gp * (1.0 - sig))).astype(BF16)
        dup = (dhid * silu).astype(BF16)
        dgp_o[0] = dgp
        dup_o[0] = dup
        dots = jnp.sum(dgp.astype(F32) * gp + dup.astype(F32) * up, 1, keepdims=True)
        dxe_o[0] = (nt(dgp, w[0, 0]) + nt(dup, w[0, 1])).astype(BF16)
        tok_o[0, 0:1, :] += jnp.sum(jnp.where(hit, dgate, 0.0), 0, keepdims=True)
        tok_o[0, 1:2, :] += jnp.sum(jnp.where(hit, dots, 0.0), 0, keepdims=True)


def expert_pass(counts, place, gate, hn, dy, w, at, capacity, shared):
    width, ff = w.shape[2:]
    micro, group, _ = hn.shape
    rows = min(256, capacity)
    blocks = capacity // rows
    tall = lambda g, i, c: (g, i, 0)
    line = lambda g, i, c: (g, 0, 0)
    slots = lambda n: jax.ShapeDtypeStruct((micro, capacity, n), BF16)
    sizes = (width, width, ff, ff, ff, width, width)
    flops = 2 * micro * capacity * width * (6 * ff + 2 * group)
    return pl.pallas_call(
        functools.partial(expert_body, shared),
        grid_spec=pltpu.PrefetchScalarGridSpec(
            num_scalar_prefetch=1,
            grid=(micro, blocks),
            in_specs=[
                pl.BlockSpec((1, 1, group), line),
                pl.BlockSpec((1, 1, group), line),
                pl.BlockSpec((1, group, width), line),
                pl.BlockSpec((1, group, width), line),
                pl.BlockSpec(
                    (1, 3, width, ff), lambda g, i, c: (at, 0, 0, 0), pipeline_mode=pl.Buffered(1)
                ),
            ],
            out_specs=[pl.BlockSpec((1, rows, n), tall) for n in sizes]
            + [pl.BlockSpec((1, 2, group), line)],
        ),
        out_shape=[slots(n) for n in sizes] + [jax.ShapeDtypeStruct((micro, 2, group), F32)],
        compiler_params=pltpu.CompilerParams(vmem_limit_bytes=VMEM_LIMIT),
        cost_estimate=pl.CostEstimate(
            flops=flops, bytes_accessed=40 << 20, transcendentals=micro * capacity * ff
        ),
        name="expert_pass",
    )(counts, place, gate, hn, dy, w)


def grads_body(xe, dgp, dup, hg, dyr, *rest):
    out = rest[-1]
    part = xe[...]
    shared = part.shape[1]
    out[0, 0] = tn(part, dgp[...]).astype(BF16)
    out[0, 1] = tn(part, dup[...]).astype(BF16)
    back = dyr[...]
    for b in range(hg.shape[1] // shared):
        low = b * shared
        out[0, 2, :, low : low + shared] = tn(hg[:, low : low + shared], back).astype(BF16)


def expert_grads(xe, dgp, dup, hg, dyr, shared, at, pair, held):
    micro, capacity, width = xe.shape
    ff = dgp.shape[2]
    rows = micro * capacity
    xe, dyr = (a.reshape(rows, width) for a in (xe, dyr))
    dgp, dup, hg = (a.reshape(rows, ff) for a in (dgp, dup, hg))
    thin = pl.BlockSpec((rows, shared), lambda r: (0, r))
    whole = pl.BlockSpec((rows, ff), lambda r: (0, 0))
    return pl.pallas_call(
        grads_body,
        grid=(width // shared,),
        in_specs=[thin, whole, whole, whole, thin] + [ANY] * len(held),
        out_specs=pl.BlockSpec((1, 3, shared, ff), lambda r: (at, 0, r, 0)),
        out_shape=jax.ShapeDtypeStruct((pair, 3, width, ff), BF16),
        input_output_aliases={5: 0} if held else {},
        compiler_params=pltpu.CompilerParams(vmem_limit_bytes=VMEM_LIMIT),
        cost_estimate=pl.CostEstimate(
            flops=6 * rows * width * ff, bytes_accessed=26 << 20, transcendentals=0
        ),
        name="expert_grads",
    )(xe, dgp, dup, hg, dyr, *held)


def pack_body(wg, wu, wd, out):
    shared = out.shape[2]
    out[0, 0] = wg[0]
    out[0, 1] = wu[0]
    for b in range(out.shape[3] // shared):
        low = b * shared
        out[0, 2, :, low : low + shared] = wd[0, low : low + shared, :]


def pack(wg, wu, wd, first, pair):
    _, shared, ff = wg.shape
    block = pl.BlockSpec((1, shared, ff), lambda i: (first + i, 0, 0))
    return pl.pallas_call(
        pack_body,
        grid=(pair,),
        in_specs=[block, block, pl.BlockSpec((1, ff, shared), lambda i: (first + i, 0, 0))],
        out_specs=pl.BlockSpec((1, 3, shared, ff), lambda i: (i, 0, 0, 0)),
        out_shape=jax.ShapeDtypeStruct((pair, 3, shared, ff), BF16),
        cost_estimate=pl.CostEstimate(
            flops=0, bytes_accessed=pair * 12 * shared * ff, transcendentals=0
        ),
        name="pack",
    )(wg, wu, wd)


def unpack_body(x, *refs):
    gg, gu, gd = refs[-3:]
    shared = x.shape[2]
    gg[0] = x[0, 0].astype(F32)
    gu[0] = x[0, 1].astype(F32)
    for b in range(x.shape[3] // shared):
        low = b * shared
        gd[0, low : low + shared, :] = x[0, 2, :, low : low + shared].astype(F32)


def unpack(x, held, first, experts):
    pair, _, shared, ff = x.shape
    block = pl.BlockSpec((1, shared, ff), lambda i: (first + i, 0, 0))
    return pl.pallas_call(
        unpack_body,
        grid=(pair,),
        in_specs=[pl.BlockSpec((1, 3, shared, ff), lambda i: (i, 0, 0, 0))] + [ANY] * len(held),
        out_specs=[block, block, pl.BlockSpec((1, ff, shared), lambda i: (first + i, 0, 0))],
        out_shape=[
            jax.ShapeDtypeStruct((experts, shared, ff), F32),
            jax.ShapeDtypeStruct((experts, shared, ff), F32),
            jax.ShapeDtypeStruct((experts, ff, shared), F32),
        ],
        input_output_aliases={1 + j: j for j in range(len(held))},
        compiler_params=pltpu.CompilerParams(vmem_limit_bytes=VMEM_LIMIT),
        cost_estimate=pl.CostEstimate(
            flops=0, bytes_accessed=pair * 18 * shared * ff, transcendentals=0
        ),
        name="unpack",
    )(x, *held)


def places():
    row, col = lax.axis_index("row"), lax.axis_index("col")
    n_row, n_col = lax.axis_size("row"), lax.axis_size("col")
    return row, col, n_row, n_col


def remote(src, dst, send_sem, recv_sem, where):
    return pltpu.make_async_remote_copy(
        src_ref=src,
        dst_ref=dst,
        send_sem=send_sem,
        recv_sem=recv_sem,
        device_id=where,
        device_id_type=MESH,
    )


def shake(sources, targets):
    barrier = pltpu.get_barrier_semaphore()
    for ok, where in sources:
        if ok is True:
            pl.semaphore_signal(barrier, inc=1, device_id=where, device_id_type=MESH)
        else:

            @pl.when(ok)
            def _():
                pl.semaphore_signal(barrier, inc=1, device_id=where, device_id_type=MESH)

    count = 0
    for ok in targets:
        count = count + (1 if ok is True else jnp.where(ok, 1, 0))
    pl.semaphore_wait(barrier, count)


def line_peers():
    row, col, n_row, n_col = places()
    pair, core = col // 2, col % 2
    return [
        (True, (row, pair * 2 + 1 - core)),
        (pair > 0, (row, (pair - 1) * 2 + core)),
        (pair < n_col // 2 - 1, (row, (pair + 1) * 2 + core)),
    ]


def row_peers():
    row, col, n_row, n_col = places()
    return [(True, ((row + k) % n_row, col)) for k in range(1, n_row)]


def col_slice(ref, index, size):
    return ref.at[..., pl.ds(pl.multiple_of(index * size, size), size)]


def line_gather(axes, ins, outs, sems):
    own_sem, right_s, right_r, left_s, left_r, side_s, side_r = sems
    n = len(ins)
    row, col, n_row, n_col = places()
    pairs, pair, core = n_col // 2, col // 2, col % 2

    def at(pair_index, core_index):
        return (row, pair_index * 2 + core_index)

    def block(j, source):
        size = ins[j].shape[axes[j]]
        if axes[j] == 0:
            return outs[j].at[pl.ds(pl.multiple_of(source * size, size), size)]
        return col_slice(outs[j], source, size)

    def right(j, s):
        source = (pair - s) * 2 + core
        src = ins[j] if s == 0 else block(j, source)
        return remote(src, block(j, source), right_s.at[j, s], right_r.at[j, s], at(pair + 1, core))

    def left(j, s):
        source = (pair + s) * 2 + core
        src = ins[j] if s == 0 else block(j, source)
        return remote(src, block(j, source), left_s.at[j, s], left_r.at[j, s], at(pair - 1, core))

    def side(j, source_pair, first=False):
        source = source_pair * 2 + core
        src = ins[j] if first else block(j, source)
        return remote(
            src,
            block(j, source),
            side_s.at[j, source_pair],
            side_r.at[j, source_pair],
            at(pair, 1 - core),
        )

    def arrived(j, recvs, slot, source):
        remote(
            ins[j], block(j, source), recvs.at[j, slot], recvs.at[j, slot], at(pair, 1 - core)
        ).wait_recv()

    def own(j):
        return pltpu.make_async_copy(ins[j], block(j, col), own_sem.at[j])

    def begin():
        for j in range(n):

            @pl.when(pair < pairs - 1)
            def _():
                right(j, 0).start()

            @pl.when(pair > 0)
            def _():
                left(j, 0).start()

        for j in range(n):
            side(j, pair, True).start()
            own(j).start()

    def middle():
        for s in range(1, pairs):
            for j in range(n):

                @pl.when(pair >= s)
                def _():
                    arrived(j, right_r, s - 1, (pair - s) * 2 + core)

                    @pl.when(pair < pairs - 1)
                    def _():
                        right(j, s).start()

                    side(j, pair - s).start()

                @pl.when(pair + s < pairs)
                def _():
                    arrived(j, left_r, s - 1, (pair + s) * 2 + core)

                    @pl.when(pair > 0)
                    def _():
                        left(j, s).start()

                    side(j, pair + s).start()

    def end():
        for j in range(n):
            own(j).wait()
            for p in range(pairs):
                side(j, p).wait_send()
                arrived(j, side_r, p, p * 2 + 1 - core)
            for s in range(pairs):

                @pl.when((pair >= s) & (pair < pairs - 1))
                def _():
                    right(j, s).wait_send()

                @pl.when((pair + s < pairs) & (pair > 0))
                def _():
                    left(j, s).wait_send()

    return begin, middle, end


def line_sems(n, pairs):
    dma = pltpu.SemaphoreType.DMA
    return [dma((n,))] + [dma((n, pairs))] * 6


def front_body(tokens, gains, wq, wk, wv, wo, wr, *refs):
    x_o, gains_o, wh_o, wo_o, wr_o = refs[:5]
    wide = refs[5:8]
    line, (heads_s, heads_r, row_s, row_r, own_s) = refs[8:15], refs[15:]
    row, col, n_row, n_col = places()
    head = wh_o.shape[2]
    part = wq.shape[0]
    begin, middle, end = line_gather((1, 1), [tokens, gains], [x_o, gains_o], line)
    small = [(wq, wide[0]), (wk, wide[1]), (wv, wide[2]), (wo, wo_o), (wr, wr_o)]

    def small_dst(k, source):
        src, dst = small[k]
        if k < 4:
            return col_slice(dst, source, src.shape[1])
        return dst.at[pl.ds(pl.multiple_of(source * src.shape[0], src.shape[0]), src.shape[0]), :]

    def small_copy(k, step):
        return remote(
            small[k][0],
            small_dst(k, row),
            row_s.at[k, step],
            row_r.at[k, step],
            ((row + step) % n_row, col),
        )

    def small_come(k, step):
        source = (row + n_row - step) % n_row
        return remote(
            small[k][0], small_dst(k, source), row_s.at[k, step], row_r.at[k, step], (source, col)
        )

    def small_own(k):
        return pltpu.make_async_copy(small[k][0], small_dst(k, row), own_s.at[k])

    def heads_dst(m, source):
        return wh_o.at[m, pl.ds(pl.multiple_of(source * part, part), part), :]

    def heads(m, step):
        where = (col + step) % n_col
        return remote(
            col_slice(wide[m], where, head),
            heads_dst(m, col),
            heads_s.at[m, step],
            heads_r.at[m, step],
            (row, where),
        )

    def heads_come(m, step):
        source = (col + n_col - step) % n_col
        return remote(
            heads_dst(m, source),
            heads_dst(m, source),
            heads_s.at[m, step],
            heads_r.at[m, step],
            (row, source),
        )

    def heads_own(m):
        return pltpu.make_async_copy(
            col_slice(wide[m], col, head), heads_dst(m, col), own_s.at[5 + m]
        )

    peers = [(True, (row, (col + k) % n_col)) for k in range(1, n_col)] + row_peers()
    shake(peers, [ok for ok, _ in peers])
    for k in range(5):
        for step in range(1, n_row):
            small_copy(k, step).start()
        small_own(k).start()
    begin()
    for k in range(3):
        small_own(k).wait()
        for step in range(1, n_row):
            small_come(k, step).wait_recv()
    for m in range(3):
        heads_own(m).start()
        for step in range(1, n_col):
            heads(m, step).start()
    middle()
    end()
    for k in range(5):
        if k >= 3:
            small_own(k).wait()
        for step in range(1, n_row):
            small_copy(k, step).wait_send()
            if k >= 3:
                small_come(k, step).wait_recv()
    for m in range(3):
        heads_own(m).wait()
        for step in range(1, n_col):
            heads(m, step).wait_send()
            heads_come(m, step).wait_recv()


def front(tokens, gains, wq, wk, wv, wo, wr, head, ident):
    n_row, n_col = lax.axis_size("row"), lax.axis_size("col")
    rows, part = tokens.shape
    width = part * n_col
    dma = pltpu.SemaphoreType.DMA
    shapes = [
        ((rows, width), BF16),
        ((gains.shape[0], width), F32),
        ((3, width, head), BF16),
        ((wo.shape[0], wo.shape[1] * n_row), BF16),
        ((wr.shape[0] * n_row, part), BF16),
    ] + [((part, wq.shape[1] * n_row), BF16)] * 3
    return pl.pallas_call(
        front_body,
        in_specs=[ANY] * 7,
        out_specs=[ANY] * 8,
        out_shape=[jax.ShapeDtypeStruct(s, t) for s, t in shapes],
        scratch_shapes=line_sems(2, n_col // 2)
        + [
            dma((3, n_col)),
            dma((3, n_col)),
            dma((5, n_row)),
            dma((5, n_row)),
            dma((8,)),
        ],
        compiler_params=pltpu.CompilerParams(collective_id=ident, has_side_effects=True),
        cost_estimate=pl.CostEstimate(
            flops=0, bytes_accessed=rows * width * 32, transcendentals=0
        ),
        name="front",
    )(tokens, gains, wq, wk, wv, wo, wr)


def middle_body(axes, *refs):
    n = len(axes)
    begin, middle, end = line_gather(axes, refs[:n], refs[n : 2 * n], refs[2 * n :])
    sources = line_peers()
    shake(sources, [ok for ok, _ in sources])
    begin()
    middle()
    end()


def middle_gather(arrays, axes, ident):
    n_col, n = lax.axis_size("col"), len(arrays)
    shapes = [
        tuple(d * n_col if at == axis else d for at, d in enumerate(a.shape))
        for a, axis in zip(arrays, axes)
    ]
    return pl.pallas_call(
        functools.partial(middle_body, axes),
        in_specs=[ANY] * n,
        out_specs=[ANY] * n,
        out_shape=[jax.ShapeDtypeStruct(s, a.dtype) for s, a in zip(shapes, arrays)],
        scratch_shapes=line_sems(n, n_col // 2),
        compiler_params=pltpu.CompilerParams(collective_id=ident, has_side_effects=True),
        cost_estimate=pl.CostEstimate(
            flops=0, bytes_accessed=sum(math.prod(s) for s in shapes) * 32, transcendentals=0
        ),
        name="middle_gather",
    )(*arrays)


def scatter_body(part, stage, local, *refs):
    n_in = (1, 2, 4, 4)[stage]
    n_out = (1, 2, 4, 4)[stage]
    if local:
        place, slots, refs = refs[0], refs[1 : 1 + local], refs[local:]
    x, ins = refs[0], refs[1:n_in]
    out, outs = refs[n_in], refs[n_in + 1 : n_in + n_out]
    rest = refs[n_in + n_out :]
    acc, side, from_left, from_right, load, side_s, side_r = rest[:7]
    right_s, right_r, left_s, left_r = rest[7:11]
    if local:
        give, chosen, held, held_s = rest[11:15]
        rest = rest[4:]
    row, col, n_row, n_col = places()
    pairs, pair, core = n_col // 2, col // 2, col % 2
    rows = out.shape[0]
    cuts = load.shape[1]
    height = rows // cuts
    tile = min(256, height)

    def at(pair_index, core_index):
        return (row, pair_index * 2 + core_index)

    def block(owner, q):
        return x.at[
            pl.ds(q * height, height), pl.ds(pl.multiple_of(owner * part, part), part)
        ]

    def cut(ref, d, q):
        return ref.at[d, pl.ds(q * height, height)]

    def fetch(d, q):
        return pltpu.make_async_copy(block(d * 2 + core, q), cut(acc, d, q), load.at[d, q])

    def across(d, q):
        return remote(
            cut(give, d, q) if local else block(d * 2 + 1 - core, q),
            cut(side, d, q),
            side_s.at[d, q],
            side_r.at[d, q],
            at(pair, 1 - core),
        )

    def right(d, q):
        return remote(
            cut(acc, d, q),
            cut(from_left, d, q),
            right_s.at[d, q],
            right_r.at[d, q],
            at(pair + 1, core),
        )

    def left(d, q):
        return remote(
            cut(acc, d, q),
            cut(from_right, d, q),
            left_s.at[d, q],
            left_r.at[d, q],
            at(pair - 1, core),
        )

    copies, arrivals, own = [], [], []
    if stage:
        small_s, small_r, own_s = rest[11:14]
        extra, extra_o = ins[0], outs[0]
        here, ring = (row, n_row) if stage == 2 else (col, n_col)
        for k in range(1, ring):
            where, source = (here + k) % ring, (here + ring - k) % ring
            to = (where, col) if stage == 2 else (row, where)
            copies.append(remote(extra, extra_o.at[here], small_s.at[k], small_r.at[k], to))
            arrivals.append(remote(extra, extra_o.at[source], small_s.at[k], small_r.at[k], to))
        own.append(pltpu.make_async_copy(extra, extra_o.at[here], own_s))
    if stage == 2:
        give_s, give_r, keep_s = rest[14:]
        per = n_col // n_row
        for m in range(2):
            src, dst = ins[1 + m], outs[1 + m]

            def block_of(r):
                return src.at[pl.ds(r * per, per)]

            for step in range(1, n_row):
                where, source = (row + step) % n_row, (row + n_row - step) % n_row
                sems = (give_s.at[m, step], give_r.at[m, step])
                copies.append(remote(block_of(where), dst.at[row], *sems, (where, col)))
                arrivals.append(remote(block_of(where), dst.at[source], *sems, (where, col)))
            own.append(pltpu.make_async_copy(block_of(row), dst.at[row], keep_s.at[m]))
    if stage == 3:
        give_s, give_r, keep_s = rest[14:]
        for m in range(2):
            src, dst = ins[1 + m], outs[1 + m]
            size = src.shape[1 - m] // n_col

            def block_for(c):
                at_c = pl.ds(pl.multiple_of(c * size, size), size)
                return src.at[:, at_c, :] if m == 0 else src.at[at_c, :]

            for step in range(1, n_col):
                where, source = (col + step) % n_col, (col + n_col - step) % n_col
                sems = (give_s.at[m, step], give_r.at[m, step])
                copies.append(remote(block_for(where), dst.at[col], *sems, (row, where)))
                arrivals.append(remote(block_for(where), dst.at[source], *sems, (row, where)))
            own.append(pltpu.make_async_copy(block_for(col), dst.at[col], keep_s.at[m]))
    if stage:
        peers = [(True, (row, (col + k) % n_col)) for k in range(1, n_col)]
    else:
        peers = line_peers()
    if stage == 2:
        peers += row_peers()
    shake(peers, [ok for ok, _ in peers])
    order = []
    for t in range(pairs):
        for d in (pairs - 1 - t, t):
            if d not in order:
                order.append(d)
    if local:
        micro, capacity = held.shape[2], held.shape[3]
        group = chosen.shape[1]
        upper = pair // (pairs // 2)
        turns = [(pairs - 1 - m) * (1 - upper) + m * upper for m in range(pairs)]
        owners = []
        for d in turns:
            owners += [d * 2 + 1 - core, d * 2 + core]

        def bring(n):
            return [
                pltpu.make_async_copy(
                    slots[e].at[:, :, pl.ds(pl.multiple_of(owners[n] * part, part), part)],
                    held.at[n % 2, e],
                    held_s.at[n % 2, e],
                )
                for e in range(local)
            ]

        def make(n, into):
            for c in bring(n):
                c.wait()
            if n + 1 < len(owners):
                for c in bring(n + 1):
                    c.start()
            steps = group // tile

            def step(i, _):
                g, at_row = i // steps, pl.multiple_of((i % steps) * tile, tile)
                total = None
                for e in range(local):
                    term = nn(
                        chosen[g, pl.ds(at_row, tile), e * capacity : (e + 1) * capacity],
                        held[n % 2, e, g],
                    )
                    total = term if total is None else total + term
                into[pl.ds(pl.multiple_of(i * tile, tile), tile), :] = total.astype(BF16)
                return 0

            lax.fori_loop(0, micro * steps, step, 0)

        def make_pair(m):
            d = turns[m]
            make(2 * m, give.at[d])
            for q in range(cuts):
                across(d, q).start()
            make(2 * m + 1, acc.at[d])

        for c in bring(0):
            c.start()

        def choose(i, _):
            steps = group // tile
            g, at_row = i // steps, pl.multiple_of((i % steps) * tile, tile)
            for e in range(local):
                slot = lax.broadcasted_iota(jnp.int32, (tile, capacity), 1)
                hit = slot == place[g, pl.ds(at_row, tile), e : e + 1]
                chosen[g, pl.ds(at_row, tile), e * capacity : (e + 1) * capacity] = jnp.where(
                    hit, 1.0, 0.0
                ).astype(BF16)
            return 0

        lax.fori_loop(0, micro * (group // tile), choose, 0)
    else:
        for d in order:
            for q in range(cuts):
                across(d, q).start()
                fetch(d, q).start()
    for c in copies + own:
        c.start()

    def add(q, into, *sources):
        def step(i, _):
            lines = pl.ds(pl.multiple_of(q * height + i * tile, tile), tile)
            total = sources[0][lines, :].astype(F32)
            for ref in sources[1:]:
                total = total + ref[lines, :].astype(F32)
            into[lines, :] = total.astype(into.dtype)
            return 0

        lax.fori_loop(0, height // tile, step, 0)

    def ready(d, q):
        if not local:
            fetch(d, q).wait()
        across(d, q).wait_recv()

    def go_right(d, q):
        ready(d, q)

        @pl.when(pair > 0)
        def _():
            right(d, q).wait_recv()
            add(q, acc.at[d], acc.at[d], side.at[d], from_left.at[d])

        @pl.when(pair == 0)
        def _():
            add(q, acc.at[d], acc.at[d], side.at[d])

        right(d, q).start()

    def go_left(d, q):
        ready(d, q)

        @pl.when(pair < pairs - 1)
        def _():
            left(d, q).wait_recv()
            add(q, acc.at[d], acc.at[d], side.at[d], from_right.at[d])

        @pl.when(pair == pairs - 1)
        def _():
            add(q, acc.at[d], acc.at[d], side.at[d])

        left(d, q).start()

    if local:
        half = pairs // 2
        for m in range(pairs):
            make_pair(m)
            for q in range(cuts):
                if m < pairs - 1:

                    @pl.when(pair == 0)
                    def _():
                        go_right(pairs - 1 - m, q)

                    @pl.when(pair == pairs - 1)
                    def _():
                        go_left(m, q)

                if m == 1:

                    @pl.when((pair > 0) & (pair < half))
                    def _():
                        go_right(pairs - 1, q)

                    @pl.when((pair >= half) & (pair < pairs - 1))
                    def _():
                        go_left(0, q)

    for t in range(pairs - 1):
        far, near = pairs - 1 - t, t
        go_far, go_near = far > pair, near < pair
        if local:
            go_far, go_near = go_far & (pair > 0), go_near & (pair < pairs - 1)
        if local and t == 0:
            go_far, go_near = go_far & (pair >= half), go_near & (pair < half)
        for q in range(cuts):

            @pl.when(go_far)
            def _():
                go_right(far, q)

            @pl.when(go_near)
            def _():
                go_left(near, q)

    for q in range(cuts):
        ready(pair, q)

        @pl.when(pair == 0)
        def _():
            left(pair, q).wait_recv()
            add(q, out, acc.at[pair], side.at[pair], from_right.at[pair])

        @pl.when(pair == pairs - 1)
        def _():
            right(pair, q).wait_recv()
            add(q, out, acc.at[pair], side.at[pair], from_left.at[pair])

        @pl.when((pair > 0) & (pair < pairs - 1))
        def _():
            left(pair, q).wait_recv()
            right(pair, q).wait_recv()
            add(q, out, acc.at[pair], side.at[pair], from_left.at[pair], from_right.at[pair])

    for d in range(pairs):
        for q in range(cuts):
            across(d, q).wait_send()

            @pl.when(pair < d)
            def _():
                right(d, q).wait_send()

            @pl.when(pair > d)
            def _():
                left(d, q).wait_send()

    for c in copies:
        c.wait_send()
    for c in arrivals:
        c.wait_recv()
    for c in own:
        c.wait()


def scatter_col(x, ident, stage=0, others=(), place=None):
    n_row, n_col = lax.axis_size("row"), lax.axis_size("col")
    pairs, per = n_col // 2, n_col // n_row
    local = 0 if place is None else len(x)
    if local:
        micro, group, _ = place.shape
        capacity = x[0].shape[1]
        rows, part = micro * group, x[0].shape[2] // n_col
    else:
        rows, part = x.shape[0], x.shape[1] // n_col
    cuts = 4 if rows % 1024 == 0 else 1
    dma = pltpu.SemaphoreType.DMA
    buffer = pltpu.VMEM((pairs, rows, part), BF16)
    scratch = [buffer] * 4 + [dma((pairs, cuts))] * 7
    if local:
        scratch += [
            buffer,
            pltpu.VMEM((micro, group, local * capacity), BF16),
            pltpu.VMEM((2, local, micro, capacity, part), BF16),
            dma((2, local)),
        ]
    out_shape = [jax.ShapeDtypeStruct((rows, part), F32)]
    if stage:
        extra, ring = others[0], n_row if stage == 2 else n_col
        out_shape.append(jax.ShapeDtypeStruct((ring,) + extra.shape, extra.dtype))
        scratch += [dma((ring,)), dma((ring,)), dma(())]
    if stage == 2:
        scratch += [dma((2, n_row)), dma((2, n_row)), dma((2,))]
        for value in others[1:]:
            out_shape.append(jax.ShapeDtypeStruct((n_row, per) + value.shape[1:], BF16))
    if stage == 3:
        heads, branch = others[1:]
        scratch += [dma((2, n_col)), dma((2, n_col)), dma((2,))]
        out_shape += [
            jax.ShapeDtypeStruct((n_col, 3, heads.shape[1] // n_col, heads.shape[2]), BF16),
            jax.ShapeDtypeStruct((n_col, branch.shape[0] // n_col, branch.shape[1]), BF16),
        ]
    first = [pl.BlockSpec(memory_space=pltpu.VMEM)] + [ANY] * local if local else [ANY]
    values = (place, *x) if local else (x,)
    return pl.pallas_call(
        functools.partial(scatter_body, part, stage, local),
        in_specs=first + [ANY] * len(others),
        out_specs=[pl.BlockSpec(memory_space=pltpu.VMEM)] + [ANY] * (len(out_shape) - 1),
        out_shape=out_shape,
        scratch_shapes=scratch,
        compiler_params=pltpu.CompilerParams(
            vmem_limit_bytes=VMEM_LIMIT, collective_id=ident, has_side_effects=True
        ),
        cost_estimate=pl.CostEstimate(
            flops=0, bytes_accessed=rows * part * n_col * 40, transcendentals=0
        ),
        name="scatter_col",
    )(*values, *others)


def shards(
    tokens,
    gain_attn,
    gain_ffn,
    gain_query,
    gain_key,
    w_query,
    w_key,
    w_value,
    w_out,
    w_router,
    w_gate,
    w_up,
    w_down,
    routes,
    lengths,
    cotangent,
):
    n_col = lax.axis_size("col")
    n_row = lax.axis_size("row")
    col = lax.axis_index("col")
    micro, spans = lengths.shape
    rows, part = tokens.shape
    group = rows // micro
    width = part * n_col
    head = gain_query.shape[0]
    local_exp = w_gate.shape[0]
    experts = local_exp * n_col
    topk = routes.shape[1]
    capacity = 2 * group * topk // experts
    local_heads = w_out.shape[0] // head
    hd = w_out.shape[0] * n_col
    scale = head ** (-0.5)

    def gather(value, axis_name, axis):
        return lax.all_gather(value, axis_name, axis=axis, tiled=True)

    def mine(value, axis):
        size = value.shape[axis] // n_col
        return lax.dynamic_slice_in_dim(value, col * size, size, axis)

    shared = w_down.shape[2]
    pair = 2 if local_exp % 2 == 0 else 1
    spans = [(0, pair)] + [(at, 1) for at in range(pair, local_exp)]
    big = {}
    for first, count in spans:
        whole = gather(pack(w_gate, w_up, w_down, first, count), "row", 2)
        for e in range(count):
            big[first + e] = (whole, e)
    inputs_low, gains, w_heads, rows_o, rows_r, *wide = front(
        tokens,
        jnp.stack([gain_attn, gain_ffn]),
        w_query,
        w_key,
        w_value,
        w_out,
        w_router.T,
        head,
        0,
    )

    segment, position, live = jax.vmap(lambda l: layout(l, group))(lengths)
    position = position.reshape(rows)
    live = live.reshape(rows)
    upstream_part = cotangent.astype(F32) * live[:, None]
    member = jnp.any(
        routes[:, None, :] == jnp.arange(experts, dtype=jnp.int32)[None, :, None], -1
    )
    member_f = member.astype(F32)
    member_loc = mine(member_f, 1).reshape(micro, group, local_exp)
    lower = (
        jnp.arange(group, dtype=jnp.int32)[:, None] > jnp.arange(group, dtype=jnp.int32)[None, :]
    ).astype(BF16)
    before = jnp.einsum("st,gte->gse", lower, member_loc.astype(BF16), preferred_element_type=F32)
    place = jnp.where(member_loc > 0, before, -1.0).astype(jnp.int32)
    counts = jnp.sum(member_loc, 1).astype(jnp.int32).T
    place_t = place.transpose(2, 0, 1)[:, :, None, :]

    inputs = inputs_low.astype(F32)
    scale_one = inverse_rms(inputs)
    normed = (inputs * scale_one * gains[0]).astype(BF16)
    all_heads = jnp.concatenate([w_heads[j] for j in range(3)], 1)
    query_pre, key_pre, value_pre = jnp.split(nn(normed, all_heads), 3, 1)
    shape = (rows, local_heads, head)
    cosine, sine = rope_tables(position, head)

    def head_norm(values, gain):
        return rotary(values * inverse_rms(values) * gain, cosine, sine)

    query_rot, query_pull = jax.vjp(head_norm, query_pre.reshape(shape), gain_query)
    key_rot, key_pull = jax.vjp(head_norm, key_pre.reshape(shape), gain_key)
    batch = (micro, group, local_heads, head)
    queries = query_rot.astype(BF16).reshape(batch)
    keys_low = key_rot.astype(BF16).reshape(batch)
    values_low = value_pre.astype(BF16).reshape(batch)
    same = (segment[:, :, None] == segment[:, None, :])[:, None]

    def scores_of():
        raw = jnp.einsum("gqhd,gkhd->ghqk", queries, keys_low, preferred_element_type=F32) * scale
        return jnp.where(same, raw, MASKED)

    scores = scores_of()
    highest = jnp.max(scores, -1, keepdims=True)
    log_total = highest + jnp.log(jnp.sum(jnp.exp(scores - highest), -1, keepdims=True))
    probs_low = jnp.exp(scores - log_total).astype(BF16)
    attended = jnp.einsum(
        "ghqk,gkhd->gqhd", probs_low, values_low, preferred_element_type=F32
    ).astype(BF16)
    attended_full, full_o, full_rt, upstream_low = middle_gather(
        [attended.reshape(rows, local_heads * head), rows_o, rows_r, upstream_part.astype(BF16)],
        (1, 0, 1, 1),
        1,
    )
    full_r = full_rt.T

    hidden = inputs + nn(attended_full, full_o)
    scale_two = inverse_rms(hidden)
    normed_ffn = (hidden * scale_two * gains[1]).astype(BF16)
    logits = nn(normed_ffn, full_r)
    peak = jnp.max(jnp.where(member, logits, -jnp.inf), -1, keepdims=True)
    raised = jnp.where(member, jnp.exp(jnp.where(member, logits - peak, 0.0)), 0.0)
    gates = raised / jnp.sum(raised, -1, keepdims=True)
    gate_t = mine(gates, 1).reshape(micro, group, local_exp).transpose(2, 0, 1)[:, :, None, :]
    upstream_full = upstream_low.reshape(micro, group, width)
    hn = normed_ffn.reshape(micro, group, width)

    outs, weight_grads, grad = [], [], None
    for e in range(local_exp):
        xe, dyr, hg, dgp, dup, ye, dxe, tok = expert_pass(
            counts[e],
            place_t[e],
            gate_t[e],
            hn,
            upstream_full,
            *big[e],
            capacity,
            shared,
        )
        held = () if e % pair == 0 else (grad,)
        grad = expert_grads(xe, dgp, dup, hg, dyr, shared, e % pair, pair, held)
        hn, upstream_full, ye, dxe, tok, grad = lax.optimization_barrier(
            (hn, upstream_full, ye, dxe, tok, grad)
        )
        outs.append((ye, dxe, tok))
        if e % pair == pair - 1:
            weight_grads.append(lax.psum_scatter(grad, "row", scatter_dimension=2, tiled=True))

    def tie(value, e):
        value, weight_grads[e] = lax.optimization_barrier((value, weight_grads[e]))
        return value

    row = lax.axis_index("row")
    back_sum, tok = scatter_col(
        [o[1] for o in outs], 2, 1, (jnp.stack([o[2] for o in outs]),), place
    )
    tok = tok.reshape((experts,) + tok.shape[2:])
    hidden_part = tokens.astype(F32) + nn(attended_full, mine(full_o, 1))
    gate_dots = tok[:, :, 0].reshape(experts, rows).T
    hidden_part = mine(hidden, 1)

    selected = gates * (gate_dots - jnp.sum(gates * gate_dots, -1, keepdims=True))
    logit_grad = selected.astype(BF16)
    router_part = mine(full_r, 0)
    normed_grad = back_sum + nt(logit_grad, router_part)
    grad_router = tn(mine(normed_ffn, 1), logit_grad)
    scaled_two = hidden_part * scale_two
    grad_gain_ffn = jnp.sum(normed_grad * scaled_two, 0)
    dot_two = jnp.sum(tok[:, :, 1].reshape(experts, rows), 0) + jnp.sum(
        logit_grad.astype(F32) * logits, 1
    )
    hidden_grad = (
        upstream_part
        + scale_two * (normed_grad * gain_ffn)
        - hidden_part * scale_two**2 * dot_two[:, None] / width
    )

    branch_grad = hidden_grad.astype(BF16)
    (attended_grad,) = scatter_col(nt(branch_grad, mine(full_o, 1)).astype(BF16), 3)
    attended_grad = attended_grad.astype(BF16).reshape(batch)
    grad_out = tn(attended_full, branch_grad)
    scores_again = scores_of()
    probs = jnp.exp(scores_again - log_total)
    probs_again = probs.astype(BF16)
    probs_grad = jnp.einsum(
        "gqhd,gkhd->ghqk", attended_grad, values_low, preferred_element_type=F32
    )
    values_grad = jnp.einsum(
        "ghqk,gqhd->gkhd", probs_again, attended_grad, preferred_element_type=F32
    )
    score_grad = (probs * (probs_grad - jnp.sum(probs_grad * probs, -1, keepdims=True))).astype(
        BF16
    )
    query_grad_rot = (
        jnp.einsum("ghqk,gkhd->gqhd", score_grad, keys_low, preferred_element_type=F32) * scale
    )
    key_grad_rot = (
        jnp.einsum("ghqk,gqhd->gkhd", score_grad, queries, preferred_element_type=F32) * scale
    )
    query_grad, gain_query_part = query_pull(query_grad_rot.reshape(shape))
    key_grad, gain_key_part = key_pull(key_grad_rot.reshape(shape))
    flat = (rows, local_heads * head)
    heads_grad = [
        v.reshape(flat).astype(BF16) for v in (query_grad, key_grad, values_grad)
    ]
    all_grads = jnp.concatenate(heads_grad, 1)
    back_heads = nt(all_grads, all_heads)
    pre = (query_pre, key_pre, value_pre)
    dot_part = sum(jnp.sum(g.astype(F32) * p, -1) for g, p in zip(heads_grad, pre))
    sums = jnp.concatenate([dot_part, gain_query_part, gain_key_part])
    sums = jnp.pad(sums, (0, -sums.shape[0] % 1024)).reshape(-1, 128)
    heads_weights = tn(normed, all_grads).astype(BF16)
    heads_weights = jnp.stack(jnp.split(heads_weights, 3, 1))
    back_heads, mixed_slots = lax.optimization_barrier(
        (back_heads.astype(BF16), [o[0] for o in outs])
    )
    mixed_sum, sums, heads_terms, out_terms = scatter_col(
        mixed_slots, 4, 3, (sums, heads_weights, grad_out.astype(BF16)), place
    )
    mixed = (hidden_part + mixed_sum).astype(BF16)
    sums = jnp.sum(sums, 0).reshape(-1)
    dot_one = sums[:rows]
    gain_attn_part = 0.0
    for m in range(3):
        for c in range(n_col):
            columns = wide[m][:, c * local_heads * head : (c + 1) * local_heads * head]
            gain_attn_part = gain_attn_part + jnp.sum(
                columns.astype(F32) * heads_terms[c, m].astype(F32), -1
            )
    smalls = jnp.concatenate(
        [
            gain_attn_part,
            grad_gain_ffn,
            sums[rows : rows + 2 * head],
            grad_router.T.reshape(-1),
        ]
    ).reshape(-1, 128)
    back_heads, mixed = lax.optimization_barrier((back_heads, mixed))
    normed_back, smalls, heads_terms, out_terms = scatter_col(
        tie(back_heads, 0), 5, 2, (smalls, heads_terms, out_terms)
    )
    scale_one_part = scale_one
    inputs_part = tokens.astype(F32)
    input_grad = (
        hidden_grad
        + scale_one_part * (normed_back * gain_attn)
        - inputs_part * scale_one_part**2 * dot_one[:, None] / width
    )

    held = ()
    for e, grad in enumerate(weight_grads):
        held = unpack(grad, held, e * pair, local_exp)
    grad_gate, grad_up, grad_down = held

    heads_terms = jnp.sum(heads_terms.astype(F32), 0)
    heads_sum = jnp.concatenate([heads_terms[j] for j in range(heads_terms.shape[0])], -1)
    grad_query, grad_key, grad_value = heads_sum[0], heads_sum[1], heads_sum[2]
    out_terms = jnp.sum(out_terms.astype(F32), 0)
    grad_out = jnp.concatenate([out_terms[j] for j in range(out_terms.shape[0])], -1)
    row = lax.axis_index("row")
    total = jnp.sum(smalls, 0).reshape(-1)
    grad_gain_attn, grad_gain_ffn = total[:part] / gain_attn, total[part : 2 * part]
    grad_gain_query = total[2 * part : 2 * part + head]
    grad_gain_key = total[2 * part + head : 2 * part + 2 * head]
    grad_router = lax.dynamic_slice_in_dim(
        total[2 * part + 2 * head :].reshape(experts, part), row * (experts // n_row), experts // n_row, 0
    ).T
    return (
        mixed,
        input_grad,
        grad_gain_attn,
        grad_gain_ffn,
        grad_gain_query,
        grad_gain_key,
        grad_query,
        grad_key,
        grad_value,
        grad_out,
        grad_router,
        grad_gate,
        grad_up,
        grad_down,
    )


def solution(mesh):
    placed = (
        P("row", "col"),
        P("col"),
        P("col"),
        P(),
        P(),
        P("col", "row"),
        P("col", "row"),
        P("col", "row"),
        P("col", "row"),
        P("col", "row"),
        P("col", "row", None),
        P("col", "row", None),
        P("col", None, "row"),
        P("row", None),
        P("row", None),
        P("row", "col"),
    )
    return jax.shard_map(
        shards,
        mesh=mesh,
        in_specs=placed,
        out_specs=(
            P("row", "col"),
            P("row", "col"),
            P("col"),
            P("col"),
            P(),
            P(),
            P("col", "row"),
            P("col", "row"),
            P("col", "row"),
            P("col", "row"),
            P("col", "row"),
            P("col", "row", None),
            P("col", "row", None),
            P("col", None, "row"),
        ),
        check_vma=False,
    )
```
